32 devices in a mesh: batch: 4 (over y, x), ctx: 4 (over z), wt: 2 (over core).
Axes of the slice: x: 2, y: 2, z: 4, core: 2. Of those that a mesh axis runs over, the one named last changes fastest.
Arguments:
- inputs: bfloat16 [8, 512, 768], P(('batch', 'wt'), 'ctx'), may hold values from -6 to 6
- prefix_keys: bfloat16 [8, 20, 768], P(('batch', 'wt')), may hold values from -8 to 8
- prefix_values: bfloat16 [8, 20, 768], P(('batch', 'wt')), may hold values from -6 to 6
- gain_attn: bfloat16 [768], P('wt'), may hold values from 0.099609375 to 1.8984375
- w_query: bfloat16 [768, 768], P('wt'), may hold values from -0.02734375 to 0.02734375
- w_key: bfloat16 [768, 768], P('wt'), may hold values from -0.21875 to 0.21875
- w_value: bfloat16 [768, 768], P('wt'), may hold values from -0.21875 to 0.21875
- w_out: bfloat16 [768, 768], P('wt'), may hold values from -2.5 to 2.5
- bias_table: bfloat16 [32, 12], P('wt'), may hold values from -5 to 5
- gain_ffn: bfloat16 [768], P('wt'), may hold values from 0.099609375 to 1.8984375
- w_in: bfloat16 [768, 3072], P('wt'), may hold values from -0.21875 to 0.21875
- w_back: bfloat16 [3072, 768], P('wt'), may hold values from -0.15625 to 0.15625
- buckets: int32 [1023], replicated, may hold values from 0 to 31
- out_grad: bfloat16 [8, 512, 768], P(('batch', 'wt'), 'ctx'), may hold values from -6 to 6
Outputs:
- outputs: bfloat16 [8, 512, 768], P(('batch', 'wt'), 'ctx')
- grad_inputs: bfloat16 [8, 512, 768], P(('batch', 'wt'), 'ctx')
- grad_prefix_keys: float32 [8, 20, 768], P(('batch', 'wt'))
- grad_prefix_values: float32 [8, 20, 768], P(('batch', 'wt'))
- grad_gain_attn: float32 [768], P('wt')
- grad_gain_ffn: float32 [768], P('wt')
- grad_bias_table: float32 [32, 12], P('wt')
- grad_query: float32 [768, 768], P('wt')
- grad_key: float32 [768, 768], P('wt')
- grad_value: float32 [768, 768], P('wt')
- grad_out: float32 [768, 768], P('wt')
- grad_in: float32 [768, 3072], P('wt')
- grad_back: float32 [3072, 768], P('wt')
The draws below stay inside these ranges and needn't reach their ends.
All inputs are finite; a program needn't handle non-finite values.
Results may differ from the reference program's by a relative error of at most 0.028.
Values may be sent and summed in bfloat16 or wider, within the bound.
No kernel may reach another device: no remote copies, remote signals or barrier semaphores. Data moves between devices by JAX's collectives and lax.ppermute only.
A program may use at most 128 MiB of HBM per device.

```python
import jax
import jax.numpy as jnp
from jax import lax

D = 768
H = 12
DH = 64
FF = 3072
NB = 32
MEM_ROWS = 20
KB = 256
LEN = 512
NSEQ = 8


def plant(values, own_key, least, largest):
    place = [jax.random.randint(jax.random.fold_in(own_key, axis), (), 0, length) for axis, length in enumerate(values.shape)]
    main_axis = values.shape.index(max(values.shape))
    neighbour = place[:main_axis] + [(place[main_axis] + 1) % values.shape[main_axis]] + place[main_axis + 1:]
    return values.at[tuple(place)].set(least).at[tuple(neighbour)].set(largest)


def block_scale(stream_key, extent, pieces, least, largest):
    loudness, own = 1.0, jax.random.fold_in(stream_key, 6)
    for dim, blocks in pieces:
        draws = jnp.exp(jax.random.uniform(jax.random.fold_in(own, dim), (blocks,), jnp.float32, least / len(pieces), largest / len(pieces)))
        loudness = loudness * jnp.repeat(draws, extent[dim] // blocks).reshape([-1 if axis == dim else 1 for axis in range(len(extent))])
    return loudness


def noise(own_key, extent, deviation, bound, split=(), kind=jnp.bfloat16):
    array = jax.random.normal(own_key, extent, jnp.float32) * deviation
    if len(split) > 0:
        array = block_scale(own_key, extent, split, -0.22, 0.18) * array
    return jnp.clip(array, min=-bound, max=bound).astype(kind)


def setup_inputs(seed: int = 0) -> dict:
    arg_keys = jax.random.split(jax.random.key(seed), 15)
    inputs = noise(arg_keys[0], (NSEQ, LEN, D), 1.0, 6.0, ((0, 8), (1, 4)))
    prefix_keys = noise(arg_keys[1], (NSEQ, MEM_ROWS, D), 1.5, 8.0, ((0, 8),))
    prefix_values = noise(arg_keys[2], (NSEQ, MEM_ROWS, D), 1.0, 6.0, ((0, 8),))
    gain_attn = jnp.clip(1.0 + 0.18 * jax.random.normal(arg_keys[3], (D,), jnp.float32), 0.099609375, 1.8984375).astype(jnp.bfloat16)
    w_query = noise(arg_keys[4], (D, D), (D * DH) ** -0.5, 0.02734375, ((0, 2),))
    w_key = noise(arg_keys[5], (D, D), D ** -0.5, 0.21875, ((0, 2),))
    w_value = noise(arg_keys[6], (D, D), D ** -0.5, 0.21875, ((0, 2),))
    w_out = noise(arg_keys[7], (D, D), (max(1, 4 * D // LEN)) ** -0.5, 2.5, ((0, 2),))
    bias_table = noise(arg_keys[8], (NB, H), 1.0, 5.0, ((0, 2),))
    gain_ffn = jnp.clip(1.0 + 0.18 * jax.random.normal(arg_keys[9], (D,), jnp.float32), 0.099609375, 1.8984375).astype(jnp.bfloat16)
    w_in = noise(arg_keys[10], (D, FF), D ** -0.5, 0.21875, ((0, 2),))
    w_back = noise(arg_keys[11], (FF, D), (FF // 2) ** -0.5, 0.15625, ((0, 2),))
    buckets = plant(jax.random.randint(arg_keys[12], (2 * LEN - 1,), 0, NB), jax.random.fold_in(arg_keys[12], 1), 0, NB - 1).astype(jnp.int32)
    out_grad = noise(arg_keys[13], (NSEQ, LEN, D), 1.0, 6.0, ((0, 8), (1, 4)))
    return dict(inputs=inputs, prefix_keys=prefix_keys, prefix_values=prefix_values, gain_attn=gain_attn, w_query=w_query, w_key=w_key, w_value=w_value, w_out=w_out, bias_table=bias_table, gain_ffn=gain_ffn, w_in=w_in, w_back=w_back, buckets=buckets, out_grad=out_grad)


@jax.custom_vjp
def low(v):
    return lax.optimization_barrier(v.astype(jnp.bfloat16)).astype(jnp.float32)

@jax.custom_vjp
def low_back(v):
    return v

def low_keep(v):
    return (low(v), None)

def low_pass(kept, grad):
    return (grad,)

def back_keep(v):
    return (v, None)

def back_low(kept, grad):
    return (low(grad),)
low.defvjp(low_keep, low_pass)
low_back.defvjp(back_keep, back_low)
EPS = 1e-06
HIGH = lax.Precision.HIGHEST

def rms_scale(values, gain):
    return values * lax.rsqrt(lax.optimization_barrier(jnp.mean(values * values, axis=-1, keepdims=True)) + EPS) * gain

def matmul(left, right):
    return jnp.dot(left, right, precision=HIGH)

def soft_rows(score):
    shifted = score - lax.optimization_barrier(jnp.max(score, axis=2, keepdims=True))
    weights = jnp.exp(shifted)
    return weights / lax.optimization_barrier(jnp.sum(weights, axis=2, keepdims=True))

def one_sequence(tokens, mem_keys, mem_values, gain_one, wq, wk, wv, wo, table, gain_two, w_first, w_second, buckets):
    normed1 = low(rms_scale(tokens, gain_one))
    query = low_back(low(matmul(normed1, wq))).reshape(LEN, H, DH)
    keys = low_back(low(matmul(normed1, wk))).reshape(LEN, H, DH)
    vals = low_back(low(matmul(normed1, wv))).reshape(LEN, H, DH)
    keys_mem = mem_keys.reshape(MEM_ROWS, H, DH)
    vals_mem = mem_values.reshape(MEM_ROWS, H, DH)
    offset_bias = table[buckets]

    def attend(start):
        query_block = lax.dynamic_slice_in_dim(query, start, KB, 0)
        rows = start + jnp.arange(KB, dtype=jnp.int32)
        cols = jnp.arange(LEN, dtype=jnp.int32)
        where = cols[None, :] - rows[:, None] + (LEN - 1)
        bias = jnp.transpose(offset_bias[where], (2, 0, 1))
        main = jnp.einsum('qhd,khd->hqk', query_block, keys, precision=HIGH) + bias
        front = jnp.einsum('qhd,khd->hqk', query_block, keys_mem, precision=HIGH)
        score = low_back(jnp.concatenate([front, main], axis=2))
        prob = low(soft_rows(score))
        mixed = jnp.einsum('hqk,khd->qhd', prob[:, :, :MEM_ROWS], vals_mem, precision=HIGH)
        mixed = mixed + jnp.einsum('hqk,khd->qhd', prob[:, :, MEM_ROWS:], vals, precision=HIGH)
        return mixed.reshape(KB, D)
    starts = jnp.arange(LEN // KB, dtype=jnp.int32) * KB
    attended = lax.map(jax.checkpoint(attend), starts).reshape(LEN, D)
    attended = low_back(low(attended))
    hidden = tokens + low_back(matmul(attended, wo))
    normed2 = low(rms_scale(hidden, gain_two))
    inner = low_back(matmul(normed2, w_first))
    gelu_out = low_back(low(jax.nn.gelu(inner, approximate=True)))
    return hidden + matmul(gelu_out, w_second)

def reference(inputs, prefix_keys, prefix_values, gain_attn, w_query, w_key, w_value, w_out, bias_table, gain_ffn, w_in, w_back, buckets, out_grad):
    floats = tuple((a.astype(jnp.float32) for a in (inputs, prefix_keys, prefix_values, gain_attn, w_query, w_key, w_value, w_out, bias_table, gain_ffn, w_in, w_back)))

    def forward(tokens, mem_keys, mem_values, gain_one, wq, wk, wv, wo, table, gain_two, w_first, w_second):

        def per_sequence(index):
            return one_sequence(tokens[index], mem_keys[index], mem_values[index], gain_one, wq, wk, wv, wo, table, gain_two, w_first, w_second, buckets)
        return lax.map(per_sequence, jnp.arange(NSEQ, dtype=jnp.int32))
    result, pull = jax.vjp(forward, *floats)
    grads = pull(out_grad.astype(jnp.float32))
    return (result.astype(jnp.bfloat16), grads[0].astype(jnp.bfloat16), grads[1], grads[2], grads[3], grads[9], grads[8], grads[4], grads[5], grads[6], grads[7], grads[10], grads[11])
```

```python
import functools

import jax
import jax.numpy as jnp
from jax import lax
from jax.experimental import pallas as pl
from jax.experimental.pallas import tpu as pltpu
from jax.sharding import PartitionSpec as P

EPS = 1e-06
F32 = jnp.float32
BF = jnp.bfloat16
LANES = 128


def nn(left, right):
    return lax.dot_general(left, right, (((1,), (0,)), ((), ())), preferred_element_type=F32)


def nt(left, right):
    return lax.dot_general(left, right, (((1,), (1,)), ((), ())), preferred_element_type=F32)


def tn(left, right):
    return lax.dot_general(left, right, (((0,), (0,)), ((), ())), preferred_element_type=F32)


def vmem(count):
    return [pl.BlockSpec(memory_space=pltpu.VMEM)] * count


def smem():
    return pl.BlockSpec(memory_space=pltpu.SMEM)


def shape(dims, kind):
    return jax.ShapeDtypeStruct(dims, kind)


def params(mib):
    return pltpu.CompilerParams(vmem_limit_bytes=mib << 20)


def flip(value, axis, size, step):
    return lax.ppermute(value, axis, [(i, i ^ step) for i in range(size)])


def gather_flip(value, axis, size):
    return [value] + [flip(value, axis, size, step) for step in range(1, size)]


def canonical(parts, index):
    whole = jnp.zeros((len(parts),) + parts[0].shape, parts[0].dtype)
    for step, part in enumerate(parts):
        whole = lax.dynamic_update_index_in_dim(whole, part, index ^ step, 0)
    return whole


def gather_wt(value, size):
    if size == 2:
        own = lax.axis_index("wt") == 0
        other = flip(value, "wt", 2, 1)
        return jnp.stack([jnp.where(own, value, other), jnp.where(own, other, value)])
    return lax.all_gather(value, "wt", axis=0)


def sum_wt(value, size):
    rows = value.shape[0] // size
    if size == 2:
        index = lax.axis_index("wt")
        mine = lax.dynamic_slice_in_dim(value, index * rows, rows, 0)
        theirs = lax.dynamic_slice_in_dim(value, (1 - index) * rows, rows, 0)
        return mine.astype(F32) + flip(theirs, "wt", 2, 1).astype(F32)
    return lax.psum_scatter(value, "wt", scatter_dimension=0, tiled=True).astype(F32)


def sum_flip(blocks, index, axis, size):
    total = lax.dynamic_index_in_dim(blocks, index, 0, keepdims=False).astype(F32)
    for step in range(1, size):
        block = lax.dynamic_index_in_dim(blocks, index ^ step, 0, keepdims=False)
        total = total + flip(block, axis, size, step).astype(F32)
    return total


def norm(values):
    inverse = lax.rsqrt(jnp.mean(values * values, axis=-1, keepdims=True) + EPS)
    return values * inverse, inverse


def one_hot_rows(bucket_row, buckets):
    ids = lax.broadcasted_iota(jnp.int32, (buckets, bucket_row.shape[1]), 0)
    return (ids == bucket_row).astype(F32)


def attend_kernel(nc, heads, hsize, mem, idx, *refs):
    xs = refs[:nc]
    wq, wk, wv, gain, pk, pv, tab, bucket_row = refs[nc : nc + 8]
    n1_ref, q_ref, k_ref, v_ref, pt_ref, pm_ref, mix_ref = refs[nc + 8 : nc + 15]
    outs = refs[nc + 15 : nc + 15 + nc]
    att_scr = refs[nc + 15 + nc]
    here = idx[0]
    rows = xs[0].shape[0]
    length = nc * rows
    for step in range(nc):
        scaled, _ = norm(xs[step][...].astype(F32))
        at = pl.multiple_of((here ^ step) * rows, rows)
        n1_ref[pl.ds(at, rows), :] = (scaled * gain[...]).astype(BF)
    normed = n1_ref[...]
    q_ref[...] = nn(normed, wq[...]).astype(BF)
    k_ref[...] = nn(normed, wk[...]).astype(BF)
    v_ref[...] = nn(normed, wv[...]).astype(BF)
    vals_t = v_ref[...].T
    pv_t = pv[...].astype(F32).T.astype(BF)
    hot = one_hot_rows(bucket_row[...], tab.shape[1])
    lines = nn(tab[...], hot)
    for h in range(heads):
        part = slice(h * hsize, (h + 1) * hsize)
        query = q_ref[:, part]
        line = jnp.broadcast_to(lines[h : h + 1, :], (LANES, 2 * length))
        spread = pltpu.roll(line, 0, 1, stride=1, stride_axis=0)
        bias = jnp.concatenate(
            [spread[:, length - at : 2 * length - at] for at in range(0, length, LANES)], axis=0
        )
        score = nt(k_ref[:, part], query) + bias
        front = nt(pk[:, part], query)
        top = jnp.maximum(
            jnp.max(score, axis=0, keepdims=True), jnp.max(front, axis=0, keepdims=True)
        )
        score = jnp.exp(score - top)
        front = jnp.exp(front - top)
        total = jnp.sum(score, axis=0, keepdims=True) + jnp.sum(front, axis=0, keepdims=True)
        scale = 1.0 / total
        prob = (score * scale).astype(BF)
        prob_mem = (front * scale).astype(BF)
        pt_ref[h] = prob
        pm_ref[h] = prob_mem
        mix_ref[part, :] = nn(vals_t[part, :], prob) + nn(pv_t[part, :], prob_mem)
    att_scr[...] = mix_ref[...].T.astype(BF)
    for step in range(nc):
        at = pl.multiple_of((here ^ step) * rows, rows)
        outs[step][...] = att_scr[pl.ds(at, rows), :]


def attend(nc, heads, hsize, index, xs, wq, wk, wv, gain, pk, pv, tab, bucket_row):
    rows, width = xs[0].shape
    length = rows * nc
    cols = heads * hsize
    mem = pk.shape[0]
    out = [
        shape((length, width), BF),
        shape((length, cols), BF),
        shape((length, cols), BF),
        shape((length, cols), BF),
        shape((heads, length, length), BF),
        shape((heads, mem, length), BF),
        shape((cols, length), F32),
    ] + [shape((rows, cols), BF)] * nc
    return pl.pallas_call(
        functools.partial(attend_kernel, nc, heads, hsize, mem),
        out_shape=out,
        in_specs=[smem()] + vmem(nc + 8),
        out_specs=vmem(len(out)),
        scratch_shapes=[pltpu.VMEM((length, cols), BF)],
        compiler_params=params(48),
        name="attend",
    )(index, *xs, wq, wk, wv, gain, pk, pv, tab, bucket_row)


def branch_kernel(nc, idx, *refs):
    parts = refs[:nc]
    x, wo, gain = refs[nc : nc + 3]
    hidden_ref, n2_ref, att_ref = refs[nc + 3 : nc + 6]
    here = idx[0]
    cols = parts[0].shape[1]
    for step in range(nc):
        att_ref[here ^ step] = parts[step][...]
    hidden = x[...].astype(F32)
    for c in range(nc):
        hidden = hidden + nn(att_ref[c], wo[c * cols : (c + 1) * cols, :])
    hidden_ref[...] = hidden
    scaled, _ = norm(hidden)
    n2_ref[...] = (scaled * gain[...]).astype(BF)


def branch(nc, index, parts, x, wo, gain):
    rows, cols = parts[0].shape
    out = [shape(x.shape, F32), shape(x.shape, BF), shape((nc, rows, cols), BF)]
    return pl.pallas_call(
        functools.partial(branch_kernel, nc),
        out_shape=out,
        in_specs=[smem()] + vmem(nc + 3),
        out_specs=vmem(3),
        compiler_params=params(32),
        name="branch",
    )(index, *parts, x, wo, gain)


def branch_back_kernel(nb, nc, idx, *refs):
    parts = refs[:nb]
    hidden_ref, gain, g, wo = refs[nb : nb + 4]
    grad_ref, low_ref = refs[nb + 4 : nb + 6]
    outs = refs[nb + 6 : nb + 6 + nc]
    here = idx[0]
    cols = outs[0].shape[1]
    grad_norm = parts[0][...].astype(F32)
    for part in parts[1:]:
        grad_norm = grad_norm + part[...].astype(F32)
    scaled, inverse = norm(hidden_ref[...])
    e = grad_norm * gain[...]
    grad = g[...].astype(F32) + inverse * (
        e - scaled * jnp.mean(e * scaled, axis=-1, keepdims=True)
    )
    grad_ref[...] = grad
    low = grad.astype(BF)
    low_ref[...] = low
    for step in range(nc):
        at = pl.multiple_of((here ^ step) * cols, 8)
        outs[step][...] = nt(low, wo[pl.ds(at, cols), :]).astype(BF)


def branch_back(nb, nc, index, parts, hidden, gain, g, wo):
    rows, width = hidden.shape
    cols = width // nc
    out = [shape((rows, width), F32), shape((rows, width), BF)] + [shape((rows, cols), BF)] * nc
    return pl.pallas_call(
        functools.partial(branch_back_kernel, nb, nc),
        out_shape=out,
        in_specs=[smem()] + vmem(nb + 4),
        out_specs=vmem(len(out)),
        compiler_params=params(32),
        name="branch_back",
    )(index, *parts, hidden, gain, g, wo)


MEM_K, MEM_V, MEM_END = 0, 32, 64


def attend_back_kernel(nc, heads, hsize, idx, *refs):
    gms = refs[:nc]
    pt, pm, q, k, v, mix, pk, pv, bucket_row = refs[nc : nc + 9]
    grad_ref, table_ref = refs[nc + 9 : nc + 11]
    outs = refs[nc + 11 : nc + 11 + nc]
    gm_scr, gqt_scr, acc = refs[nc + 11 + nc :]
    here = idx[0]
    rows, cols = gms[0].shape
    length = rows * nc
    mem = pk.shape[0]
    for step in range(nc):
        at = pl.multiple_of((here ^ step) * rows, rows)
        gm_scr[pl.ds(at, rows), :] = gms[step][...]
    gm_t = gm_scr[...].T
    keys_t = k[...].T
    pk_t = pk[...].astype(F32).T.astype(BF)
    lines = []
    for h in range(heads):
        part = slice(h * hsize, (h + 1) * hsize)
        gm = gm_scr[:, part]
        query = q[:, part]
        spread = jnp.sum(gm_t[part, :].astype(F32) * mix[part, :], axis=0, keepdims=True)
        prob = pt[h]
        prob_mem = pm[h]
        score = prob.astype(F32) * (nt(v[:, part], gm) - spread)
        front = (prob_mem.astype(F32) * (nt(pv[:, part], gm) - spread)).astype(BF)
        low = score.astype(BF)
        gqt_scr[part, :] = nn(keys_t[part, :], low) + nn(pk_t[part, :], front)
        grad_ref[:, cols + h * hsize : cols + (h + 1) * hsize] = nn(low, query).astype(BF)
        grad_ref[:, 2 * cols + h * hsize : 2 * cols + (h + 1) * hsize] = nn(prob, gm).astype(BF)
        mem_k = nn(front, query).astype(BF)
        mem_v = nn(prob_mem, gm).astype(BF)
        for step in range(nc):
            outs[step][3 * rows + MEM_K : 3 * rows + MEM_K + mem, part] = mem_k
            outs[step][3 * rows + MEM_V : 3 * rows + MEM_V + mem, part] = mem_v
        acc[...] = jnp.zeros_like(acc)
        for at in range(0, length, LANES):
            acc[:, length - at : 2 * length - at] += score[at : at + LANES, :]
        fold = acc[...]
        half = LANES // 2
        while half >= 8:
            fold = fold[:half] + pltpu.roll(fold[half:], 2 * length - half, 1)
            half //= 2
        line = fold[0:1]
        for i in range(1, 8):
            line = line + pltpu.roll(fold[i : i + 1], 2 * length - i, 1)
        lines.append(line)
    lines.append(jnp.zeros((8 - heads, 2 * length), F32))
    hot = one_hot_rows(bucket_row[...], table_ref.shape[0])
    table_ref[...] = lax.dot_general(
        hot,
        jnp.concatenate(lines, axis=0),
        (((1,), (1,)), ((), ())),
        precision=lax.Precision.HIGHEST,
        preferred_element_type=F32,
    )
    grad_ref[:, :cols] = gqt_scr[...].T.astype(BF)
    for step in range(nc):
        at = pl.multiple_of((here ^ step) * rows, rows)
        for p in range(3):
            outs[step][p * rows : (p + 1) * rows, :] = grad_ref[
                pl.ds(at, rows), p * cols : (p + 1) * cols
            ]


def attend_back(nc, heads, hsize, index, gms, pt, pm, q, k, v, mix, pk, pv, bucket_row, nbuck):
    rows, cols = gms[0].shape
    length = rows * nc
    out = [shape((length, 3 * cols), BF), shape((nbuck, 8), F32)] + [
        shape((3 * rows + MEM_END, cols), BF)
    ] * nc
    return pl.pallas_call(
        functools.partial(attend_back_kernel, nc, heads, hsize),
        out_shape=out,
        in_specs=[smem()] + vmem(nc + 9),
        out_specs=vmem(len(out)),
        scratch_shapes=[
            pltpu.VMEM((length, cols), BF),
            pltpu.VMEM((cols, length), F32),
            pltpu.VMEM((LANES, 2 * length), F32),
        ],
        compiler_params=params(48),
        name="attend_back",
    )(index, *gms, pt, pm, q, k, v, mix, pk, pv, bucket_row)


def input_back_kernel(nc, mem, idx, *refs):
    parts = refs[:nc]
    x, wq, wk, wv, gain, grad_hidden = refs[nc : nc + 6]
    out_ref, memk_ref, memv_ref = refs[nc + 6 : nc + 9]
    scr = refs[nc + 9]
    here = idx[0]
    rows = x.shape[0]
    for step in range(nc):
        scr[here ^ step] = parts[step][...]

    def wide(at, count):
        return jnp.concatenate([scr[c, at : at + count, :] for c in range(nc)], axis=1)

    grad_norm = (
        nt(wide(0, rows), wq[...])
        + nt(wide(rows, rows), wk[...])
        + nt(wide(2 * rows, rows), wv[...])
    )
    scaled, inverse = norm(x[...].astype(F32))
    e = grad_norm * gain[...]
    grad = grad_hidden[...] + inverse * (
        e - scaled * jnp.mean(e * scaled, axis=-1, keepdims=True)
    )
    out_ref[...] = grad.astype(BF)
    memk_ref[...] = wide(3 * rows + MEM_K, mem).astype(F32)
    memv_ref[...] = wide(3 * rows + MEM_V, mem).astype(F32)


def input_back(nc, mem, index, parts, x, wq, wk, wv, gain, grad_hidden):
    rows, width = x.shape
    out = [shape((rows, width), BF), shape((mem, width), F32), shape((mem, width), F32)]
    return pl.pallas_call(
        functools.partial(input_back_kernel, nc, mem),
        out_shape=out,
        in_specs=[smem()] + vmem(nc + 6),
        out_specs=vmem(3),
        scratch_shapes=[pltpu.VMEM((nc,) + parts[0].shape, BF)],
        compiler_params=params(32),
        name="input_back",
    )(index, *parts, x, wq, wk, wv, gain, grad_hidden)


def shards(
    sizes,
    inputs,
    prefix_keys,
    prefix_values,
    gain_attn,
    w_query,
    w_key,
    w_value,
    w_out,
    bias_table,
    gain_ffn,
    w_in,
    w_back,
    buckets,
    out_grad,
):
    nb, nc, nw = sizes
    b, c, w = lax.axis_index("batch"), lax.axis_index("ctx"), lax.axis_index("wt")
    x, g = inputs[0], out_grad[0]
    rows, width = x.shape
    all_heads = bias_table.shape[1]
    heads = all_heads // nc
    hsize = width // all_heads
    cols = heads * hsize
    mem = prefix_keys.shape[1]
    length = rows * nc
    part = width // nw
    ff_own = w_back.shape[0]
    ff_part = ff_own // nb
    nbuck = bias_table.shape[0] * nw
    index_c = jnp.reshape(c, (1,))

    xs = gather_flip(x, "ctx", nc)
    wq = gather_wt(w_query, nw).reshape(width, width)
    wk = gather_wt(w_key, nw).reshape(width, width)
    wv = gather_wt(w_value, nw).reshape(width, width)
    small = gather_wt(
        jnp.concatenate([gain_attn, gain_ffn, bias_table.reshape(-1)]).reshape(1, -1), nw
    ).reshape(nw, -1)
    gain_one = small[:, :part].reshape(1, width).astype(F32)
    gain_two = small[:, part : 2 * part].reshape(1, width).astype(F32)
    table = small[:, 2 * part :].reshape(nbuck, all_heads)
    wo = gather_wt(w_out, nw).reshape(width, width)
    in_cut = jnp.concatenate(
        [
            lax.dynamic_slice_in_dim(w_in, o * ff_own + b * ff_part, ff_part, 1)
            for o in range(nw)
        ],
        axis=1,
    )
    w_first = gather_wt(in_cut, nw).reshape(width, nw * ff_part)
    back_cut = lax.dynamic_slice_in_dim(w_back, b * ff_part, ff_part, 0)
    w_second = gather_wt(back_cut, nw).reshape(nw * ff_part, width)
    gs = gather_flip(g, "batch", nb)

    def head_cols(value):
        return lax.dynamic_slice_in_dim(value, c * cols, cols, 1)

    pk, pv = head_cols(prefix_keys[0]), head_cols(prefix_values[0])
    tab = jnp.pad(
        lax.dynamic_slice_in_dim(table, c * heads, heads, 1).T.astype(F32), ((0, 8 - heads), (0, 0))
    )
    bucket_row = jnp.pad(buckets[::-1].reshape(1, -1), ((0, 0), (1, 0)), constant_values=-1)

    (normed1, q, k, v, pt, pm, mix, *mixed) = attend(
        nc, heads, hsize, index_c, xs, head_cols(wq), head_cols(wk), head_cols(wv),
        gain_one, pk, pv, tab, bucket_row,
    )
    mixed = mixed[:1] + [flip(mixed[s], "ctx", nc, s) for s in range(1, nc)]
    hidden, normed2, attended = branch(nc, index_c, mixed, x, wo, gain_two)

    n2 = jnp.concatenate(gather_flip(normed2, "batch", nb), axis=0)
    g_all = jnp.concatenate(gs, axis=0)
    inner = nn(n2, w_first)
    act_value, act_pull = jax.vjp(functools.partial(jax.nn.gelu, approximate=True), inner)
    act = act_value.astype(BF)
    grad_act = nt(g_all, w_second)
    grad_inner = act_pull(grad_act)[0].astype(BF)
    part_norm = nt(grad_inner, w_first).astype(BF)
    part_out = nn(act, w_second).astype(BF)
    grad_second = tn(act, g_all).astype(BF)
    grad_first = tn(n2, grad_inner).astype(BF)

    def cut(value, s):
        return value[s * rows : (s + 1) * rows]

    norm_parts = [cut(part_norm, 0)] + [
        flip(cut(part_norm, s), "batch", nb, s) for s in range(1, nb)
    ]
    (grad_hidden, grad_low, *gms) = branch_back(
        nb, nc, index_c, norm_parts, hidden, gain_two, g, wo
    )
    gms = gms[:1] + [flip(gms[s], "ctx", nc, s) for s in range(1, nc)]
    (grad_heads, grad_table, *sends) = attend_back(
        nc, heads, hsize, index_c, gms, pt, pm, q, k, v, mix, pk, pv, bucket_row, nbuck
    )
    sends = sends[:1] + [flip(sends[s], "ctx", nc, s) for s in range(1, nc)]
    grad_x, grad_memk, grad_memv = input_back(
        nc, mem, index_c, sends, x, wq, wk, wv, gain_one, grad_hidden
    )

    result = hidden + cut(part_out, 0).astype(F32)
    for s in range(1, nb):
        result = result + flip(cut(part_out, s), "batch", nb, s).astype(F32)

    def ctx_total(value):
        own = sum_wt(value, nw)
        size = own.shape[0] // nc
        own = sum_flip(own.astype(BF).reshape(nc, size, own.shape[1]), c, "ctx", nc)
        whole = canonical(gather_flip(own.astype(BF), "ctx", nc), c)
        return whole.reshape(nc * size, -1)

    second = gather_flip(ctx_total(grad_second), "batch", nb)
    out_second = canonical([p.astype(F32) for p in second], b).reshape(ff_own, width)
    first = gather_flip(ctx_total(grad_first), "batch", nb)
    out_first = jnp.zeros((part, nw * ff_own), F32)
    for s, piece in enumerate(first):
        for o in range(nw):
            out_first = lax.dynamic_update_slice(
                out_first,
                piece[:, o * ff_part : (o + 1) * ff_part].astype(F32),
                (0, o * ff_own + (b ^ s) * ff_part),
            )

    grad_wo = jnp.einsum("cqd,qe->cde", attended, grad_low, preferred_element_type=F32)
    own_wo = sum_wt(grad_wo.astype(BF).reshape(width, width), nw).astype(BF)
    own_wo = sum_flip(own_wo.reshape(nc, part // nc, width), c, "ctx", nc).astype(BF)
    own_wo = sum_flip(own_wo.reshape(nb, part // nc // nb, width), b, "batch", nb).astype(BF)
    own_wo = canonical(gather_flip(own_wo, "batch", nb), b).reshape(part // nc, width)
    out_wo = canonical(gather_flip(own_wo, "ctx", nc), c).reshape(part, width).astype(F32)

    grad_qkv = sum_wt(tn(normed1, grad_heads).astype(BF), nw).astype(BF)
    line = jnp.pad(grad_table[:, :heads].reshape(1, -1), ((0, 15), (0, 3 * cols - heads * nbuck)))
    if nw == 2:
        line = line.astype(BF)
        line = line.astype(F32) + flip(line, "wt", 2, 1).astype(F32)
    else:
        line = lax.psum(line, "wt")
    size = part // nb
    blocks = jnp.concatenate(
        [
            grad_qkv.reshape(nb, size, 3 * cols),
            jnp.broadcast_to(line.astype(BF)[None], (nb, 16, 3 * cols)),
        ],
        axis=1,
    )
    block = sum_flip(blocks, b, "batch", nb).astype(BF)
    pieces = canonical(gather_flip(block, "ctx", nc), c)
    table_sum = pieces[:, size, : heads * nbuck].astype(F32).reshape(nc, nbuck, heads)
    table_sum = jnp.transpose(table_sum, (1, 0, 2)).reshape(nbuck, all_heads)
    own_buckets = nbuck // nw
    out_table = lax.dynamic_slice_in_dim(table_sum, w * own_buckets, own_buckets, 0)
    wide = canonical(gather_flip(pieces[:, :size], "batch", nb), b)
    wide = wide.reshape(nb, nc, size, 3, cols)
    wide = jnp.transpose(wide, (3, 0, 2, 1, 4)).reshape(3, part, width).astype(F32)
    out_q, out_k, out_v = wide[0], wide[1], wide[2]

    def gain_sum(pairs, gain):
        total = sum(jnp.sum(left * right.astype(F32), axis=1) for left, right in pairs)
        return total / gain.astype(F32)

    gain_two_grad = gain_sum([(out_first, w_in)], gain_ffn)
    gain_one_grad = gain_sum([(out_q, w_query), (out_k, w_key), (out_v, w_value)], gain_attn)
    return (
        result.astype(BF)[None],
        grad_x[None],
        grad_memk[None],
        grad_memv[None],
        gain_one_grad,
        gain_two_grad,
        out_table,
        out_q,
        out_k,
        out_v,
        out_wo,
        out_first,
        out_second,
    )


def solution(mesh):
    tokens = P(("batch", "wt"), "ctx", None)
    memory = P(("batch", "wt"), None, None)
    matrix = P("wt", None)
    vector = P("wt")
    sizes = (mesh.shape["batch"], mesh.shape["ctx"], mesh.shape["wt"])
    return jax.shard_map(
        functools.partial(shards, sizes),
        mesh=mesh,
        in_specs=(
            tokens, memory, memory, vector, matrix, matrix, matrix, matrix, matrix, vector,
            matrix, matrix, P(), tokens,
        ),
        out_specs=(
            tokens, tokens, memory, memory, vector, vector, matrix, matrix, matrix, matrix,
            matrix, matrix, matrix,
        ),
        check_vma=False,
    )
```

```python
import functools

import jax
import jax.numpy as jnp
from jax import lax
from jax.experimental import pallas as pl
from jax.experimental.pallas import tpu as pltpu
from jax.sharding import PartitionSpec as P

EPS = 1e-06
F32 = jnp.float32
BF = jnp.bfloat16
LANES = 128


def nn(left, right):
    return lax.dot_general(left, right, (((1,), (0,)), ((), ())), preferred_element_type=F32)


def nt(left, right):
    return lax.dot_general(left, right, (((1,), (1,)), ((), ())), preferred_element_type=F32)


def tn(left, right):
    return lax.dot_general(left, right, (((0,), (0,)), ((), ())), preferred_element_type=F32)


def vmem(count):
    return [pl.BlockSpec(memory_space=pltpu.VMEM)] * count


def smem():
    return pl.BlockSpec(memory_space=pltpu.SMEM)


def shape(dims, kind):
    return jax.ShapeDtypeStruct(dims, kind)


def params(mib):
    return pltpu.CompilerParams(vmem_limit_bytes=mib << 20)


def flip(value, axis, size, step):
    return lax.ppermute(value, axis, [(i, i ^ step) for i in range(size)])


def gather_flip(value, axis, size):
    return [value] + [flip(value, axis, size, step) for step in range(1, size)]


def canonical(parts, index):
    whole = jnp.zeros((len(parts),) + parts[0].shape, parts[0].dtype)
    for step, part in enumerate(parts):
        whole = lax.dynamic_update_index_in_dim(whole, part, index ^ step, 0)
    return whole


def gather_wt(value, size):
    if size == 2:
        own = lax.axis_index("wt") == 0
        other = flip(value, "wt", 2, 1)
        return jnp.stack([jnp.where(own, value, other), jnp.where(own, other, value)])
    return lax.all_gather(value, "wt", axis=0)


def sum_wt(value, size):
    rows = value.shape[0] // size
    if size == 2:
        index = lax.axis_index("wt")
        mine = lax.dynamic_slice_in_dim(value, index * rows, rows, 0)
        theirs = lax.dynamic_slice_in_dim(value, (1 - index) * rows, rows, 0)
        return mine.astype(F32) + flip(theirs, "wt", 2, 1).astype(F32)
    return lax.psum_scatter(value, "wt", scatter_dimension=0, tiled=True).astype(F32)


def sum_flip(blocks, index, axis, size):
    total = lax.dynamic_index_in_dim(blocks, index, 0, keepdims=False).astype(F32)
    for step in range(1, size):
        block = lax.dynamic_index_in_dim(blocks, index ^ step, 0, keepdims=False)
        total = total + flip(block, axis, size, step).astype(F32)
    return total


def after(value, *earlier):
    return lax.optimization_barrier((value, *earlier))[0]


def pair(mine, theirs, bit, axis):
    first = jnp.where(bit == 0, mine, theirs)
    second = jnp.where(bit == 0, theirs, mine)
    return jnp.stack([first, second], axis=axis)


def halves(value, bit, axis=0):
    mine = lax.dynamic_index_in_dim(value, bit, axis, keepdims=False)
    theirs = lax.dynamic_index_in_dim(value, 1 - bit, axis, keepdims=False)
    return mine, theirs


def add(left, right):
    return (left.astype(F32) + right.astype(F32)).astype(BF)


def halve(value, bit, axis, name, step):
    mine, theirs = halves(value, bit, axis)
    return add(mine, flip(theirs, name, 4, step))


def norm(values):
    inverse = lax.rsqrt(jnp.mean(values * values, axis=-1, keepdims=True) + EPS)
    return values * inverse, inverse


def one_hot_rows(bucket_row, buckets):
    ids = lax.broadcasted_iota(jnp.int32, (buckets, bucket_row.shape[1]), 0)
    return (ids == bucket_row).astype(F32)


def attend_kernel(nc, heads, hsize, mem, idx, *refs):
    xs = refs[:nc]
    wq, wk, wv, gain, pk, pv, tab, bucket_row = refs[nc : nc + 8]
    n1_ref, q_ref, k_ref, v_ref, pt_ref, pm_ref, mix_ref = refs[nc + 8 : nc + 15]
    outs = refs[nc + 15 : nc + 15 + nc]
    att_scr = refs[nc + 15 + nc]
    here = idx[0]
    rows = xs[0].shape[0]
    length = nc * rows
    for step in range(nc):
        scaled, _ = norm(xs[step][...].astype(F32))
        at = pl.multiple_of((here ^ step) * rows, rows)
        n1_ref[pl.ds(at, rows), :] = (scaled * gain[...]).astype(BF)
    normed = n1_ref[...]
    q_ref[...] = nn(normed, wq[...]).astype(BF)
    k_ref[...] = nn(normed, wk[...]).astype(BF)
    v_ref[...] = nn(normed, wv[...]).astype(BF)
    vals_t = v_ref[...].T
    pv_t = pv[...].astype(F32).T.astype(BF)
    hot = one_hot_rows(bucket_row[...], tab.shape[1])
    lines = nn(tab[...], hot)
    for h in range(heads):
        part = slice(h * hsize, (h + 1) * hsize)
        query = q_ref[:, part]
        line = jnp.broadcast_to(lines[h : h + 1, :], (LANES, 2 * length))
        spread = pltpu.roll(line, 0, 1, stride=1, stride_axis=0)
        bias = jnp.concatenate(
            [spread[:, length - at : 2 * length - at] for at in range(0, length, LANES)], axis=0
        )
        score = nt(k_ref[:, part], query) + bias
        front = nt(pk[:, part], query)
        top = jnp.maximum(
            jnp.max(score, axis=0, keepdims=True), jnp.max(front, axis=0, keepdims=True)
        )
        score = jnp.exp(score - top)
        front = jnp.exp(front - top)
        total = jnp.sum(score, axis=0, keepdims=True) + jnp.sum(front, axis=0, keepdims=True)
        scale = 1.0 / total
        prob = (score * scale).astype(BF)
        prob_mem = (front * scale).astype(BF)
        pt_ref[h] = prob
        pm_ref[h] = prob_mem
        mix_ref[part, :] = nn(vals_t[part, :], prob) + nn(pv_t[part, :], prob_mem)
    att_scr[...] = mix_ref[...].T.astype(BF)
    for step in range(nc):
        at = pl.multiple_of((here ^ step) * rows, rows)
        outs[step][...] = att_scr[pl.ds(at, rows), :]


def attend(nc, heads, hsize, index, xs, wq, wk, wv, gain, pk, pv, tab, bucket_row):
    rows, width = xs[0].shape
    length = rows * nc
    cols = heads * hsize
    mem = pk.shape[0]
    out = [
        shape((length, width), BF),
        shape((length, cols), BF),
        shape((length, cols), BF),
        shape((length, cols), BF),
        shape((heads, length, length), BF),
        shape((heads, mem, length), BF),
        shape((cols, length), F32),
    ] + [shape((rows, cols), BF)] * nc
    return pl.pallas_call(
        functools.partial(attend_kernel, nc, heads, hsize, mem),
        out_shape=out,
        in_specs=[smem()] + vmem(nc + 8),
        out_specs=vmem(len(out)),
        scratch_shapes=[pltpu.VMEM((length, cols), BF)],
        compiler_params=params(48),
        name="attend",
    )(index, *xs, wq, wk, wv, gain, pk, pv, tab, bucket_row)


def branch_kernel(nc, idx, *refs):
    parts = refs[:nc]
    x, wo, gain = refs[nc : nc + 3]
    hidden_ref, n2_ref, att_ref = refs[nc + 3 : nc + 6]
    here = idx[0]
    cols = parts[0].shape[1]
    for step in range(nc):
        att_ref[here ^ step] = parts[step][...]
    hidden = x[...].astype(F32)
    for c in range(nc):
        hidden = hidden + nn(att_ref[c], wo[c * cols : (c + 1) * cols, :])
    hidden_ref[...] = hidden
    scaled, _ = norm(hidden)
    n2_ref[...] = (scaled * gain[...]).astype(BF)


def branch(nc, index, parts, x, wo, gain):
    rows, cols = parts[0].shape
    out = [shape(x.shape, F32), shape(x.shape, BF), shape((nc, rows, cols), BF)]
    return pl.pallas_call(
        functools.partial(branch_kernel, nc),
        out_shape=out,
        in_specs=[smem()] + vmem(nc + 3),
        out_specs=vmem(3),
        compiler_params=params(32),
        name="branch",
    )(index, *parts, x, wo, gain)


def branch_back_kernel(nb, nc, idx, *refs):
    parts = refs[:nb]
    hidden_ref, gain, g, wo = refs[nb : nb + 4]
    grad_ref, low_ref = refs[nb + 4 : nb + 6]
    outs = refs[nb + 6 : nb + 6 + nc]
    here = idx[0]
    cols = outs[0].shape[1]
    grad_norm = parts[0][...].astype(F32)
    for part in parts[1:]:
        grad_norm = grad_norm + part[...].astype(F32)
    scaled, inverse = norm(hidden_ref[...])
    e = grad_norm * gain[...]
    grad = g[...].astype(F32) + inverse * (
        e - scaled * jnp.mean(e * scaled, axis=-1, keepdims=True)
    )
    grad_ref[...] = grad
    low = grad.astype(BF)
    low_ref[...] = low
    for step in range(nc):
        at = pl.multiple_of((here ^ step) * cols, 8)
        outs[step][...] = nt(low, wo[pl.ds(at, cols), :]).astype(BF)


def branch_back(nb, nc, index, parts, hidden, gain, g, wo):
    rows, width = hidden.shape
    cols = width // nc
    out = [shape((rows, width), F32), shape((rows, width), BF)] + [shape((rows, cols), BF)] * nc
    return pl.pallas_call(
        functools.partial(branch_back_kernel, nb, nc),
        out_shape=out,
        in_specs=[smem()] + vmem(nb + 4),
        out_specs=vmem(len(out)),
        compiler_params=params(32),
        name="branch_back",
    )(index, *parts, hidden, gain, g, wo)


MEM_K, MEM_V, MEM_END = 0, 32, 64


def attend_back_kernel(nc, heads, hsize, idx, *refs):
    gms = refs[:nc]
    pt, pm, q, k, v, mix, pk, pv, bucket_row = refs[nc : nc + 9]
    grad_ref, table_ref = refs[nc + 9 : nc + 11]
    outs = refs[nc + 11 : nc + 11 + nc]
    gm_scr, gqt_scr, acc = refs[nc + 11 + nc :]
    here = idx[0]
    rows, cols = gms[0].shape
    length = rows * nc
    mem = pk.shape[0]
    for step in range(nc):
        at = pl.multiple_of((here ^ step) * rows, rows)
        gm_scr[pl.ds(at, rows), :] = gms[step][...]
    gm_t = gm_scr[...].T
    keys_t = k[...].T
    pk_t = pk[...].astype(F32).T.astype(BF)
    lines = []
    for h in range(heads):
        part = slice(h * hsize, (h + 1) * hsize)
        gm = gm_scr[:, part]
        query = q[:, part]
        spread = jnp.sum(gm_t[part, :].astype(F32) * mix[part, :], axis=0, keepdims=True)
        prob = pt[h]
        prob_mem = pm[h]
        score = prob.astype(F32) * (nt(v[:, part], gm) - spread)
        front = (prob_mem.astype(F32) * (nt(pv[:, part], gm) - spread)).astype(BF)
        low = score.astype(BF)
        gqt_scr[part, :] = nn(keys_t[part, :], low) + nn(pk_t[part, :], front)
        grad_ref[:, cols + h * hsize : cols + (h + 1) * hsize] = nn(low, query).astype(BF)
        grad_ref[:, 2 * cols + h * hsize : 2 * cols + (h + 1) * hsize] = nn(prob, gm).astype(BF)
        mem_k = nn(front, query).astype(BF)
        mem_v = nn(prob_mem, gm).astype(BF)
        for step in range(nc):
            outs[step][3 * rows + MEM_K : 3 * rows + MEM_K + mem, part] = mem_k
            outs[step][3 * rows + MEM_V : 3 * rows + MEM_V + mem, part] = mem_v
        acc[...] = jnp.zeros_like(acc)
        for at in range(0, length, LANES):
            acc[:, length - at : 2 * length - at] += score[at : at + LANES, :]
        fold = acc[...]
        half = LANES // 2
        while half >= 8:
            fold = fold[:half] + pltpu.roll(fold[half:], 2 * length - half, 1)
            half //= 2
        line = fold[0:1]
        for i in range(1, 8):
            line = line + pltpu.roll(fold[i : i + 1], 2 * length - i, 1)
        lines.append(line)
    lines.append(jnp.zeros((8 - heads, 2 * length), F32))
    hot = one_hot_rows(bucket_row[...], table_ref.shape[0])
    table_ref[...] = lax.dot_general(
        hot,
        jnp.concatenate(lines, axis=0),
        (((1,), (1,)), ((), ())),
        precision=lax.Precision.HIGHEST,
        preferred_element_type=F32,
    )
    grad_ref[:, :cols] = gqt_scr[...].T.astype(BF)
    for step in range(nc):
        at = pl.multiple_of((here ^ step) * rows, rows)
        for p in range(3):
            outs[step][p * rows : (p + 1) * rows, :] = grad_ref[
                pl.ds(at, rows), p * cols : (p + 1) * cols
            ]


def attend_back(nc, heads, hsize, index, gms, pt, pm, q, k, v, mix, pk, pv, bucket_row, nbuck):
    rows, cols = gms[0].shape
    length = rows * nc
    out = [shape((length, 3 * cols), BF), shape((nbuck, 8), F32)] + [
        shape((3 * rows + MEM_END, cols), BF)
    ] * nc
    return pl.pallas_call(
        functools.partial(attend_back_kernel, nc, heads, hsize),
        out_shape=out,
        in_specs=[smem()] + vmem(nc + 9),
        out_specs=vmem(len(out)),
        scratch_shapes=[
            pltpu.VMEM((length, cols), BF),
            pltpu.VMEM((cols, length), F32),
            pltpu.VMEM((LANES, 2 * length), F32),
        ],
        compiler_params=params(48),
        name="attend_back",
    )(index, *gms, pt, pm, q, k, v, mix, pk, pv, bucket_row)


NEAR_LAST = (0, 2, 1, 3)


def weight_back_kernel(pairs, extra, idx, *refs):
    ins = refs[: 2 * pairs + extra]
    outs = refs[2 * pairs + extra : -1]
    scr = refs[-1]
    wt, here = idx[0], idx[1]
    for p in range(pairs):
        left, right = ins[2 * p], ins[2 * p + 1]
        total = left.shape[-1] if len(left.shape) == 2 else left.shape[0] * left.shape[2]
        if len(left.shape) == 2:
            scr[...] = tn(left[...], right[...]).astype(BF)
        else:
            size = left.shape[2]
            for j in range(left.shape[0]):
                scr[j * size : (j + 1) * size, :] = tn(left[j], right[...]).astype(BF)
        rows = total // 8
        for i, out in enumerate(outs):
            for j, place in enumerate(NEAR_LAST):
                at = pl.multiple_of(((wt ^ i) * 4 + (here ^ place)) * rows, rows)
                out[p, j * rows : (j + 1) * rows, :] = scr[pl.ds(at, rows), :]
            if extra:
                out[p, 4 * rows :, :] = ins[2 * pairs][...]


def weight_back(name, index, pairs, extra=()):
    count, width = len(pairs), pairs[0][1].shape[1]
    left = pairs[0][0]
    rows = (left.shape[1] if left.ndim == 2 else left.shape[0] * left.shape[2]) // 2
    more = sum(e.shape[0] for e in extra)
    return pl.pallas_call(
        functools.partial(weight_back_kernel, count, len(extra)),
        out_shape=[shape((count, rows + more, width), BF)] * 2,
        in_specs=[smem()] + vmem(2 * count + len(extra)),
        out_specs=vmem(2),
        scratch_shapes=[pltpu.VMEM((2 * rows, width), BF)],
        compiler_params=params(48),
        name=name,
    )(index, *[side for pair in pairs for side in pair], *extra)


def input_back_kernel(nc, mem, idx, *refs):
    parts = refs[:nc]
    x, wq, wk, wv, gain, grad_hidden = refs[nc : nc + 6]
    out_ref, memk_ref, memv_ref = refs[nc + 6 : nc + 9]
    scr = refs[nc + 9]
    here = idx[0]
    rows = x.shape[0]
    for step in range(nc):
        scr[here ^ step] = parts[step][...]

    def wide(at, count):
        return jnp.concatenate([scr[c, at : at + count, :] for c in range(nc)], axis=1)

    grad_norm = (
        nt(wide(0, rows), wq[...])
        + nt(wide(rows, rows), wk[...])
        + nt(wide(2 * rows, rows), wv[...])
    )
    scaled, inverse = norm(x[...].astype(F32))
    e = grad_norm * gain[...]
    grad = grad_hidden[...] + inverse * (
        e - scaled * jnp.mean(e * scaled, axis=-1, keepdims=True)
    )
    out_ref[...] = grad.astype(BF)
    memk_ref[...] = wide(3 * rows + MEM_K, mem).astype(F32)
    memv_ref[...] = wide(3 * rows + MEM_V, mem).astype(F32)


def input_back(nc, mem, index, parts, x, wq, wk, wv, gain, grad_hidden):
    rows, width = x.shape
    out = [shape((rows, width), BF), shape((mem, width), F32), shape((mem, width), F32)]
    return pl.pallas_call(
        functools.partial(input_back_kernel, nc, mem),
        out_shape=out,
        in_specs=[smem()] + vmem(nc + 6),
        out_specs=vmem(3),
        scratch_shapes=[pltpu.VMEM((nc,) + parts[0].shape, BF)],
        compiler_params=params(32),
        name="input_back",
    )(index, *parts, x, wq, wk, wv, gain, grad_hidden)


def row_sums(values):
    return lax.dot_general(
        jnp.ones((8, values.shape[1]), F32),
        values,
        (((1,), (1,)), ((), ())),
        precision=lax.Precision.HIGHEST,
        preferred_element_type=F32,
    )


def batch_piece(refs, at):
    own, one, two, own2, one2, two2 = refs
    near = (own, one, two.at[0], two.at[1])[at]
    far = (own2, two2.at[0], one2, two2.at[1])[at]
    return ((0, near.at[0]), (2, near.at[1]), (1, far.at[0]), (3, far.at[1]))


def fill_rows_kernel(idx, *refs):
    out = refs[6]
    step = pl.program_id(0)
    for at in range(4):

        @pl.when(step == at)
        def _():
            for place, piece in batch_piece(refs[:6], at):
                size = piece.shape[0]
                row = pl.multiple_of((idx[1] ^ place) * size, 8)
                out[pl.ds(row, size), :] = piece[...].astype(F32)


def fill_rows(index, pieces):
    _, size, width = pieces[0].shape
    specs = [
        pl.BlockSpec(p.shape, functools.partial(lambda n, step, idx: (0,) * n, p.ndim))
        for p in pieces
    ]
    return pl.pallas_call(
        fill_rows_kernel,
        out_shape=shape((16 * size, width), F32),
        grid_spec=pltpu.PrefetchScalarGridSpec(
            num_scalar_prefetch=1,
            grid=(4,),
            in_specs=specs,
            out_specs=pl.BlockSpec((4 * size, width), lambda step, idx: (idx[0] ^ step, 0)),
        ),
        compiler_params=params(32),
        name="fill_rows",
    )(index, *pieces)


def fill_cols_kernel(idx, *refs):
    weight, gain, out, sums = refs[6:]
    step = pl.program_id(0)

    @pl.when(step == 0)
    def _():
        sums[...] = jnp.zeros_like(sums)

    for at in range(4):

        @pl.when(step // 2 == at)
        def _():
            for place, piece in batch_piece(refs[:6], at):
                size = piece.shape[0]
                row = pl.multiple_of((idx[1] ^ place) * size, 8)
                out[pl.ds(row, size), :] = piece[...].astype(F32)

    sums[...] += row_sums(out[...] * weight[...].astype(F32))

    @pl.when(step == 7)
    def _():
        sums[...] = sums[...] / gain[...]


def fill_cols(index, pieces, weight, gain):
    _, size, width = pieces[0].shape
    rows, block = 4 * size, width // 2

    def source(n, step, idx):
        return (0,) * (n - 1) + (step % 2,)

    def place(step, idx):
        return (0, (step % 2) * 4 + (idx[0] ^ (step // 2)))

    specs = [
        pl.BlockSpec(p.shape[:-1] + (block,), functools.partial(source, p.ndim)) for p in pieces
    ]
    return pl.pallas_call(
        fill_cols_kernel,
        out_shape=[shape((rows, 4 * width), F32), shape((8, rows), F32)],
        grid_spec=pltpu.PrefetchScalarGridSpec(
            num_scalar_prefetch=1,
            grid=(8,),
            in_specs=specs
            + [
                pl.BlockSpec((rows, block), place),
                pl.BlockSpec((1, rows), lambda step, idx: (0, 0)),
            ],
            out_specs=[
                pl.BlockSpec((rows, block), place),
                pl.BlockSpec((8, rows), lambda step, idx: (0, 0)),
            ],
        ),
        compiler_params=params(32),
        name="fill_cols",
    )(index, *pieces, weight, gain)


def fill_heads_kernel(size, idx, *refs):
    wq, wk, wv, gain = refs[6:10]
    oq, ok, ov, oo, sums, scr = refs[10:]
    cols = oq.shape[1] // 4
    wide = 3 * cols
    more = size // 4
    third = more // 3
    for at in range(4):
        there = idx[0] ^ at
        for place, piece in batch_piece(refs[:6], at):
            scr[idx[1] ^ place] = piece[...]
        at_row = pl.multiple_of(there * size, 8)
        for c in range(4):
            part = scr[c].astype(F32)
            for o, out in enumerate((oq, ok, ov)):
                out[pl.ds(at_row, size), c * cols : (c + 1) * cols] = part[
                    :size, o * cols : (o + 1) * cols
                ]
            row = pl.multiple_of(c * size + there * more, 8)
            oo[pl.ds(row, more), :wide] = part[size : size + more]
            for o in range(3):
                row = pl.multiple_of(c * size + there * more + o * third, 8)
                oo[pl.ds(row, third), wide:] = part[size + more :, o * cols : (o + 1) * cols]
    sums[...] = (
        row_sums(oq[...] * wq[...].astype(F32))
        + row_sums(ok[...] * wk[...].astype(F32))
        + row_sums(ov[...] * wv[...].astype(F32))
    ) / gain[...]


def fill_heads(index, size, pieces, wq, wk, wv, gain):
    out = [shape(wq.shape, F32)] * 4 + [shape((8, wq.shape[0]), F32)]
    return pl.pallas_call(
        functools.partial(fill_heads_kernel, size),
        out_shape=out,
        in_specs=[smem()] + vmem(10),
        out_specs=vmem(5),
        scratch_shapes=[pltpu.VMEM((4,) + pieces[0].shape[1:], BF)],
        compiler_params=params(48),
        name="fill_heads",
    )(index, *pieces, wq, wk, wv, gain)


def spread_grads(
    sizes, grad_first, grad_second, attended, grad_low, normed1, grad_heads, grad_table,
    weights, gains, nbuck, all_heads,
):
    nb, nc, nw = sizes
    b, c, w = lax.axis_index("batch"), lax.axis_index("ctx"), lax.axis_index("wt")
    w_query, w_key, w_value, w_in = weights
    gain_attn, gain_ffn = gains
    width = attended.shape[0] * attended.shape[2]
    heads = all_heads // nc
    cols = width // nc
    part = width // nw
    ff_part = grad_second.shape[0] // nw
    ff_own = ff_part * nb

    def ctx_total(value):
        own = sum_wt(value, nw)
        size = own.shape[0] // nc
        own = sum_flip(own.astype(BF).reshape(nc, size, own.shape[1]), c, "ctx", nc)
        whole = canonical(gather_flip(own.astype(BF), "ctx", nc), c)
        return whole.reshape(nc * size, -1)

    second = gather_flip(ctx_total(grad_second), "batch", nb)
    out_second = canonical([p.astype(F32) for p in second], b).reshape(ff_own, width)
    first = gather_flip(ctx_total(grad_first), "batch", nb)
    out_first = jnp.zeros((part, nw * ff_own), F32)
    for s, piece in enumerate(first):
        for o in range(nw):
            out_first = lax.dynamic_update_slice(
                out_first,
                piece[:, o * ff_part : (o + 1) * ff_part].astype(F32),
                (0, o * ff_own + (b ^ s) * ff_part),
            )

    grad_wo = jnp.einsum("cqd,qe->cde", attended, grad_low, preferred_element_type=F32)
    own_wo = sum_wt(grad_wo.astype(BF).reshape(width, width), nw).astype(BF)
    own_wo = sum_flip(own_wo.reshape(nc, part // nc, width), c, "ctx", nc).astype(BF)
    own_wo = sum_flip(own_wo.reshape(nb, part // nc // nb, width), b, "batch", nb).astype(BF)
    own_wo = canonical(gather_flip(own_wo, "batch", nb), b).reshape(part // nc, width)
    out_wo = canonical(gather_flip(own_wo, "ctx", nc), c).reshape(part, width).astype(F32)

    grad_qkv = sum_wt(tn(normed1, grad_heads).astype(BF), nw).astype(BF)
    line = jnp.pad(grad_table[:, :heads].reshape(1, -1), ((0, 15), (0, 3 * cols - heads * nbuck)))
    if nw == 2:
        line = line.astype(BF)
        line = line.astype(F32) + flip(line, "wt", 2, 1).astype(F32)
    else:
        line = lax.psum(line, "wt")
    size = part // nb
    blocks = jnp.concatenate(
        [
            grad_qkv.reshape(nb, size, 3 * cols),
            jnp.broadcast_to(line.astype(BF)[None], (nb, 16, 3 * cols)),
        ],
        axis=1,
    )
    block = sum_flip(blocks, b, "batch", nb).astype(BF)
    pieces = canonical(gather_flip(block, "ctx", nc), c)
    table_sum = pieces[:, size, : heads * nbuck].astype(F32).reshape(nc, nbuck, heads)
    table_sum = jnp.transpose(table_sum, (1, 0, 2)).reshape(nbuck, all_heads)
    own_buckets = nbuck // nw
    out_table = lax.dynamic_slice_in_dim(table_sum, w * own_buckets, own_buckets, 0)
    wide = canonical(gather_flip(pieces[:, :size], "batch", nb), b)
    wide = wide.reshape(nb, nc, size, 3, cols)
    wide = jnp.transpose(wide, (3, 0, 2, 1, 4)).reshape(3, part, width).astype(F32)
    out_q, out_k, out_v = wide[0], wide[1], wide[2]

    def gain_sum(pairs, gain):
        total = sum(jnp.sum(left * right.astype(F32), axis=1) for left, right in pairs)
        return total / gain.astype(F32)

    gain_two_grad = gain_sum([(out_first, w_in)], gain_ffn)
    gain_one_grad = gain_sum([(out_q, w_query), (out_k, w_key), (out_v, w_value)], gain_attn)
    return gain_one_grad, gain_two_grad, out_table, out_q, out_k, out_v, out_wo, out_first, out_second


def shards(
    sizes,
    inputs,
    prefix_keys,
    prefix_values,
    gain_attn,
    w_query,
    w_key,
    w_value,
    w_out,
    bias_table,
    gain_ffn,
    w_in,
    w_back,
    buckets,
    out_grad,
):
    nb, nc, nw = sizes
    b, c, w = lax.axis_index("batch"), lax.axis_index("ctx"), lax.axis_index("wt")
    x, g = inputs[0], out_grad[0]
    rows, width = x.shape
    all_heads = bias_table.shape[1]
    heads = all_heads // nc
    hsize = width // all_heads
    cols = heads * hsize
    mem = prefix_keys.shape[1]
    length = rows * nc
    part = width // nw
    ff_own = w_back.shape[0]
    ff_part = ff_own // nb
    nbuck = bias_table.shape[0] * nw
    index_c = jnp.reshape(c, (1,))

    xs = gather_flip(x, "ctx", nc)
    wq = gather_wt(w_query, nw).reshape(width, width)
    wk = gather_wt(w_key, nw).reshape(width, width)
    wv = gather_wt(w_value, nw).reshape(width, width)
    small = gather_wt(
        jnp.concatenate([gain_attn, gain_ffn, bias_table.reshape(-1)]).reshape(1, -1), nw
    ).reshape(nw, -1)
    gain_one = small[:, :part].reshape(1, width).astype(F32)
    gain_two = small[:, part : 2 * part].reshape(1, width).astype(F32)
    table = small[:, 2 * part :].reshape(nbuck, all_heads)
    wo = gather_wt(w_out, nw).reshape(width, width)
    in_cut = jnp.concatenate(
        [
            lax.dynamic_slice_in_dim(w_in, o * ff_own + b * ff_part, ff_part, 1)
            for o in range(nw)
        ],
        axis=1,
    )
    w_first = gather_wt(in_cut, nw).reshape(width, nw * ff_part)
    back_cut = lax.dynamic_slice_in_dim(w_back, b * ff_part, ff_part, 0)
    w_second = gather_wt(back_cut, nw).reshape(nw * ff_part, width)
    gs = gather_flip(g, "batch", nb)

    def head_cols(value):
        return lax.dynamic_slice_in_dim(value, c * cols, cols, 1)

    pk, pv = head_cols(prefix_keys[0]), head_cols(prefix_values[0])
    tab = jnp.pad(
        lax.dynamic_slice_in_dim(table, c * heads, heads, 1).T.astype(F32), ((0, 8 - heads), (0, 0))
    )
    bucket_row = jnp.pad(buckets[::-1].reshape(1, -1), ((0, 0), (1, 0)), constant_values=-1)

    paired = sizes == (4, 4, 2)
    (normed1, q, k, v, pt, pm, mix, *mixed) = attend(
        nc, heads, hsize, index_c, xs, head_cols(wq), head_cols(wk), head_cols(wv),
        gain_one, pk, pv, tab, bucket_row,
    )
    mixed = mixed[:1] + [flip(mixed[s], "ctx", nc, s) for s in range(1, nc)]
    hidden, normed2, attended = branch(nc, index_c, mixed, x, wo, gain_two)

    n2 = jnp.concatenate(gather_flip(normed2, "batch", nb), axis=0)
    g_all = jnp.concatenate(gs, axis=0)
    inner = nn(n2, w_first)
    act_value, act_pull = jax.vjp(functools.partial(jax.nn.gelu, approximate=True), inner)
    act = act_value.astype(BF)
    grad_act = nt(g_all, w_second)
    grad_inner = act_pull(grad_act)[0].astype(BF)
    part_norm = nt(grad_inner, w_first).astype(BF)
    part_out = nn(act, w_second).astype(BF)
    def cut(value, s):
        return value[s * rows : (s + 1) * rows]

    norm_parts = [cut(part_norm, 0)] + [
        flip(cut(part_norm, s), "batch", nb, s) for s in range(1, nb)
    ]
    if paired:
        index_bc = jnp.stack([b, c])
        index_wb = jnp.stack([w, b])
        index_wc = jnp.stack([w, c])
        mine, theirs = weight_back("ffn_back", index_wc, [(n2, grad_inner), (act, g_all)])
        ffn = add(mine, flip(theirs, "wt", 2, 1))
        half = ffn.shape[1] // 2
        ffn_keep, ffn_send = ffn[:, :half], ffn[:, half:]
        norm_parts[0] = after(norm_parts[0], ffn_keep, ffn_send)
    (grad_hidden, grad_low, *gms) = branch_back(
        nb, nc, index_c, norm_parts, hidden, gain_two, g, wo
    )
    gms = gms[:1] + [flip(gms[s], "ctx", nc, s) for s in range(1, nc)]
    if paired:
        ffn = add(ffn_keep, flip(ffn_send, "ctx", nc, 1))
        gms[0] = after(gms[0], ffn)
        half = ffn.shape[1] // 2
        ffn = add(ffn[:, :half], flip(ffn[:, half:], "ctx", nc, 2))
    (grad_heads, grad_table, *sends) = attend_back(
        nc, heads, hsize, index_c, gms, pt, pm, q, k, v, mix, pk, pv, bucket_row, nbuck
    )
    outs = part_out.reshape(nb, rows, width)
    if paired:
        outs = add(outs[0::2], flip(outs[1::2], "batch", nb, 1))
        result = hidden + outs[0].astype(F32) + flip(outs[1], "batch", nb, 2).astype(F32)
    else:
        result = hidden + outs[0].astype(F32)
        for s in range(1, nb):
            result = result + flip(outs[s], "batch", nb, s).astype(F32)

    if paired:

        def spread_ctx(value):
            near = jnp.stack([value, flip(value, "ctx", nc, 2)])
            return near, flip(near, "ctx", nc, 1)

        def spread_batch(near, far):
            one = flip(near, "batch", nb, 1)
            one2 = flip(far, "batch", nb, 2)
            two = flip(jnp.stack([near, one]), "batch", nb, 2)
            two2 = flip(jnp.stack([far, one2]), "batch", nb, 1)
            return near, one, two, far, one2, two2

        wide = 3 * cols
        quarter = part // 4
        line = jnp.pad(
            grad_table[:, :heads].reshape(1, -1), ((0, 15), (0, wide - heads * nbuck))
        ).astype(BF)
        mine, theirs = weight_back("qkv_back", index_wb, [(normed1, grad_heads)], (line,))
        total = add(mine[0], flip(theirs[0], "wt", 2, 1))
        total, line = total[:part], total[part:]
        for step in (1, 2):
            half = total.shape[0] // 2
            send = jnp.concatenate([total[half:], line])
            keep = jnp.concatenate([total[:half], line])
            total = add(keep, flip(send, "batch", nb, step))
            total, line = total[:half], total[half:]

        mine, theirs = weight_back("wo_back", index_wc, [(attended, grad_low)])
        wo_sum = add(mine[0], flip(theirs[0], "wt", 2, 1)).reshape(4, quarter, width)
        small = quarter // 4
        wo_sum = wo_sum.reshape(4, 4, small, width)
        for name, step, bit in (("batch", 1, b & 1), ("batch", 2, b >> 1)):
            pair_at = wo_sum.reshape(4, -1, 2, small, width) if step == 1 else wo_sum
            axis = pair_at.ndim - 3
            mine, theirs = halves(pair_at, bit, axis)
            wo_sum = add(mine, flip(theirs, name, 4, step))
        wo_sum = add(wo_sum[:2], flip(wo_sum[2:], "ctx", 4, 1))
        wo_sum = add(wo_sum[0], flip(wo_sum[1], "ctx", 4, 2)).reshape(small, width)
        third = small // 3
        rest = [wo_sum[o * third : (o + 1) * third, wide:] for o in range(3)]
        piece = jnp.concatenate([total, wo_sum[:, :wide], jnp.concatenate(rest, axis=1), line])
        height = piece.shape[0] - 16
        first_ctx, second_ctx = spread_ctx(ffn[0]), spread_ctx(ffn[1])
        out_second = fill_rows(index_bc, spread_batch(*second_ctx))
        out_first, sum_first = fill_cols(
            index_bc, spread_batch(*first_ctx), w_in, gain_ffn.astype(F32).reshape(1, part)
        )
        near, far = spread_ctx(piece)
        tables = pair(
            pair(near[0, height], near[1, height], c >> 1, 0),
            pair(far[0, height], far[1, height], c >> 1, 0),
            c & 1,
            1,
        )
        tables = tables[:, :, : heads * nbuck].astype(F32).reshape(nc, nbuck, heads)
        tables = jnp.transpose(tables, (1, 0, 2)).reshape(nbuck, all_heads)
        out_table = lax.dynamic_slice_in_dim(tables, w * (nbuck // nw), nbuck // nw, 0)
        out_q, out_k, out_v, out_wo, sum_heads = fill_heads(
            index_bc,
            quarter,
            spread_batch(near[:, :height], far[:, :height]),
            w_query,
            w_key,
            w_value,
            gain_attn.astype(F32).reshape(1, part),
        )
        gain_one_grad, gain_two_grad = sum_heads[0], sum_first[0]
        sends[1:] = lax.optimization_barrier((*sends[1:], *first_ctx, *second_ctx))[: nc - 1]
    else:
        grad_second = tn(act, g_all).astype(BF)
        grad_first = tn(n2, grad_inner).astype(BF)
        (gain_one_grad, gain_two_grad, out_table, out_q, out_k, out_v, out_wo, out_first,
         out_second) = spread_grads(
            sizes, grad_first, grad_second, attended, grad_low, normed1, grad_heads, grad_table,
            (w_query, w_key, w_value, w_in), (gain_attn, gain_ffn), nbuck, all_heads,
        )
    sends = sends[:1] + [flip(sends[s], "ctx", nc, s) for s in range(1, nc)]
    grad_x, grad_memk, grad_memv = input_back(
        nc, mem, index_c, sends, x, wq, wk, wv, gain_one, grad_hidden
    )
    return (
        result.astype(BF)[None],
        grad_x[None],
        grad_memk[None],
        grad_memv[None],
        gain_one_grad,
        gain_two_grad,
        out_table,
        out_q,
        out_k,
        out_v,
        out_wo,
        out_first,
        out_second,
    )


def solution(mesh):
    tokens = P(("batch", "wt"), "ctx", None)
    memory = P(("batch", "wt"), None, None)
    matrix = P("wt", None)
    vector = P("wt")
    sizes = (mesh.shape["batch"], mesh.shape["ctx"], mesh.shape["wt"])
    return jax.shard_map(
        functools.partial(shards, sizes),
        mesh=mesh,
        in_specs=(
            tokens, memory, memory, vector, matrix, matrix, matrix, matrix, matrix, vector,
            matrix, matrix, P(), tokens,
        ),
        out_specs=(
            tokens, tokens, memory, memory, vector, vector, matrix, matrix, matrix, matrix,
            matrix, matrix, matrix,
        ),
        check_vma=False,
    )
```

```python
import functools

import jax
import jax.numpy as jnp
from jax import lax
from jax.experimental import pallas as pl
from jax.experimental.pallas import tpu as pltpu
from jax.sharding import PartitionSpec as P

EPS = 1e-06
F32 = jnp.float32
BF = jnp.bfloat16
LANES = 128


def nn(left, right):
    return lax.dot_general(left, right, (((1,), (0,)), ((), ())), preferred_element_type=F32)


def nt(left, right):
    return lax.dot_general(left, right, (((1,), (1,)), ((), ())), preferred_element_type=F32)


def tn(left, right):
    return lax.dot_general(left, right, (((0,), (0,)), ((), ())), preferred_element_type=F32)


def vmem(count):
    return [pl.BlockSpec(memory_space=pltpu.VMEM)] * count


def smem():
    return pl.BlockSpec(memory_space=pltpu.SMEM)


def shape(dims, kind):
    return jax.ShapeDtypeStruct(dims, kind)


def params(mib):
    return pltpu.CompilerParams(vmem_limit_bytes=mib << 20)


def flip(value, axis, size, step):
    return lax.ppermute(value, axis, [(i, i ^ step) for i in range(size)])


def gather_flip(value, axis, size):
    return [value] + [flip(value, axis, size, step) for step in range(1, size)]


def canonical(parts, index):
    whole = jnp.zeros((len(parts),) + parts[0].shape, parts[0].dtype)
    for step, part in enumerate(parts):
        whole = lax.dynamic_update_index_in_dim(whole, part, index ^ step, 0)
    return whole


def gather_wt(value, size):
    if size == 2:
        own = lax.axis_index("wt") == 0
        other = flip(value, "wt", 2, 1)
        return jnp.stack([jnp.where(own, value, other), jnp.where(own, other, value)])
    return lax.all_gather(value, "wt", axis=0)


def sum_wt(value, size):
    rows = value.shape[0] // size
    if size == 2:
        index = lax.axis_index("wt")
        mine = lax.dynamic_slice_in_dim(value, index * rows, rows, 0)
        theirs = lax.dynamic_slice_in_dim(value, (1 - index) * rows, rows, 0)
        return mine.astype(F32) + flip(theirs, "wt", 2, 1).astype(F32)
    return lax.psum_scatter(value, "wt", scatter_dimension=0, tiled=True).astype(F32)


def sum_flip(blocks, index, axis, size):
    total = lax.dynamic_index_in_dim(blocks, index, 0, keepdims=False).astype(F32)
    for step in range(1, size):
        block = lax.dynamic_index_in_dim(blocks, index ^ step, 0, keepdims=False)
        total = total + flip(block, axis, size, step).astype(F32)
    return total


def norm(values):
    inverse = lax.rsqrt(jnp.mean(values * values, axis=-1, keepdims=True) + EPS)
    return values * inverse, inverse


def one_hot_rows(bucket_row, buckets):
    ids = lax.broadcasted_iota(jnp.int32, (buckets, bucket_row.shape[1]), 0)
    return (ids == bucket_row).astype(F32)


def attend_kernel(nc, heads, hsize, mem, idx, *refs):
    xs = refs[:nc]
    wq, wk, wv, gain, pk, pv, tab, bucket_row = refs[nc : nc + 8]
    n1_ref, q_ref, k_ref, v_ref, pt_ref, pm_ref, mix_ref = refs[nc + 8 : nc + 15]
    outs = refs[nc + 15 : nc + 15 + nc]
    att_scr = refs[nc + 15 + nc]
    here = idx[0]
    rows = xs[0].shape[0]
    length = nc * rows
    for step in range(nc):
        scaled, _ = norm(xs[step][...].astype(F32))
        at = pl.multiple_of((here ^ step) * rows, rows)
        n1_ref[pl.ds(at, rows), :] = (scaled * gain[...]).astype(BF)
    normed = n1_ref[...]
    q_ref[...] = nn(normed, wq[...]).astype(BF)
    k_ref[...] = nn(normed, wk[...]).astype(BF)
    v_ref[...] = nn(normed, wv[...]).astype(BF)
    vals_t = v_ref[...].T
    pv_t = pv[...].astype(F32).T.astype(BF)
    hot = one_hot_rows(bucket_row[...], tab.shape[1])
    lines = nn(tab[...], hot)
    for h in range(heads):
        part = slice(h * hsize, (h + 1) * hsize)
        query = q_ref[:, part]
        line = jnp.broadcast_to(lines[h : h + 1, :], (LANES, 2 * length))
        spread = pltpu.roll(line, 0, 1, stride=1, stride_axis=0)
        bias = jnp.concatenate(
            [spread[:, length - at : 2 * length - at] for at in range(0, length, LANES)], axis=0
        )
        score = nt(k_ref[:, part], query) + bias
        front = nt(pk[:, part], query)
        top = jnp.maximum(
            jnp.max(score, axis=0, keepdims=True), jnp.max(front, axis=0, keepdims=True)
        )
        score = jnp.exp(score - top)
        front = jnp.exp(front - top)
        total = jnp.sum(score, axis=0, keepdims=True) + jnp.sum(front, axis=0, keepdims=True)
        scale = 1.0 / total
        prob = (score * scale).astype(BF)
        prob_mem = (front * scale).astype(BF)
        pt_ref[h] = prob
        pm_ref[h] = prob_mem
        mix_ref[part, :] = nn(vals_t[part, :], prob) + nn(pv_t[part, :], prob_mem)
    att_scr[...] = mix_ref[...].T.astype(BF)
    for step in range(nc):
        at = pl.multiple_of((here ^ step) * rows, rows)
        outs[step][...] = att_scr[pl.ds(at, rows), :]


def attend(nc, heads, hsize, index, xs, wq, wk, wv, gain, pk, pv, tab, bucket_row):
    rows, width = xs[0].shape
    length = rows * nc
    cols = heads * hsize
    mem = pk.shape[0]
    out = [
        shape((length, width), BF),
        shape((length, cols), BF),
        shape((length, cols), BF),
        shape((length, cols), BF),
        shape((heads, length, length), BF),
        shape((heads, mem, length), BF),
        shape((cols, length), F32),
    ] + [shape((rows, cols), BF)] * nc
    return pl.pallas_call(
        functools.partial(attend_kernel, nc, heads, hsize, mem),
        out_shape=out,
        in_specs=[smem()] + vmem(nc + 8),
        out_specs=vmem(len(out)),
        scratch_shapes=[pltpu.VMEM((length, cols), BF)],
        compiler_params=params(24),
        name="attend",
    )(index, *xs, wq, wk, wv, gain, pk, pv, tab, bucket_row)


def branch_kernel(nc, idx, *refs):
    parts = refs[:nc]
    x, wo, gain = refs[nc : nc + 3]
    hidden_ref, n2_ref, att_ref = refs[nc + 3 : nc + 6]
    here = idx[0]
    cols = parts[0].shape[1]
    for step in range(nc):
        att_ref[here ^ step] = parts[step][...]
    hidden = x[...].astype(F32)
    for c in range(nc):
        hidden = hidden + nn(att_ref[c], wo[c * cols : (c + 1) * cols, :])
    hidden_ref[...] = hidden
    scaled, _ = norm(hidden)
    n2_ref[...] = (scaled * gain[...]).astype(BF)


def branch(nc, index, parts, x, wo, gain):
    rows, cols = parts[0].shape
    out = [shape(x.shape, F32), shape(x.shape, BF), shape((nc, rows, cols), BF)]
    return pl.pallas_call(
        functools.partial(branch_kernel, nc),
        out_shape=out,
        in_specs=[smem()] + vmem(nc + 3),
        out_specs=vmem(3),
        compiler_params=params(32),
        name="branch",
    )(index, *parts, x, wo, gain)


def branch_back_kernel(nb, nc, idx, *refs):
    parts = refs[:nb]
    hidden_ref, gain, g, wo = refs[nb : nb + 4]
    grad_ref, low_ref = refs[nb + 4 : nb + 6]
    outs = refs[nb + 6 : nb + 6 + nc]
    here = idx[0]
    cols = outs[0].shape[1]
    grad_norm = parts[0][...].astype(F32)
    for part in parts[1:]:
        grad_norm = grad_norm + part[...].astype(F32)
    scaled, inverse = norm(hidden_ref[...])
    e = grad_norm * gain[...]
    grad = g[...].astype(F32) + inverse * (
        e - scaled * jnp.mean(e * scaled, axis=-1, keepdims=True)
    )
    grad_ref[...] = grad
    low = grad.astype(BF)
    low_ref[...] = low
    for step in range(nc):
        at = pl.multiple_of((here ^ step) * cols, 8)
        outs[step][...] = nt(low, wo[pl.ds(at, cols), :]).astype(BF)


def branch_back(nb, nc, index, parts, hidden, gain, g, wo):
    rows, width = hidden.shape
    cols = width // nc
    out = [shape((rows, width), F32), shape((rows, width), BF)] + [shape((rows, cols), BF)] * nc
    return pl.pallas_call(
        functools.partial(branch_back_kernel, nb, nc),
        out_shape=out,
        in_specs=[smem()] + vmem(nb + 4),
        out_specs=vmem(len(out)),
        compiler_params=params(32),
        name="branch_back",
    )(index, *parts, hidden, gain, g, wo)


MEM_K, MEM_V, MEM_END = 0, 32, 64


def attend_back_kernel(nc, heads, hsize, idx, *refs):
    gms = refs[:nc]
    pt, pm, q, k, v, mix, pk, pv, bucket_row = refs[nc : nc + 9]
    grad_ref, table_ref = refs[nc + 9 : nc + 11]
    outs = refs[nc + 11 : nc + 11 + nc]
    gm_scr, gqt_scr, acc = refs[nc + 11 + nc :]
    here = idx[0]
    rows, cols = gms[0].shape
    length = rows * nc
    mem = pk.shape[0]
    for step in range(nc):
        at = pl.multiple_of((here ^ step) * rows, rows)
        gm_scr[pl.ds(at, rows), :] = gms[step][...]
    gm_t = gm_scr[...].T
    keys_t = k[...].T
    pk_t = pk[...].astype(F32).T.astype(BF)
    lines = []
    for h in range(heads):
        part = slice(h * hsize, (h + 1) * hsize)
        gm = gm_scr[:, part]
        query = q[:, part]
        spread = jnp.sum(gm_t[part, :].astype(F32) * mix[part, :], axis=0, keepdims=True)
        prob = pt[h]
        prob_mem = pm[h]
        score = prob.astype(F32) * (nt(v[:, part], gm) - spread)
        front = (prob_mem.astype(F32) * (nt(pv[:, part], gm) - spread)).astype(BF)
        low = score.astype(BF)
        gqt_scr[part, :] = nn(keys_t[part, :], low) + nn(pk_t[part, :], front)
        grad_ref[:, cols + h * hsize : cols + (h + 1) * hsize] = nn(low, query).astype(BF)
        grad_ref[:, 2 * cols + h * hsize : 2 * cols + (h + 1) * hsize] = nn(prob, gm).astype(BF)
        mem_k = nn(front, query).astype(BF)
        mem_v = nn(prob_mem, gm).astype(BF)
        for step in range(nc):
            outs[step][3 * rows + MEM_K : 3 * rows + MEM_K + mem, part] = mem_k
            outs[step][3 * rows + MEM_V : 3 * rows + MEM_V + mem, part] = mem_v
        acc[...] = jnp.zeros_like(acc)
        for at in range(0, length, LANES):
            acc[:, length - at : 2 * length - at] += score[at : at + LANES, :]
        fold = acc[...]
        half = LANES // 2
        while half >= 8:
            fold = fold[:half] + pltpu.roll(fold[half:], 2 * length - half, 1)
            half //= 2
        line = fold[0:1]
        for i in range(1, 8):
            line = line + pltpu.roll(fold[i : i + 1], 2 * length - i, 1)
        lines.append(line)
    lines.append(jnp.zeros((8 - heads, 2 * length), F32))
    hot = one_hot_rows(bucket_row[...], table_ref.shape[0])
    table_ref[...] = lax.dot_general(
        hot,
        jnp.concatenate(lines, axis=0),
        (((1,), (1,)), ((), ())),
        precision=lax.Precision.HIGHEST,
        preferred_element_type=F32,
    )
    grad_ref[:, :cols] = gqt_scr[...].T.astype(BF)
    for step in range(nc):
        at = pl.multiple_of((here ^ step) * rows, rows)
        for p in range(3):
            outs[step][p * rows : (p + 1) * rows, :] = grad_ref[
                pl.ds(at, rows), p * cols : (p + 1) * cols
            ]


def attend_back(nc, heads, hsize, index, gms, pt, pm, q, k, v, mix, pk, pv, bucket_row, nbuck):
    rows, cols = gms[0].shape
    length = rows * nc
    out = [shape((length, 3 * cols), BF), shape((nbuck, 8), F32)] + [
        shape((3 * rows + MEM_END, cols), BF)
    ] * nc
    return pl.pallas_call(
        functools.partial(attend_back_kernel, nc, heads, hsize),
        out_shape=out,
        in_specs=[smem()] + vmem(nc + 9),
        out_specs=vmem(len(out)),
        scratch_shapes=[
            pltpu.VMEM((length, cols), BF),
            pltpu.VMEM((cols, length), F32),
            pltpu.VMEM((LANES, 2 * length), F32),
        ],
        compiler_params=params(24),
        name="attend_back",
    )(index, *gms, pt, pm, q, k, v, mix, pk, pv, bucket_row)


def input_back_kernel(nc, mem, idx, *refs):
    parts = refs[:nc]
    x, wq, wk, wv, gain, grad_hidden = refs[nc : nc + 6]
    out_ref, memk_ref, memv_ref = refs[nc + 6 : nc + 9]
    scr = refs[nc + 9]
    here = idx[0]
    rows = x.shape[0]
    for step in range(nc):
        scr[here ^ step] = parts[step][...]

    def wide(at, count):
        return jnp.concatenate([scr[c, at : at + count, :] for c in range(nc)], axis=1)

    grad_norm = (
        nt(wide(0, rows), wq[...])
        + nt(wide(rows, rows), wk[...])
        + nt(wide(2 * rows, rows), wv[...])
    )
    scaled, inverse = norm(x[...].astype(F32))
    e = grad_norm * gain[...]
    grad = grad_hidden[...] + inverse * (
        e - scaled * jnp.mean(e * scaled, axis=-1, keepdims=True)
    )
    out_ref[...] = grad.astype(BF)
    memk_ref[...] = wide(3 * rows + MEM_K, mem).astype(F32)
    memv_ref[...] = wide(3 * rows + MEM_V, mem).astype(F32)


def input_back(nc, mem, index, parts, x, wq, wk, wv, gain, grad_hidden):
    rows, width = x.shape
    out = [shape((rows, width), BF), shape((mem, width), F32), shape((mem, width), F32)]
    return pl.pallas_call(
        functools.partial(input_back_kernel, nc, mem),
        out_shape=out,
        in_specs=[smem()] + vmem(nc + 6),
        out_specs=vmem(3),
        scratch_shapes=[pltpu.VMEM((nc,) + parts[0].shape, BF)],
        compiler_params=params(32),
        name="input_back",
    )(index, *parts, x, wq, wk, wv, gain, grad_hidden)


def general(
    sizes,
    inputs,
    prefix_keys,
    prefix_values,
    gain_attn,
    w_query,
    w_key,
    w_value,
    w_out,
    bias_table,
    gain_ffn,
    w_in,
    w_back,
    buckets,
    out_grad,
):
    nb, nc, nw = sizes
    b, c, w = lax.axis_index("batch"), lax.axis_index("ctx"), lax.axis_index("wt")
    x, g = inputs[0], out_grad[0]
    rows, width = x.shape
    all_heads = bias_table.shape[1]
    heads = all_heads // nc
    hsize = width // all_heads
    cols = heads * hsize
    mem = prefix_keys.shape[1]
    length = rows * nc
    part = width // nw
    ff_own = w_back.shape[0]
    ff_part = ff_own // nb
    nbuck = bias_table.shape[0] * nw
    index_c = jnp.reshape(c, (1,))

    xs = gather_flip(x, "ctx", nc)
    wq = gather_wt(w_query, nw).reshape(width, width)
    wk = gather_wt(w_key, nw).reshape(width, width)
    wv = gather_wt(w_value, nw).reshape(width, width)
    small = gather_wt(
        jnp.concatenate([gain_attn, gain_ffn, bias_table.reshape(-1)]).reshape(1, -1), nw
    ).reshape(nw, -1)
    gain_one = small[:, :part].reshape(1, width).astype(F32)
    gain_two = small[:, part : 2 * part].reshape(1, width).astype(F32)
    table = small[:, 2 * part :].reshape(nbuck, all_heads)
    wo = gather_wt(w_out, nw).reshape(width, width)
    in_cut = jnp.concatenate(
        [
            lax.dynamic_slice_in_dim(w_in, o * ff_own + b * ff_part, ff_part, 1)
            for o in range(nw)
        ],
        axis=1,
    )
    w_first = gather_wt(in_cut, nw).reshape(width, nw * ff_part)
    back_cut = lax.dynamic_slice_in_dim(w_back, b * ff_part, ff_part, 0)
    w_second = gather_wt(back_cut, nw).reshape(nw * ff_part, width)
    gs = gather_flip(g, "batch", nb)

    def head_cols(value):
        return lax.dynamic_slice_in_dim(value, c * cols, cols, 1)

    pk, pv = head_cols(prefix_keys[0]), head_cols(prefix_values[0])
    tab = jnp.pad(
        lax.dynamic_slice_in_dim(table, c * heads, heads, 1).T.astype(F32), ((0, 8 - heads), (0, 0))
    )
    bucket_row = jnp.pad(buckets[::-1].reshape(1, -1), ((0, 0), (1, 0)), constant_values=-1)

    (normed1, q, k, v, pt, pm, mix, *mixed) = attend(
        nc, heads, hsize, index_c, xs, head_cols(wq), head_cols(wk), head_cols(wv),
        gain_one, pk, pv, tab, bucket_row,
    )
    mixed = mixed[:1] + [flip(mixed[s], "ctx", nc, s) for s in range(1, nc)]
    hidden, normed2, attended = branch(nc, index_c, mixed, x, wo, gain_two)

    n2 = jnp.concatenate(gather_flip(normed2, "batch", nb), axis=0)
    g_all = jnp.concatenate(gs, axis=0)
    inner = nn(n2, w_first)
    act_value, act_pull = jax.vjp(functools.partial(jax.nn.gelu, approximate=True), inner)
    act = act_value.astype(BF)
    grad_act = nt(g_all, w_second)
    grad_inner = act_pull(grad_act)[0].astype(BF)
    part_norm = nt(grad_inner, w_first).astype(BF)
    part_out = nn(act, w_second).astype(BF)
    grad_second = tn(act, g_all).astype(BF)
    grad_first = tn(n2, grad_inner).astype(BF)

    def cut(value, s):
        return value[s * rows : (s + 1) * rows]

    norm_parts = [cut(part_norm, 0)] + [
        flip(cut(part_norm, s), "batch", nb, s) for s in range(1, nb)
    ]
    (grad_hidden, grad_low, *gms) = branch_back(
        nb, nc, index_c, norm_parts, hidden, gain_two, g, wo
    )
    gms = gms[:1] + [flip(gms[s], "ctx", nc, s) for s in range(1, nc)]
    (grad_heads, grad_table, *sends) = attend_back(
        nc, heads, hsize, index_c, gms, pt, pm, q, k, v, mix, pk, pv, bucket_row, nbuck
    )
    sends = sends[:1] + [flip(sends[s], "ctx", nc, s) for s in range(1, nc)]
    grad_x, grad_memk, grad_memv = input_back(
        nc, mem, index_c, sends, x, wq, wk, wv, gain_one, grad_hidden
    )

    result = hidden + cut(part_out, 0).astype(F32)
    for s in range(1, nb):
        result = result + flip(cut(part_out, s), "batch", nb, s).astype(F32)

    def ctx_total(value):
        own = sum_wt(value, nw)
        size = own.shape[0] // nc
        own = sum_flip(own.astype(BF).reshape(nc, size, own.shape[1]), c, "ctx", nc)
        whole = canonical(gather_flip(own.astype(BF), "ctx", nc), c)
        return whole.reshape(nc * size, -1)

    second = gather_flip(ctx_total(grad_second), "batch", nb)
    out_second = canonical([p.astype(F32) for p in second], b).reshape(ff_own, width)
    first = gather_flip(ctx_total(grad_first), "batch", nb)
    out_first = jnp.zeros((part, nw * ff_own), F32)
    for s, piece in enumerate(first):
        for o in range(nw):
            out_first = lax.dynamic_update_slice(
                out_first,
                piece[:, o * ff_part : (o + 1) * ff_part].astype(F32),
                (0, o * ff_own + (b ^ s) * ff_part),
            )

    grad_wo = jnp.einsum("cqd,qe->cde", attended, grad_low, preferred_element_type=F32)
    own_wo = sum_wt(grad_wo.astype(BF).reshape(width, width), nw).astype(BF)
    own_wo = sum_flip(own_wo.reshape(nc, part // nc, width), c, "ctx", nc).astype(BF)
    own_wo = sum_flip(own_wo.reshape(nb, part // nc // nb, width), b, "batch", nb).astype(BF)
    own_wo = canonical(gather_flip(own_wo, "batch", nb), b).reshape(part // nc, width)
    out_wo = canonical(gather_flip(own_wo, "ctx", nc), c).reshape(part, width).astype(F32)

    grad_qkv = sum_wt(tn(normed1, grad_heads).astype(BF), nw).astype(BF)
    line = jnp.pad(grad_table[:, :heads].reshape(1, -1), ((0, 15), (0, 3 * cols - heads * nbuck)))
    if nw == 2:
        line = line.astype(BF)
        line = line.astype(F32) + flip(line, "wt", 2, 1).astype(F32)
    else:
        line = lax.psum(line, "wt")
    size = part // nb
    blocks = jnp.concatenate(
        [
            grad_qkv.reshape(nb, size, 3 * cols),
            jnp.broadcast_to(line.astype(BF)[None], (nb, 16, 3 * cols)),
        ],
        axis=1,
    )
    block = sum_flip(blocks, b, "batch", nb).astype(BF)
    pieces = canonical(gather_flip(block, "ctx", nc), c)
    table_sum = pieces[:, size, : heads * nbuck].astype(F32).reshape(nc, nbuck, heads)
    table_sum = jnp.transpose(table_sum, (1, 0, 2)).reshape(nbuck, all_heads)
    own_buckets = nbuck // nw
    out_table = lax.dynamic_slice_in_dim(table_sum, w * own_buckets, own_buckets, 0)
    wide = canonical(gather_flip(pieces[:, :size], "batch", nb), b)
    wide = wide.reshape(nb, nc, size, 3, cols)
    wide = jnp.transpose(wide, (3, 0, 2, 1, 4)).reshape(3, part, width).astype(F32)
    out_q, out_k, out_v = wide[0], wide[1], wide[2]

    def gain_sum(pairs, gain):
        total = sum(jnp.sum(left * right.astype(F32), axis=1) for left, right in pairs)
        return total / gain.astype(F32)

    gain_two_grad = gain_sum([(out_first, w_in)], gain_ffn)
    gain_one_grad = gain_sum([(out_q, w_query), (out_k, w_key), (out_v, w_value)], gain_attn)
    return (
        result.astype(BF)[None],
        grad_x[None],
        grad_memk[None],
        grad_memv[None],
        gain_one_grad,
        gain_two_grad,
        out_table,
        out_q,
        out_k,
        out_v,
        out_wo,
        out_first,
        out_second,
    )


NEAR_LAST = (0, 2, 1, 3)
LINE = 8


def call(kernel, name, index, args, out, scratch=(), mib=24, far=()):
    stay = [pl.BlockSpec(memory_space=pltpu.HBM)] * len(far)
    return pl.pallas_call(
        kernel,
        out_shape=out,
        in_specs=[smem()] + stay + vmem(len(args)),
        out_specs=vmem(len(out)),
        scratch_shapes=list(scratch),
        compiler_params=params(mib),
        name=name,
    )(index, *far, *args)


def after(values, earlier):
    return lax.optimization_barrier((tuple(values), tuple(earlier)))[0]


def both_gains(wt, own, other, at, size):
    mine, theirs = own[:, at : at + size].astype(F32), other[:, at : at + size].astype(F32)
    first = jnp.where(wt == 0, mine, theirs)
    second = jnp.where(wt == 0, theirs, mine)
    return jnp.concatenate([first, second], axis=1)


def fetch_rows(sems, wt, pairs):
    copies = []
    for i, (scr, own, other) in enumerate(pairs):
        rows = own.shape[0]
        for j, (source, place) in enumerate(((own, wt), (other, 1 - wt))):
            to = scr.at[pl.ds(pl.multiple_of(place * rows, rows), rows), :]
            copies.append(pltpu.make_async_copy(source, to, sems.at[2 * i + j]))
            copies[-1].start()
    return copies


def heads_kernel(heads, hsize, idx, *refs):
    wq, wk, wv, wq2, wk2, wv2 = refs[:6]
    fars = refs[6:13]
    xs = refs[13:17]
    n1_ref, q_ref, k_ref, v_ref, pt_ref, pm_ref, mix_ref, wrow_ref, pk_ref, pv_ref = refs[17:27]
    outs = refs[27:31]
    att_scr, line_scr, sems, more_sems, *scrs = refs[31:]
    w_scr, nears = scrs[:3], scrs[3:]
    small, small2, tab, tab2, pk_all, pv_all, bucket_row = nears
    more = [
        pltpu.make_async_copy(source, to, more_sems.at[i])
        for i, (source, to) in enumerate(zip(fars, nears))
    ]
    for copy in more:
        copy.start()
    batch, here, wt = idx[0], idx[1], idx[2]
    rows, width = xs[0].shape
    length = 4 * rows
    half = wq.shape[0]
    cols = heads * hsize
    window = w_scr[0].shape[1]
    shift = window - cols
    odd = here % 2
    lanes = pl.ds(pl.multiple_of((here * cols - odd * shift), LANES), window)
    copies = fetch_rows(
        sems,
        wt,
        [
            (scr, own.at[:, lanes], other.at[:, lanes])
            for scr, own, other in zip(w_scr, (wq, wk, wv), (wq2, wk2, wv2))
        ],
    )
    for copy in more:
        copy.wait()
    for j in range(4):

        @pl.when(here == j)
        def _():
            take = slice(j * cols, (j + 1) * cols)
            pk_ref[...] = pk_all[:, take]
            pv_ref[...] = pv_all[:, take]

    def own_cols(value):
        return jnp.where(odd == 0, value[:, :cols], value[:, shift:])

    gain = both_gains(wt, small, small2, 0, half)
    for step in range(4):
        scaled, _ = norm(xs[step][...].astype(F32))
        at = pl.multiple_of((here ^ step) * rows, rows)
        n1_ref[pl.ds(at, rows), :] = (scaled * gain).astype(BF)
    normed = n1_ref[...]
    for copy in copies:
        copy.wait()
    quarter = half // 4
    at = pl.multiple_of(wt * half + batch * quarter, quarter)
    for p, (scr, out) in enumerate(zip(w_scr, (q_ref, k_ref, v_ref))):
        out[...] = own_cols(nn(normed, scr[...])).astype(BF)
        wrow_ref[:, p * cols : (p + 1) * cols] = own_cols(
            scr[pl.ds(at, quarter), :].astype(F32)
        ).astype(BF)
    vals_t = v_ref[...].T
    pv_t = pv_ref[...].astype(F32).T.astype(BF)
    own_buckets = tab.shape[0]
    ids = lax.broadcasted_iota(jnp.int32, (own_buckets, 2 * length), 0)
    lines = tn(tab[...].astype(F32), (ids + wt * own_buckets == bucket_row[...]).astype(F32))
    lines = lines + tn(
        tab2[...].astype(F32), (ids + (1 - wt) * own_buckets == bucket_row[...]).astype(F32)
    )
    line_scr[: lines.shape[0], :] = lines
    for h in range(heads):
        part = slice(h * hsize, (h + 1) * hsize)
        query = q_ref[:, part]
        line = jnp.broadcast_to(line_scr[pl.ds(here * heads + h, 1), :], (LANES, 2 * length))
        spread = pltpu.roll(line, 0, 1, stride=1, stride_axis=0)
        bias = jnp.concatenate(
            [spread[:, length - at : 2 * length - at] for at in range(0, length, LANES)], axis=0
        )
        score = nt(k_ref[:, part], query) + bias
        front = nt(pk_ref[:, part], query)
        top = jnp.maximum(
            jnp.max(score, axis=0, keepdims=True), jnp.max(front, axis=0, keepdims=True)
        )
        score = jnp.exp(score - top)
        front = jnp.exp(front - top)
        total = jnp.sum(score, axis=0, keepdims=True) + jnp.sum(front, axis=0, keepdims=True)
        scale = 1.0 / total
        prob = (score * scale).astype(BF)
        prob_mem = (front * scale).astype(BF)
        pt_ref[h] = prob
        pm_ref[h] = prob_mem
        mix_ref[part, :] = nn(vals_t[part, :], prob) + nn(pv_t[part, :], prob_mem)
    att_scr[...] = mix_ref[...].T.astype(BF)
    for step in range(4):
        at = pl.multiple_of((here ^ step) * rows, rows)
        outs[step][...] = att_scr[pl.ds(at, rows), :]


def hidden_kernel(idx, *refs):
    wo, wo2 = refs[:2]
    parts = refs[2:6]
    x, small, small2 = refs[6:9]
    hidden_ref, n2_ref, att_ref, wo_ref, sems = refs[9:]
    here, wt = idx[1], idx[2]
    cols = parts[0].shape[1]
    half = wo.shape[0]
    copies = fetch_rows(sems, wt, [(wo_ref, wo, wo2)])
    for step in range(4):
        att_ref[here ^ step] = parts[step][...]
    for copy in copies:
        copy.wait()
    hidden = x[...].astype(F32)
    for c in range(4):
        hidden = hidden + nn(att_ref[c], wo_ref[c * cols : (c + 1) * cols, :])
    hidden_ref[...] = hidden
    scaled, _ = norm(hidden)
    n2_ref[...] = (scaled * both_gains(wt, small, small2, half, half)).astype(BF)


def gelu_parts(v):
    scale = 0.7978845608028654
    square = v * v
    t = jnp.tanh(scale * v * (1.0 + 0.044715 * square))
    grad = 0.5 * (1.0 + t) + 0.5 * v * (1.0 - t * t) * scale * (1.0 + 0.134145 * square)
    return 0.5 * v * (1.0 + t), grad


def ffn_kernel(idx, *refs):
    w1, w1b, w2, w2b = refs[:4]
    n2s, gs = refs[4:8], refs[8:12]
    norms = refs[12:16]
    act_ref, gi_ref, w2_ref, w1_scr, sems = refs[16:]
    wt = idx[2]
    copies = fetch_rows(sems, wt, [(w1_scr, w1, w1b), (w2_ref, w2, w2b)])
    for copy in copies[:2]:
        copy.wait()
    rows = n2s[0].shape[0]
    for s in range(4):
        at = slice(s * rows, (s + 1) * rows)
        act, slope = gelu_parts(nn(n2s[s][...], w1_scr[...]))
        if s == 0:
            for copy in copies[2:]:
                copy.wait()
        act_ref[at, :] = act.astype(BF)
        grad = (nt(gs[s][...], w2_ref[...]).astype(BF).astype(F32) * slope).astype(BF)
        gi_ref[at, :] = grad
        norms[s][...] = nt(grad, w1_scr[...]).astype(BF)


def ffn_back_kernel(idx, *refs):
    n2s, gs = refs[:4], refs[4:8]
    act, gi = refs[8:10]
    mine, theirs, all_scr, scr = refs[10:]
    here, wt = idx[1], idx[2]
    rows = n2s[0].shape[0]
    size = scr.shape[0] // 8

    def spread(p):
        for i, out in enumerate((mine, theirs)):
            for j, place in enumerate(NEAR_LAST):
                at = pl.multiple_of(((wt ^ i) * 4 + (here ^ place)) * size, size)
                to = (2 * j + p) * size
                out[to : to + size, :] = scr[pl.ds(at, size), :]

    for s in range(4):
        all_scr[s * rows : (s + 1) * rows, :] = n2s[s][...]
    scr[...] = tn(all_scr[...], gi[...]).astype(BF)
    spread(0)
    for s in range(4):
        all_scr[s * rows : (s + 1) * rows, :] = gs[s][...]
    scr[...] = tn(act[...], all_scr[...]).astype(BF)
    spread(1)


def hidden_back_kernel(idx, *refs):
    parts = refs[:4]
    hidden_ref, small, small2, g, wo = refs[4:9]
    grad_ref, low_ref = refs[9:11]
    outs = refs[11:]
    here, wt = idx[1], idx[2]
    cols = outs[0].shape[1]
    half = wo.shape[0] // 2
    grad_norm = parts[0][...].astype(F32)
    for part in parts[1:]:
        grad_norm = grad_norm + part[...].astype(F32)
    scaled, inverse = norm(hidden_ref[...])
    e = grad_norm * both_gains(wt, small, small2, half, half)
    grad = g[...].astype(F32) + inverse * (
        e - scaled * jnp.mean(e * scaled, axis=-1, keepdims=True)
    )
    grad_ref[...] = grad
    low = grad.astype(BF)
    low_ref[...] = low
    for step in range(4):
        at = pl.multiple_of((here ^ step) * cols, cols)
        outs[step][...] = nt(low, wo[pl.ds(at, cols), :]).astype(BF)


def wo_back_kernel(idx, att, low, act, w2, mine, theirs, keep, send, scr):
    batch, here, wt = idx[0], idx[1], idx[2]
    rows = low.shape[0]
    size = att.shape[2]
    for c in range(4):
        scr[c * size : (c + 1) * size, :] = tn(att[c], low[...])
    size = scr.shape[0] // 32
    for i, out in enumerate((mine, theirs)):
        for q, far in enumerate(NEAR_LAST):
            for p, place in enumerate(NEAR_LAST):
                at = (((wt ^ i) * 4 + (here ^ place)) * 4 + (batch ^ far)) * size
                to = (4 * q + p) * size
                out[to : to + size, :] = scr[pl.ds(pl.multiple_of(at, 8), size), :].astype(BF)
    for s, (out, to) in enumerate(((keep, 0), (keep, rows), (send, 0), (send, rows))):
        out[to : to + rows, :] = nn(act[s * rows : (s + 1) * rows, :], w2[...]).astype(BF)


def heads_back_kernel(heads, hsize, idx, *refs):
    gms = refs[:4]
    pt, pm, q, k, v, mix, pk, pv, bucket_row, n1 = refs[4:14]
    mine, theirs = refs[14:16]
    outs = refs[16:20]
    gm_scr, gqt_scr, acc, grad_scr, w_scr = refs[20:]
    batch, here, wt = idx[0], idx[1], idx[2]
    rows, cols = gms[0].shape
    length = 4 * rows
    mem = pk.shape[0]
    for step in range(4):
        at = pl.multiple_of((here ^ step) * rows, rows)
        gm_scr[pl.ds(at, rows), :] = gms[step][...]
    gm_t = gm_scr[...].T
    keys_t = k[...].T
    pk_t = pk[...].astype(F32).T.astype(BF)
    lines = []
    for h in range(heads):
        part = slice(h * hsize, (h + 1) * hsize)
        gm = gm_scr[:, part]
        query = q[:, part]
        spread = jnp.sum(gm_t[part, :].astype(F32) * mix[part, :], axis=0, keepdims=True)
        prob = pt[h]
        prob_mem = pm[h]
        score = prob.astype(F32) * (nt(v[:, part], gm) - spread)
        front = (prob_mem.astype(F32) * (nt(pv[:, part], gm) - spread)).astype(BF)
        low = score.astype(BF)
        gqt_scr[part, :] = nn(keys_t[part, :], low) + nn(pk_t[part, :], front)
        grad_scr[1, :, part] = nn(low, query).astype(BF)
        grad_scr[2, :, part] = nn(prob, gm).astype(BF)
        mem_k = nn(front, query).astype(BF)
        mem_v = nn(prob_mem, gm).astype(BF)
        for step in range(4):
            outs[step][3 * rows + MEM_K : 3 * rows + MEM_K + mem, part] = mem_k
            outs[step][3 * rows + MEM_V : 3 * rows + MEM_V + mem, part] = mem_v
        acc[...] = jnp.zeros_like(acc)
        for at in range(0, length, LANES):
            acc[:, length - at : 2 * length - at] += score[at : at + LANES, :]
        fold = acc[...]
        size = LANES // 2
        while size >= 8:
            fold = fold[:size] + pltpu.roll(fold[size:], 2 * length - size, 1)
            size //= 2
        line = fold[0:1]
        for i in range(1, 8):
            line = line + pltpu.roll(fold[i : i + 1], 2 * length - i, 1)
        lines.append(line)
    grad_scr[0] = gqt_scr[...].T.astype(BF)
    normed = n1[...]
    for p in range(3):
        w_scr[:, p * cols : (p + 1) * cols] = tn(normed, grad_scr[p]).astype(BF)
    size = w_scr.shape[0] // 8
    for i, out in enumerate((mine, theirs)):
        for j, far in enumerate(NEAR_LAST):
            at = pl.multiple_of(((wt ^ i) * 4 + (batch ^ far)) * size, size)
            out[j * size : (j + 1) * size, :] = w_scr[pl.ds(at, size), :]
    lines.append(jnp.zeros((LINE - heads, 2 * length), F32))
    table = lax.dot_general(
        jnp.concatenate(lines, axis=0),
        one_hot_rows(bucket_row[...], LANES),
        (((1,), (1,)), ((), ())),
        precision=lax.Precision.HIGHEST,
        preferred_element_type=F32,
    )
    wide = w_scr.shape[1]
    table = jnp.concatenate([table, jnp.zeros((LINE, wide - LANES), F32)], axis=1)
    for out in (mine, theirs):
        out[4 * size :, :] = table.astype(BF)
    for step in range(4):
        at = pl.multiple_of((here ^ step) * rows, rows)
        for p in range(3):
            outs[step][p * rows : (p + 1) * rows, :] = grad_scr[p, pl.ds(at, rows), :]


def halving_kernel(lines, *refs):
    count = len(lines)
    for i, line in enumerate(lines):
        own, got = refs[2 * i], refs[2 * i + 1]
        keep, send = refs[2 * count + 2 * i], refs[2 * count + 2 * i + 1]
        total = (own[...].astype(F32) + got[...].astype(F32)).astype(BF)
        half = (total.shape[0] - line) // 2
        keep[:half, :] = total[:half]
        send[:half, :] = total[half : 2 * half]
        if line:
            keep[half:, :] = total[2 * half :]
            send[half:, :] = total[2 * half :]


def halving(name, items):
    args, out = [], []
    for own, got, line in items:
        args += [own, got]
        out += [shape(((own.shape[0] - line) // 2 + line, own.shape[1]), BF)] * 2
    return pl.pallas_call(
        functools.partial(halving_kernel, [line for _, _, line in items]),
        out_shape=out,
        in_specs=vmem(len(args)),
        out_specs=vmem(len(out)),
        compiler_params=params(32),
        name=name,
    )(*args)


def row_sums(values):
    return lax.dot_general(
        jnp.ones((8, values.shape[1]), F32),
        values,
        (((1,), (1,)), ((), ())),
        precision=lax.Precision.HIGHEST,
        preferred_element_type=F32,
    )


def ffn_piece_kernel(idx, ffn, ffn2, w_in, first_ref, second_ref, sum_ref):
    here = idx[1]
    quarter = first_ref.shape[0]
    grad = ffn[...].astype(F32) + ffn2[...].astype(F32)
    first_ref[...] = grad[:quarter].astype(BF)
    second_ref[...] = grad[quarter:].astype(BF)
    rows = w_in[pl.ds(pl.multiple_of(here * quarter, quarter), quarter), :].astype(F32)
    sum_ref[...] = row_sums(grad[:quarter] * rows)


def heads_piece_kernel(qkv, qkv2, wo, wo2, wrow, sum_in, piece_ref):
    size, width = wo.shape
    quarter = wrow.shape[0]
    wide = wrow.shape[1]
    heads = qkv[...].astype(F32) + qkv2[...].astype(F32)
    piece_ref[:quarter, :] = heads[:quarter].astype(BF)
    sum_heads = row_sums(heads[:quarter] * wrow[...].astype(F32))
    out = wo[...].astype(F32) + wo2[...].astype(F32)
    piece_ref[quarter : quarter + size, :] = out[:, :wide].astype(BF)
    third = size // 3
    cols = width - wide
    for o in range(3):
        piece_ref[quarter + size : quarter + size + third, o * cols : (o + 1) * cols] = out[
            o * third : (o + 1) * third, wide:
        ].astype(BF)
    row = lax.broadcasted_iota(jnp.int32, (LINE, quarter), 0)
    sums = jnp.where(row == LINE - 2, sum_heads, jnp.where(row == LINE - 1, sum_in[...], 0.0))
    at = quarter + size + third
    line = heads[quarter:]
    pad = jnp.zeros((LINE, LANES), F32)
    sums = jnp.concatenate([sums, jnp.zeros((LINE, LANES - quarter), F32)], axis=1)
    line = line + jnp.concatenate([pad, sums, jnp.zeros((LINE, wide - 2 * LANES), F32)], axis=1)
    piece_ref[at:, :] = line.astype(BF)


def ctx_pieces(refs, at, order):
    one, two, four, one2, two2, four2 = refs
    rows = one.shape[0]
    size = rows // 2
    first = ((one, 0), (two, 0), (four, 0), (four, rows))
    last = ((one2, 0), (four2, 0), (two2, 0), (four2, rows))
    if order == 2:
        first = ((one, 0), (four, 0), (two, 0), (four, rows))
        last = ((one2, 0), (two2, 0), (four2, 0), (four2, rows))
    near, far = first[at], last[at]
    found = []
    for (ref, start), places in ((near, (0, 2)), (far, (1, 3))):
        for i, place in enumerate(places):
            found.append((place, ref, start + i * size, size))
    return found


def rows_out_kernel(idx, *refs):
    out = refs[6]
    step = pl.program_id(0)
    for at in range(4):

        @pl.when(step == at)
        def _():
            for place, ref, start, size in ctx_pieces(refs[:6], at, 2):
                row = pl.multiple_of((idx[1] ^ place) * size, 8)
                out[pl.ds(row, size), :] = ref[start : start + size, :].astype(F32)


def rows_out(index, pieces):
    rows, width = pieces[0].shape
    return pl.pallas_call(
        rows_out_kernel,
        out_shape=shape((8 * rows, width), F32),
        grid_spec=pltpu.PrefetchScalarGridSpec(
            num_scalar_prefetch=1,
            grid=(4,),
            in_specs=[pl.BlockSpec(p.shape, lambda step, idx: (0, 0)) for p in pieces],
            out_specs=pl.BlockSpec((2 * rows, width), lambda step, idx: (idx[0] ^ step, 0)),
        ),
        compiler_params=params(32),
        name="rows_out",
    )(index, *pieces)


def cols_out_kernel(idx, *refs):
    out = refs[6]
    step = pl.program_id(0)
    for at in range(4):

        @pl.when(step // 2 == at)
        def _():
            for place, ref, start, size in ctx_pieces(refs[:6], at, 1):
                row = pl.multiple_of((idx[1] ^ place) * size, 8)
                out[pl.ds(row, size), :] = ref[start : start + size, :].astype(F32)


def cols_out(index, pieces):
    rows, width = pieces[0].shape
    block = width // 2

    def place(step, idx):
        return (0, (step % 2) * 4 + (idx[0] ^ (step // 2)))

    return pl.pallas_call(
        cols_out_kernel,
        out_shape=shape((2 * rows, 4 * width), F32),
        grid_spec=pltpu.PrefetchScalarGridSpec(
            num_scalar_prefetch=1,
            grid=(8,),
            in_specs=[
                pl.BlockSpec((p.shape[0], block), lambda step, idx: (0, step % 2)) for p in pieces
            ],
            out_specs=pl.BlockSpec((2 * rows, block), place),
        ),
        compiler_params=params(32),
        name="cols_out",
    )(index, *pieces)


def heads_out_kernel(heads, buckets, idx, *refs):
    small = refs[6]
    oq, ok, ov, oo, gain_one, gain_two, table, scr, lines, tab_scr = refs[7:]
    step = pl.program_id(0)
    quarter, width = oq.shape
    cols = width // 4
    wide = 3 * cols
    size = quarter // 4
    third = size // 3
    for at in range(4):

        @pl.when(step == at)
        def _():
            for place, ref, start, height in ctx_pieces(refs[:6], at, 1):
                scr[idx[1] ^ place] = ref[start : start + height, :]

    for c in range(4):
        part = scr[c].astype(F32)
        for o, out in enumerate((oq, ok, ov)):
            out[:, c * cols : (c + 1) * cols] = part[:quarter, o * cols : (o + 1) * cols]
        oo[c, 0, :, :wide] = part[quarter : quarter + size]
        for o in range(3):
            oo[c, 0, o * third : (o + 1) * third, wide:] = part[
                quarter + size : quarter + size + third, o * cols : (o + 1) * cols
            ]
        lines[idx[0] ^ step, c] = part[quarter + size + third :]

    @pl.when(step == 3)
    def _():
        seen = [[lines[b, c] for c in range(4)] for b in range(4)]
        take = slice(LANES, LANES + quarter)
        for b in range(4):
            total = sum(seen[b][c][LINE - 2 : LINE - 1, take] for c in range(4))
            gain_one[:, b * quarter : (b + 1) * quarter] = total
        for c in range(4):
            total = sum(seen[b][c][LINE - 1 : LINE, take] for b in range(4))
            gain_two[:, c * quarter : (c + 1) * quarter] = total
        own = small[...].astype(F32)
        rows = 4 * quarter
        gain_one[...] = gain_one[...] / own[:, :rows]
        gain_two[...] = gain_two[...] / own[:, rows : 2 * rows]
        rest = [seen[0][c][:heads, :LANES] for c in range(4)]
        rest.append(jnp.zeros((LANES - 4 * heads, LANES), F32))
        tab_scr[...] = jnp.concatenate(rest, axis=0).T
        own_buckets = buckets // 2
        at = pl.multiple_of(idx[2] * own_buckets, 8)
        table[...] = tab_scr[pl.ds(at, own_buckets), : 4 * heads]


def heads_out(index, pieces, small, width, heads, buckets):
    height, wide = pieces[0].shape[0] // 2, pieces[0].shape[1]
    part = width // 2
    quarter = part // 4
    size = quarter // 4
    block = pl.BlockSpec((quarter, width), lambda step, idx: (idx[0] ^ step, 0))
    whole = [pl.BlockSpec(p.shape, lambda step, idx: (0, 0)) for p in (*pieces, small)]
    return pl.pallas_call(
        functools.partial(heads_out_kernel, heads, buckets),
        out_shape=[shape((part, width), F32)] * 3
        + [
            shape((4, 4, size, width), F32),
            shape((1, part), F32),
            shape((1, part), F32),
            shape((buckets // 2, 4 * heads), F32),
        ],
        grid_spec=pltpu.PrefetchScalarGridSpec(
            num_scalar_prefetch=1,
            grid=(4,),
            in_specs=whole,
            out_specs=[block] * 3
            + [
                pl.BlockSpec((4, 1, size, width), lambda step, idx: (0, idx[0] ^ step, 0, 0)),
                pl.BlockSpec((1, part), lambda step, idx: (0, 0)),
                pl.BlockSpec((1, part), lambda step, idx: (0, 0)),
                pl.BlockSpec((buckets // 2, 4 * heads), lambda step, idx: (0, 0)),
            ],
            scratch_shapes=[
                pltpu.VMEM((4, height, wide), BF),
                pltpu.VMEM((4, 4, LINE, wide), F32),
                pltpu.VMEM((LANES, LANES), F32),
            ],
        ),
        compiler_params=params(32),
        name="heads_out",
    )(index, *pieces, small)


def paired(
    inputs,
    prefix_keys,
    prefix_values,
    gain_attn,
    w_query,
    w_key,
    w_value,
    w_out,
    bias_table,
    gain_ffn,
    w_in,
    w_back,
    buckets,
    out_grad,
):
    b, c, w = lax.axis_index("batch"), lax.axis_index("ctx"), lax.axis_index("wt")
    index = jnp.stack([b, c, w])
    x, g = inputs[0], out_grad[0]
    rows, width = x.shape
    all_heads = bias_table.shape[1]
    heads = all_heads // 4
    hsize = width // all_heads
    cols = heads * hsize
    wide = 3 * cols
    mem = prefix_keys.shape[1]
    length = 4 * rows
    part = width // 2
    quarter = part // 4
    ff_own = w_back.shape[0]
    ff_part = ff_own // 4
    nbuck = 2 * bias_table.shape[0]

    def over_wt(value, name):
        with jax.named_scope(name + "_w"):
            return flip(value, "wt", 2, 1)

    def over_ctx(value, step, name):
        with jax.named_scope(name + "_z" + str(step)):
            return flip(value, "ctx", 4, step)

    def over_batch(value, step, name):
        with jax.named_scope(name + "_b" + str(step)):
            return flip(value, "batch", 4, step)

    xs = [x] + [over_ctx(x, s, "x") for s in range(1, 4)]
    bucket_row = jnp.pad(buckets[::-1].reshape(1, -1), ((0, 0), (1, 0)), constant_values=-1)
    small = jnp.concatenate([gain_attn, gain_ffn]).reshape(1, -1)
    w_query2, w_key2, w_value2, w_out2 = [
        over_wt(v, "weight") for v in (w_query, w_key, w_value, w_out)
    ]
    table2 = over_wt(bias_table, "table")
    small2 = over_wt(small, "gain")
    gs = [g] + [over_batch(g, s, "g") for s in range(1, 4)]
    w_in_cut, w_back_cut = after((w_in, w_back), (xs[1], bucket_row, small))
    cut_in = jnp.concatenate(
        [
            lax.dynamic_slice_in_dim(w_in_cut, o * ff_own + b * ff_part, ff_part, 1)
            for o in range(2)
        ],
        axis=1,
    )
    cut_back = lax.dynamic_slice_in_dim(w_back_cut, b * ff_part, ff_part, 0)
    cut_in2, cut_back2 = over_wt(cut_in, "in"), over_wt(cut_back, "back")
    xs = after(xs, (*gs, w_out2, cut_in2, cut_back2))

    tokens = shape((length, cols), BF)
    few = (small, small2, bias_table, table2, prefix_keys[0], prefix_values[0], bucket_row)
    (n1, q, k, v, pt, pm, mix, wrow, pk, pv, *mixed) = call(
        functools.partial(heads_kernel, heads, hsize),
        "attend",
        index,
        [*xs],
        [shape((length, width), BF)]
        + [tokens] * 3
        + [
            shape((heads, length, length), BF),
            shape((heads, mem, length), BF),
            shape((cols, length), F32),
            shape((quarter, wide), BF),
            shape((mem, cols), BF),
            shape((mem, cols), BF),
        ]
        + [shape((rows, cols), BF)] * 4,
        [
            pltpu.VMEM((length, cols), BF),
            pltpu.VMEM((16, 2 * length), F32),
            pltpu.SemaphoreType.DMA((6,)),
            pltpu.SemaphoreType.DMA((len(few),)),
        ]
        + [pltpu.VMEM((width, -(-cols // LANES) * LANES), BF)] * 3
        + [pltpu.VMEM(v.shape, v.dtype) for v in few],
        far=(w_query, w_key, w_value, w_query2, w_key2, w_value2, *few),
    )
    mixed = mixed[:1] + [over_ctx(mixed[s], s, "mixed") for s in range(1, 4)]
    square = shape((width, width), BF)
    hidden, n2, attended, wo = call(
        hidden_kernel,
        "hidden",
        index,
        [*mixed, x, small, small2],
        [shape((rows, width), F32), shape((rows, width), BF), shape((4, rows, cols), BF), square],
        [pltpu.SemaphoreType.DMA((2,))],
        far=(w_out, w_out2),
    )

    n2s = [n2] + [over_batch(n2, s, "n2") for s in range(1, 4)]
    hid = shape((length, 2 * ff_part), BF)
    *norms, act, gi, w_second = call(
        ffn_kernel,
        "ffn",
        index,
        [*n2s, *gs],
        [shape((rows, width), BF)] * 4 + [hid, hid, shape((2 * ff_part, width), BF)],
        [pltpu.VMEM((width, 2 * ff_part), BF), pltpu.SemaphoreType.DMA((4,))],
        far=(cut_in, cut_in2, cut_back, cut_back2),
    )
    norms = norms[:1] + [over_batch(norms[s], s, "norm") for s in range(1, 4)]
    ffn, ffn_sent = call(
        ffn_back_kernel,
        "ffn_back",
        index,
        [*n2s, *gs, act, gi],
        [square, square],
        [pltpu.VMEM((length, width), BF), pltpu.VMEM((width, width), BF)],
    )
    ffn, ffn_sent = halving("ffn_wt", [(ffn, over_wt(ffn_sent, "ffn"), 0)])
    ffn_got = over_ctx(ffn_sent, 1, "ffn")
    norms = after(norms, (ffn, ffn_got))
    grad_hidden, low, *gms = call(
        hidden_back_kernel,
        "hidden_back",
        index,
        [*norms, hidden, small, small2, g, wo],
        [shape((rows, width), F32), shape((rows, width), BF)] + [shape((rows, cols), BF)] * 4,
    )
    ffn, ffn_sent = halving("ffn_near", [(ffn, ffn_got, 0)])
    ffn_got = over_ctx(ffn_sent, 2, "ffn")
    gms = after(gms, (ffn, ffn_sent))
    gms = list(gms[:1]) + [over_ctx(gms[s], s, "gm") for s in range(1, 4)]
    wo_sum, wo_sent, outs, outs_sent = call(
        wo_back_kernel,
        "wo_back",
        index,
        [attended, low, act, w_second],
        [shape((part, width), BF)] * 2 + [shape((2 * rows, width), BF)] * 2,
        [pltpu.VMEM((width, width), F32)],
    )
    outs_got = over_batch(outs_sent, 2, "outs")
    wo_sum, wo_sent = halving("wo_wt", [(wo_sum, over_wt(wo_sent, "wo"), 0)])
    wo_got = over_batch(wo_sent, 1, "wo")
    first, second, sum_in = call(
        ffn_piece_kernel,
        "ffn_piece",
        index,
        [ffn, ffn_got, cut_in],
        [shape((quarter, width), BF)] * 2 + [shape((8, quarter), F32)],
    )
    gms = after(gms, (first, second, wo_got, outs_got))
    (qkv, qkv_sent, *sends) = call(
        functools.partial(heads_back_kernel, heads, hsize),
        "attend_back",
        index,
        [*gms, pt, pm, q, k, v, mix, pk, pv, bucket_row, n1],
        [shape((part + LINE, wide), BF)] * 2 + [shape((3 * rows + MEM_END, cols), BF)] * 4,
        [
            pltpu.VMEM((length, cols), BF),
            pltpu.VMEM((cols, length), F32),
            pltpu.VMEM((LANES, 2 * length), F32),
            pltpu.VMEM((3, length, cols), BF),
            pltpu.VMEM((width, wide), BF),
        ],
    )

    qkv, qkv_sent, wo_sum, wo_sent, outs, outs_sent = halving(
        "step_a",
        [
            (qkv, over_wt(qkv_sent, "qkv"), LINE),
            (wo_sum, wo_got, 0),
            (outs, outs_got, 0),
        ],
    )
    outs_got = over_batch(outs_sent, 1, "outs")
    qkv, qkv_sent, wo_sum, wo_sent = halving(
        "step_b",
        [(qkv, over_batch(qkv_sent, 1, "qkv"), LINE), (wo_sum, over_batch(wo_sent, 2, "wo"), 0)],
    )
    qkv_got = over_batch(qkv_sent, 2, "qkv")
    result = (hidden + outs.astype(F32) + outs_got.astype(F32)).astype(BF)
    wo_sum, wo_sent = halving("step_c", [(wo_sum, over_ctx(wo_sent, 1, "wo"), 0)])
    wo_got = over_ctx(wo_sent, 2, "wo")
    height = quarter + quarter // 4 + quarter // 12 + LINE
    piece = pl.pallas_call(
        heads_piece_kernel,
        out_shape=shape((height, wide), BF),
        in_specs=vmem(6),
        out_specs=vmem(1)[0],
        compiler_params=params(32),
        name="heads_piece",
    )(qkv, qkv_got, wo_sum, wo_got, wrow, sum_in)

    def pile(one, two):
        return jnp.concatenate([one, two])

    in_far, out_far = over_ctx(first, 2, "in_back"), over_ctx(second, 2, "out_back")
    (piece,) = after((piece,), (in_far, out_far, result))
    heads_far = over_ctx(piece, 2, "heads_back")
    a1, b1 = pile(first, in_far), pile(second, out_far)
    a2, b2 = over_batch(a1, 1, "in_near"), over_batch(b1, 2, "out_near")
    c1, d1 = over_ctx(a1, 1, "in_back"), over_ctx(b1, 1, "out_back")
    pile_a, pile_b = pile(a1, a2), pile(b1, b2)
    a3 = over_batch(pile_a, 2, "in_near2")
    b3 = over_batch(pile_b, 1, "out_near2")
    (heads_far,) = after((heads_far,), (c1, d1))
    e1 = pile(piece, heads_far)
    f1 = over_ctx(e1, 1, "heads_back")
    (c1, d1) = after((c1, d1), (pile_a, pile_b))
    c2, d2 = over_batch(c1, 2, "in_far"), over_batch(d1, 1, "out_far")
    (e1, f1) = after((e1, f1), (a3, b3, c2, d2))
    c3 = over_batch(pile(c1, c2), 1, "in_far2")
    d3 = over_batch(pile(d1, d2), 2, "out_far2")
    e2, f2 = over_batch(e1, 1, "heads_near"), over_batch(f1, 2, "heads_far")
    sends[1:] = after(sends[1:], (f1,))
    sends = sends[:1] + [over_ctx(sends[s], s, "sends") for s in range(1, 4)]
    (e1, e2, f1, f2) = after((e1, e2, f1, f2), (c3, d3))
    e3 = over_batch(pile(e1, e2), 2, "heads_near2")
    f3 = over_batch(pile(f1, f2), 1, "heads_far2")
    out_second = rows_out(index, (b1, b2, b3, d1, d2, d3))
    out_first = cols_out(index, (a1, a2, a3, c1, c2, c3))
    out_q, out_k, out_v, out_wo, gain_one, gain_two, out_table = heads_out(
        index, (e1, e2, e3, f1, f2, f3), small, width, heads, nbuck
    )
    grad_x, grad_memk, grad_memv = call(
        input_end_kernel,
        "input_back",
        index,
        [*sends, x, small, small2, grad_hidden],
        [shape((rows, width), BF), shape((mem, width), F32), shape((mem, width), F32)],
        [pltpu.VMEM((4,) + sends[0].shape, BF), pltpu.SemaphoreType.DMA((6,))]
        + [pltpu.VMEM((width, width), BF)] * 3,
        far=(w_query, w_key, w_value, w_query2, w_key2, w_value2),
    )
    return (
        result[None],
        grad_x[None],
        grad_memk[None],
        grad_memv[None],
        gain_one.reshape(part),
        gain_two.reshape(part),
        out_table,
        out_q,
        out_k,
        out_v,
        out_wo.reshape(part, width),
        out_first,
        out_second,
    )


def input_end_kernel(idx, *refs):
    wq, wk, wv, wq2, wk2, wv2 = refs[:6]
    parts = refs[6:10]
    x, small, small2, grad_hidden = refs[10:14]
    out_ref, memk_ref, memv_ref, scr, sems, *w_scr = refs[14:]
    here, wt = idx[1], idx[2]
    rows = x.shape[0]
    mem = memk_ref.shape[0]
    copies = fetch_rows(sems, wt, list(zip(w_scr, (wq, wk, wv), (wq2, wk2, wv2))))
    for step in range(4):
        scr[here ^ step] = parts[step][...]
    for copy in copies:
        copy.wait()

    def wide(at, count):
        return jnp.concatenate([scr[c, at : at + count, :] for c in range(4)], axis=1)

    grad_norm = sum(nt(wide(p * rows, rows), whole[...]) for p, whole in enumerate(w_scr))
    scaled, inverse = norm(x[...].astype(F32))
    e = grad_norm * both_gains(wt, small, small2, 0, wq.shape[0])
    grad = grad_hidden[...] + inverse * (
        e - scaled * jnp.mean(e * scaled, axis=-1, keepdims=True)
    )
    out_ref[...] = grad.astype(BF)
    memk_ref[...] = wide(3 * rows + MEM_K, mem).astype(F32)
    memv_ref[...] = wide(3 * rows + MEM_V, mem).astype(F32)


def solution(mesh):
    tokens = P(("batch", "wt"), "ctx", None)
    memory = P(("batch", "wt"), None, None)
    matrix = P("wt", None)
    vector = P("wt")
    sizes = (mesh.shape["batch"], mesh.shape["ctx"], mesh.shape["wt"])
    body = paired if sizes == (4, 4, 2) else functools.partial(general, sizes)
    return jax.shard_map(
        body,
        mesh=mesh,
        in_specs=(
            tokens, memory, memory, vector, matrix, matrix, matrix, matrix, matrix, vector,
            matrix, matrix, P(), tokens,
        ),
        out_specs=(
            tokens, tokens, memory, memory, vector, vector, matrix, matrix, matrix, matrix,
            matrix, matrix, matrix,
        ),
        check_vma=False,
    )
```

```python
import functools

import jax
import jax.numpy as jnp
from jax import lax
from jax.experimental import pallas as pl
from jax.experimental.pallas import tpu as pltpu
from jax.sharding import PartitionSpec as P

EPS = 1e-06
F32 = jnp.float32
BF = jnp.bfloat16
LANES = 128


def nn(left, right):
    return lax.dot_general(left, right, (((1,), (0,)), ((), ())), preferred_element_type=F32)


def nt(left, right):
    return lax.dot_general(left, right, (((1,), (1,)), ((), ())), preferred_element_type=F32)


def tn(left, right):
    return lax.dot_general(left, right, (((0,), (0,)), ((), ())), preferred_element_type=F32)


def vmem(count):
    return [pl.BlockSpec(memory_space=pltpu.VMEM)] * count


def smem():
    return pl.BlockSpec(memory_space=pltpu.SMEM)


def shape(dims, kind):
    return jax.ShapeDtypeStruct(dims, kind)


def params(mib):
    return pltpu.CompilerParams(vmem_limit_bytes=mib << 20)


def flip(value, axis, size, step):
    return lax.ppermute(value, axis, [(i, i ^ step) for i in range(size)])


def gather_flip(value, axis, size):
    return [value] + [flip(value, axis, size, step) for step in range(1, size)]


def canonical(parts, index):
    whole = jnp.zeros((len(parts),) + parts[0].shape, parts[0].dtype)
    for step, part in enumerate(parts):
        whole = lax.dynamic_update_index_in_dim(whole, part, index ^ step, 0)
    return whole


def gather_wt(value, size):
    if size == 2:
        own = lax.axis_index("wt") == 0
        other = flip(value, "wt", 2, 1)
        return jnp.stack([jnp.where(own, value, other), jnp.where(own, other, value)])
    return lax.all_gather(value, "wt", axis=0)


def sum_wt(value, size):
    rows = value.shape[0] // size
    if size == 2:
        index = lax.axis_index("wt")
        mine = lax.dynamic_slice_in_dim(value, index * rows, rows, 0)
        theirs = lax.dynamic_slice_in_dim(value, (1 - index) * rows, rows, 0)
        return mine.astype(F32) + flip(theirs, "wt", 2, 1).astype(F32)
    return lax.psum_scatter(value, "wt", scatter_dimension=0, tiled=True).astype(F32)


def sum_flip(blocks, index, axis, size):
    total = lax.dynamic_index_in_dim(blocks, index, 0, keepdims=False).astype(F32)
    for step in range(1, size):
        block = lax.dynamic_index_in_dim(blocks, index ^ step, 0, keepdims=False)
        total = total + flip(block, axis, size, step).astype(F32)
    return total


def norm(values):
    inverse = lax.rsqrt(jnp.mean(values * values, axis=-1, keepdims=True) + EPS)
    return values * inverse, inverse


def one_hot_rows(bucket_row, buckets):
    ids = lax.broadcasted_iota(jnp.int32, (buckets, bucket_row.shape[1]), 0)
    return (ids == bucket_row).astype(F32)


def attend_kernel(nc, heads, hsize, mem, idx, *refs):
    xs = refs[:nc]
    wq, wk, wv, gain, pk, pv, tab, bucket_row = refs[nc : nc + 8]
    n1_ref, q_ref, k_ref, v_ref, pt_ref, pm_ref, mix_ref = refs[nc + 8 : nc + 15]
    outs = refs[nc + 15 : nc + 15 + nc]
    att_scr = refs[nc + 15 + nc]
    here = idx[0]
    rows = xs[0].shape[0]
    length = nc * rows
    for step in range(nc):
        scaled, _ = norm(xs[step][...].astype(F32))
        at = pl.multiple_of((here ^ step) * rows, rows)
        n1_ref[pl.ds(at, rows), :] = (scaled * gain[...]).astype(BF)
    normed = n1_ref[...]
    q_ref[...] = nn(normed, wq[...]).astype(BF)
    k_ref[...] = nn(normed, wk[...]).astype(BF)
    v_ref[...] = nn(normed, wv[...]).astype(BF)
    vals_t = v_ref[...].T
    pv_t = pv[...].astype(F32).T.astype(BF)
    hot = one_hot_rows(bucket_row[...], tab.shape[1])
    lines = nn(tab[...], hot)
    for h in range(heads):
        part = slice(h * hsize, (h + 1) * hsize)
        query = q_ref[:, part]
        line = jnp.broadcast_to(lines[h : h + 1, :], (LANES, 2 * length))
        spread = pltpu.roll(line, 0, 1, stride=1, stride_axis=0)
        bias = jnp.concatenate(
            [spread[:, length - at : 2 * length - at] for at in range(0, length, LANES)], axis=0
        )
        score = nt(k_ref[:, part], query) + bias
        front = nt(pk[:, part], query)
        top = jnp.maximum(
            jnp.max(score, axis=0, keepdims=True), jnp.max(front, axis=0, keepdims=True)
        )
        score = jnp.exp(score - top)
        front = jnp.exp(front - top)
        total = jnp.sum(score, axis=0, keepdims=True) + jnp.sum(front, axis=0, keepdims=True)
        scale = 1.0 / total
        prob = (score * scale).astype(BF)
        prob_mem = (front * scale).astype(BF)
        pt_ref[h] = prob
        pm_ref[h] = prob_mem
        mix_ref[part, :] = nn(vals_t[part, :], prob) + nn(pv_t[part, :], prob_mem)
    att_scr[...] = mix_ref[...].T.astype(BF)
    for step in range(nc):
        at = pl.multiple_of((here ^ step) * rows, rows)
        outs[step][...] = att_scr[pl.ds(at, rows), :]


def attend(nc, heads, hsize, index, xs, wq, wk, wv, gain, pk, pv, tab, bucket_row):
    rows, width = xs[0].shape
    length = rows * nc
    cols = heads * hsize
    mem = pk.shape[0]
    out = [
        shape((length, width), BF),
        shape((length, cols), BF),
        shape((length, cols), BF),
        shape((length, cols), BF),
        shape((heads, length, length), BF),
        shape((heads, mem, length), BF),
        shape((cols, length), F32),
    ] + [shape((rows, cols), BF)] * nc
    return pl.pallas_call(
        functools.partial(attend_kernel, nc, heads, hsize, mem),
        out_shape=out,
        in_specs=[smem()] + vmem(nc + 8),
        out_specs=vmem(len(out)),
        scratch_shapes=[pltpu.VMEM((length, cols), BF)],
        compiler_params=params(24),
        name="attend",
    )(index, *xs, wq, wk, wv, gain, pk, pv, tab, bucket_row)


def branch_kernel(nc, idx, *refs):
    parts = refs[:nc]
    x, wo, gain = refs[nc : nc + 3]
    hidden_ref, n2_ref, att_ref = refs[nc + 3 : nc + 6]
    here = idx[0]
    cols = parts[0].shape[1]
    for step in range(nc):
        att_ref[here ^ step] = parts[step][...]
    hidden = x[...].astype(F32)
    for c in range(nc):
        hidden = hidden + nn(att_ref[c], wo[c * cols : (c + 1) * cols, :])
    hidden_ref[...] = hidden
    scaled, _ = norm(hidden)
    n2_ref[...] = (scaled * gain[...]).astype(BF)


def branch(nc, index, parts, x, wo, gain):
    rows, cols = parts[0].shape
    out = [shape(x.shape, F32), shape(x.shape, BF), shape((nc, rows, cols), BF)]
    return pl.pallas_call(
        functools.partial(branch_kernel, nc),
        out_shape=out,
        in_specs=[smem()] + vmem(nc + 3),
        out_specs=vmem(3),
        compiler_params=params(32),
        name="branch",
    )(index, *parts, x, wo, gain)


def branch_back_kernel(nb, nc, idx, *refs):
    parts = refs[:nb]
    hidden_ref, gain, g, wo = refs[nb : nb + 4]
    grad_ref, low_ref = refs[nb + 4 : nb + 6]
    outs = refs[nb + 6 : nb + 6 + nc]
    here = idx[0]
    cols = outs[0].shape[1]
    grad_norm = parts[0][...].astype(F32)
    for part in parts[1:]:
        grad_norm = grad_norm + part[...].astype(F32)
    scaled, inverse = norm(hidden_ref[...])
    e = grad_norm * gain[...]
    grad = g[...].astype(F32) + inverse * (
        e - scaled * jnp.mean(e * scaled, axis=-1, keepdims=True)
    )
    grad_ref[...] = grad
    low = grad.astype(BF)
    low_ref[...] = low
    for step in range(nc):
        at = pl.multiple_of((here ^ step) * cols, 8)
        outs[step][...] = nt(low, wo[pl.ds(at, cols), :]).astype(BF)


def branch_back(nb, nc, index, parts, hidden, gain, g, wo):
    rows, width = hidden.shape
    cols = width // nc
    out = [shape((rows, width), F32), shape((rows, width), BF)] + [shape((rows, cols), BF)] * nc
    return pl.pallas_call(
        functools.partial(branch_back_kernel, nb, nc),
        out_shape=out,
        in_specs=[smem()] + vmem(nb + 4),
        out_specs=vmem(len(out)),
        compiler_params=params(32),
        name="branch_back",
    )(index, *parts, hidden, gain, g, wo)


MEM_K, MEM_V, MEM_END = 0, 32, 64


def attend_back_kernel(nc, heads, hsize, idx, *refs):
    gms = refs[:nc]
    pt, pm, q, k, v, mix, pk, pv, bucket_row = refs[nc : nc + 9]
    grad_ref, table_ref = refs[nc + 9 : nc + 11]
    outs = refs[nc + 11 : nc + 11 + nc]
    gm_scr, gqt_scr, acc = refs[nc + 11 + nc :]
    here = idx[0]
    rows, cols = gms[0].shape
    length = rows * nc
    mem = pk.shape[0]
    for step in range(nc):
        at = pl.multiple_of((here ^ step) * rows, rows)
        gm_scr[pl.ds(at, rows), :] = gms[step][...]
    gm_t = gm_scr[...].T
    keys_t = k[...].T
    pk_t = pk[...].astype(F32).T.astype(BF)
    lines = []
    for h in range(heads):
        part = slice(h * hsize, (h + 1) * hsize)
        gm = gm_scr[:, part]
        query = q[:, part]
        spread = jnp.sum(gm_t[part, :].astype(F32) * mix[part, :], axis=0, keepdims=True)
        prob = pt[h]
        prob_mem = pm[h]
        score = prob.astype(F32) * (nt(v[:, part], gm) - spread)
        front = (prob_mem.astype(F32) * (nt(pv[:, part], gm) - spread)).astype(BF)
        low = score.astype(BF)
        gqt_scr[part, :] = nn(keys_t[part, :], low) + nn(pk_t[part, :], front)
        grad_ref[:, cols + h * hsize : cols + (h + 1) * hsize] = nn(low, query).astype(BF)
        grad_ref[:, 2 * cols + h * hsize : 2 * cols + (h + 1) * hsize] = nn(prob, gm).astype(BF)
        mem_k = nn(front, query).astype(BF)
        mem_v = nn(prob_mem, gm).astype(BF)
        for step in range(nc):
            outs[step][3 * rows + MEM_K : 3 * rows + MEM_K + mem, part] = mem_k
            outs[step][3 * rows + MEM_V : 3 * rows + MEM_V + mem, part] = mem_v
        acc[...] = jnp.zeros_like(acc)
        for at in range(0, length, LANES):
            acc[:, length - at : 2 * length - at] += score[at : at + LANES, :]
        fold = acc[...]
        half = LANES // 2
        while half >= 8:
            fold = fold[:half] + pltpu.roll(fold[half:], 2 * length - half, 1)
            half //= 2
        line = fold[0:1]
        for i in range(1, 8):
            line = line + pltpu.roll(fold[i : i + 1], 2 * length - i, 1)
        lines.append(line)
    lines.append(jnp.zeros((8 - heads, 2 * length), F32))
    hot = one_hot_rows(bucket_row[...], table_ref.shape[0])
    table_ref[...] = lax.dot_general(
        hot,
        jnp.concatenate(lines, axis=0),
        (((1,), (1,)), ((), ())),
        precision=lax.Precision.HIGHEST,
        preferred_element_type=F32,
    )
    grad_ref[:, :cols] = gqt_scr[...].T.astype(BF)
    for step in range(nc):
        at = pl.multiple_of((here ^ step) * rows, rows)
        for p in range(3):
            outs[step][p * rows : (p + 1) * rows, :] = grad_ref[
                pl.ds(at, rows), p * cols : (p + 1) * cols
            ]


def attend_back(nc, heads, hsize, index, gms, pt, pm, q, k, v, mix, pk, pv, bucket_row, nbuck):
    rows, cols = gms[0].shape
    length = rows * nc
    out = [shape((length, 3 * cols), BF), shape((nbuck, 8), F32)] + [
        shape((3 * rows + MEM_END, cols), BF)
    ] * nc
    return pl.pallas_call(
        functools.partial(attend_back_kernel, nc, heads, hsize),
        out_shape=out,
        in_specs=[smem()] + vmem(nc + 9),
        out_specs=vmem(len(out)),
        scratch_shapes=[
            pltpu.VMEM((length, cols), BF),
            pltpu.VMEM((cols, length), F32),
            pltpu.VMEM((LANES, 2 * length), F32),
        ],
        compiler_params=params(24),
        name="attend_back",
    )(index, *gms, pt, pm, q, k, v, mix, pk, pv, bucket_row)


def input_back_kernel(nc, mem, idx, *refs):
    parts = refs[:nc]
    x, wq, wk, wv, gain, grad_hidden = refs[nc : nc + 6]
    out_ref, memk_ref, memv_ref = refs[nc + 6 : nc + 9]
    scr = refs[nc + 9]
    here = idx[0]
    rows = x.shape[0]
    for step in range(nc):
        scr[here ^ step] = parts[step][...]

    def wide(at, count):
        return jnp.concatenate([scr[c, at : at + count, :] for c in range(nc)], axis=1)

    grad_norm = (
        nt(wide(0, rows), wq[...])
        + nt(wide(rows, rows), wk[...])
        + nt(wide(2 * rows, rows), wv[...])
    )
    scaled, inverse = norm(x[...].astype(F32))
    e = grad_norm * gain[...]
    grad = grad_hidden[...] + inverse * (
        e - scaled * jnp.mean(e * scaled, axis=-1, keepdims=True)
    )
    out_ref[...] = grad.astype(BF)
    memk_ref[...] = wide(3 * rows + MEM_K, mem).astype(F32)
    memv_ref[...] = wide(3 * rows + MEM_V, mem).astype(F32)


def input_back(nc, mem, index, parts, x, wq, wk, wv, gain, grad_hidden):
    rows, width = x.shape
    out = [shape((rows, width), BF), shape((mem, width), F32), shape((mem, width), F32)]
    return pl.pallas_call(
        functools.partial(input_back_kernel, nc, mem),
        out_shape=out,
        in_specs=[smem()] + vmem(nc + 6),
        out_specs=vmem(3),
        scratch_shapes=[pltpu.VMEM((nc,) + parts[0].shape, BF)],
        compiler_params=params(32),
        name="input_back",
    )(index, *parts, x, wq, wk, wv, gain, grad_hidden)


def general(
    sizes,
    inputs,
    prefix_keys,
    prefix_values,
    gain_attn,
    w_query,
    w_key,
    w_value,
    w_out,
    bias_table,
    gain_ffn,
    w_in,
    w_back,
    buckets,
    out_grad,
):
    nb, nc, nw = sizes
    b, c, w = lax.axis_index("batch"), lax.axis_index("ctx"), lax.axis_index("wt")
    x, g = inputs[0], out_grad[0]
    rows, width = x.shape
    all_heads = bias_table.shape[1]
    heads = all_heads // nc
    hsize = width // all_heads
    cols = heads * hsize
    mem = prefix_keys.shape[1]
    length = rows * nc
    part = width // nw
    ff_own = w_back.shape[0]
    ff_part = ff_own // nb
    nbuck = bias_table.shape[0] * nw
    index_c = jnp.reshape(c, (1,))

    xs = gather_flip(x, "ctx", nc)
    wq = gather_wt(w_query, nw).reshape(width, width)
    wk = gather_wt(w_key, nw).reshape(width, width)
    wv = gather_wt(w_value, nw).reshape(width, width)
    small = gather_wt(
        jnp.concatenate([gain_attn, gain_ffn, bias_table.reshape(-1)]).reshape(1, -1), nw
    ).reshape(nw, -1)
    gain_one = small[:, :part].reshape(1, width).astype(F32)
    gain_two = small[:, part : 2 * part].reshape(1, width).astype(F32)
    table = small[:, 2 * part :].reshape(nbuck, all_heads)
    wo = gather_wt(w_out, nw).reshape(width, width)
    in_cut = jnp.concatenate(
        [
            lax.dynamic_slice_in_dim(w_in, o * ff_own + b * ff_part, ff_part, 1)
            for o in range(nw)
        ],
        axis=1,
    )
    w_first = gather_wt(in_cut, nw).reshape(width, nw * ff_part)
    back_cut = lax.dynamic_slice_in_dim(w_back, b * ff_part, ff_part, 0)
    w_second = gather_wt(back_cut, nw).reshape(nw * ff_part, width)
    gs = gather_flip(g, "batch", nb)

    def head_cols(value):
        return lax.dynamic_slice_in_dim(value, c * cols, cols, 1)

    pk, pv = head_cols(prefix_keys[0]), head_cols(prefix_values[0])
    tab = jnp.pad(
        lax.dynamic_slice_in_dim(table, c * heads, heads, 1).T.astype(F32), ((0, 8 - heads), (0, 0))
    )
    bucket_row = jnp.pad(buckets[::-1].reshape(1, -1), ((0, 0), (1, 0)), constant_values=-1)

    (normed1, q, k, v, pt, pm, mix, *mixed) = attend(
        nc, heads, hsize, index_c, xs, head_cols(wq), head_cols(wk), head_cols(wv),
        gain_one, pk, pv, tab, bucket_row,
    )
    mixed = mixed[:1] + [flip(mixed[s], "ctx", nc, s) for s in range(1, nc)]
    hidden, normed2, attended = branch(nc, index_c, mixed, x, wo, gain_two)

    n2 = jnp.concatenate(gather_flip(normed2, "batch", nb), axis=0)
    g_all = jnp.concatenate(gs, axis=0)
    inner = nn(n2, w_first)
    act_value, act_pull = jax.vjp(functools.partial(jax.nn.gelu, approximate=True), inner)
    act = act_value.astype(BF)
    grad_act = nt(g_all, w_second)
    grad_inner = act_pull(grad_act)[0].astype(BF)
    part_norm = nt(grad_inner, w_first).astype(BF)
    part_out = nn(act, w_second).astype(BF)
    grad_second = tn(act, g_all).astype(BF)
    grad_first = tn(n2, grad_inner).astype(BF)

    def cut(value, s):
        return value[s * rows : (s + 1) * rows]

    norm_parts = [cut(part_norm, 0)] + [
        flip(cut(part_norm, s), "batch", nb, s) for s in range(1, nb)
    ]
    (grad_hidden, grad_low, *gms) = branch_back(
        nb, nc, index_c, norm_parts, hidden, gain_two, g, wo
    )
    gms = gms[:1] + [flip(gms[s], "ctx", nc, s) for s in range(1, nc)]
    (grad_heads, grad_table, *sends) = attend_back(
        nc, heads, hsize, index_c, gms, pt, pm, q, k, v, mix, pk, pv, bucket_row, nbuck
    )
    sends = sends[:1] + [flip(sends[s], "ctx", nc, s) for s in range(1, nc)]
    grad_x, grad_memk, grad_memv = input_back(
        nc, mem, index_c, sends, x, wq, wk, wv, gain_one, grad_hidden
    )

    result = hidden + cut(part_out, 0).astype(F32)
    for s in range(1, nb):
        result = result + flip(cut(part_out, s), "batch", nb, s).astype(F32)

    def ctx_total(value):
        own = sum_wt(value, nw)
        size = own.shape[0] // nc
        own = sum_flip(own.astype(BF).reshape(nc, size, own.shape[1]), c, "ctx", nc)
        whole = canonical(gather_flip(own.astype(BF), "ctx", nc), c)
        return whole.reshape(nc * size, -1)

    second = gather_flip(ctx_total(grad_second), "batch", nb)
    out_second = canonical([p.astype(F32) for p in second], b).reshape(ff_own, width)
    first = gather_flip(ctx_total(grad_first), "batch", nb)
    out_first = jnp.zeros((part, nw * ff_own), F32)
    for s, piece in enumerate(first):
        for o in range(nw):
            out_first = lax.dynamic_update_slice(
                out_first,
                piece[:, o * ff_part : (o + 1) * ff_part].astype(F32),
                (0, o * ff_own + (b ^ s) * ff_part),
            )

    grad_wo = jnp.einsum("cqd,qe->cde", attended, grad_low, preferred_element_type=F32)
    own_wo = sum_wt(grad_wo.astype(BF).reshape(width, width), nw).astype(BF)
    own_wo = sum_flip(own_wo.reshape(nc, part // nc, width), c, "ctx", nc).astype(BF)
    own_wo = sum_flip(own_wo.reshape(nb, part // nc // nb, width), b, "batch", nb).astype(BF)
    own_wo = canonical(gather_flip(own_wo, "batch", nb), b).reshape(part // nc, width)
    out_wo = canonical(gather_flip(own_wo, "ctx", nc), c).reshape(part, width).astype(F32)

    grad_qkv = sum_wt(tn(normed1, grad_heads).astype(BF), nw).astype(BF)
    line = jnp.pad(grad_table[:, :heads].reshape(1, -1), ((0, 15), (0, 3 * cols - heads * nbuck)))
    if nw == 2:
        line = line.astype(BF)
        line = line.astype(F32) + flip(line, "wt", 2, 1).astype(F32)
    else:
        line = lax.psum(line, "wt")
    size = part // nb
    blocks = jnp.concatenate(
        [
            grad_qkv.reshape(nb, size, 3 * cols),
            jnp.broadcast_to(line.astype(BF)[None], (nb, 16, 3 * cols)),
        ],
        axis=1,
    )
    block = sum_flip(blocks, b, "batch", nb).astype(BF)
    pieces = canonical(gather_flip(block, "ctx", nc), c)
    table_sum = pieces[:, size, : heads * nbuck].astype(F32).reshape(nc, nbuck, heads)
    table_sum = jnp.transpose(table_sum, (1, 0, 2)).reshape(nbuck, all_heads)
    own_buckets = nbuck // nw
    out_table = lax.dynamic_slice_in_dim(table_sum, w * own_buckets, own_buckets, 0)
    wide = canonical(gather_flip(pieces[:, :size], "batch", nb), b)
    wide = wide.reshape(nb, nc, size, 3, cols)
    wide = jnp.transpose(wide, (3, 0, 2, 1, 4)).reshape(3, part, width).astype(F32)
    out_q, out_k, out_v = wide[0], wide[1], wide[2]

    def gain_sum(pairs, gain):
        total = sum(jnp.sum(left * right.astype(F32), axis=1) for left, right in pairs)
        return total / gain.astype(F32)

    gain_two_grad = gain_sum([(out_first, w_in)], gain_ffn)
    gain_one_grad = gain_sum([(out_q, w_query), (out_k, w_key), (out_v, w_value)], gain_attn)
    return (
        result.astype(BF)[None],
        grad_x[None],
        grad_memk[None],
        grad_memv[None],
        gain_one_grad,
        gain_two_grad,
        out_table,
        out_q,
        out_k,
        out_v,
        out_wo,
        out_first,
        out_second,
    )


NEAR_LAST = (0, 2, 1, 3)
LINE = 8


def call(kernel, name, index, args, out, scratch=(), mib=24, far=()):
    stay = [pl.BlockSpec(memory_space=pltpu.HBM)] * len(far)
    return pl.pallas_call(
        kernel,
        out_shape=out,
        in_specs=[smem()] + stay + vmem(len(args)),
        out_specs=vmem(len(out)),
        scratch_shapes=list(scratch),
        compiler_params=params(mib),
        name=name,
    )(index, *far, *args)


def after(values, earlier):
    return lax.optimization_barrier((tuple(values), tuple(earlier)))[0]


def both_gains(wt, own, other, row):
    mine, theirs = own[row : row + 1, :].astype(F32), other[row : row + 1, :].astype(F32)
    first = jnp.where(wt == 0, mine, theirs)
    second = jnp.where(wt == 0, theirs, mine)
    return jnp.concatenate([first, second], axis=1)


def fetch_rows(sems, wt, pairs):
    copies = []
    for i, (scr, own, other) in enumerate(pairs):
        rows = own.shape[0]
        for j, (source, place) in enumerate(((own, wt), (other, 1 - wt))):
            to = scr.at[pl.ds(pl.multiple_of(place * rows, rows), rows), :]
            copies.append(pltpu.make_async_copy(source, to, sems.at[2 * i + j]))
            copies[-1].start()
    return copies


TABLE_ROW = 8


def heads_kernel(heads, hsize, own_buckets, idx, *refs):
    wq, wk, wv, wq2, wk2, wv2 = refs[:6]
    fars = refs[6:11]
    x = refs[11]
    n1_ref, q_ref, k_ref, v_ref, pt_ref, pm_ref, mix_ref, wrow_ref, pk_ref, pv_ref = refs[12:22]
    outs = refs[22:26]
    att_scr, line_scr, sems, more_sems, *scrs = refs[26:]
    w_scr, nears = scrs[:3], scrs[3:]
    small, small2, pk_all, pv_all, bucket_row = nears
    more = [
        pltpu.make_async_copy(source, to, more_sems.at[i])
        for i, (source, to) in enumerate(zip(fars, nears))
    ]
    for copy in more:
        copy.start()
    batch, here, wt = idx[0], idx[1], idx[2]
    length, width = x.shape
    rows = length // 4
    half = wq.shape[0]
    cols = heads * hsize
    window = w_scr[0].shape[1]
    shift = window - cols
    odd = here % 2
    lanes = pl.ds(pl.multiple_of((here * cols - odd * shift), LANES), window)
    copies = fetch_rows(
        sems,
        wt,
        [
            (scr, own.at[:, lanes], other.at[:, lanes])
            for scr, own, other in zip(w_scr, (wq, wk, wv), (wq2, wk2, wv2))
        ],
    )
    for copy in more:
        copy.wait()
    for j in range(4):

        @pl.when(here == j)
        def _():
            take = slice(j * cols, (j + 1) * cols)
            pk_ref[...] = pk_all[:, take]
            pv_ref[...] = pv_all[:, take]

    def own_cols(value):
        return jnp.where(odd == 0, value[:, :cols], value[:, shift:])

    gain = both_gains(wt, small, small2, 0)
    scaled, _ = norm(x[...].astype(F32))
    n1_ref[...] = (scaled * gain).astype(BF)
    normed = n1_ref[...]
    for copy in copies:
        copy.wait()
    quarter = half // 4
    at = pl.multiple_of(wt * half + batch * quarter, quarter)
    for p, (scr, out) in enumerate(zip(w_scr, (q_ref, k_ref, v_ref))):
        out[...] = own_cols(nn(normed, scr[...])).astype(BF)
        wrow_ref[:, p * cols : (p + 1) * cols] = own_cols(
            scr[pl.ds(at, quarter), :].astype(F32)
        ).astype(BF)
    vals_t = v_ref[...].T
    pv_t = pv_ref[...].astype(F32).T.astype(BF)
    tab, tab2 = (
        ref[TABLE_ROW : TABLE_ROW + own_buckets, :LANES].astype(F32) for ref in (small, small2)
    )
    ids = lax.broadcasted_iota(jnp.int32, (own_buckets, 2 * length), 0)
    lines = tn(tab, (ids + wt * own_buckets == bucket_row[...]).astype(F32))
    lines = lines + tn(
        tab2, (ids + (1 - wt) * own_buckets == bucket_row[...]).astype(F32)
    )
    line_scr[...] = lines[: line_scr.shape[0]]
    for h in range(heads):
        part = slice(h * hsize, (h + 1) * hsize)
        query = q_ref[:, part]
        line = jnp.broadcast_to(line_scr[pl.ds(here * heads + h, 1), :], (LANES, 2 * length))
        spread = pltpu.roll(line, 0, 1, stride=1, stride_axis=0)
        bias = jnp.concatenate(
            [spread[:, length - at : 2 * length - at] for at in range(0, length, LANES)], axis=0
        )
        score = nt(k_ref[:, part], query) + bias
        front = nt(pk_ref[:, part], query)
        top = jnp.maximum(
            jnp.max(score, axis=0, keepdims=True), jnp.max(front, axis=0, keepdims=True)
        )
        score = jnp.exp(score - top)
        front = jnp.exp(front - top)
        total = jnp.sum(score, axis=0, keepdims=True) + jnp.sum(front, axis=0, keepdims=True)
        scale = 1.0 / total
        prob = (score * scale).astype(BF)
        prob_mem = (front * scale).astype(BF)
        pt_ref[h] = prob
        pm_ref[h] = prob_mem
        mix_ref[part, :] = nn(vals_t[part, :], prob) + nn(pv_t[part, :], prob_mem)
    att_scr[...] = mix_ref[...].T.astype(BF)
    for step in range(4):
        at = pl.multiple_of((here ^ step) * rows, rows)
        outs[step][...] = att_scr[pl.ds(at, rows), :]


def hidden_kernel(idx, *refs):
    wo, wo2 = refs[:2]
    parts = refs[2:6]
    x, small, small2 = refs[6:9]
    hidden_ref, n2_ref, att_ref, wo_ref, sems = refs[9:]
    here, wt = idx[1], idx[2]
    cols = parts[0].shape[1]
    half = wo.shape[0]
    copies = fetch_rows(sems, wt, [(wo_ref, wo, wo2)])
    for step in range(4):
        att_ref[here ^ step] = parts[step][...]
    for copy in copies:
        copy.wait()
    hidden = x[...].astype(F32)
    for c in range(4):
        hidden = hidden + nn(att_ref[c], wo_ref[c * cols : (c + 1) * cols, :])
    hidden_ref[...] = hidden
    scaled, _ = norm(hidden)
    n2_ref[...] = (scaled * both_gains(wt, small, small2, 1)).astype(BF)


def gelu_parts(v):
    scale = 0.7978845608028654
    square = v * v
    t = jnp.tanh(scale * v * (1.0 + 0.044715 * square))
    grad = 0.5 * (1.0 + t) + 0.5 * v * (1.0 - t * t) * scale * (1.0 + 0.134145 * square)
    return 0.5 * v * (1.0 + t), grad


def own_columns(batch, ff_own, block):
    return [pl.ds(pl.multiple_of(o * ff_own + batch * block, block), block) for o in range(2)]


def ffn_kernel(idx, *refs):
    w1, w1b, w2, w2b = refs[:4]
    n2s, gs = refs[4:8], refs[8:12]
    norms = refs[12:16]
    act_ref, gi_ref, w2_ref, w1_scr, sems = refs[16:]
    batch, wt = idx[0], idx[2]
    half = w1.shape[0]
    block = w1_scr.shape[1] // 2
    ff_own = w2.shape[0]
    copies = []
    for j, (source, place) in enumerate(((w1, wt), (w1b, 1 - wt))):
        to = pl.ds(pl.multiple_of(place * half, half), half)
        for o, cut in enumerate(own_columns(batch, ff_own, block)):
            copies.append(
                pltpu.make_async_copy(
                    source.at[:, cut],
                    w1_scr.at[to, o * block : (o + 1) * block],
                    sems.at[2 * j + o],
                )
            )
    cut = pl.ds(pl.multiple_of(batch * block, block), block)
    for j, (source, place) in enumerate(((w2, wt), (w2b, 1 - wt))):
        to = pl.ds(pl.multiple_of(place * block, block), block)
        copies.append(pltpu.make_async_copy(source.at[cut, :], w2_ref.at[to, :], sems.at[4 + j]))
    for copy in copies:
        copy.start()
    for copy in copies[:4]:
        copy.wait()
    rows = n2s[0].shape[0]
    for s in range(4):
        at = slice(s * rows, (s + 1) * rows)
        act, slope = gelu_parts(nn(n2s[s][...], w1_scr[...]))
        if s == 0:
            for copy in copies[4:]:
                copy.wait()
        act_ref[at, :] = act.astype(BF)
        grad = (nt(gs[s][...], w2_ref[...]).astype(BF).astype(F32) * slope).astype(BF)
        gi_ref[at, :] = grad
        norms[s][...] = nt(grad, w1_scr[...]).astype(BF)


def ffn_back_kernel(idx, *refs):
    n2s, gs = refs[:4], refs[4:8]
    act, gi, w2 = refs[8:11]
    mine, theirs, keep, send, all_scr, scr = refs[11:]
    here, wt = idx[1], idx[2]
    rows = n2s[0].shape[0]
    size = scr.shape[0] // 8

    def spread(p):
        for i, out in enumerate((mine, theirs)):
            for j, place in enumerate(NEAR_LAST):
                at = pl.multiple_of(((wt ^ i) * 4 + (here ^ place)) * size, size)
                to = (2 * j + p) * size
                out[to : to + size, :] = scr[pl.ds(at, size), :]

    for s in range(4):
        all_scr[s * rows : (s + 1) * rows, :] = n2s[s][...]
    scr[...] = tn(all_scr[...], gi[...]).astype(BF)
    spread(0)
    for s in range(4):
        all_scr[s * rows : (s + 1) * rows, :] = gs[s][...]
    scr[...] = tn(act[...], all_scr[...]).astype(BF)
    spread(1)
    for s, (out, to) in enumerate(((keep, 0), (keep, rows), (send, 0), (send, rows))):
        out[to : to + rows, :] = nn(act[s * rows : (s + 1) * rows, :], w2[...]).astype(BF)


def hidden_back_kernel(idx, *refs):
    parts = refs[:4]
    hidden_ref, small, small2, g, wo = refs[4:9]
    grad_ref, low_ref = refs[9:11]
    outs = refs[11:]
    here, wt = idx[1], idx[2]
    cols = outs[0].shape[1]
    half = wo.shape[0] // 2
    grad_norm = parts[0][...].astype(F32)
    for part in parts[1:]:
        grad_norm = grad_norm + part[...].astype(F32)
    scaled, inverse = norm(hidden_ref[...])
    e = grad_norm * both_gains(wt, small, small2, 1)
    grad = g[...].astype(F32) + inverse * (
        e - scaled * jnp.mean(e * scaled, axis=-1, keepdims=True)
    )
    grad_ref[...] = grad
    low = grad.astype(BF)
    low_ref[...] = low
    for step in range(4):
        at = pl.multiple_of((here ^ step) * cols, cols)
        outs[step][...] = nt(low, wo[pl.ds(at, cols), :]).astype(BF)


def wo_back_kernel(idx, att, low, mine, theirs, scr):
    batch, here, wt = idx[0], idx[1], idx[2]
    size = att.shape[2]
    for c in range(4):
        scr[c * size : (c + 1) * size, :] = tn(att[c], low[...])
    size = scr.shape[0] // 32
    for i, out in enumerate((mine, theirs)):
        for q, far in enumerate(NEAR_LAST):
            for p, place in enumerate(NEAR_LAST):
                at = (((wt ^ i) * 4 + (here ^ place)) * 4 + (batch ^ far)) * size
                to = (4 * q + p) * size
                out[to : to + size, :] = scr[pl.ds(pl.multiple_of(at, 8), size), :].astype(BF)


def heads_back_kernel(heads, hsize, idx, *refs):
    gms = refs[:4]
    pt, pm, q, k, v, mix, pk, pv, bucket_row, n1 = refs[4:14]
    mine, theirs = refs[14:16]
    own_out, near_out, far_out = refs[16:19]
    gm_scr, gqt_scr, acc, grad_scr, w_scr = refs[19:]
    batch, here, wt = idx[0], idx[1], idx[2]
    rows, cols = gms[0].shape
    length = 4 * rows
    mem = pk.shape[0]
    high = own_out.shape[0]
    outs = (own_out, far_out, near_out.at[:high], near_out.at[high:])
    for step in range(4):
        at = pl.multiple_of((here ^ step) * rows, rows)
        gm_scr[pl.ds(at, rows), :] = gms[step][...]
    gm_t = gm_scr[...].T
    keys_t = k[...].T
    pk_t = pk[...].astype(F32).T.astype(BF)
    lines = []
    for h in range(heads):
        part = slice(h * hsize, (h + 1) * hsize)
        gm = gm_scr[:, part]
        query = q[:, part]
        spread = jnp.sum(gm_t[part, :].astype(F32) * mix[part, :], axis=0, keepdims=True)
        prob = pt[h]
        prob_mem = pm[h]
        score = prob.astype(F32) * (nt(v[:, part], gm) - spread)
        front = (prob_mem.astype(F32) * (nt(pv[:, part], gm) - spread)).astype(BF)
        low = score.astype(BF)
        gqt_scr[part, :] = nn(keys_t[part, :], low) + nn(pk_t[part, :], front)
        grad_scr[1, :, part] = nn(low, query).astype(BF)
        grad_scr[2, :, part] = nn(prob, gm).astype(BF)
        mem_k = nn(front, query).astype(BF)
        mem_v = nn(prob_mem, gm).astype(BF)
        for step in range(4):
            outs[step][3 * rows + MEM_K : 3 * rows + MEM_K + mem, part] = mem_k
            outs[step][3 * rows + MEM_V : 3 * rows + MEM_V + mem, part] = mem_v
        acc[...] = jnp.zeros_like(acc)
        for at in range(0, length, LANES):
            acc[:, length - at : 2 * length - at] += score[at : at + LANES, :]
        fold = acc[...]
        size = LANES // 2
        while size >= 8:
            fold = fold[:size] + pltpu.roll(fold[size:], 2 * length - size, 1)
            size //= 2
        line = fold[0:1]
        for i in range(1, 8):
            line = line + pltpu.roll(fold[i : i + 1], 2 * length - i, 1)
        lines.append(line)
    grad_scr[0] = gqt_scr[...].T.astype(BF)
    normed = n1[...]
    for p in range(3):
        w_scr[:, p * cols : (p + 1) * cols] = tn(normed, grad_scr[p]).astype(BF)
    size = w_scr.shape[0] // 8
    for i, out in enumerate((mine, theirs)):
        for j, far in enumerate(NEAR_LAST):
            at = pl.multiple_of(((wt ^ i) * 4 + (batch ^ far)) * size, size)
            out[j * size : (j + 1) * size, :] = w_scr[pl.ds(at, size), :]
    lines.append(jnp.zeros((LINE - heads, 2 * length), F32))
    table = lax.dot_general(
        jnp.concatenate(lines, axis=0),
        one_hot_rows(bucket_row[...], LANES),
        (((1,), (1,)), ((), ())),
        precision=lax.Precision.HIGHEST,
        preferred_element_type=F32,
    )
    wide = w_scr.shape[1]
    table = jnp.concatenate([table, jnp.zeros((LINE, wide - LANES), F32)], axis=1)
    for out in (mine, theirs):
        out[4 * size :, :] = table.astype(BF)
    for step in range(4):
        at = pl.multiple_of((here ^ step) * rows, rows)
        for p in range(3):
            outs[step][p * rows : (p + 1) * rows, :] = grad_scr[p, pl.ds(at, rows), :]


def halving_kernel(lines, *refs):
    count = len(lines)
    for i, line in enumerate(lines):
        own, got = refs[2 * i], refs[2 * i + 1]
        keep, send = refs[2 * count + 2 * i], refs[2 * count + 2 * i + 1]
        total = (own[...].astype(F32) + got[...].astype(F32)).astype(BF)
        half = (total.shape[0] - line) // 2
        keep[:half, :] = total[:half]
        send[:half, :] = total[half : 2 * half]
        if line:
            keep[half:, :] = total[2 * half :]
            send[half:, :] = total[2 * half :]


def halving(name, items):
    args, out = [], []
    for own, got, line in items:
        args += [own, got]
        out += [shape(((own.shape[0] - line) // 2 + line, own.shape[1]), BF)] * 2
    return pl.pallas_call(
        functools.partial(halving_kernel, [line for _, _, line in items]),
        out_shape=out,
        in_specs=vmem(len(args)),
        out_specs=vmem(len(out)),
        compiler_params=params(32),
        name=name,
    )(*args)


def row_sums(values):
    return lax.dot_general(
        jnp.ones((8, values.shape[1]), F32),
        values,
        (((1,), (1,)), ((), ())),
        precision=lax.Precision.HIGHEST,
        preferred_element_type=F32,
    )


def ffn_piece_kernel(idx, w_in, ffn, ffn2, piece_ref, sum_ref, w_scr, sems):
    batch, here = idx[0], idx[1]
    quarter, width = w_scr.shape
    block = width // 2
    rows = pl.ds(pl.multiple_of(here * quarter, quarter), quarter)
    copies = [
        pltpu.make_async_copy(
            w_in.at[rows, cut], w_scr.at[:, o * block : (o + 1) * block], sems.at[o]
        )
        for o, cut in enumerate(own_columns(batch, w_in.shape[1] // 2, block))
    ]
    for copy in copies:
        copy.start()
    grad = ffn[...].astype(F32) + ffn2[...].astype(F32)
    piece_ref[...] = grad.astype(BF)
    for copy in copies:
        copy.wait()
    sum_ref[...] = row_sums(grad[:quarter] * w_scr[...].astype(F32))


def heads_piece_kernel(qkv, qkv2, wo, wo2, wrow, sum_in, piece_ref):
    size, width = wo.shape
    quarter = wrow.shape[0]
    wide = wrow.shape[1]
    heads = qkv[...].astype(F32) + qkv2[...].astype(F32)
    piece_ref[:quarter, :] = heads[:quarter].astype(BF)
    sum_heads = row_sums(heads[:quarter] * wrow[...].astype(F32))
    out = wo[...].astype(F32) + wo2[...].astype(F32)
    piece_ref[quarter : quarter + size, :] = out[:, :wide].astype(BF)
    third = size // 3
    cols = width - wide
    for o in range(3):
        piece_ref[quarter + size : quarter + size + third, o * cols : (o + 1) * cols] = out[
            o * third : (o + 1) * third, wide:
        ].astype(BF)
    row = lax.broadcasted_iota(jnp.int32, (LINE, quarter), 0)
    sums = jnp.where(row == LINE - 2, sum_heads, jnp.where(row == LINE - 1, sum_in[...], 0.0))
    at = quarter + size + third
    line = heads[quarter:]
    pad = jnp.zeros((LINE, LANES), F32)
    sums = jnp.concatenate([sums, jnp.zeros((LINE, LANES - quarter), F32)], axis=1)
    line = line + jnp.concatenate([pad, sums, jnp.zeros((LINE, wide - 2 * LANES), F32)], axis=1)
    piece_ref[at:, :] = line.astype(BF)


def ctx_pieces(refs, at, order):
    one, two, four, one2, two2, four2 = refs
    rows = one.shape[0]
    size = rows // 2
    first = ((one, 0), (two, 0), (four, 0), (four, rows))
    last = ((one2, 0), (four2, 0), (two2, 0), (four2, rows))
    if order == 2:
        first = ((one, 0), (four, 0), (two, 0), (four, rows))
        last = ((one2, 0), (two2, 0), (four2, 0), (four2, rows))
    near, far = first[at], last[at]
    found = []
    for (ref, start), places in ((near, (0, 2)), (far, (1, 3))):
        for i, place in enumerate(places):
            found.append((place, ref, start + i * size, size))
    return found


def rows_out_kernel(idx, *refs):
    out, scr, sems = refs[6:]
    copies = []
    for at in range(4):
        for place, ref, start, size in ctx_pieces(refs[:6], at, 2):
            row = len(copies) * size
            scr[row : row + size, :] = ref[start : start + size, :].astype(F32)
            to = pl.multiple_of(((idx[0] ^ at) * 4 + (idx[1] ^ place)) * size, size)
            copies.append(
                pltpu.make_async_copy(
                    scr.at[row : row + size, :], out.at[pl.ds(to, size), :], sems.at[len(copies)]
                )
            )
            copies[-1].start()
    for copy in copies:
        copy.wait()


def cols_out_kernel(idx, *refs):
    out, scr, sems = refs[6:]
    copies = []
    block = scr.shape[1] // 2
    for at in range(4):
        for place, ref, start, size in ctx_pieces(refs[:6], at, 1):
            row = (len(copies) // 2) * size
            scr[row : row + size, :] = ref[start : start + size, :].astype(F32)
            to = pl.multiple_of((idx[1] ^ place) * size, size)
            for o in range(2):
                col = pl.multiple_of((4 * o + (idx[0] ^ at)) * block, block)
                copies.append(
                    pltpu.make_async_copy(
                        scr.at[row : row + size, o * block : (o + 1) * block],
                        out.at[pl.ds(to, size), pl.ds(col, block)],
                        sems.at[len(copies)],
                    )
                )
                copies[-1].start()
    for copy in copies:
        copy.wait()


def pieces_out(kernel, name, index, pieces, dims, copies):
    rows, width = pieces[0].shape
    return pl.pallas_call(
        kernel,
        out_shape=shape(dims, F32),
        in_specs=[smem()] + vmem(6),
        out_specs=pl.BlockSpec(memory_space=pltpu.HBM),
        scratch_shapes=[
            pltpu.VMEM((8 * rows, width), F32),
            pltpu.SemaphoreType.DMA((copies,)),
        ],
        compiler_params=params(16),
        name=name,
    )(index, *pieces)


def heads_out_kernel(heads, buckets, idx, *refs):
    small = refs[6]
    oq, ok, ov, oo, gain_one, gain_two, table, scr, lines, tab_scr = refs[7:]
    step = pl.program_id(0)
    quarter, width = oq.shape
    cols = width // 4
    wide = 3 * cols
    size = quarter // 4
    third = size // 3
    for at in range(4):

        @pl.when(step == at)
        def _():
            for place, ref, start, height in ctx_pieces(refs[:6], at, 1):
                scr[idx[1] ^ place] = ref[start : start + height, :]

    for c in range(4):
        part = scr[c].astype(F32)
        for o, out in enumerate((oq, ok, ov)):
            out[:, c * cols : (c + 1) * cols] = part[:quarter, o * cols : (o + 1) * cols]
        oo[c, 0, :, :wide] = part[quarter : quarter + size]
        for o in range(3):
            oo[c, 0, o * third : (o + 1) * third, wide:] = part[
                quarter + size : quarter + size + third, o * cols : (o + 1) * cols
            ]
        lines[idx[0] ^ step, c] = part[quarter + size + third :]

    @pl.when(step == 3)
    def _():
        seen = [[lines[b, c] for c in range(4)] for b in range(4)]
        take = slice(LANES, LANES + quarter)
        one = jnp.concatenate(
            [sum(seen[b][c][LINE - 2 : LINE - 1, take] for c in range(4)) for b in range(4)], axis=1
        )
        two = jnp.concatenate(
            [sum(seen[b][c][LINE - 1 : LINE, take] for b in range(4)) for c in range(4)], axis=1
        )
        gain_one[...] = (one / small[0:1, :].astype(F32))[0]
        gain_two[...] = (two / small[1:2, :].astype(F32))[0]
        rest = [seen[0][c][:heads, :LANES] for c in range(4)]
        rest.append(jnp.zeros((LANES - 4 * heads, LANES), F32))
        tab_scr[...] = jnp.concatenate(rest, axis=0).T
        own_buckets = buckets // 2
        at = pl.multiple_of(idx[2] * own_buckets, 8)
        table[...] = tab_scr[pl.ds(at, own_buckets), : 4 * heads]


def heads_out(index, pieces, small, width, heads, buckets):
    height, wide = pieces[0].shape[0] // 2, pieces[0].shape[1]
    part = width // 2
    quarter = part // 4
    size = quarter // 4
    block = pl.BlockSpec((quarter, width), lambda step, idx: (idx[0] ^ step, 0))
    whole = [pl.BlockSpec(p.shape, lambda step, idx: (0, 0)) for p in (*pieces, small)]
    return pl.pallas_call(
        functools.partial(heads_out_kernel, heads, buckets),
        out_shape=[shape((part, width), F32)] * 3
        + [
            shape((4, 4, size, width), F32),
            shape((part,), F32),
            shape((part,), F32),
            shape((buckets // 2, 4 * heads), F32),
        ],
        grid_spec=pltpu.PrefetchScalarGridSpec(
            num_scalar_prefetch=1,
            grid=(4,),
            in_specs=whole,
            out_specs=[block] * 3
            + [
                pl.BlockSpec((4, 1, size, width), lambda step, idx: (0, idx[0] ^ step, 0, 0)),
                pl.BlockSpec((part,), lambda step, idx: (0,)),
                pl.BlockSpec((part,), lambda step, idx: (0,)),
                pl.BlockSpec((buckets // 2, 4 * heads), lambda step, idx: (0, 0)),
            ],
            scratch_shapes=[
                pltpu.VMEM((4, height, wide), BF),
                pltpu.VMEM((4, 4, LINE, wide), F32),
                pltpu.VMEM((LANES, LANES), F32),
            ],
        ),
        compiler_params=params(32),
        name="heads_out",
    )(index, *pieces, small)


def paired(
    inputs,
    prefix_keys,
    prefix_values,
    gain_attn,
    w_query,
    w_key,
    w_value,
    w_out,
    bias_table,
    gain_ffn,
    w_in,
    w_back,
    buckets,
    out_grad,
):
    b, c, w = lax.axis_index("batch"), lax.axis_index("ctx"), lax.axis_index("wt")
    index = jnp.stack([b, c, w])
    x, g = inputs[0], out_grad[0]
    rows, width = x.shape
    all_heads = bias_table.shape[1]
    heads = all_heads // 4
    hsize = width // all_heads
    cols = heads * hsize
    wide = 3 * cols
    mem = prefix_keys.shape[1]
    length = 4 * rows
    part = width // 2
    quarter = part // 4
    ff_own = w_back.shape[0]
    ff_part = ff_own // 4
    nbuck = 2 * bias_table.shape[0]

    def over_wt(value, name):
        with jax.named_scope(name + "_w"):
            return flip(value, "wt", 2, 1)

    def over_ctx(value, step, name):
        with jax.named_scope(name + "_z" + str(step)):
            return flip(value, "ctx", 4, step)

    def over_batch(value, step, name):
        with jax.named_scope(name + "_b" + str(step)):
            return flip(value, "batch", 4, step)

    own_buckets = nbuck // 2
    small = jnp.concatenate(
        [
            jnp.pad(jnp.stack([gain_attn, gain_ffn]), ((0, TABLE_ROW - 2), (0, 0))),
            jnp.pad(bias_table, ((0, 0), (0, part - all_heads))),
        ]
    )
    w_query2, w_key2, w_value2 = [over_wt(v, "weight") for v in (w_query, w_key, w_value)]
    small2 = over_wt(small, "small")
    g_near = over_batch(g, 1, "g")
    x_all = lax.all_gather(x, "ctx", axis=0, tiled=True)
    bucket_row = jnp.pad(buckets[::-1].reshape(1, -1), ((0, 0), (1, 0)), constant_values=-1)

    tokens = shape((length, cols), BF)
    few = (small, small2, prefix_keys[0], prefix_values[0], bucket_row)
    (n1, q, k, v, pt, pm, mix, wrow, pk, pv, *mixed) = call(
        functools.partial(heads_kernel, heads, hsize, own_buckets),
        "attend",
        index,
        [x_all],
        [shape((length, width), BF)]
        + [tokens] * 3
        + [
            shape((heads, length, length), BF),
            shape((heads, mem, length), BF),
            shape((cols, length), F32),
            shape((quarter, wide), BF),
            shape((mem, cols), BF),
            shape((mem, cols), BF),
        ]
        + [shape((rows, cols), BF)] * 4,
        [
            pltpu.VMEM((length, cols), BF),
            pltpu.VMEM((16, 2 * length), F32),
            pltpu.SemaphoreType.DMA((6,)),
            pltpu.SemaphoreType.DMA((len(few),)),
        ]
        + [pltpu.VMEM((width, -(-cols // LANES) * LANES), BF)] * 3
        + [pltpu.VMEM(v.shape, v.dtype) for v in few],
        far=(w_query, w_key, w_value, w_query2, w_key2, w_value2, *few),
    )
    (g_pair, w_out_sent) = after((jnp.concatenate([g, g_near]), w_out), mixed[:1])
    w_out2 = over_wt(w_out_sent, "weight")
    g_far = over_batch(g_pair, 2, "g")
    mixed = mixed[:1] + [over_ctx(mixed[s], s, "mixed") for s in range(1, 4)]
    (*mixed, w_out2, g_far) = after((*mixed, w_out2, g_far), ())
    square = shape((width, width), BF)
    hidden, n2, attended, wo = call(
        hidden_kernel,
        "hidden",
        index,
        [*mixed, x, small, small2],
        [shape((rows, width), F32), shape((rows, width), BF), shape((4, rows, cols), BF), square],
        [pltpu.SemaphoreType.DMA((2,))],
        far=(w_out, w_out2),
    )

    n2s = [n2] + [over_batch(n2, s, "n2") for s in range(1, 4)]
    (w_in_sent, w_back_sent) = after((w_in, w_back), (n2,))
    w_in2, w_back2 = over_wt(w_in_sent, "in"), over_wt(w_back_sent, "back")
    gs = (g, g_near, g_far[:rows], g_far[rows:])
    hid = shape((length, 2 * ff_part), BF)
    *norms, act, gi, w_second = call(
        ffn_kernel,
        "ffn",
        index,
        [*n2s, *gs],
        [shape((rows, width), BF)] * 4 + [hid, hid, shape((2 * ff_part, width), BF)],
        [pltpu.VMEM((width, 2 * ff_part), BF), pltpu.SemaphoreType.DMA((6,))],
        far=(w_in, w_in2, w_back, w_back2),
    )
    norms = norms[:1] + [over_batch(norms[s], s, "norm") for s in range(1, 4)]
    ffn, ffn_sent, outs, outs_sent = call(
        ffn_back_kernel,
        "ffn_back",
        index,
        [*n2s, *gs, act, gi, w_second],
        [square, square] + [shape((2 * rows, width), BF)] * 2,
        [pltpu.VMEM((length, width), BF), pltpu.VMEM((width, width), BF)],
    )
    ffn, ffn_sent = halving("ffn_wt", [(ffn, over_wt(ffn_sent, "ffn"), 0)])
    ffn_got = over_ctx(ffn_sent, 1, "ffn")
    norms = after(norms, (ffn, ffn_got))
    grad_hidden, low, *gms = call(
        hidden_back_kernel,
        "hidden_back",
        index,
        [*norms, hidden, small, small2, g, wo],
        [shape((rows, width), F32), shape((rows, width), BF)] + [shape((rows, cols), BF)] * 4,
    )
    ffn, ffn_sent = halving("ffn_near", [(ffn, ffn_got, 0)])
    outs_got = over_batch(outs_sent, 2, "outs")
    wo_sum, wo_sent = call(
        wo_back_kernel,
        "wo_back",
        index,
        [attended, low],
        [shape((part, width), BF)] * 2,
        [pltpu.VMEM((width, width), F32)],
    )
    gms = after(gms, (ffn, ffn_sent, outs_got))
    ffn_got = over_ctx(ffn_sent, 2, "ffn")
    wo_sum, wo_sent = halving("wo_wt", [(wo_sum, over_wt(wo_sent, "wo"), 0)])
    wo_sum, wo_sent = halving("wo_near", [(wo_sum, over_batch(wo_sent, 1, "wo"), 0)])
    wo_got = over_batch(wo_sent, 2, "wo")
    gms = list(gms[:1]) + [over_ctx(gms[s], s, "gm") for s in range(1, 4)]
    (ffn_got, wo_got, *gms) = after((ffn_got, wo_got, *gms), ())
    ffn, sum_in = call(
        ffn_piece_kernel,
        "ffn_piece",
        index,
        [ffn, ffn_got],
        [shape((2 * quarter, width), BF), shape((8, quarter), F32)],
        [pltpu.VMEM((quarter, width), BF), pltpu.SemaphoreType.DMA((2,))],
        far=(w_in,),
    )
    wo_sum, wo_sent = halving("wo_far", [(wo_sum, wo_got, 0)])
    gms = after(gms, (ffn, wo_sum, wo_sent))
    outs, outs_sent = halving("outs_far", [(outs, outs_got, 0)])
    (outs_sent,) = after((outs_sent,), (ffn, wo_sum))
    ffn_far = over_ctx(ffn, 2, "ffn_back")
    high = 3 * rows + MEM_END
    (qkv, qkv_sent, own_block, near_blocks, far_block) = call(
        functools.partial(heads_back_kernel, heads, hsize),
        "attend_back",
        index,
        [*gms, pt, pm, q, k, v, mix, pk, pv, bucket_row, n1],
        [shape((part + LINE, wide), BF)] * 2
        + [shape((n * high, cols), BF) for n in (1, 2, 1)],
        [
            pltpu.VMEM((length, cols), BF),
            pltpu.VMEM((cols, length), F32),
            pltpu.VMEM((LANES, 2 * length), F32),
            pltpu.VMEM((3, length, cols), BF),
            pltpu.VMEM((width, wide), BF),
        ],
    )
    wo_sum, wo_sent = halving("wo_last", [(wo_sum, over_ctx(wo_sent, 1, "wo"), 0)])
    wo_got = over_ctx(wo_sent, 2, "wo")
    outs_got = over_batch(outs_sent, 1, "outs")
    qkv, qkv_sent = halving("qkv_wt", [(qkv, over_wt(qkv_sent, "qkv"), LINE)])
    qkv_got = over_batch(qkv_sent, 1, "qkv")
    (qkv_got,) = after((qkv_got,), (ffn_far, outs_got))
    qkv, qkv_sent = halving("qkv_near", [(qkv, qkv_got, LINE)])
    qkv_got = over_batch(qkv_sent, 2, "qkv")
    (ffn_far, wo_got) = after((ffn_far, wo_got), (qkv_sent,))

    def pile(one, two):
        return jnp.concatenate([one, two])

    result = (hidden + outs.astype(F32) + outs_got.astype(F32)).astype(BF)
    a1 = pile(ffn[:quarter], ffn_far[:quarter])
    b1 = pile(ffn[quarter:], ffn_far[quarter:])
    a2, b2 = over_batch(a1, 1, "in_near"), over_batch(b1, 2, "out_near")
    c1, d1 = over_ctx(a1, 1, "in_back"), over_ctx(b1, 1, "out_back")
    pile_a, pile_b = pile(a1, a2), pile(b1, b2)
    a3, b3 = over_batch(pile_a, 2, "in_near2"), over_batch(pile_b, 1, "out_near2")
    (c1, d1) = after((c1, d1), (pile_a, pile_b))
    c2, d2 = over_batch(c1, 2, "in_far"), over_batch(d1, 1, "out_far")
    height = quarter + quarter // 4 + quarter // 12 + LINE
    piece = pl.pallas_call(
        heads_piece_kernel,
        out_shape=shape((height, wide), BF),
        in_specs=vmem(6),
        out_specs=vmem(1)[0],
        compiler_params=params(32),
        name="heads_piece",
    )(qkv, qkv_got, wo_sum, wo_got, wrow, sum_in)

    (piece,) = after((piece,), (c1, d1))
    heads_far = over_ctx(piece, 2, "heads_back")
    pile_c, pile_d = pile(c1, c2), pile(d1, d2)
    c3, d3 = over_batch(pile_c, 1, "in_far2"), over_batch(pile_d, 2, "out_far2")
    (heads_far,) = after((heads_far,), (a3, b3))
    (near_blocks,) = after((near_blocks,), (heads_far,))
    near_got = over_ctx(near_blocks, 2, "sends")
    far_pile = pile(far_block, near_got[high:])
    far_got = over_ctx(far_pile, 1, "sends")
    e1 = pile(piece, heads_far)
    f1 = over_ctx(e1, 1, "heads_back")
    (e1, f1) = after((e1, f1), (pile_c, pile_d))
    e2, f2 = over_batch(e1, 1, "heads_near"), over_batch(f1, 2, "heads_far")
    (e1, e2, f1, f2) = after((e1, e2, f1, f2), (c3, d3, far_pile))
    e3 = over_batch(pile(e1, e2), 2, "heads_near2")
    f3 = over_batch(pile(f1, f2), 1, "heads_far2")
    out_second = pieces_out(
        rows_out_kernel, "rows_out", index, (b1, b2, b3, d1, d2, d3), (ff_own, width), 16
    )
    out_first = pieces_out(
        cols_out_kernel, "cols_out", index, (a1, a2, a3, c1, c2, c3), (part, 2 * ff_own), 32
    )
    out_q, out_k, out_v, out_wo, gain_one, gain_two, out_table = heads_out(
        index, (e1, e2, e3, f1, f2, f3), small, width, heads, nbuck
    )
    grad_x, grad_memk, grad_memv = call(
        input_end_kernel,
        "input_back",
        index,
        [own_block, near_got, far_got, x, small, small2, grad_hidden],
        [shape((rows, width), BF), shape((mem, width), F32), shape((mem, width), F32)],
        [pltpu.VMEM((4,) + own_block.shape, BF), pltpu.SemaphoreType.DMA((6,))]
        + [pltpu.VMEM((width, width), BF)] * 3,
        far=(w_query, w_key, w_value, w_query2, w_key2, w_value2),
    )
    return (
        result[None],
        grad_x[None],
        grad_memk[None],
        grad_memv[None],
        gain_one,
        gain_two,
        out_table,
        out_q,
        out_k,
        out_v,
        out_wo.reshape(part, width),
        out_first,
        out_second,
    )


def input_end_kernel(idx, *refs):
    wq, wk, wv, wq2, wk2, wv2 = refs[:6]
    own, near, far, x, small, small2, grad_hidden = refs[6:13]
    out_ref, memk_ref, memv_ref, scr, sems, *w_scr = refs[13:]
    high = own.shape[0]
    parts = (own, far.at[:high], near.at[:high], far.at[high:])
    here, wt = idx[1], idx[2]
    rows = x.shape[0]
    mem = memk_ref.shape[0]
    copies = fetch_rows(sems, wt, list(zip(w_scr, (wq, wk, wv), (wq2, wk2, wv2))))
    for step in range(4):
        scr[here ^ step] = parts[step][...]
    for copy in copies:
        copy.wait()

    def wide(at, count):
        return jnp.concatenate([scr[c, at : at + count, :] for c in range(4)], axis=1)

    grad_norm = sum(nt(wide(p * rows, rows), whole[...]) for p, whole in enumerate(w_scr))
    scaled, inverse = norm(x[...].astype(F32))
    e = grad_norm * both_gains(wt, small, small2, 0)
    grad = grad_hidden[...] + inverse * (
        e - scaled * jnp.mean(e * scaled, axis=-1, keepdims=True)
    )
    out_ref[...] = grad.astype(BF)
    memk_ref[...] = wide(3 * rows + MEM_K, mem).astype(F32)
    memv_ref[...] = wide(3 * rows + MEM_V, mem).astype(F32)


def solution(mesh):
    tokens = P(("batch", "wt"), "ctx", None)
    memory = P(("batch", "wt"), None, None)
    matrix = P("wt", None)
    vector = P("wt")
    sizes = (mesh.shape["batch"], mesh.shape["ctx"], mesh.shape["wt"])
    body = paired if sizes == (4, 4, 2) else functools.partial(general, sizes)
    return jax.shard_map(
        body,
        mesh=mesh,
        in_specs=(
            tokens, memory, memory, vector, matrix, matrix, matrix, matrix, matrix, vector,
            matrix, matrix, P(), tokens,
        ),
        out_specs=(
            tokens, tokens, memory, memory, vector, vector, matrix, matrix, matrix, matrix,
            matrix, matrix, matrix,
        ),
        check_vma=False,
    )
```

```python
import functools

import jax
import jax.numpy as jnp
from jax import lax
from jax.experimental import pallas as pl
from jax.experimental.pallas import tpu as pltpu
from jax.sharding import PartitionSpec as P

EPS = 1e-06
F32 = jnp.float32
BF = jnp.bfloat16
LANES = 128


def nn(left, right):
    return lax.dot_general(left, right, (((1,), (0,)), ((), ())), preferred_element_type=F32)


def nt(left, right):
    return lax.dot_general(left, right, (((1,), (1,)), ((), ())), preferred_element_type=F32)


def tn(left, right):
    return lax.dot_general(left, right, (((0,), (0,)), ((), ())), preferred_element_type=F32)


def vmem(count):
    return [pl.BlockSpec(memory_space=pltpu.VMEM)] * count


def smem():
    return pl.BlockSpec(memory_space=pltpu.SMEM)


def shape(dims, kind):
    return jax.ShapeDtypeStruct(dims, kind)


def params(mib):
    return pltpu.CompilerParams(vmem_limit_bytes=mib << 20)


def flip(value, axis, size, step):
    return lax.ppermute(value, axis, [(i, i ^ step) for i in range(size)])


def gather_flip(value, axis, size):
    return [value] + [flip(value, axis, size, step) for step in range(1, size)]


def canonical(parts, index):
    whole = jnp.zeros((len(parts),) + parts[0].shape, parts[0].dtype)
    for step, part in enumerate(parts):
        whole = lax.dynamic_update_index_in_dim(whole, part, index ^ step, 0)
    return whole


def gather_wt(value, size):
    if size == 2:
        own = lax.axis_index("wt") == 0
        other = flip(value, "wt", 2, 1)
        return jnp.stack([jnp.where(own, value, other), jnp.where(own, other, value)])
    return lax.all_gather(value, "wt", axis=0)


def sum_wt(value, size):
    rows = value.shape[0] // size
    if size == 2:
        index = lax.axis_index("wt")
        mine = lax.dynamic_slice_in_dim(value, index * rows, rows, 0)
        theirs = lax.dynamic_slice_in_dim(value, (1 - index) * rows, rows, 0)
        return mine.astype(F32) + flip(theirs, "wt", 2, 1).astype(F32)
    return lax.psum_scatter(value, "wt", scatter_dimension=0, tiled=True).astype(F32)


def sum_flip(blocks, index, axis, size):
    total = lax.dynamic_index_in_dim(blocks, index, 0, keepdims=False).astype(F32)
    for step in range(1, size):
        block = lax.dynamic_index_in_dim(blocks, index ^ step, 0, keepdims=False)
        total = total + flip(block, axis, size, step).astype(F32)
    return total


def norm(values):
    inverse = lax.rsqrt(jnp.mean(values * values, axis=-1, keepdims=True) + EPS)
    return values * inverse, inverse


def one_hot_rows(bucket_row, buckets):
    ids = lax.broadcasted_iota(jnp.int32, (buckets, bucket_row.shape[1]), 0)
    return (ids == bucket_row).astype(F32)


def attend_kernel(nc, heads, hsize, mem, idx, *refs):
    xs = refs[:nc]
    wq, wk, wv, gain, pk, pv, tab, bucket_row = refs[nc : nc + 8]
    n1_ref, q_ref, k_ref, v_ref, pt_ref, pm_ref, mix_ref = refs[nc + 8 : nc + 15]
    outs = refs[nc + 15 : nc + 15 + nc]
    att_scr = refs[nc + 15 + nc]
    here = idx[0]
    rows = xs[0].shape[0]
    length = nc * rows
    for step in range(nc):
        scaled, _ = norm(xs[step][...].astype(F32))
        at = pl.multiple_of((here ^ step) * rows, rows)
        n1_ref[pl.ds(at, rows), :] = (scaled * gain[...]).astype(BF)
    normed = n1_ref[...]
    q_ref[...] = nn(normed, wq[...]).astype(BF)
    k_ref[...] = nn(normed, wk[...]).astype(BF)
    v_ref[...] = nn(normed, wv[...]).astype(BF)
    vals_t = v_ref[...].T
    pv_t = pv[...].astype(F32).T.astype(BF)
    hot = one_hot_rows(bucket_row[...], tab.shape[1])
    lines = nn(tab[...], hot)
    for h in range(heads):
        part = slice(h * hsize, (h + 1) * hsize)
        query = q_ref[:, part]
        line = jnp.broadcast_to(lines[h : h + 1, :], (LANES, 2 * length))
        spread = pltpu.roll(line, 0, 1, stride=1, stride_axis=0)
        bias = jnp.concatenate(
            [spread[:, length - at : 2 * length - at] for at in range(0, length, LANES)], axis=0
        )
        score = nt(k_ref[:, part], query) + bias
        front = nt(pk[:, part], query)
        top = jnp.maximum(
            jnp.max(score, axis=0, keepdims=True), jnp.max(front, axis=0, keepdims=True)
        )
        score = jnp.exp(score - top)
        front = jnp.exp(front - top)
        total = jnp.sum(score, axis=0, keepdims=True) + jnp.sum(front, axis=0, keepdims=True)
        scale = 1.0 / total
        prob = (score * scale).astype(BF)
        prob_mem = (front * scale).astype(BF)
        pt_ref[h] = prob
        pm_ref[h] = prob_mem
        mix_ref[part, :] = nn(vals_t[part, :], prob) + nn(pv_t[part, :], prob_mem)
    att_scr[...] = mix_ref[...].T.astype(BF)
    for step in range(nc):
        at = pl.multiple_of((here ^ step) * rows, rows)
        outs[step][...] = att_scr[pl.ds(at, rows), :]


def attend(nc, heads, hsize, index, xs, wq, wk, wv, gain, pk, pv, tab, bucket_row):
    rows, width = xs[0].shape
    length = rows * nc
    cols = heads * hsize
    mem = pk.shape[0]
    out = [
        shape((length, width), BF),
        shape((length, cols), BF),
        shape((length, cols), BF),
        shape((length, cols), BF),
        shape((heads, length, length), BF),
        shape((heads, mem, length), BF),
        shape((cols, length), F32),
    ] + [shape((rows, cols), BF)] * nc
    return pl.pallas_call(
        functools.partial(attend_kernel, nc, heads, hsize, mem),
        out_shape=out,
        in_specs=[smem()] + vmem(nc + 8),
        out_specs=vmem(len(out)),
        scratch_shapes=[pltpu.VMEM((length, cols), BF)],
        compiler_params=params(24),
        name="attend",
    )(index, *xs, wq, wk, wv, gain, pk, pv, tab, bucket_row)


def branch_kernel(nc, idx, *refs):
    parts = refs[:nc]
    x, wo, gain = refs[nc : nc + 3]
    hidden_ref, n2_ref, att_ref = refs[nc + 3 : nc + 6]
    here = idx[0]
    cols = parts[0].shape[1]
    for step in range(nc):
        att_ref[here ^ step] = parts[step][...]
    hidden = x[...].astype(F32)
    for c in range(nc):
        hidden = hidden + nn(att_ref[c], wo[c * cols : (c + 1) * cols, :])
    hidden_ref[...] = hidden
    scaled, _ = norm(hidden)
    n2_ref[...] = (scaled * gain[...]).astype(BF)


def branch(nc, index, parts, x, wo, gain):
    rows, cols = parts[0].shape
    out = [shape(x.shape, F32), shape(x.shape, BF), shape((nc, rows, cols), BF)]
    return pl.pallas_call(
        functools.partial(branch_kernel, nc),
        out_shape=out,
        in_specs=[smem()] + vmem(nc + 3),
        out_specs=vmem(3),
        compiler_params=params(32),
        name="branch",
    )(index, *parts, x, wo, gain)


def branch_back_kernel(nb, nc, idx, *refs):
    parts = refs[:nb]
    hidden_ref, gain, g, wo = refs[nb : nb + 4]
    grad_ref, low_ref = refs[nb + 4 : nb + 6]
    outs = refs[nb + 6 : nb + 6 + nc]
    here = idx[0]
    cols = outs[0].shape[1]
    grad_norm = parts[0][...].astype(F32)
    for part in parts[1:]:
        grad_norm = grad_norm + part[...].astype(F32)
    scaled, inverse = norm(hidden_ref[...])
    e = grad_norm * gain[...]
    grad = g[...].astype(F32) + inverse * (
        e - scaled * jnp.mean(e * scaled, axis=-1, keepdims=True)
    )
    grad_ref[...] = grad
    low = grad.astype(BF)
    low_ref[...] = low
    for step in range(nc):
        at = pl.multiple_of((here ^ step) * cols, 8)
        outs[step][...] = nt(low, wo[pl.ds(at, cols), :]).astype(BF)


def branch_back(nb, nc, index, parts, hidden, gain, g, wo):
    rows, width = hidden.shape
    cols = width // nc
    out = [shape((rows, width), F32), shape((rows, width), BF)] + [shape((rows, cols), BF)] * nc
    return pl.pallas_call(
        functools.partial(branch_back_kernel, nb, nc),
        out_shape=out,
        in_specs=[smem()] + vmem(nb + 4),
        out_specs=vmem(len(out)),
        compiler_params=params(32),
        name="branch_back",
    )(index, *parts, hidden, gain, g, wo)


MEM_K, MEM_V, MEM_END = 0, 32, 64


def attend_back_kernel(nc, heads, hsize, idx, *refs):
    gms = refs[:nc]
    pt, pm, q, k, v, mix, pk, pv, bucket_row = refs[nc : nc + 9]
    grad_ref, table_ref = refs[nc + 9 : nc + 11]
    outs = refs[nc + 11 : nc + 11 + nc]
    gm_scr, gqt_scr, acc = refs[nc + 11 + nc :]
    here = idx[0]
    rows, cols = gms[0].shape
    length = rows * nc
    mem = pk.shape[0]
    for step in range(nc):
        at = pl.multiple_of((here ^ step) * rows, rows)
        gm_scr[pl.ds(at, rows), :] = gms[step][...]
    gm_t = gm_scr[...].T
    keys_t = k[...].T
    pk_t = pk[...].astype(F32).T.astype(BF)
    lines = []
    for h in range(heads):
        part = slice(h * hsize, (h + 1) * hsize)
        gm = gm_scr[:, part]
        query = q[:, part]
        spread = jnp.sum(gm_t[part, :].astype(F32) * mix[part, :], axis=0, keepdims=True)
        prob = pt[h]
        prob_mem = pm[h]
        score = prob.astype(F32) * (nt(v[:, part], gm) - spread)
        front = (prob_mem.astype(F32) * (nt(pv[:, part], gm) - spread)).astype(BF)
        low = score.astype(BF)
        gqt_scr[part, :] = nn(keys_t[part, :], low) + nn(pk_t[part, :], front)
        grad_ref[:, cols + h * hsize : cols + (h + 1) * hsize] = nn(low, query).astype(BF)
        grad_ref[:, 2 * cols + h * hsize : 2 * cols + (h + 1) * hsize] = nn(prob, gm).astype(BF)
        mem_k = nn(front, query).astype(BF)
        mem_v = nn(prob_mem, gm).astype(BF)
        for step in range(nc):
            outs[step][3 * rows + MEM_K : 3 * rows + MEM_K + mem, part] = mem_k
            outs[step][3 * rows + MEM_V : 3 * rows + MEM_V + mem, part] = mem_v
        acc[...] = jnp.zeros_like(acc)
        for at in range(0, length, LANES):
            acc[:, length - at : 2 * length - at] += score[at : at + LANES, :]
        fold = acc[...]
        half = LANES // 2
        while half >= 8:
            fold = fold[:half] + pltpu.roll(fold[half:], 2 * length - half, 1)
            half //= 2
        line = fold[0:1]
        for i in range(1, 8):
            line = line + pltpu.roll(fold[i : i + 1], 2 * length - i, 1)
        lines.append(line)
    lines.append(jnp.zeros((8 - heads, 2 * length), F32))
    hot = one_hot_rows(bucket_row[...], table_ref.shape[0])
    table_ref[...] = lax.dot_general(
        hot,
        jnp.concatenate(lines, axis=0),
        (((1,), (1,)), ((), ())),
        precision=lax.Precision.HIGHEST,
        preferred_element_type=F32,
    )
    grad_ref[:, :cols] = gqt_scr[...].T.astype(BF)
    for step in range(nc):
        at = pl.multiple_of((here ^ step) * rows, rows)
        for p in range(3):
            outs[step][p * rows : (p + 1) * rows, :] = grad_ref[
                pl.ds(at, rows), p * cols : (p + 1) * cols
            ]


def attend_back(nc, heads, hsize, index, gms, pt, pm, q, k, v, mix, pk, pv, bucket_row, nbuck):
    rows, cols = gms[0].shape
    length = rows * nc
    out = [shape((length, 3 * cols), BF), shape((nbuck, 8), F32)] + [
        shape((3 * rows + MEM_END, cols), BF)
    ] * nc
    return pl.pallas_call(
        functools.partial(attend_back_kernel, nc, heads, hsize),
        out_shape=out,
        in_specs=[smem()] + vmem(nc + 9),
        out_specs=vmem(len(out)),
        scratch_shapes=[
            pltpu.VMEM((length, cols), BF),
            pltpu.VMEM((cols, length), F32),
            pltpu.VMEM((LANES, 2 * length), F32),
        ],
        compiler_params=params(24),
        name="attend_back",
    )(index, *gms, pt, pm, q, k, v, mix, pk, pv, bucket_row)


def input_back_kernel(nc, mem, idx, *refs):
    parts = refs[:nc]
    x, wq, wk, wv, gain, grad_hidden = refs[nc : nc + 6]
    out_ref, memk_ref, memv_ref = refs[nc + 6 : nc + 9]
    scr = refs[nc + 9]
    here = idx[0]
    rows = x.shape[0]
    for step in range(nc):
        scr[here ^ step] = parts[step][...]

    def wide(at, count):
        return jnp.concatenate([scr[c, at : at + count, :] for c in range(nc)], axis=1)

    grad_norm = (
        nt(wide(0, rows), wq[...])
        + nt(wide(rows, rows), wk[...])
        + nt(wide(2 * rows, rows), wv[...])
    )
    scaled, inverse = norm(x[...].astype(F32))
    e = grad_norm * gain[...]
    grad = grad_hidden[...] + inverse * (
        e - scaled * jnp.mean(e * scaled, axis=-1, keepdims=True)
    )
    out_ref[...] = grad.astype(BF)
    memk_ref[...] = wide(3 * rows + MEM_K, mem).astype(F32)
    memv_ref[...] = wide(3 * rows + MEM_V, mem).astype(F32)


def input_back(nc, mem, index, parts, x, wq, wk, wv, gain, grad_hidden):
    rows, width = x.shape
    out = [shape((rows, width), BF), shape((mem, width), F32), shape((mem, width), F32)]
    return pl.pallas_call(
        functools.partial(input_back_kernel, nc, mem),
        out_shape=out,
        in_specs=[smem()] + vmem(nc + 6),
        out_specs=vmem(3),
        scratch_shapes=[pltpu.VMEM((nc,) + parts[0].shape, BF)],
        compiler_params=params(32),
        name="input_back",
    )(index, *parts, x, wq, wk, wv, gain, grad_hidden)


def general(
    sizes,
    inputs,
    prefix_keys,
    prefix_values,
    gain_attn,
    w_query,
    w_key,
    w_value,
    w_out,
    bias_table,
    gain_ffn,
    w_in,
    w_back,
    buckets,
    out_grad,
):
    nb, nc, nw = sizes
    b, c, w = lax.axis_index("batch"), lax.axis_index("ctx"), lax.axis_index("wt")
    x, g = inputs[0], out_grad[0]
    rows, width = x.shape
    all_heads = bias_table.shape[1]
    heads = all_heads // nc
    hsize = width // all_heads
    cols = heads * hsize
    mem = prefix_keys.shape[1]
    length = rows * nc
    part = width // nw
    ff_own = w_back.shape[0]
    ff_part = ff_own // nb
    nbuck = bias_table.shape[0] * nw
    index_c = jnp.reshape(c, (1,))

    xs = gather_flip(x, "ctx", nc)
    wq = gather_wt(w_query, nw).reshape(width, width)
    wk = gather_wt(w_key, nw).reshape(width, width)
    wv = gather_wt(w_value, nw).reshape(width, width)
    small = gather_wt(
        jnp.concatenate([gain_attn, gain_ffn, bias_table.reshape(-1)]).reshape(1, -1), nw
    ).reshape(nw, -1)
    gain_one = small[:, :part].reshape(1, width).astype(F32)
    gain_two = small[:, part : 2 * part].reshape(1, width).astype(F32)
    table = small[:, 2 * part :].reshape(nbuck, all_heads)
    wo = gather_wt(w_out, nw).reshape(width, width)
    in_cut = jnp.concatenate(
        [
            lax.dynamic_slice_in_dim(w_in, o * ff_own + b * ff_part, ff_part, 1)
            for o in range(nw)
        ],
        axis=1,
    )
    w_first = gather_wt(in_cut, nw).reshape(width, nw * ff_part)
    back_cut = lax.dynamic_slice_in_dim(w_back, b * ff_part, ff_part, 0)
    w_second = gather_wt(back_cut, nw).reshape(nw * ff_part, width)
    gs = gather_flip(g, "batch", nb)

    def head_cols(value):
        return lax.dynamic_slice_in_dim(value, c * cols, cols, 1)

    pk, pv = head_cols(prefix_keys[0]), head_cols(prefix_values[0])
    tab = jnp.pad(
        lax.dynamic_slice_in_dim(table, c * heads, heads, 1).T.astype(F32), ((0, 8 - heads), (0, 0))
    )
    bucket_row = jnp.pad(buckets[::-1].reshape(1, -1), ((0, 0), (1, 0)), constant_values=-1)

    (normed1, q, k, v, pt, pm, mix, *mixed) = attend(
        nc, heads, hsize, index_c, xs, head_cols(wq), head_cols(wk), head_cols(wv),
        gain_one, pk, pv, tab, bucket_row,
    )
    mixed = mixed[:1] + [flip(mixed[s], "ctx", nc, s) for s in range(1, nc)]
    hidden, normed2, attended = branch(nc, index_c, mixed, x, wo, gain_two)

    n2 = jnp.concatenate(gather_flip(normed2, "batch", nb), axis=0)
    g_all = jnp.concatenate(gs, axis=0)
    inner = nn(n2, w_first)
    act_value, act_pull = jax.vjp(functools.partial(jax.nn.gelu, approximate=True), inner)
    act = act_value.astype(BF)
    grad_act = nt(g_all, w_second)
    grad_inner = act_pull(grad_act)[0].astype(BF)
    part_norm = nt(grad_inner, w_first).astype(BF)
    part_out = nn(act, w_second).astype(BF)
    grad_second = tn(act, g_all).astype(BF)
    grad_first = tn(n2, grad_inner).astype(BF)

    def cut(value, s):
        return value[s * rows : (s + 1) * rows]

    norm_parts = [cut(part_norm, 0)] + [
        flip(cut(part_norm, s), "batch", nb, s) for s in range(1, nb)
    ]
    (grad_hidden, grad_low, *gms) = branch_back(
        nb, nc, index_c, norm_parts, hidden, gain_two, g, wo
    )
    gms = gms[:1] + [flip(gms[s], "ctx", nc, s) for s in range(1, nc)]
    (grad_heads, grad_table, *sends) = attend_back(
        nc, heads, hsize, index_c, gms, pt, pm, q, k, v, mix, pk, pv, bucket_row, nbuck
    )
    sends = sends[:1] + [flip(sends[s], "ctx", nc, s) for s in range(1, nc)]
    grad_x, grad_memk, grad_memv = input_back(
        nc, mem, index_c, sends, x, wq, wk, wv, gain_one, grad_hidden
    )

    result = hidden + cut(part_out, 0).astype(F32)
    for s in range(1, nb):
        result = result + flip(cut(part_out, s), "batch", nb, s).astype(F32)

    def ctx_total(value):
        own = sum_wt(value, nw)
        size = own.shape[0] // nc
        own = sum_flip(own.astype(BF).reshape(nc, size, own.shape[1]), c, "ctx", nc)
        whole = canonical(gather_flip(own.astype(BF), "ctx", nc), c)
        return whole.reshape(nc * size, -1)

    second = gather_flip(ctx_total(grad_second), "batch", nb)
    out_second = canonical([p.astype(F32) for p in second], b).reshape(ff_own, width)
    first = gather_flip(ctx_total(grad_first), "batch", nb)
    out_first = jnp.zeros((part, nw * ff_own), F32)
    for s, piece in enumerate(first):
        for o in range(nw):
            out_first = lax.dynamic_update_slice(
                out_first,
                piece[:, o * ff_part : (o + 1) * ff_part].astype(F32),
                (0, o * ff_own + (b ^ s) * ff_part),
            )

    grad_wo = jnp.einsum("cqd,qe->cde", attended, grad_low, preferred_element_type=F32)
    own_wo = sum_wt(grad_wo.astype(BF).reshape(width, width), nw).astype(BF)
    own_wo = sum_flip(own_wo.reshape(nc, part // nc, width), c, "ctx", nc).astype(BF)
    own_wo = sum_flip(own_wo.reshape(nb, part // nc // nb, width), b, "batch", nb).astype(BF)
    own_wo = canonical(gather_flip(own_wo, "batch", nb), b).reshape(part // nc, width)
    out_wo = canonical(gather_flip(own_wo, "ctx", nc), c).reshape(part, width).astype(F32)

    grad_qkv = sum_wt(tn(normed1, grad_heads).astype(BF), nw).astype(BF)
    line = jnp.pad(grad_table[:, :heads].reshape(1, -1), ((0, 15), (0, 3 * cols - heads * nbuck)))
    if nw == 2:
        line = line.astype(BF)
        line = line.astype(F32) + flip(line, "wt", 2, 1).astype(F32)
    else:
        line = lax.psum(line, "wt")
    size = part // nb
    blocks = jnp.concatenate(
        [
            grad_qkv.reshape(nb, size, 3 * cols),
            jnp.broadcast_to(line.astype(BF)[None], (nb, 16, 3 * cols)),
        ],
        axis=1,
    )
    block = sum_flip(blocks, b, "batch", nb).astype(BF)
    pieces = canonical(gather_flip(block, "ctx", nc), c)
    table_sum = pieces[:, size, : heads * nbuck].astype(F32).reshape(nc, nbuck, heads)
    table_sum = jnp.transpose(table_sum, (1, 0, 2)).reshape(nbuck, all_heads)
    own_buckets = nbuck // nw
    out_table = lax.dynamic_slice_in_dim(table_sum, w * own_buckets, own_buckets, 0)
    wide = canonical(gather_flip(pieces[:, :size], "batch", nb), b)
    wide = wide.reshape(nb, nc, size, 3, cols)
    wide = jnp.transpose(wide, (3, 0, 2, 1, 4)).reshape(3, part, width).astype(F32)
    out_q, out_k, out_v = wide[0], wide[1], wide[2]

    def gain_sum(pairs, gain):
        total = sum(jnp.sum(left * right.astype(F32), axis=1) for left, right in pairs)
        return total / gain.astype(F32)

    gain_two_grad = gain_sum([(out_first, w_in)], gain_ffn)
    gain_one_grad = gain_sum([(out_q, w_query), (out_k, w_key), (out_v, w_value)], gain_attn)
    return (
        result.astype(BF)[None],
        grad_x[None],
        grad_memk[None],
        grad_memv[None],
        gain_one_grad,
        gain_two_grad,
        out_table,
        out_q,
        out_k,
        out_v,
        out_wo,
        out_first,
        out_second,
    )


NEAR_LAST = (0, 2, 1, 3)
LINE = 8


def call(kernel, name, index, args, out, scratch=(), mib=24, far=()):
    stay = [pl.BlockSpec(memory_space=pltpu.HBM)] * len(far)
    return pl.pallas_call(
        kernel,
        out_shape=out,
        in_specs=[smem()] + stay + vmem(len(args)),
        out_specs=vmem(len(out)),
        scratch_shapes=list(scratch),
        compiler_params=params(mib),
        name=name,
    )(index, *far, *args)


def after(values, earlier):
    return lax.optimization_barrier((tuple(values), tuple(earlier)))[0]


def both_gains(wt, own, other, row):
    mine, theirs = own[row : row + 1, :].astype(F32), other[row : row + 1, :].astype(F32)
    first = jnp.where(wt == 0, mine, theirs)
    second = jnp.where(wt == 0, theirs, mine)
    return jnp.concatenate([first, second], axis=1)


def fetch_rows(sems, wt, pairs):
    copies = []
    for i, (scr, own, other) in enumerate(pairs):
        rows = own.shape[0]
        for j, (source, place) in enumerate(((own, wt), (other, 1 - wt))):
            to = scr.at[pl.ds(pl.multiple_of(place * rows, rows), rows), :]
            copies.append(pltpu.make_async_copy(source, to, sems.at[2 * i + j]))
            copies[-1].start()
    return copies


TABLE_ROW = 8


def heads_kernel(heads, hsize, own_buckets, idx, *refs):
    wq, wk, wv, wq2, wk2, wv2 = refs[:6]
    fars = refs[6:11]
    x = refs[11]
    n1_ref, q_ref, k_ref, v_ref, pt_ref, pm_ref, mix_ref, wrow_ref, pk_ref, pv_ref = refs[12:22]
    outs = refs[22:26]
    att_scr, line_scr, sems, more_sems, *scrs = refs[26:]
    w_scr, nears = scrs[:3], scrs[3:]
    small, small2, pk_all, pv_all, bucket_row = nears
    more = [
        pltpu.make_async_copy(source, to, more_sems.at[i])
        for i, (source, to) in enumerate(zip(fars, nears))
    ]
    for copy in more:
        copy.start()
    batch, here, wt = idx[0], idx[1], idx[2]
    length, width = x.shape
    rows = length // 4
    half = wq.shape[0]
    cols = heads * hsize
    window = w_scr[0].shape[1]
    shift = window - cols
    odd = here % 2
    lanes = pl.ds(pl.multiple_of((here * cols - odd * shift), LANES), window)
    copies = fetch_rows(
        sems,
        wt,
        [
            (scr, own.at[:, lanes], other.at[:, lanes])
            for scr, own, other in zip(w_scr, (wq, wk, wv), (wq2, wk2, wv2))
        ],
    )
    for copy in more:
        copy.wait()
    for j in range(4):

        @pl.when(here == j)
        def _():
            take = slice(j * cols, (j + 1) * cols)
            pk_ref[...] = pk_all[:, take]
            pv_ref[...] = pv_all[:, take]

    def own_cols(value):
        return jnp.where(odd == 0, value[:, :cols], value[:, shift:])

    gain = both_gains(wt, small, small2, 0)
    scaled, _ = norm(x[...].astype(F32))
    n1_ref[...] = (scaled * gain).astype(BF)
    normed = n1_ref[...]
    for copy in copies:
        copy.wait()
    quarter = half // 4
    at = pl.multiple_of(wt * half + batch * quarter, quarter)
    for p, (scr, out) in enumerate(zip(w_scr, (q_ref, k_ref, v_ref))):
        out[...] = own_cols(nn(normed, scr[...])).astype(BF)
        wrow_ref[:, p * cols : (p + 1) * cols] = own_cols(
            scr[pl.ds(at, quarter), :].astype(F32)
        ).astype(BF)
    vals_t = v_ref[...].T
    pv_t = pv_ref[...].astype(F32).T.astype(BF)
    tab, tab2 = (
        ref[TABLE_ROW : TABLE_ROW + own_buckets, :LANES].astype(F32) for ref in (small, small2)
    )
    ids = lax.broadcasted_iota(jnp.int32, (own_buckets, 2 * length), 0)
    lines = tn(tab, (ids + wt * own_buckets == bucket_row[...]).astype(F32))
    lines = lines + tn(
        tab2, (ids + (1 - wt) * own_buckets == bucket_row[...]).astype(F32)
    )
    line_scr[...] = lines[: line_scr.shape[0]]
    for h in range(heads):
        part = slice(h * hsize, (h + 1) * hsize)
        query = q_ref[:, part]
        line = jnp.broadcast_to(line_scr[pl.ds(here * heads + h, 1), :], (LANES, 2 * length))
        spread = pltpu.roll(line, 0, 1, stride=1, stride_axis=0)
        bias = jnp.concatenate(
            [spread[:, length - at : 2 * length - at] for at in range(0, length, LANES)], axis=0
        )
        score = nt(k_ref[:, part], query) + bias
        front = nt(pk_ref[:, part], query)
        top = jnp.maximum(
            jnp.max(score, axis=0, keepdims=True), jnp.max(front, axis=0, keepdims=True)
        )
        score = jnp.exp(score - top)
        front = jnp.exp(front - top)
        total = jnp.sum(score, axis=0, keepdims=True) + jnp.sum(front, axis=0, keepdims=True)
        scale = 1.0 / total
        prob = (score * scale).astype(BF)
        prob_mem = (front * scale).astype(BF)
        pt_ref[h] = prob
        pm_ref[h] = prob_mem
        mix_ref[part, :] = nn(vals_t[part, :], prob) + nn(pv_t[part, :], prob_mem)
    att_scr[...] = mix_ref[...].T.astype(BF)
    for step in range(4):
        at = pl.multiple_of((here ^ step) * rows, rows)
        outs[step][...] = att_scr[pl.ds(at, rows), :]


def hidden_kernel(idx, *refs):
    wo, wo2 = refs[:2]
    parts = refs[2:6]
    x, small, small2 = refs[6:9]
    hidden_ref, n2_ref, att_ref, wo_ref, sems = refs[9:]
    here, wt = idx[1], idx[2]
    cols = parts[0].shape[1]
    half = wo.shape[0]
    copies = fetch_rows(sems, wt, [(wo_ref, wo, wo2)])
    for step in range(4):
        att_ref[here ^ step] = parts[step][...]
    for copy in copies:
        copy.wait()
    hidden = x[...].astype(F32)
    for c in range(4):
        hidden = hidden + nn(att_ref[c], wo_ref[c * cols : (c + 1) * cols, :])
    hidden_ref[...] = hidden
    scaled, _ = norm(hidden)
    n2_ref[...] = (scaled * both_gains(wt, small, small2, 1)).astype(BF)


def gelu_parts(v):
    scale = 0.7978845608028654
    square = v * v
    t = jnp.tanh(scale * v * (1.0 + 0.044715 * square))
    grad = 0.5 * (1.0 + t) + 0.5 * v * (1.0 - t * t) * scale * (1.0 + 0.134145 * square)
    return 0.5 * v * (1.0 + t), grad


def own_columns(batch, ff_own, block):
    return [pl.ds(pl.multiple_of(o * ff_own + batch * block, block), block) for o in range(2)]


def ffn_kernel(idx, *refs):
    w1, w1b, w2, w2b = refs[:4]
    n2s, gs = refs[4:8], refs[8:12]
    norms = refs[12:16]
    act_ref, gi_ref, w2_ref, w1_scr, sems = refs[16:]
    batch, wt = idx[0], idx[2]
    half = w1.shape[0]
    block = w1_scr.shape[1] // 2
    ff_own = w2.shape[0]
    copies = []
    for j, (source, place) in enumerate(((w1, wt), (w1b, 1 - wt))):
        to = pl.ds(pl.multiple_of(place * half, half), half)
        for o, cut in enumerate(own_columns(batch, ff_own, block)):
            copies.append(
                pltpu.make_async_copy(
                    source.at[:, cut],
                    w1_scr.at[to, o * block : (o + 1) * block],
                    sems.at[2 * j + o],
                )
            )
    cut = pl.ds(pl.multiple_of(batch * block, block), block)
    for j, (source, place) in enumerate(((w2, wt), (w2b, 1 - wt))):
        to = pl.ds(pl.multiple_of(place * block, block), block)
        copies.append(pltpu.make_async_copy(source.at[cut, :], w2_ref.at[to, :], sems.at[4 + j]))
    for copy in copies:
        copy.start()
    for copy in copies[:4]:
        copy.wait()
    rows = n2s[0].shape[0]
    for s in range(4):
        at = slice(s * rows, (s + 1) * rows)
        act, slope = gelu_parts(nn(n2s[s][...], w1_scr[...]))
        if s == 0:
            for copy in copies[4:]:
                copy.wait()
        act_ref[at, :] = act.astype(BF)
        grad = (nt(gs[s][...], w2_ref[...]).astype(BF).astype(F32) * slope).astype(BF)
        gi_ref[at, :] = grad
        norms[s][...] = nt(grad, w1_scr[...]).astype(BF)


def ffn_back_kernel(idx, *refs):
    n2s, gs = refs[:4], refs[4:8]
    act, gi = refs[8:10]
    mine, theirs, all_scr, scr = refs[10:]
    here, wt = idx[1], idx[2]
    rows = n2s[0].shape[0]
    size = scr.shape[0] // 8

    def spread(p):
        for i, out in enumerate((mine, theirs)):
            for j, place in enumerate(NEAR_LAST):
                at = pl.multiple_of(((wt ^ i) * 4 + (here ^ place)) * size, size)
                to = (4 * (j // 2) + 2 * p + j % 2) * size
                out[to : to + size, :] = scr[pl.ds(at, size), :]

    for s in range(4):
        all_scr[s * rows : (s + 1) * rows, :] = n2s[s][...]
    scr[...] = tn(all_scr[...], gi[...]).astype(BF)
    spread(0)
    for s in range(4):
        all_scr[s * rows : (s + 1) * rows, :] = gs[s][...]
    scr[...] = tn(act[...], all_scr[...]).astype(BF)
    spread(1)


def hidden_back_kernel(idx, *refs):
    parts = refs[:4]
    hidden_ref, small, small2, g, wo = refs[4:9]
    grad_ref, low_ref = refs[9:11]
    outs = refs[11:]
    here, wt = idx[1], idx[2]
    cols = outs[0].shape[1]
    half = wo.shape[0] // 2
    grad_norm = parts[0][...].astype(F32)
    for part in parts[1:]:
        grad_norm = grad_norm + part[...].astype(F32)
    scaled, inverse = norm(hidden_ref[...])
    e = grad_norm * both_gains(wt, small, small2, 1)
    grad = g[...].astype(F32) + inverse * (
        e - scaled * jnp.mean(e * scaled, axis=-1, keepdims=True)
    )
    grad_ref[...] = grad
    low = grad.astype(BF)
    low_ref[...] = low
    for step in range(4):
        at = pl.multiple_of((here ^ step) * cols, cols)
        outs[step][...] = nt(low, wo[pl.ds(at, cols), :]).astype(BF)


def wo_back_kernel(idx, att, low, act, w2, mine, theirs, keep, send, scr):
    rows = low.shape[0]
    batch, here, wt = idx[0], idx[1], idx[2]
    size = att.shape[2]
    for c in range(4):
        scr[c * size : (c + 1) * size, :] = tn(att[c], low[...])
    size = scr.shape[0] // 32
    for i, out in enumerate((mine, theirs)):
        for q, far in enumerate(NEAR_LAST):
            for p, place in enumerate(NEAR_LAST):
                at = (((wt ^ i) * 4 + (here ^ place)) * 4 + (batch ^ far)) * size
                to = (4 * q + p) * size
                out[to : to + size, :] = scr[pl.ds(pl.multiple_of(at, 8), size), :].astype(BF)
    for s, (out, to) in enumerate(((keep, 0), (keep, rows), (send, 0), (send, rows))):
        out[to : to + rows, :] = nn(act[s * rows : (s + 1) * rows, :], w2[...]).astype(BF)


def heads_back_kernel(heads, hsize, idx, *refs):
    gms = refs[:4]
    pt, pm, q, k, v, mix, pk, pv, bucket_row, n1 = refs[4:14]
    mine, theirs = refs[14:16]
    own_out, near_out, far_out = refs[16:19]
    gm_scr, gqt_scr, acc, grad_scr, w_scr = refs[19:]
    batch, here, wt = idx[0], idx[1], idx[2]
    rows, cols = gms[0].shape
    length = 4 * rows
    mem = pk.shape[0]
    high = own_out.shape[0]
    outs = (own_out, far_out, near_out.at[:high], near_out.at[high:])
    for step in range(4):
        at = pl.multiple_of((here ^ step) * rows, rows)
        gm_scr[pl.ds(at, rows), :] = gms[step][...]
    gm_t = gm_scr[...].T
    keys_t = k[...].T
    pk_t = pk[...].astype(F32).T.astype(BF)
    lines = []
    for h in range(heads):
        part = slice(h * hsize, (h + 1) * hsize)
        gm = gm_scr[:, part]
        query = q[:, part]
        spread = jnp.sum(gm_t[part, :].astype(F32) * mix[part, :], axis=0, keepdims=True)
        prob = pt[h]
        prob_mem = pm[h]
        score = prob.astype(F32) * (nt(v[:, part], gm) - spread)
        front = (prob_mem.astype(F32) * (nt(pv[:, part], gm) - spread)).astype(BF)
        low = score.astype(BF)
        gqt_scr[part, :] = nn(keys_t[part, :], low) + nn(pk_t[part, :], front)
        grad_scr[1, :, part] = nn(low, query).astype(BF)
        grad_scr[2, :, part] = nn(prob, gm).astype(BF)
        mem_k = nn(front, query).astype(BF)
        mem_v = nn(prob_mem, gm).astype(BF)
        for step in range(4):
            outs[step][3 * rows + MEM_K : 3 * rows + MEM_K + mem, part] = mem_k
            outs[step][3 * rows + MEM_V : 3 * rows + MEM_V + mem, part] = mem_v
        acc[...] = jnp.zeros_like(acc)
        for at in range(0, length, LANES):
            acc[:, length - at : 2 * length - at] += score[at : at + LANES, :]
        fold = acc[...]
        size = LANES // 2
        while size >= 8:
            fold = fold[:size] + pltpu.roll(fold[size:], 2 * length - size, 1)
            size //= 2
        line = fold[0:1]
        for i in range(1, 8):
            line = line + pltpu.roll(fold[i : i + 1], 2 * length - i, 1)
        lines.append(line)
    grad_scr[0] = gqt_scr[...].T.astype(BF)
    normed = n1[...]
    for p in range(3):
        w_scr[:, p * cols : (p + 1) * cols] = tn(normed, grad_scr[p]).astype(BF)
    size = w_scr.shape[0] // 8
    for i, out in enumerate((mine, theirs)):
        for j, far in enumerate(NEAR_LAST):
            at = pl.multiple_of(((wt ^ i) * 4 + (batch ^ far)) * size, size)
            out[j * size : (j + 1) * size, :] = w_scr[pl.ds(at, size), :]
    lines.append(jnp.zeros((LINE - heads, 2 * length), F32))
    table = lax.dot_general(
        jnp.concatenate(lines, axis=0),
        one_hot_rows(bucket_row[...], LANES),
        (((1,), (1,)), ((), ())),
        precision=lax.Precision.HIGHEST,
        preferred_element_type=F32,
    )
    wide = w_scr.shape[1]
    table = jnp.concatenate([table, jnp.zeros((LINE, wide - LANES), F32)], axis=1)
    for out in (mine, theirs):
        out[4 * size :, :] = table.astype(BF)
    for step in range(4):
        at = pl.multiple_of((here ^ step) * rows, rows)
        for p in range(3):
            outs[step][p * rows : (p + 1) * rows, :] = grad_scr[p, pl.ds(at, rows), :]


def halving_kernel(lines, *refs):
    count = len(lines)
    for i, line in enumerate(lines):
        own, got = refs[2 * i], refs[2 * i + 1]
        keep, send = refs[2 * count + 2 * i], refs[2 * count + 2 * i + 1]
        total = (own[...].astype(F32) + got[...].astype(F32)).astype(BF)
        half = (total.shape[0] - line) // 2
        keep[:half, :] = total[:half]
        send[:half, :] = total[half : 2 * half]
        if line:
            keep[half:, :] = total[2 * half :]
            send[half:, :] = total[2 * half :]


def halving(name, items):
    args, out = [], []
    for own, got, line in items:
        args += [own, got]
        out += [shape(((own.shape[0] - line) // 2 + line, own.shape[1]), BF)] * 2
    return pl.pallas_call(
        functools.partial(halving_kernel, [line for _, _, line in items]),
        out_shape=out,
        in_specs=vmem(len(args)),
        out_specs=vmem(len(out)),
        compiler_params=params(32),
        name=name,
    )(*args)


def add_kernel(left, right, out):
    out[...] = (left[...].astype(F32) + right[...].astype(F32)).astype(BF)


def row_sums(values):
    return lax.dot_general(
        jnp.ones((8, values.shape[1]), F32),
        values,
        (((1,), (1,)), ((), ())),
        precision=lax.Precision.HIGHEST,
        preferred_element_type=F32,
    )


def add_swapped(out, own, got, half):
    for i in range(2):
        left = own[i * half : (i + 1) * half, :].astype(F32)
        right = got[(1 - i) * half : (2 - i) * half, :].astype(F32)
        out[i * half : (i + 1) * half, :] = (left + right).astype(BF)


def ffn_piece_kernel(idx, w_in, own, got, a_ref, b_ref, sum_ref, w_scr, sems):
    batch, here = idx[0], idx[1]
    quarter, width = w_scr.shape
    block = width // 2
    rows = pl.ds(pl.multiple_of(here * quarter, quarter), quarter)
    copies = [
        pltpu.make_async_copy(
            w_in.at[rows, cut], w_scr.at[:, o * block : (o + 1) * block], sems.at[o]
        )
        for o, cut in enumerate(own_columns(batch, w_in.shape[1] // 2, block))
    ]
    for copy in copies:
        copy.start()
    add_swapped(a_ref, own.at[: 2 * quarter], got.at[: 2 * quarter], quarter)
    add_swapped(b_ref, own.at[2 * quarter :], got.at[2 * quarter :], quarter)
    for copy in copies:
        copy.wait()
    sum_ref[...] = row_sums(a_ref[:quarter, :].astype(F32) * w_scr[...].astype(F32))


def heads_pair_kernel(size, height, own, got, out):
    rest = own.shape[0] - height
    out[:height, :] = own[:height, :]
    out[height:, :] = got[:height, :]
    for at, left, right in ((size, size, height), (height + size, height, size)):
        out[at : at + rest, :] = (
            own[left : left + rest, :].astype(F32) + got[right : right + rest, :].astype(F32)
        ).astype(BF)


def heads_piece_kernel(qkv, qkv2, wo, wo2, wrow, sum_in, piece_ref):
    size, width = wo.shape
    quarter = wrow.shape[0]
    wide = wrow.shape[1]
    heads = qkv[...].astype(F32) + qkv2[...].astype(F32)
    piece_ref[:quarter, :] = heads[:quarter].astype(BF)
    sum_heads = row_sums(heads[:quarter] * wrow[...].astype(F32))
    third = size // 3
    cols = width - wide
    for part, at in ((wo, quarter), (wo2, quarter + size + third + LINE)):
        piece_ref[at : at + size, :] = part[:, :wide]
        for o in range(3):
            piece_ref[at + size : at + size + third, o * cols : (o + 1) * cols] = part[
                o * third : (o + 1) * third, wide:
            ]
    row = lax.broadcasted_iota(jnp.int32, (LINE, quarter), 0)
    sums = jnp.where(row == LINE - 2, sum_heads, jnp.where(row == LINE - 1, sum_in[...], 0.0))
    at = quarter + size + third
    line = heads[quarter:]
    pad = jnp.zeros((LINE, LANES), F32)
    sums = jnp.concatenate([sums, jnp.zeros((LINE, LANES - quarter), F32)], axis=1)
    line = line + jnp.concatenate([pad, sums, jnp.zeros((LINE, wide - 2 * LANES), F32)], axis=1)
    piece_ref[at : at + LINE, :] = line.astype(BF)


def ctx_pieces(refs, at, order):
    one, two, four, one2, two2, four2 = refs
    rows = one.shape[0]
    size = rows // 2
    first = ((one, 0), (two, 0), (four, 0), (four, rows))
    last = ((one2, 0), (four2, 0), (two2, 0), (four2, rows))
    if order == 2:
        first = ((one, 0), (four, 0), (two, 0), (four, rows))
        last = ((one2, 0), (two2, 0), (four2, 0), (four2, rows))
    near, far = first[at], last[at]
    found = []
    for (ref, start), places in ((near, (0, 2)), (far, (1, 3))):
        for i, place in enumerate(places):
            found.append((place, ref, start + i * size, size))
    return found


def rows_out_kernel(idx, *refs):
    out, scr, sems = refs[6:]
    copies = []
    for at in range(4):
        for place, ref, start, size in ctx_pieces(refs[:6], at, 2):
            row = len(copies) * size
            scr[row : row + size, :] = ref[start : start + size, :].astype(F32)
            to = pl.multiple_of(((idx[0] ^ at) * 4 + (idx[1] ^ place)) * size, size)
            copies.append(
                pltpu.make_async_copy(
                    scr.at[row : row + size, :], out.at[pl.ds(to, size), :], sems.at[len(copies)]
                )
            )
            copies[-1].start()
    for copy in copies:
        copy.wait()


def cols_out_kernel(idx, *refs):
    out, scr, sems = refs[6:]
    copies = []
    block = scr.shape[1] // 2
    for at in range(4):
        for place, ref, start, size in ctx_pieces(refs[:6], at, 1):
            row = (len(copies) // 2) * size
            scr[row : row + size, :] = ref[start : start + size, :].astype(F32)
            to = pl.multiple_of((idx[1] ^ place) * size, size)
            for o in range(2):
                col = pl.multiple_of((4 * o + (idx[0] ^ at)) * block, block)
                copies.append(
                    pltpu.make_async_copy(
                        scr.at[row : row + size, o * block : (o + 1) * block],
                        out.at[pl.ds(to, size), pl.ds(col, block)],
                        sems.at[len(copies)],
                    )
                )
                copies[-1].start()
    for copy in copies:
        copy.wait()


def pieces_out(kernel, name, index, pieces, dims, copies):
    rows, width = pieces[0].shape
    return pl.pallas_call(
        kernel,
        out_shape=shape(dims, F32),
        in_specs=[smem()] + vmem(6),
        out_specs=pl.BlockSpec(memory_space=pltpu.HBM),
        scratch_shapes=[
            pltpu.VMEM((8 * rows, width), F32),
            pltpu.SemaphoreType.DMA((copies,)),
        ],
        compiler_params=params(16),
        name=name,
    )(index, *pieces)


def heads_out_kernel(heads, buckets, idx, *refs):
    small = refs[6]
    oq, ok, ov, oo, gain_one, gain_two, table, scr, lines, tab_scr = refs[7:]
    step = pl.program_id(0)
    quarter, width = oq.shape
    cols = width // 4
    wide = 3 * cols
    size = quarter // 4
    third = size // 3
    for at in range(4):

        @pl.when(step == at)
        def _():
            for place, ref, start, height in ctx_pieces(refs[:6], at, 1):
                scr[idx[1] ^ place] = ref[start : start + height, :]

    for c in range(4):
        part = scr[c].astype(F32)
        for o, out in enumerate((oq, ok, ov)):
            out[:, c * cols : (c + 1) * cols] = part[:quarter, o * cols : (o + 1) * cols]
        oo[c, 0, :, :wide] = part[quarter : quarter + size]
        for o in range(3):
            oo[c, 0, o * third : (o + 1) * third, wide:] = part[
                quarter + size : quarter + size + third, o * cols : (o + 1) * cols
            ]
        lines[idx[0] ^ step, c] = part[quarter + size + third :]

    @pl.when(step == 3)
    def _():
        seen = [[lines[b, c] for c in range(4)] for b in range(4)]
        take = slice(LANES, LANES + quarter)
        one = jnp.concatenate(
            [sum(seen[b][c][LINE - 2 : LINE - 1, take] for c in range(4)) for b in range(4)], axis=1
        )
        two = jnp.concatenate(
            [sum(seen[b][c][LINE - 1 : LINE, take] for b in range(4)) for c in range(4)], axis=1
        )
        gain_one[...] = (one / small[0:1, :].astype(F32))[0]
        gain_two[...] = (two / small[1:2, :].astype(F32))[0]
        rest = [seen[0][c][:heads, :LANES] for c in range(4)]
        rest.append(jnp.zeros((LANES - 4 * heads, LANES), F32))
        tab_scr[...] = jnp.concatenate(rest, axis=0).T
        own_buckets = buckets // 2
        at = pl.multiple_of(idx[2] * own_buckets, 8)
        table[...] = tab_scr[pl.ds(at, own_buckets), : 4 * heads]


def heads_out(index, pieces, small, width, heads, buckets):
    height, wide = pieces[0].shape[0] // 2, pieces[0].shape[1]
    part = width // 2
    quarter = part // 4
    size = quarter // 4
    block = pl.BlockSpec((quarter, width), lambda step, idx: (idx[0] ^ step, 0))
    whole = [pl.BlockSpec(p.shape, lambda step, idx: (0, 0)) for p in (*pieces, small)]
    return pl.pallas_call(
        functools.partial(heads_out_kernel, heads, buckets),
        out_shape=[shape((part, width), F32)] * 3
        + [
            shape((4, 4, size, width), F32),
            shape((part,), F32),
            shape((part,), F32),
            shape((buckets // 2, 4 * heads), F32),
        ],
        grid_spec=pltpu.PrefetchScalarGridSpec(
            num_scalar_prefetch=1,
            grid=(4,),
            in_specs=whole,
            out_specs=[block] * 3
            + [
                pl.BlockSpec((4, 1, size, width), lambda step, idx: (0, idx[0] ^ step, 0, 0)),
                pl.BlockSpec((part,), lambda step, idx: (0,)),
                pl.BlockSpec((part,), lambda step, idx: (0,)),
                pl.BlockSpec((buckets // 2, 4 * heads), lambda step, idx: (0, 0)),
            ],
            scratch_shapes=[
                pltpu.VMEM((4, height, wide), BF),
                pltpu.VMEM((4, 4, LINE, wide), F32),
                pltpu.VMEM((LANES, LANES), F32),
            ],
        ),
        compiler_params=params(32),
        name="heads_out",
    )(index, *pieces, small)


def paired(
    inputs,
    prefix_keys,
    prefix_values,
    gain_attn,
    w_query,
    w_key,
    w_value,
    w_out,
    bias_table,
    gain_ffn,
    w_in,
    w_back,
    buckets,
    out_grad,
):
    b, c, w = lax.axis_index("batch"), lax.axis_index("ctx"), lax.axis_index("wt")
    index = jnp.stack([b, c, w])
    x, g = inputs[0], out_grad[0]
    rows, width = x.shape
    all_heads = bias_table.shape[1]
    heads = all_heads // 4
    hsize = width // all_heads
    cols = heads * hsize
    wide = 3 * cols
    mem = prefix_keys.shape[1]
    length = 4 * rows
    part = width // 2
    quarter = part // 4
    ff_own = w_back.shape[0]
    ff_part = ff_own // 4
    nbuck = 2 * bias_table.shape[0]

    def over_wt(value, name):
        with jax.named_scope(name + "_w"):
            return flip(value, "wt", 2, 1)

    def over_ctx(value, step, name):
        with jax.named_scope(name + "_z" + str(step)):
            return flip(value, "ctx", 4, step)

    def over_batch(value, step, name):
        with jax.named_scope(name + "_b" + str(step)):
            return flip(value, "batch", 4, step)

    own_buckets = nbuck // 2
    small = jnp.concatenate(
        [
            jnp.pad(jnp.stack([gain_attn, gain_ffn]), ((0, TABLE_ROW - 2), (0, 0))),
            jnp.pad(bias_table, ((0, 0), (0, part - all_heads))),
        ]
    )
    w_query2, w_key2, w_value2 = [over_wt(v, "weight") for v in (w_query, w_key, w_value)]
    small2 = over_wt(small, "small")
    g_near = over_batch(g, 1, "g")
    x_all = lax.all_gather(x, "ctx", axis=0, tiled=True)
    bucket_row = jnp.pad(buckets[::-1].reshape(1, -1), ((0, 0), (1, 0)), constant_values=-1)

    tokens = shape((length, cols), BF)
    few = (small, small2, prefix_keys[0], prefix_values[0], bucket_row)
    (n1, q, k, v, pt, pm, mix, wrow, pk, pv, *mixed) = call(
        functools.partial(heads_kernel, heads, hsize, own_buckets),
        "attend",
        index,
        [x_all],
        [shape((length, width), BF)]
        + [tokens] * 3
        + [
            shape((heads, length, length), BF),
            shape((heads, mem, length), BF),
            shape((cols, length), F32),
            shape((quarter, wide), BF),
            shape((mem, cols), BF),
            shape((mem, cols), BF),
        ]
        + [shape((rows, cols), BF)] * 4,
        [
            pltpu.VMEM((length, cols), BF),
            pltpu.VMEM((16, 2 * length), F32),
            pltpu.SemaphoreType.DMA((6,)),
            pltpu.SemaphoreType.DMA((len(few),)),
        ]
        + [pltpu.VMEM((width, -(-cols // LANES) * LANES), BF)] * 3
        + [pltpu.VMEM(v.shape, v.dtype) for v in few],
        far=(w_query, w_key, w_value, w_query2, w_key2, w_value2, *few),
    )
    (g_pair, w_out_sent) = after((jnp.concatenate([g, g_near]), w_out), mixed[:1])
    w_out2 = over_wt(w_out_sent, "weight")
    g_far = over_batch(g_pair, 2, "g")
    mixed = mixed[:1] + [over_ctx(mixed[s], s, "mixed") for s in range(1, 4)]
    (*mixed, w_out2, g_far) = after((*mixed, w_out2, g_far), ())
    square = shape((width, width), BF)
    hidden, n2, attended, wo = call(
        hidden_kernel,
        "hidden",
        index,
        [*mixed, x, small, small2],
        [shape((rows, width), F32), shape((rows, width), BF), shape((4, rows, cols), BF), square],
        [pltpu.SemaphoreType.DMA((2,))],
        far=(w_out, w_out2),
    )

    n2s = [n2] + [over_batch(n2, s, "n2") for s in range(1, 4)]
    (w_in_sent, w_back_sent) = after((w_in, w_back), (n2,))
    w_in2, w_back2 = over_wt(w_in_sent, "in"), over_wt(w_back_sent, "back")
    gs = (g, g_near, g_far[:rows], g_far[rows:])
    hid = shape((length, 2 * ff_part), BF)
    *norms, act, gi, w_second = call(
        ffn_kernel,
        "ffn",
        index,
        [*n2s, *gs],
        [shape((rows, width), BF)] * 4 + [hid, hid, shape((2 * ff_part, width), BF)],
        [pltpu.VMEM((width, 2 * ff_part), BF), pltpu.SemaphoreType.DMA((6,))],
        far=(w_in, w_in2, w_back, w_back2),
    )
    norms = norms[:1] + [over_batch(norms[s], s, "norm") for s in range(1, 4)]
    ffn, ffn_sent = call(
        ffn_back_kernel,
        "ffn_back",
        index,
        [*n2s, *gs, act, gi],
        [square, square],
        [pltpu.VMEM((length, width), BF), pltpu.VMEM((width, width), BF)],
    )
    ffn, ffn_sent = halving("ffn_wt", [(ffn, over_wt(ffn_sent, "ffn"), 0)])
    ffn_got = over_ctx(ffn_sent, 1, "ffn")
    norms = after(norms, (ffn, ffn_sent))
    grad_hidden, low, *gms = call(
        hidden_back_kernel,
        "hidden_back",
        index,
        [*norms, hidden, small, small2, g, wo],
        [shape((rows, width), F32), shape((rows, width), BF)] + [shape((rows, cols), BF)] * 4,
    )
    ffn = pl.pallas_call(
        add_kernel,
        out_shape=shape((part, width), BF),
        in_specs=vmem(2),
        out_specs=vmem(1)[0],
        compiler_params=params(16),
        name="ffn_near",
    )(ffn, ffn_got)
    gms = list(gms[:1]) + [over_ctx(gms[s], s, "gm") for s in range(1, 4)]
    (ffn_sent, low) = after((ffn, low), gms[1:])
    ffn_got = over_ctx(ffn_sent, 2, "ffn")
    wo_sum, wo_sent, outs, outs_sent = call(
        wo_back_kernel,
        "wo_back",
        index,
        [attended, low, act, w_second],
        [shape((part, width), BF)] * 2 + [shape((2 * rows, width), BF)] * 2,
        [pltpu.VMEM((width, width), F32)],
    )
    outs_got = over_batch(outs_sent, 2, "outs")
    wo_sum, wo_sent = halving("wo_wt", [(wo_sum, over_wt(wo_sent, "wo"), 0)])
    wo_sum, wo_sent = halving("wo_near", [(wo_sum, over_batch(wo_sent, 1, "wo"), 0)])

    high = 3 * rows + MEM_END
    (qkv, qkv_sent, own_block, near_blocks, far_block) = call(
        functools.partial(heads_back_kernel, heads, hsize),
        "attend_back",
        index,
        [*gms, pt, pm, q, k, v, mix, pk, pv, bucket_row, n1],
        [shape((part + LINE, wide), BF)] * 2
        + [shape((n * high, cols), BF) for n in (1, 2, 1)],
        [
            pltpu.VMEM((length, cols), BF),
            pltpu.VMEM((cols, length), F32),
            pltpu.VMEM((LANES, 2 * length), F32),
            pltpu.VMEM((3, length, cols), BF),
            pltpu.VMEM((width, wide), BF),
        ],
    )
    outs, outs_sent = halving("outs_far", [(outs, outs_got, 0)])
    (outs_sent, wo_sent) = after((outs_sent, wo_sent), (outs, wo_sum))
    wo_sum, wo_sent = halving("wo_far", [(wo_sum, over_batch(wo_sent, 2, "wo"), 0)])
    wo_sum, wo_sent = halving("wo_last", [(wo_sum, over_ctx(wo_sent, 1, "wo"), 0)])
    outs_got = over_batch(outs_sent, 1, "outs")
    qkv, qkv_sent = halving("qkv_wt", [(qkv, over_wt(qkv_sent, "qkv"), LINE)])
    qkv, qkv_sent = halving("qkv_near", [(qkv, over_batch(qkv_sent, 1, "qkv"), LINE)])
    qkv_got = over_batch(qkv_sent, 2, "qkv")
    (ffn_got,) = after((ffn_got,), (qkv_got, outs_got, wo_sum, wo_sent))
    a1, b1, sum_in = call(
        ffn_piece_kernel,
        "ffn_piece",
        index,
        [ffn, ffn_got],
        [shape((2 * quarter, width), BF)] * 2 + [shape((8, quarter), F32)],
        [pltpu.VMEM((quarter, width), BF), pltpu.SemaphoreType.DMA((2,))],
        far=(w_in,),
    )

    def pile(one, two):
        return jnp.concatenate([one, two])

    result = (hidden + outs.astype(F32) + outs_got.astype(F32)).astype(BF)
    a2, b2 = over_batch(a1, 1, "in_near"), over_batch(b1, 2, "out_near")
    c1, d1 = over_ctx(a1, 1, "in_back"), over_ctx(b1, 1, "out_back")
    pile_a, pile_b = pile(a1, a2), pile(b1, b2)
    a3, b3 = over_batch(pile_a, 2, "in_near2"), over_batch(pile_b, 1, "out_near2")
    (c1, d1) = after((c1, d1), (pile_a, pile_b))
    c2, d2 = over_batch(c1, 2, "in_far"), over_batch(d1, 1, "out_far")
    height = quarter + quarter // 4 + quarter // 12 + LINE
    piece = pl.pallas_call(
        heads_piece_kernel,
        out_shape=shape((2 * height - quarter - LINE, wide), BF),
        in_specs=vmem(6),
        out_specs=vmem(1)[0],
        compiler_params=params(32),
        name="heads_piece",
    )(qkv, qkv_got, wo_sum, wo_sent, wrow, sum_in)

    (piece,) = after((piece,), (c1, d1))
    heads_far = over_ctx(piece, 2, "heads_back")
    pile_c, pile_d = pile(c1, c2), pile(d1, d2)
    c3, d3 = over_batch(pile_c, 1, "in_far2"), over_batch(pile_d, 2, "out_far2")
    (heads_far,) = after((heads_far,), (a3, b3))
    (near_blocks,) = after((near_blocks,), (heads_far,))
    near_got = over_ctx(near_blocks, 2, "sends")
    far_pile = pile(far_block, near_got[high:])
    far_got = over_ctx(far_pile, 1, "sends")
    e1 = pl.pallas_call(
        functools.partial(heads_pair_kernel, quarter, height),
        out_shape=shape((2 * height, wide), BF),
        in_specs=vmem(2),
        out_specs=vmem(1)[0],
        compiler_params=params(16),
        name="heads_pair",
    )(piece, heads_far)
    f1 = over_ctx(e1, 1, "heads_back")
    (e1, f1) = after((e1, f1), (pile_c, pile_d))
    e2, f2 = over_batch(e1, 1, "heads_near"), over_batch(f1, 2, "heads_far")
    (e1, e2, f1, f2) = after((e1, e2, f1, f2), (c3, d3, far_pile))
    e3 = over_batch(pile(e1, e2), 2, "heads_near2")
    f3 = over_batch(pile(f1, f2), 1, "heads_far2")
    out_second = pieces_out(
        rows_out_kernel, "rows_out", index, (b1, b2, b3, d1, d2, d3), (ff_own, width), 16
    )
    out_first = pieces_out(
        cols_out_kernel, "cols_out", index, (a1, a2, a3, c1, c2, c3), (part, 2 * ff_own), 32
    )
    out_q, out_k, out_v, out_wo, gain_one, gain_two, out_table = heads_out(
        index, (e1, e2, e3, f1, f2, f3), small, width, heads, nbuck
    )
    grad_x, grad_memk, grad_memv = call(
        input_end_kernel,
        "input_back",
        index,
        [own_block, near_got, far_got, x, small, small2, grad_hidden],
        [shape((rows, width), BF), shape((mem, width), F32), shape((mem, width), F32)],
        [pltpu.VMEM((4,) + own_block.shape, BF), pltpu.SemaphoreType.DMA((6,))]
        + [pltpu.VMEM((width, width), BF)] * 3,
        far=(w_query, w_key, w_value, w_query2, w_key2, w_value2),
    )
    return (
        result[None],
        grad_x[None],
        grad_memk[None],
        grad_memv[None],
        gain_one,
        gain_two,
        out_table,
        out_q,
        out_k,
        out_v,
        out_wo.reshape(part, width),
        out_first,
        out_second,
    )


def input_end_kernel(idx, *refs):
    wq, wk, wv, wq2, wk2, wv2 = refs[:6]
    own, near, far, x, small, small2, grad_hidden = refs[6:13]
    out_ref, memk_ref, memv_ref, scr, sems, *w_scr = refs[13:]
    high = own.shape[0]
    parts = (own, far.at[:high], near.at[:high], far.at[high:])
    here, wt = idx[1], idx[2]
    rows = x.shape[0]
    mem = memk_ref.shape[0]
    copies = fetch_rows(sems, wt, list(zip(w_scr, (wq, wk, wv), (wq2, wk2, wv2))))
    for step in range(4):
        scr[here ^ step] = parts[step][...]
    for copy in copies:
        copy.wait()

    def wide(at, count):
        return jnp.concatenate([scr[c, at : at + count, :] for c in range(4)], axis=1)

    grad_norm = sum(nt(wide(p * rows, rows), whole[...]) for p, whole in enumerate(w_scr))
    scaled, inverse = norm(x[...].astype(F32))
    e = grad_norm * both_gains(wt, small, small2, 0)
    grad = grad_hidden[...] + inverse * (
        e - scaled * jnp.mean(e * scaled, axis=-1, keepdims=True)
    )
    out_ref[...] = grad.astype(BF)
    memk_ref[...] = wide(3 * rows + MEM_K, mem).astype(F32)
    memv_ref[...] = wide(3 * rows + MEM_V, mem).astype(F32)


def solution(mesh):
    tokens = P(("batch", "wt"), "ctx", None)
    memory = P(("batch", "wt"), None, None)
    matrix = P("wt", None)
    vector = P("wt")
    sizes = (mesh.shape["batch"], mesh.shape["ctx"], mesh.shape["wt"])
    body = paired if sizes == (4, 4, 2) else functools.partial(general, sizes)
    return jax.shard_map(
        body,
        mesh=mesh,
        in_specs=(
            tokens, memory, memory, vector, matrix, matrix, matrix, matrix, matrix, vector,
            matrix, matrix, P(), tokens,
        ),
        out_specs=(
            tokens, tokens, memory, memory, vector, vector, matrix, matrix, matrix, matrix,
            matrix, matrix, matrix,
        ),
        check_vma=False,
    )
```

```python
import functools

import jax
import jax.numpy as jnp
from jax import lax
from jax.experimental import pallas as pl
from jax.experimental.pallas import tpu as pltpu
from jax.sharding import PartitionSpec as P

EPS = 1e-06
F32 = jnp.float32
BF = jnp.bfloat16
LANES = 128


def nn(left, right):
    return lax.dot_general(left, right, (((1,), (0,)), ((), ())), preferred_element_type=F32)


def nt(left, right):
    return lax.dot_general(left, right, (((1,), (1,)), ((), ())), preferred_element_type=F32)


def tn(left, right):
    return lax.dot_general(left, right, (((0,), (0,)), ((), ())), preferred_element_type=F32)


def vmem(count):
    return [pl.BlockSpec(memory_space=pltpu.VMEM)] * count


def smem():
    return pl.BlockSpec(memory_space=pltpu.SMEM)


def shape(dims, kind):
    return jax.ShapeDtypeStruct(dims, kind)


def params(mib):
    return pltpu.CompilerParams(vmem_limit_bytes=mib << 20)


def flip(value, axis, size, step):
    return lax.ppermute(value, axis, [(i, i ^ step) for i in range(size)])


def gather_flip(value, axis, size):
    return [value] + [flip(value, axis, size, step) for step in range(1, size)]


def canonical(parts, index):
    whole = jnp.zeros((len(parts),) + parts[0].shape, parts[0].dtype)
    for step, part in enumerate(parts):
        whole = lax.dynamic_update_index_in_dim(whole, part, index ^ step, 0)
    return whole


def gather_wt(value, size):
    if size == 2:
        own = lax.axis_index("wt") == 0
        other = flip(value, "wt", 2, 1)
        return jnp.stack([jnp.where(own, value, other), jnp.where(own, other, value)])
    return lax.all_gather(value, "wt", axis=0)


def sum_wt(value, size):
    rows = value.shape[0] // size
    if size == 2:
        index = lax.axis_index("wt")
        mine = lax.dynamic_slice_in_dim(value, index * rows, rows, 0)
        theirs = lax.dynamic_slice_in_dim(value, (1 - index) * rows, rows, 0)
        return mine.astype(F32) + flip(theirs, "wt", 2, 1).astype(F32)
    return lax.psum_scatter(value, "wt", scatter_dimension=0, tiled=True).astype(F32)


def sum_flip(blocks, index, axis, size):
    total = lax.dynamic_index_in_dim(blocks, index, 0, keepdims=False).astype(F32)
    for step in range(1, size):
        block = lax.dynamic_index_in_dim(blocks, index ^ step, 0, keepdims=False)
        total = total + flip(block, axis, size, step).astype(F32)
    return total


def norm(values):
    inverse = lax.rsqrt(jnp.mean(values * values, axis=-1, keepdims=True) + EPS)
    return values * inverse, inverse


def one_hot_rows(bucket_row, buckets):
    ids = lax.broadcasted_iota(jnp.int32, (buckets, bucket_row.shape[1]), 0)
    return (ids == bucket_row).astype(F32)


def attend_kernel(nc, heads, hsize, mem, idx, *refs):
    xs = refs[:nc]
    wq, wk, wv, gain, pk, pv, tab, bucket_row = refs[nc : nc + 8]
    n1_ref, q_ref, k_ref, v_ref, pt_ref, pm_ref, mix_ref = refs[nc + 8 : nc + 15]
    outs = refs[nc + 15 : nc + 15 + nc]
    att_scr = refs[nc + 15 + nc]
    here = idx[0]
    rows = xs[0].shape[0]
    length = nc * rows
    for step in range(nc):
        scaled, _ = norm(xs[step][...].astype(F32))
        at = pl.multiple_of((here ^ step) * rows, rows)
        n1_ref[pl.ds(at, rows), :] = (scaled * gain[...]).astype(BF)
    normed = n1_ref[...]
    q_ref[...] = nn(normed, wq[...]).astype(BF)
    k_ref[...] = nn(normed, wk[...]).astype(BF)
    v_ref[...] = nn(normed, wv[...]).astype(BF)
    vals_t = v_ref[...].T
    pv_t = pv[...].astype(F32).T.astype(BF)
    hot = one_hot_rows(bucket_row[...], tab.shape[1])
    lines = nn(tab[...], hot)
    for h in range(heads):
        part = slice(h * hsize, (h + 1) * hsize)
        query = q_ref[:, part]
        line = jnp.broadcast_to(lines[h : h + 1, :], (LANES, 2 * length))
        spread = pltpu.roll(line, 0, 1, stride=1, stride_axis=0)
        bias = jnp.concatenate(
            [spread[:, length - at : 2 * length - at] for at in range(0, length, LANES)], axis=0
        )
        score = nt(k_ref[:, part], query) + bias
        front = nt(pk[:, part], query)
        top = jnp.maximum(
            jnp.max(score, axis=0, keepdims=True), jnp.max(front, axis=0, keepdims=True)
        )
        score = jnp.exp(score - top)
        front = jnp.exp(front - top)
        total = jnp.sum(score, axis=0, keepdims=True) + jnp.sum(front, axis=0, keepdims=True)
        scale = 1.0 / total
        prob = (score * scale).astype(BF)
        prob_mem = (front * scale).astype(BF)
        pt_ref[h] = prob
        pm_ref[h] = prob_mem
        mix_ref[part, :] = nn(vals_t[part, :], prob) + nn(pv_t[part, :], prob_mem)
    att_scr[...] = mix_ref[...].T.astype(BF)
    for step in range(nc):
        at = pl.multiple_of((here ^ step) * rows, rows)
        outs[step][...] = att_scr[pl.ds(at, rows), :]


def attend(nc, heads, hsize, index, xs, wq, wk, wv, gain, pk, pv, tab, bucket_row):
    rows, width = xs[0].shape
    length = rows * nc
    cols = heads * hsize
    mem = pk.shape[0]
    out = [
        shape((length, width), BF),
        shape((length, cols), BF),
        shape((length, cols), BF),
        shape((length, cols), BF),
        shape((heads, length, length), BF),
        shape((heads, mem, length), BF),
        shape((cols, length), F32),
    ] + [shape((rows, cols), BF)] * nc
    return pl.pallas_call(
        functools.partial(attend_kernel, nc, heads, hsize, mem),
        out_shape=out,
        in_specs=[smem()] + vmem(nc + 8),
        out_specs=vmem(len(out)),
        scratch_shapes=[pltpu.VMEM((length, cols), BF)],
        compiler_params=params(24),
        name="attend",
    )(index, *xs, wq, wk, wv, gain, pk, pv, tab, bucket_row)


def branch_kernel(nc, idx, *refs):
    parts = refs[:nc]
    x, wo, gain = refs[nc : nc + 3]
    hidden_ref, n2_ref, att_ref = refs[nc + 3 : nc + 6]
    here = idx[0]
    cols = parts[0].shape[1]
    for step in range(nc):
        att_ref[here ^ step] = parts[step][...]
    hidden = x[...].astype(F32)
    for c in range(nc):
        hidden = hidden + nn(att_ref[c], wo[c * cols : (c + 1) * cols, :])
    hidden_ref[...] = hidden
    scaled, _ = norm(hidden)
    n2_ref[...] = (scaled * gain[...]).astype(BF)


def branch(nc, index, parts, x, wo, gain):
    rows, cols = parts[0].shape
    out = [shape(x.shape, F32), shape(x.shape, BF), shape((nc, rows, cols), BF)]
    return pl.pallas_call(
        functools.partial(branch_kernel, nc),
        out_shape=out,
        in_specs=[smem()] + vmem(nc + 3),
        out_specs=vmem(3),
        compiler_params=params(32),
        name="branch",
    )(index, *parts, x, wo, gain)


def branch_back_kernel(nb, nc, idx, *refs):
    parts = refs[:nb]
    hidden_ref, gain, g, wo = refs[nb : nb + 4]
    grad_ref, low_ref = refs[nb + 4 : nb + 6]
    outs = refs[nb + 6 : nb + 6 + nc]
    here = idx[0]
    cols = outs[0].shape[1]
    grad_norm = parts[0][...].astype(F32)
    for part in parts[1:]:
        grad_norm = grad_norm + part[...].astype(F32)
    scaled, inverse = norm(hidden_ref[...])
    e = grad_norm * gain[...]
    grad = g[...].astype(F32) + inverse * (
        e - scaled * jnp.mean(e * scaled, axis=-1, keepdims=True)
    )
    grad_ref[...] = grad
    low = grad.astype(BF)
    low_ref[...] = low
    for step in range(nc):
        at = pl.multiple_of((here ^ step) * cols, 8)
        outs[step][...] = nt(low, wo[pl.ds(at, cols), :]).astype(BF)


def branch_back(nb, nc, index, parts, hidden, gain, g, wo):
    rows, width = hidden.shape
    cols = width // nc
    out = [shape((rows, width), F32), shape((rows, width), BF)] + [shape((rows, cols), BF)] * nc
    return pl.pallas_call(
        functools.partial(branch_back_kernel, nb, nc),
        out_shape=out,
        in_specs=[smem()] + vmem(nb + 4),
        out_specs=vmem(len(out)),
        compiler_params=params(32),
        name="branch_back",
    )(index, *parts, hidden, gain, g, wo)


MEM_K, MEM_V, MEM_END = 0, 32, 64


def attend_back_kernel(nc, heads, hsize, idx, *refs):
    gms = refs[:nc]
    pt, pm, q, k, v, mix, pk, pv, bucket_row = refs[nc : nc + 9]
    grad_ref, table_ref = refs[nc + 9 : nc + 11]
    outs = refs[nc + 11 : nc + 11 + nc]
    gm_scr, gqt_scr, acc = refs[nc + 11 + nc :]
    here = idx[0]
    rows, cols = gms[0].shape
    length = rows * nc
    mem = pk.shape[0]
    for step in range(nc):
        at = pl.multiple_of((here ^ step) * rows, rows)
        gm_scr[pl.ds(at, rows), :] = gms[step][...]
    gm_t = gm_scr[...].T
    keys_t = k[...].T
    pk_t = pk[...].astype(F32).T.astype(BF)
    lines = []
    for h in range(heads):
        part = slice(h * hsize, (h + 1) * hsize)
        gm = gm_scr[:, part]
        query = q[:, part]
        spread = jnp.sum(gm_t[part, :].astype(F32) * mix[part, :], axis=0, keepdims=True)
        prob = pt[h]
        prob_mem = pm[h]
        score = prob.astype(F32) * (nt(v[:, part], gm) - spread)
        front = (prob_mem.astype(F32) * (nt(pv[:, part], gm) - spread)).astype(BF)
        low = score.astype(BF)
        gqt_scr[part, :] = nn(keys_t[part, :], low) + nn(pk_t[part, :], front)
        grad_ref[:, cols + h * hsize : cols + (h + 1) * hsize] = nn(low, query).astype(BF)
        grad_ref[:, 2 * cols + h * hsize : 2 * cols + (h + 1) * hsize] = nn(prob, gm).astype(BF)
        mem_k = nn(front, query).astype(BF)
        mem_v = nn(prob_mem, gm).astype(BF)
        for step in range(nc):
            outs[step][3 * rows + MEM_K : 3 * rows + MEM_K + mem, part] = mem_k
            outs[step][3 * rows + MEM_V : 3 * rows + MEM_V + mem, part] = mem_v
        acc[...] = jnp.zeros_like(acc)
        for at in range(0, length, LANES):
            acc[:, length - at : 2 * length - at] += score[at : at + LANES, :]
        fold = acc[...]
        half = LANES // 2
        while half >= 8:
            fold = fold[:half] + pltpu.roll(fold[half:], 2 * length - half, 1)
            half //= 2
        line = fold[0:1]
        for i in range(1, 8):
            line = line + pltpu.roll(fold[i : i + 1], 2 * length - i, 1)
        lines.append(line)
    lines.append(jnp.zeros((8 - heads, 2 * length), F32))
    hot = one_hot_rows(bucket_row[...], table_ref.shape[0])
    table_ref[...] = lax.dot_general(
        hot,
        jnp.concatenate(lines, axis=0),
        (((1,), (1,)), ((), ())),
        precision=lax.Precision.HIGHEST,
        preferred_element_type=F32,
    )
    grad_ref[:, :cols] = gqt_scr[...].T.astype(BF)
    for step in range(nc):
        at = pl.multiple_of((here ^ step) * rows, rows)
        for p in range(3):
            outs[step][p * rows : (p + 1) * rows, :] = grad_ref[
                pl.ds(at, rows), p * cols : (p + 1) * cols
            ]


def attend_back(nc, heads, hsize, index, gms, pt, pm, q, k, v, mix, pk, pv, bucket_row, nbuck):
    rows, cols = gms[0].shape
    length = rows * nc
    out = [shape((length, 3 * cols), BF), shape((nbuck, 8), F32)] + [
        shape((3 * rows + MEM_END, cols), BF)
    ] * nc
    return pl.pallas_call(
        functools.partial(attend_back_kernel, nc, heads, hsize),
        out_shape=out,
        in_specs=[smem()] + vmem(nc + 9),
        out_specs=vmem(len(out)),
        scratch_shapes=[
            pltpu.VMEM((length, cols), BF),
            pltpu.VMEM((cols, length), F32),
            pltpu.VMEM((LANES, 2 * length), F32),
        ],
        compiler_params=params(24),
        name="attend_back",
    )(index, *gms, pt, pm, q, k, v, mix, pk, pv, bucket_row)


def input_back_kernel(nc, mem, idx, *refs):
    parts = refs[:nc]
    x, wq, wk, wv, gain, grad_hidden = refs[nc : nc + 6]
    out_ref, memk_ref, memv_ref = refs[nc + 6 : nc + 9]
    scr = refs[nc + 9]
    here = idx[0]
    rows = x.shape[0]
    for step in range(nc):
        scr[here ^ step] = parts[step][...]

    def wide(at, count):
        return jnp.concatenate([scr[c, at : at + count, :] for c in range(nc)], axis=1)

    grad_norm = (
        nt(wide(0, rows), wq[...])
        + nt(wide(rows, rows), wk[...])
        + nt(wide(2 * rows, rows), wv[...])
    )
    scaled, inverse = norm(x[...].astype(F32))
    e = grad_norm * gain[...]
    grad = grad_hidden[...] + inverse * (
        e - scaled * jnp.mean(e * scaled, axis=-1, keepdims=True)
    )
    out_ref[...] = grad.astype(BF)
    memk_ref[...] = wide(3 * rows + MEM_K, mem).astype(F32)
    memv_ref[...] = wide(3 * rows + MEM_V, mem).astype(F32)


def input_back(nc, mem, index, parts, x, wq, wk, wv, gain, grad_hidden):
    rows, width = x.shape
    out = [shape((rows, width), BF), shape((mem, width), F32), shape((mem, width), F32)]
    return pl.pallas_call(
        functools.partial(input_back_kernel, nc, mem),
        out_shape=out,
        in_specs=[smem()] + vmem(nc + 6),
        out_specs=vmem(3),
        scratch_shapes=[pltpu.VMEM((nc,) + parts[0].shape, BF)],
        compiler_params=params(32),
        name="input_back",
    )(index, *parts, x, wq, wk, wv, gain, grad_hidden)


def general(
    sizes,
    inputs,
    prefix_keys,
    prefix_values,
    gain_attn,
    w_query,
    w_key,
    w_value,
    w_out,
    bias_table,
    gain_ffn,
    w_in,
    w_back,
    buckets,
    out_grad,
):
    nb, nc, nw = sizes
    b, c, w = lax.axis_index("batch"), lax.axis_index("ctx"), lax.axis_index("wt")
    x, g = inputs[0], out_grad[0]
    rows, width = x.shape
    all_heads = bias_table.shape[1]
    heads = all_heads // nc
    hsize = width // all_heads
    cols = heads * hsize
    mem = prefix_keys.shape[1]
    length = rows * nc
    part = width // nw
    ff_own = w_back.shape[0]
    ff_part = ff_own // nb
    nbuck = bias_table.shape[0] * nw
    index_c = jnp.reshape(c, (1,))

    xs = gather_flip(x, "ctx", nc)
    wq = gather_wt(w_query, nw).reshape(width, width)
    wk = gather_wt(w_key, nw).reshape(width, width)
    wv = gather_wt(w_value, nw).reshape(width, width)
    small = gather_wt(
        jnp.concatenate([gain_attn, gain_ffn, bias_table.reshape(-1)]).reshape(1, -1), nw
    ).reshape(nw, -1)
    gain_one = small[:, :part].reshape(1, width).astype(F32)
    gain_two = small[:, part : 2 * part].reshape(1, width).astype(F32)
    table = small[:, 2 * part :].reshape(nbuck, all_heads)
    wo = gather_wt(w_out, nw).reshape(width, width)
    in_cut = jnp.concatenate(
        [
            lax.dynamic_slice_in_dim(w_in, o * ff_own + b * ff_part, ff_part, 1)
            for o in range(nw)
        ],
        axis=1,
    )
    w_first = gather_wt(in_cut, nw).reshape(width, nw * ff_part)
    back_cut = lax.dynamic_slice_in_dim(w_back, b * ff_part, ff_part, 0)
    w_second = gather_wt(back_cut, nw).reshape(nw * ff_part, width)
    gs = gather_flip(g, "batch", nb)

    def head_cols(value):
        return lax.dynamic_slice_in_dim(value, c * cols, cols, 1)

    pk, pv = head_cols(prefix_keys[0]), head_cols(prefix_values[0])
    tab = jnp.pad(
        lax.dynamic_slice_in_dim(table, c * heads, heads, 1).T.astype(F32), ((0, 8 - heads), (0, 0))
    )
    bucket_row = jnp.pad(buckets[::-1].reshape(1, -1), ((0, 0), (1, 0)), constant_values=-1)

    (normed1, q, k, v, pt, pm, mix, *mixed) = attend(
        nc, heads, hsize, index_c, xs, head_cols(wq), head_cols(wk), head_cols(wv),
        gain_one, pk, pv, tab, bucket_row,
    )
    mixed = mixed[:1] + [flip(mixed[s], "ctx", nc, s) for s in range(1, nc)]
    hidden, normed2, attended = branch(nc, index_c, mixed, x, wo, gain_two)

    n2 = jnp.concatenate(gather_flip(normed2, "batch", nb), axis=0)
    g_all = jnp.concatenate(gs, axis=0)
    inner = nn(n2, w_first)
    act_value, act_pull = jax.vjp(functools.partial(jax.nn.gelu, approximate=True), inner)
    act = act_value.astype(BF)
    grad_act = nt(g_all, w_second)
    grad_inner = act_pull(grad_act)[0].astype(BF)
    part_norm = nt(grad_inner, w_first).astype(BF)
    part_out = nn(act, w_second).astype(BF)
    grad_second = tn(act, g_all).astype(BF)
    grad_first = tn(n2, grad_inner).astype(BF)

    def cut(value, s):
        return value[s * rows : (s + 1) * rows]

    norm_parts = [cut(part_norm, 0)] + [
        flip(cut(part_norm, s), "batch", nb, s) for s in range(1, nb)
    ]
    (grad_hidden, grad_low, *gms) = branch_back(
        nb, nc, index_c, norm_parts, hidden, gain_two, g, wo
    )
    gms = gms[:1] + [flip(gms[s], "ctx", nc, s) for s in range(1, nc)]
    (grad_heads, grad_table, *sends) = attend_back(
        nc, heads, hsize, index_c, gms, pt, pm, q, k, v, mix, pk, pv, bucket_row, nbuck
    )
    sends = sends[:1] + [flip(sends[s], "ctx", nc, s) for s in range(1, nc)]
    grad_x, grad_memk, grad_memv = input_back(
        nc, mem, index_c, sends, x, wq, wk, wv, gain_one, grad_hidden
    )

    result = hidden + cut(part_out, 0).astype(F32)
    for s in range(1, nb):
        result = result + flip(cut(part_out, s), "batch", nb, s).astype(F32)

    def ctx_total(value):
        own = sum_wt(value, nw)
        size = own.shape[0] // nc
        own = sum_flip(own.astype(BF).reshape(nc, size, own.shape[1]), c, "ctx", nc)
        whole = canonical(gather_flip(own.astype(BF), "ctx", nc), c)
        return whole.reshape(nc * size, -1)

    second = gather_flip(ctx_total(grad_second), "batch", nb)
    out_second = canonical([p.astype(F32) for p in second], b).reshape(ff_own, width)
    first = gather_flip(ctx_total(grad_first), "batch", nb)
    out_first = jnp.zeros((part, nw * ff_own), F32)
    for s, piece in enumerate(first):
        for o in range(nw):
            out_first = lax.dynamic_update_slice(
                out_first,
                piece[:, o * ff_part : (o + 1) * ff_part].astype(F32),
                (0, o * ff_own + (b ^ s) * ff_part),
            )

    grad_wo = jnp.einsum("cqd,qe->cde", attended, grad_low, preferred_element_type=F32)
    own_wo = sum_wt(grad_wo.astype(BF).reshape(width, width), nw).astype(BF)
    own_wo = sum_flip(own_wo.reshape(nc, part // nc, width), c, "ctx", nc).astype(BF)
    own_wo = sum_flip(own_wo.reshape(nb, part // nc // nb, width), b, "batch", nb).astype(BF)
    own_wo = canonical(gather_flip(own_wo, "batch", nb), b).reshape(part // nc, width)
    out_wo = canonical(gather_flip(own_wo, "ctx", nc), c).reshape(part, width).astype(F32)

    grad_qkv = sum_wt(tn(normed1, grad_heads).astype(BF), nw).astype(BF)
    line = jnp.pad(grad_table[:, :heads].reshape(1, -1), ((0, 15), (0, 3 * cols - heads * nbuck)))
    if nw == 2:
        line = line.astype(BF)
        line = line.astype(F32) + flip(line, "wt", 2, 1).astype(F32)
    else:
        line = lax.psum(line, "wt")
    size = part // nb
    blocks = jnp.concatenate(
        [
            grad_qkv.reshape(nb, size, 3 * cols),
            jnp.broadcast_to(line.astype(BF)[None], (nb, 16, 3 * cols)),
        ],
        axis=1,
    )
    block = sum_flip(blocks, b, "batch", nb).astype(BF)
    pieces = canonical(gather_flip(block, "ctx", nc), c)
    table_sum = pieces[:, size, : heads * nbuck].astype(F32).reshape(nc, nbuck, heads)
    table_sum = jnp.transpose(table_sum, (1, 0, 2)).reshape(nbuck, all_heads)
    own_buckets = nbuck // nw
    out_table = lax.dynamic_slice_in_dim(table_sum, w * own_buckets, own_buckets, 0)
    wide = canonical(gather_flip(pieces[:, :size], "batch", nb), b)
    wide = wide.reshape(nb, nc, size, 3, cols)
    wide = jnp.transpose(wide, (3, 0, 2, 1, 4)).reshape(3, part, width).astype(F32)
    out_q, out_k, out_v = wide[0], wide[1], wide[2]

    def gain_sum(pairs, gain):
        total = sum(jnp.sum(left * right.astype(F32), axis=1) for left, right in pairs)
        return total / gain.astype(F32)

    gain_two_grad = gain_sum([(out_first, w_in)], gain_ffn)
    gain_one_grad = gain_sum([(out_q, w_query), (out_k, w_key), (out_v, w_value)], gain_attn)
    return (
        result.astype(BF)[None],
        grad_x[None],
        grad_memk[None],
        grad_memv[None],
        gain_one_grad,
        gain_two_grad,
        out_table,
        out_q,
        out_k,
        out_v,
        out_wo,
        out_first,
        out_second,
    )


NEAR_LAST = (0, 2, 1, 3)
LINE = 8


def call(kernel, name, index, args, out, scratch=(), mib=24, far=()):
    stay = [pl.BlockSpec(memory_space=pltpu.HBM)] * len(far)
    return pl.pallas_call(
        kernel,
        out_shape=out,
        in_specs=[smem()] + stay + vmem(len(args)),
        out_specs=vmem(len(out)),
        scratch_shapes=list(scratch),
        compiler_params=params(mib),
        name=name,
    )(index, *far, *args)


def after(values, earlier):
    return lax.optimization_barrier((tuple(values), tuple(earlier)))[0]


def both_gains(wt, own, other, row):
    mine, theirs = own[row : row + 1, :].astype(F32), other[row : row + 1, :].astype(F32)
    first = jnp.where(wt == 0, mine, theirs)
    second = jnp.where(wt == 0, theirs, mine)
    return jnp.concatenate([first, second], axis=1)


def fetch_rows(sems, wt, pairs):
    copies = []
    for i, (scr, own, other) in enumerate(pairs):
        rows = own.shape[0]
        for j, (source, place) in enumerate(((own, wt), (other, 1 - wt))):
            to = scr.at[pl.ds(pl.multiple_of(place * rows, rows), rows), :]
            copies.append(pltpu.make_async_copy(source, to, sems.at[2 * i + j]))
            copies[-1].start()
    return copies


TABLE_ROW = 8


def heads_kernel(heads, hsize, own_buckets, idx, *refs):
    wq, wk, wv, wq2, wk2, wv2 = refs[:6]
    fars = refs[6:11]
    x = refs[11]
    n1_ref, q_ref, k_ref, v_ref, pt_ref, pm_ref, mix_ref, wrow_ref, pk_ref, pv_ref = refs[12:22]
    outs = refs[22:26]
    att_scr, line_scr, sems, more_sems, *scrs = refs[26:]
    w_scr, nears = scrs[:3], scrs[3:]
    small, small2, pk_all, pv_all, bucket_row = nears
    more = [
        pltpu.make_async_copy(source, to, more_sems.at[i])
        for i, (source, to) in enumerate(zip(fars, nears))
    ]
    for copy in more:
        copy.start()
    batch, here, wt = idx[0], idx[1], idx[2]
    length, width = x.shape
    rows = length // 4
    half = wq.shape[0]
    cols = heads * hsize
    window = w_scr[0].shape[1]
    shift = window - cols
    odd = here % 2
    lanes = pl.ds(pl.multiple_of((here * cols - odd * shift), LANES), window)
    copies = fetch_rows(
        sems,
        wt,
        [
            (scr, own.at[:, lanes], other.at[:, lanes])
            for scr, own, other in zip(w_scr, (wq, wk, wv), (wq2, wk2, wv2))
        ],
    )
    for copy in more:
        copy.wait()
    for j in range(4):

        @pl.when(here == j)
        def _():
            take = slice(j * cols, (j + 1) * cols)
            pk_ref[...] = pk_all[:, take]
            pv_ref[...] = pv_all[:, take]

    def own_cols(value):
        return jnp.where(odd == 0, value[:, :cols], value[:, shift:])

    gain = both_gains(wt, small, small2, 0)
    scaled, _ = norm(x[...].astype(F32))
    n1_ref[...] = (scaled * gain).astype(BF)
    normed = n1_ref[...]
    for copy in copies:
        copy.wait()
    quarter = half // 4
    at = pl.multiple_of(wt * half + batch * quarter, quarter)
    for p, (scr, out) in enumerate(zip(w_scr, (q_ref, k_ref, v_ref))):
        out[...] = own_cols(nn(normed, scr[...])).astype(BF)
        wrow_ref[:, p * cols : (p + 1) * cols] = own_cols(
            scr[pl.ds(at, quarter), :].astype(F32)
        ).astype(BF)
    vals_t = v_ref[...].T
    pv_t = pv_ref[...].astype(F32).T.astype(BF)
    tab, tab2 = (
        ref[TABLE_ROW : TABLE_ROW + own_buckets, :LANES].astype(F32) for ref in (small, small2)
    )
    ids = lax.broadcasted_iota(jnp.int32, (own_buckets, 2 * length), 0)
    lines = tn(tab, (ids + wt * own_buckets == bucket_row[...]).astype(F32))
    lines = lines + tn(
        tab2, (ids + (1 - wt) * own_buckets == bucket_row[...]).astype(F32)
    )
    line_scr[...] = lines[: line_scr.shape[0]]
    for h in range(heads):
        part = slice(h * hsize, (h + 1) * hsize)
        query = q_ref[:, part]
        line = jnp.broadcast_to(line_scr[pl.ds(here * heads + h, 1), :], (LANES, 2 * length))
        spread = pltpu.roll(line, 0, 1, stride=1, stride_axis=0)
        bias = jnp.concatenate(
            [spread[:, length - at : 2 * length - at] for at in range(0, length, LANES)], axis=0
        )
        score = nt(k_ref[:, part], query) + bias
        front = nt(pk_ref[:, part], query)
        top = jnp.maximum(
            jnp.max(score, axis=0, keepdims=True), jnp.max(front, axis=0, keepdims=True)
        )
        score = jnp.exp(score - top)
        front = jnp.exp(front - top)
        total = jnp.sum(score, axis=0, keepdims=True) + jnp.sum(front, axis=0, keepdims=True)
        scale = 1.0 / total
        prob = (score * scale).astype(BF)
        prob_mem = (front * scale).astype(BF)
        pt_ref[h] = prob
        pm_ref[h] = prob_mem
        mix_ref[part, :] = nn(vals_t[part, :], prob) + nn(pv_t[part, :], prob_mem)
    att_scr[...] = mix_ref[...].T.astype(BF)
    for step in range(4):
        at = pl.multiple_of((here ^ step) * rows, rows)
        outs[step][...] = att_scr[pl.ds(at, rows), :]


def hidden_kernel(idx, *refs):
    wo, wo2 = refs[:2]
    parts = refs[2:6]
    x, small, small2 = refs[6:9]
    hidden_ref, n2_ref, att_ref, wo_ref, sems = refs[9:]
    here, wt = idx[1], idx[2]
    cols = parts[0].shape[1]
    half = wo.shape[0]
    copies = fetch_rows(sems, wt, [(wo_ref, wo, wo2)])
    for step in range(4):
        att_ref[here ^ step] = parts[step][...]
    for copy in copies:
        copy.wait()
    hidden = x[...].astype(F32)
    for c in range(4):
        hidden = hidden + nn(att_ref[c], wo_ref[c * cols : (c + 1) * cols, :])
    hidden_ref[...] = hidden
    scaled, _ = norm(hidden)
    n2_ref[...] = (scaled * both_gains(wt, small, small2, 1)).astype(BF)


def gelu_parts(v):
    scale = 0.7978845608028654
    square = v * v
    t = jnp.tanh(scale * v * (1.0 + 0.044715 * square))
    grad = 0.5 * (1.0 + t) + 0.5 * v * (1.0 - t * t) * scale * (1.0 + 0.134145 * square)
    return 0.5 * v * (1.0 + t), grad


def own_columns(batch, ff_own, block):
    return [pl.ds(pl.multiple_of(o * ff_own + batch * block, block), block) for o in range(2)]


def ffn_kernel(idx, *refs):
    w1, w1b, w2, w2b = refs[:4]
    n2s, gs = refs[4:8], refs[8:12]
    norms = refs[12:16]
    act_ref, gi_ref, w2_ref, w1_scr, sems = refs[16:]
    batch, wt = idx[0], idx[2]
    half = w1.shape[0]
    block = w1_scr.shape[1] // 2
    ff_own = w2.shape[0]
    copies = []
    for j, (source, place) in enumerate(((w1, wt), (w1b, 1 - wt))):
        to = pl.ds(pl.multiple_of(place * half, half), half)
        for o, cut in enumerate(own_columns(batch, ff_own, block)):
            copies.append(
                pltpu.make_async_copy(
                    source.at[:, cut],
                    w1_scr.at[to, o * block : (o + 1) * block],
                    sems.at[2 * j + o],
                )
            )
    cut = pl.ds(pl.multiple_of(batch * block, block), block)
    for j, (source, place) in enumerate(((w2, wt), (w2b, 1 - wt))):
        to = pl.ds(pl.multiple_of(place * block, block), block)
        copies.append(pltpu.make_async_copy(source.at[cut, :], w2_ref.at[to, :], sems.at[4 + j]))
    for copy in copies:
        copy.start()
    for copy in copies[:4]:
        copy.wait()
    rows = n2s[0].shape[0]
    for s in range(4):
        at = slice(s * rows, (s + 1) * rows)
        act, slope = gelu_parts(nn(n2s[s][...], w1_scr[...]))
        if s == 0:
            for copy in copies[4:]:
                copy.wait()
        act_ref[at, :] = act.astype(BF)
        grad = (nt(gs[s][...], w2_ref[...]).astype(BF).astype(F32) * slope).astype(BF)
        gi_ref[at, :] = grad
        norms[s][...] = nt(grad, w1_scr[...]).astype(BF)


def ffn_back_kernel(idx, *refs):
    n2s, gs = refs[:4], refs[4:8]
    act, gi = refs[8:10]
    mine, theirs, all_scr, scr = refs[10:]
    here, wt = idx[1], idx[2]
    rows = n2s[0].shape[0]
    size = scr.shape[0] // 8

    def spread(p):
        for i, out in enumerate((mine, theirs)):
            for j, place in enumerate(NEAR_LAST):
                at = pl.multiple_of(((wt ^ i) * 4 + (here ^ place)) * size, size)
                to = (4 * (j // 2) + 2 * p + j % 2) * size
                out[to : to + size, :] = scr[pl.ds(at, size), :]

    for s in range(4):
        all_scr[s * rows : (s + 1) * rows, :] = n2s[s][...]
    scr[...] = tn(all_scr[...], gi[...]).astype(BF)
    spread(0)
    for s in range(4):
        all_scr[s * rows : (s + 1) * rows, :] = gs[s][...]
    scr[...] = tn(act[...], all_scr[...]).astype(BF)
    spread(1)


def hidden_back_kernel(idx, *refs):
    parts = refs[:4]
    hidden_ref, small, small2, g, wo = refs[4:9]
    grad_ref, low_ref = refs[9:11]
    outs = refs[11:]
    here, wt = idx[1], idx[2]
    cols = outs[0].shape[1]
    half = wo.shape[0] // 2
    grad_norm = parts[0][...].astype(F32)
    for part in parts[1:]:
        grad_norm = grad_norm + part[...].astype(F32)
    scaled, inverse = norm(hidden_ref[...])
    e = grad_norm * both_gains(wt, small, small2, 1)
    grad = g[...].astype(F32) + inverse * (
        e - scaled * jnp.mean(e * scaled, axis=-1, keepdims=True)
    )
    grad_ref[...] = grad
    low = grad.astype(BF)
    low_ref[...] = low
    for step in range(4):
        at = pl.multiple_of((here ^ step) * cols, cols)
        outs[step][...] = nt(low, wo[pl.ds(at, cols), :]).astype(BF)


def wo_back_kernel(idx, att, low, act, w2, mine, theirs, keep, send, scr):
    rows = low.shape[0]
    batch, here, wt = idx[0], idx[1], idx[2]
    size = att.shape[2]
    for c in range(4):
        scr[c * size : (c + 1) * size, :] = tn(att[c], low[...])
    size = scr.shape[0] // 32
    for i, out in enumerate((mine, theirs)):
        for q, far in enumerate(NEAR_LAST):
            for p, place in enumerate(NEAR_LAST):
                at = (((wt ^ i) * 4 + (here ^ place)) * 4 + (batch ^ far)) * size
                to = (4 * q + p) * size
                out[to : to + size, :] = scr[pl.ds(pl.multiple_of(at, 8), size), :].astype(BF)
    for s, (out, to) in enumerate(((keep, 0), (keep, rows), (send, 0), (send, rows))):
        out[to : to + rows, :] = nn(act[s * rows : (s + 1) * rows, :], w2[...]).astype(BF)


def heads_back_kernel(heads, hsize, idx, *refs):
    gms = refs[:4]
    pt, pm, q, k, v, mix, pk, pv, bucket_row, n1 = refs[4:14]
    mine, theirs = refs[14:16]
    own_out, near_out, far_out = refs[16:19]
    gm_scr, gqt_scr, acc, grad_scr, w_scr = refs[19:]
    batch, here, wt = idx[0], idx[1], idx[2]
    rows, cols = gms[0].shape
    length = 4 * rows
    mem = pk.shape[0]
    high = own_out.shape[0]
    outs = (own_out, far_out, near_out.at[:high], near_out.at[high:])
    for step in range(4):
        at = pl.multiple_of((here ^ step) * rows, rows)
        gm_scr[pl.ds(at, rows), :] = gms[step][...]
    gm_t = gm_scr[...].T
    keys_t = k[...].T
    pk_t = pk[...].astype(F32).T.astype(BF)
    lines = []
    for h in range(heads):
        part = slice(h * hsize, (h + 1) * hsize)
        gm = gm_scr[:, part]
        query = q[:, part]
        spread = jnp.sum(gm_t[part, :].astype(F32) * mix[part, :], axis=0, keepdims=True)
        prob = pt[h]
        prob_mem = pm[h]
        score = prob.astype(F32) * (nt(v[:, part], gm) - spread)
        front = (prob_mem.astype(F32) * (nt(pv[:, part], gm) - spread)).astype(BF)
        low = score.astype(BF)
        gqt_scr[part, :] = nn(keys_t[part, :], low) + nn(pk_t[part, :], front)
        grad_scr[1, :, part] = nn(low, query).astype(BF)
        grad_scr[2, :, part] = nn(prob, gm).astype(BF)
        mem_k = nn(front, query).astype(BF)
        mem_v = nn(prob_mem, gm).astype(BF)
        for step in range(4):
            outs[step][3 * rows + MEM_K : 3 * rows + MEM_K + mem, part] = mem_k
            outs[step][3 * rows + MEM_V : 3 * rows + MEM_V + mem, part] = mem_v
        acc[...] = jnp.zeros_like(acc)
        for at in range(0, length, LANES):
            acc[:, length - at : 2 * length - at] += score[at : at + LANES, :]
        fold = acc[...]
        size = LANES // 2
        while size >= 8:
            fold = fold[:size] + pltpu.roll(fold[size:], 2 * length - size, 1)
            size //= 2
        line = fold[0:1]
        for i in range(1, 8):
            line = line + pltpu.roll(fold[i : i + 1], 2 * length - i, 1)
        lines.append(line)
    grad_scr[0] = gqt_scr[...].T.astype(BF)
    normed = n1[...]
    for p in range(3):
        w_scr[:, p * cols : (p + 1) * cols] = tn(normed, grad_scr[p]).astype(BF)
    size = w_scr.shape[0] // 8
    for i, out in enumerate((mine, theirs)):
        for j, far in enumerate(NEAR_LAST):
            at = pl.multiple_of(((wt ^ i) * 4 + (batch ^ far)) * size, size)
            out[j * size : (j + 1) * size, :] = w_scr[pl.ds(at, size), :]
    lines.append(jnp.zeros((LINE - heads, 2 * length), F32))
    table = lax.dot_general(
        jnp.concatenate(lines, axis=0),
        one_hot_rows(bucket_row[...], LANES),
        (((1,), (1,)), ((), ())),
        precision=lax.Precision.HIGHEST,
        preferred_element_type=F32,
    )
    wide = w_scr.shape[1]
    table = jnp.concatenate([table, jnp.zeros((LINE, wide - LANES), F32)], axis=1)
    for out in (mine, theirs):
        out[4 * size :, :] = table.astype(BF)
    for step in range(4):
        at = pl.multiple_of((here ^ step) * rows, rows)
        for p in range(3):
            outs[step][p * rows : (p + 1) * rows, :] = grad_scr[p, pl.ds(at, rows), :]


def halving_kernel(lines, *refs):
    count = len(lines)
    for i, line in enumerate(lines):
        own, got = refs[2 * i], refs[2 * i + 1]
        keep, send = refs[2 * count + 2 * i], refs[2 * count + 2 * i + 1]
        total = (own[...].astype(F32) + got[...].astype(F32)).astype(BF)
        half = (total.shape[0] - line) // 2
        keep[:half, :] = total[:half]
        send[:half, :] = total[half : 2 * half]
        if line:
            keep[half:, :] = total[2 * half :]
            send[half:, :] = total[2 * half :]


def halving(name, items):
    args, out = [], []
    for own, got, line in items:
        args += [own, got]
        out += [shape(((own.shape[0] - line) // 2 + line, own.shape[1]), BF)] * 2
    return pl.pallas_call(
        functools.partial(halving_kernel, [line for _, _, line in items]),
        out_shape=out,
        in_specs=vmem(len(args)),
        out_specs=vmem(len(out)),
        compiler_params=params(32),
        name=name,
    )(*args)


def add_kernel(left, right, out):
    out[...] = (left[...].astype(F32) + right[...].astype(F32)).astype(BF)


def row_sums(values):
    return lax.dot_general(
        jnp.ones((8, values.shape[1]), F32),
        values,
        (((1,), (1,)), ((), ())),
        precision=lax.Precision.HIGHEST,
        preferred_element_type=F32,
    )


def add_swapped(out, own, got, half):
    for i in range(2):
        left = own[i * half : (i + 1) * half, :].astype(F32)
        right = got[(1 - i) * half : (2 - i) * half, :].astype(F32)
        out[i * half : (i + 1) * half, :] = (left + right).astype(BF)


def ffn_piece_kernel(idx, w_in, own, got, a_ref, b_ref, sum_ref, w_scr, sems):
    batch, here = idx[0], idx[1]
    quarter, width = w_scr.shape
    block = width // 2
    rows = pl.ds(pl.multiple_of(here * quarter, quarter), quarter)
    copies = [
        pltpu.make_async_copy(
            w_in.at[rows, cut], w_scr.at[:, o * block : (o + 1) * block], sems.at[o]
        )
        for o, cut in enumerate(own_columns(batch, w_in.shape[1] // 2, block))
    ]
    for copy in copies:
        copy.start()
    add_swapped(a_ref, own.at[: 2 * quarter], got.at[: 2 * quarter], quarter)
    add_swapped(b_ref, own.at[2 * quarter :], got.at[2 * quarter :], quarter)
    for copy in copies:
        copy.wait()
    sum_ref[...] = row_sums(a_ref[:quarter, :].astype(F32) * w_scr[...].astype(F32))


def heads_pair_kernel(size, height, own, got, out):
    rest = own.shape[0] - height
    out[:height, :] = own[:height, :]
    out[height:, :] = got[:height, :]
    for at, left, right in ((size, size, height), (height + size, height, size)):
        out[at : at + rest, :] = (
            own[left : left + rest, :].astype(F32) + got[right : right + rest, :].astype(F32)
        ).astype(BF)


def heads_piece_kernel(qkv, qkv2, wo, wo2, wrow, sum_in, piece_ref):
    size, width = wo.shape
    quarter = wrow.shape[0]
    wide = wrow.shape[1]
    heads = qkv[...].astype(F32) + qkv2[...].astype(F32)
    piece_ref[:quarter, :] = heads[:quarter].astype(BF)
    sum_heads = row_sums(heads[:quarter] * wrow[...].astype(F32))
    third = size // 3
    cols = width - wide
    for part, at in ((wo, quarter), (wo2, quarter + size + third + LINE)):
        piece_ref[at : at + size, :] = part[:, :wide]
        for o in range(3):
            piece_ref[at + size : at + size + third, o * cols : (o + 1) * cols] = part[
                o * third : (o + 1) * third, wide:
            ]
    row = lax.broadcasted_iota(jnp.int32, (LINE, quarter), 0)
    sums = jnp.where(row == LINE - 2, sum_heads, jnp.where(row == LINE - 1, sum_in[...], 0.0))
    at = quarter + size + third
    line = heads[quarter:]
    pad = jnp.zeros((LINE, LANES), F32)
    sums = jnp.concatenate([sums, jnp.zeros((LINE, LANES - quarter), F32)], axis=1)
    line = line + jnp.concatenate([pad, sums, jnp.zeros((LINE, wide - 2 * LANES), F32)], axis=1)
    piece_ref[at : at + LINE, :] = line.astype(BF)


def ctx_pieces(refs, at, order):
    one, two, four, one2, two2, four2 = refs
    rows = one.shape[0]
    size = rows // 2
    first = ((one, 0), (two, 0), (four, 0), (four, rows))
    last = ((one2, 0), (four2, 0), (two2, 0), (four2, rows))
    if order == 2:
        first = ((one, 0), (four, 0), (two, 0), (four, rows))
        last = ((one2, 0), (two2, 0), (four2, 0), (four2, rows))
    near, far = first[at], last[at]
    found = []
    for (ref, start), places in ((near, (0, 2)), (far, (1, 3))):
        for i, place in enumerate(places):
            found.append((place, ref, start + i * size, size))
    return found


def rows_out_kernel(idx, *refs):
    out, scr, sems = refs[6:]
    copies = []
    for at in range(4):
        for place, ref, start, size in ctx_pieces(refs[:6], at, 2):
            row = len(copies) * size
            scr[row : row + size, :] = ref[start : start + size, :].astype(F32)
            to = pl.multiple_of(((idx[0] ^ at) * 4 + (idx[1] ^ place)) * size, size)
            copies.append(
                pltpu.make_async_copy(
                    scr.at[row : row + size, :], out.at[pl.ds(to, size), :], sems.at[len(copies)]
                )
            )
            copies[-1].start()
    for copy in copies:
        copy.wait()


def cols_out_kernel(idx, *refs):
    out, scr, sems = refs[6:]
    copies = []
    block = scr.shape[1] // 2
    for at in range(4):
        for place, ref, start, size in ctx_pieces(refs[:6], at, 1):
            row = (len(copies) // 2) * size
            scr[row : row + size, :] = ref[start : start + size, :].astype(F32)
            to = pl.multiple_of((idx[1] ^ place) * size, size)
            for o in range(2):
                col = pl.multiple_of((4 * o + (idx[0] ^ at)) * block, block)
                copies.append(
                    pltpu.make_async_copy(
                        scr.at[row : row + size, o * block : (o + 1) * block],
                        out.at[pl.ds(to, size), pl.ds(col, block)],
                        sems.at[len(copies)],
                    )
                )
                copies[-1].start()
    for copy in copies:
        copy.wait()


def pieces_out(kernel, name, index, pieces, dims, copies):
    rows, width = pieces[0].shape
    return pl.pallas_call(
        kernel,
        out_shape=shape(dims, F32),
        in_specs=[smem()] + vmem(6),
        out_specs=pl.BlockSpec(memory_space=pltpu.HBM),
        scratch_shapes=[
            pltpu.VMEM((8 * rows, width), F32),
            pltpu.SemaphoreType.DMA((copies,)),
        ],
        compiler_params=params(16),
        name=name,
    )(index, *pieces)


def heads_out_kernel(heads, buckets, idx, *refs):
    small = refs[6]
    oq, ok, ov, oo, gain_one, gain_two, table, scr, lines, tab_scr = refs[7:]
    step = pl.program_id(0)
    quarter, width = oq.shape
    cols = width // 4
    wide = 3 * cols
    size = quarter // 4
    third = size // 3
    for at in range(4):

        @pl.when(step == at)
        def _():
            for place, ref, start, height in ctx_pieces(refs[:6], at, 1):
                scr[idx[1] ^ place] = ref[start : start + height, :]

    for c in range(4):
        part = scr[c].astype(F32)
        for o, out in enumerate((oq, ok, ov)):
            out[:, c * cols : (c + 1) * cols] = part[:quarter, o * cols : (o + 1) * cols]
        oo[c, 0, :, :wide] = part[quarter : quarter + size]
        for o in range(3):
            oo[c, 0, o * third : (o + 1) * third, wide:] = part[
                quarter + size : quarter + size + third, o * cols : (o + 1) * cols
            ]
        lines[idx[0] ^ step, c] = part[quarter + size + third :]

    @pl.when(step == 3)
    def _():
        seen = [[lines[b, c] for c in range(4)] for b in range(4)]
        take = slice(LANES, LANES + quarter)
        one = jnp.concatenate(
            [sum(seen[b][c][LINE - 2 : LINE - 1, take] for c in range(4)) for b in range(4)], axis=1
        )
        two = jnp.concatenate(
            [sum(seen[b][c][LINE - 1 : LINE, take] for b in range(4)) for c in range(4)], axis=1
        )
        gain_one[...] = (one / small[0:1, :].astype(F32))[0]
        gain_two[...] = (two / small[1:2, :].astype(F32))[0]
        rest = [seen[0][c][:heads, :LANES] for c in range(4)]
        rest.append(jnp.zeros((LANES - 4 * heads, LANES), F32))
        tab_scr[...] = jnp.concatenate(rest, axis=0).T
        own_buckets = buckets // 2
        at = pl.multiple_of(idx[2] * own_buckets, 8)
        table[...] = tab_scr[pl.ds(at, own_buckets), : 4 * heads]


def heads_out(index, pieces, small, width, heads, buckets):
    height, wide = pieces[0].shape[0] // 2, pieces[0].shape[1]
    part = width // 2
    quarter = part // 4
    size = quarter // 4
    block = pl.BlockSpec((quarter, width), lambda step, idx: (idx[0] ^ step, 0))
    whole = [pl.BlockSpec(p.shape, lambda step, idx: (0, 0)) for p in (*pieces, small)]
    return pl.pallas_call(
        functools.partial(heads_out_kernel, heads, buckets),
        out_shape=[shape((part, width), F32)] * 3
        + [
            shape((4, 4, size, width), F32),
            shape((part,), F32),
            shape((part,), F32),
            shape((buckets // 2, 4 * heads), F32),
        ],
        grid_spec=pltpu.PrefetchScalarGridSpec(
            num_scalar_prefetch=1,
            grid=(4,),
            in_specs=whole,
            out_specs=[block] * 3
            + [
                pl.BlockSpec((4, 1, size, width), lambda step, idx: (0, idx[0] ^ step, 0, 0)),
                pl.BlockSpec((part,), lambda step, idx: (0,)),
                pl.BlockSpec((part,), lambda step, idx: (0,)),
                pl.BlockSpec((buckets // 2, 4 * heads), lambda step, idx: (0, 0)),
            ],
            scratch_shapes=[
                pltpu.VMEM((4, height, wide), BF),
                pltpu.VMEM((4, 4, LINE, wide), F32),
                pltpu.VMEM((LANES, LANES), F32),
            ],
        ),
        compiler_params=params(32),
        name="heads_out",
    )(index, *pieces, small)


def paired(
    inputs,
    prefix_keys,
    prefix_values,
    gain_attn,
    w_query,
    w_key,
    w_value,
    w_out,
    bias_table,
    gain_ffn,
    w_in,
    w_back,
    buckets,
    out_grad,
):
    b, c, w = lax.axis_index("batch"), lax.axis_index("ctx"), lax.axis_index("wt")
    index = jnp.stack([b, c, w])
    x, g = inputs[0], out_grad[0]
    rows, width = x.shape
    all_heads = bias_table.shape[1]
    heads = all_heads // 4
    hsize = width // all_heads
    cols = heads * hsize
    wide = 3 * cols
    mem = prefix_keys.shape[1]
    length = 4 * rows
    part = width // 2
    quarter = part // 4
    ff_own = w_back.shape[0]
    ff_part = ff_own // 4
    nbuck = 2 * bias_table.shape[0]

    def over_wt(value, name):
        with jax.named_scope(name + "_w"):
            return flip(value, "wt", 2, 1)

    def over_ctx(value, step, name):
        with jax.named_scope(name + "_z" + str(step)):
            return flip(value, "ctx", 4, step)

    def over_batch(value, step, name):
        with jax.named_scope(name + "_b" + str(step)):
            return flip(value, "batch", 4, step)

    own_buckets = nbuck // 2
    small = jnp.concatenate(
        [
            jnp.pad(jnp.stack([gain_attn, gain_ffn]), ((0, TABLE_ROW - 2), (0, 0))),
            jnp.pad(bias_table, ((0, 0), (0, part - all_heads))),
        ]
    )
    w_query2, w_key2, w_value2 = [over_wt(v, "weight") for v in (w_query, w_key, w_value)]
    small2 = over_wt(small, "small")
    g_near = over_batch(g, 1, "g")
    x_all = lax.all_gather(x, "ctx", axis=0, tiled=True)
    bucket_row = jnp.pad(buckets[::-1].reshape(1, -1), ((0, 0), (1, 0)), constant_values=-1)

    tokens = shape((length, cols), BF)
    few = (small, small2, prefix_keys[0], prefix_values[0], bucket_row)
    (n1, q, k, v, pt, pm, mix, wrow, pk, pv, *mixed) = call(
        functools.partial(heads_kernel, heads, hsize, own_buckets),
        "attend",
        index,
        [x_all],
        [shape((length, width), BF)]
        + [tokens] * 3
        + [
            shape((heads, length, length), BF),
            shape((heads, mem, length), BF),
            shape((cols, length), F32),
            shape((quarter, wide), BF),
            shape((mem, cols), BF),
            shape((mem, cols), BF),
        ]
        + [shape((rows, cols), BF)] * 4,
        [
            pltpu.VMEM((length, cols), BF),
            pltpu.VMEM((16, 2 * length), F32),
            pltpu.SemaphoreType.DMA((6,)),
            pltpu.SemaphoreType.DMA((len(few),)),
        ]
        + [pltpu.VMEM((width, -(-cols // LANES) * LANES), BF)] * 3
        + [pltpu.VMEM(v.shape, v.dtype) for v in few],
        far=(w_query, w_key, w_value, w_query2, w_key2, w_value2, *few),
    )
    (g_pair, w_out_sent) = after((jnp.concatenate([g, g_near]), w_out), mixed[:1])
    w_out2 = over_wt(w_out_sent, "weight")
    g_far = over_batch(g_pair, 2, "g")
    mixed = mixed[:1] + [over_ctx(mixed[s], s, "mixed") for s in range(1, 4)]
    (*mixed, w_out2, g_far) = after((*mixed, w_out2, g_far), ())
    square = shape((width, width), BF)
    hidden, n2, attended, wo = call(
        hidden_kernel,
        "hidden",
        index,
        [*mixed, x, small, small2],
        [shape((rows, width), F32), shape((rows, width), BF), shape((4, rows, cols), BF), square],
        [pltpu.SemaphoreType.DMA((2,))],
        far=(w_out, w_out2),
    )

    n2s = [n2] + [over_batch(n2, s, "n2") for s in range(1, 4)]
    (w_in_sent, w_back_sent) = after((w_in, w_back), (n2,))
    w_in2, w_back2 = over_wt(w_in_sent, "in"), over_wt(w_back_sent, "back")
    gs = (g, g_near, g_far[:rows], g_far[rows:])
    hid = shape((length, 2 * ff_part), BF)
    *norms, act, gi, w_second = call(
        ffn_kernel,
        "ffn",
        index,
        [*n2s, *gs],
        [shape((rows, width), BF)] * 4 + [hid, hid, shape((2 * ff_part, width), BF)],
        [pltpu.VMEM((width, 2 * ff_part), BF), pltpu.SemaphoreType.DMA((6,))],
        far=(w_in, w_in2, w_back, w_back2),
    )
    norms = norms[:1] + [over_batch(norms[s], s, "norm") for s in range(1, 4)]
    ffn, ffn_sent = call(
        ffn_back_kernel,
        "ffn_back",
        index,
        [*n2s, *gs, act, gi],
        [square, square],
        [pltpu.VMEM((length, width), BF), pltpu.VMEM((width, width), BF)],
    )
    ffn, ffn_sent = halving("ffn_wt", [(ffn, over_wt(ffn_sent, "ffn"), 0)])
    ffn_got = over_ctx(ffn_sent, 1, "ffn")
    norms = after(norms, (ffn, ffn_sent))
    grad_hidden, low, *gms = call(
        hidden_back_kernel,
        "hidden_back",
        index,
        [*norms, hidden, small, small2, g, wo],
        [shape((rows, width), F32), shape((rows, width), BF)] + [shape((rows, cols), BF)] * 4,
    )
    ffn = pl.pallas_call(
        add_kernel,
        out_shape=shape((part, width), BF),
        in_specs=vmem(2),
        out_specs=vmem(1)[0],
        compiler_params=params(16),
        name="ffn_near",
    )(ffn, ffn_got)
    gms = list(gms[:1]) + [over_ctx(gms[s], s, "gm") for s in range(1, 4)]
    (ffn_sent,) = after((ffn,), gms[1:])
    ffn_got = over_ctx(ffn_sent, 2, "ffn")
    high = 3 * rows + MEM_END
    (qkv, qkv_sent, own_block, near_blocks, far_block) = call(
        functools.partial(heads_back_kernel, heads, hsize),
        "attend_back",
        index,
        [*gms, pt, pm, q, k, v, mix, pk, pv, bucket_row, n1],
        [shape((part + LINE, wide), BF)] * 2
        + [shape((n * high, cols), BF) for n in (1, 2, 1)],
        [
            pltpu.VMEM((length, cols), BF),
            pltpu.VMEM((cols, length), F32),
            pltpu.VMEM((LANES, 2 * length), F32),
            pltpu.VMEM((3, length, cols), BF),
            pltpu.VMEM((width, wide), BF),
        ],
    )
    (low,) = after((low,), (qkv,))
    wo_sum, wo_sent, outs, outs_sent = call(
        wo_back_kernel,
        "wo_back",
        index,
        [attended, low, act, w_second],
        [shape((part, width), BF)] * 2 + [shape((2 * rows, width), BF)] * 2,
        [pltpu.VMEM((width, width), F32)],
    )
    outs_got = over_batch(outs_sent, 2, "outs")
    wo_sum, wo_sent = halving("wo_wt", [(wo_sum, over_wt(wo_sent, "wo"), 0)])
    wo_sum, wo_sent = halving("wo_near", [(wo_sum, over_batch(wo_sent, 1, "wo"), 0)])

    outs, outs_sent = halving("outs_far", [(outs, outs_got, 0)])
    (outs_sent, wo_sent) = after((outs_sent, wo_sent), (outs, wo_sum))
    wo_sum, wo_sent = halving("wo_far", [(wo_sum, over_batch(wo_sent, 2, "wo"), 0)])
    wo_sum, wo_sent = halving("wo_last", [(wo_sum, over_ctx(wo_sent, 1, "wo"), 0)])
    outs_got = over_batch(outs_sent, 1, "outs")
    qkv, qkv_sent = halving("qkv_wt", [(qkv, over_wt(qkv_sent, "qkv"), LINE)])
    qkv, qkv_sent = halving("qkv_near", [(qkv, over_batch(qkv_sent, 1, "qkv"), LINE)])
    qkv_got = over_batch(qkv_sent, 2, "qkv")
    (ffn_got,) = after((ffn_got,), (qkv_got, outs_got, wo_sum, wo_sent))
    a1, b1, sum_in = call(
        ffn_piece_kernel,
        "ffn_piece",
        index,
        [ffn, ffn_got],
        [shape((2 * quarter, width), BF)] * 2 + [shape((8, quarter), F32)],
        [pltpu.VMEM((quarter, width), BF), pltpu.SemaphoreType.DMA((2,))],
        far=(w_in,),
    )

    def pile(one, two):
        return jnp.concatenate([one, two])

    result = (hidden + outs.astype(F32) + outs_got.astype(F32)).astype(BF)
    a2, b2 = over_batch(a1, 1, "in_near"), over_batch(b1, 2, "out_near")
    c1, d1 = over_ctx(a1, 1, "in_back"), over_ctx(b1, 1, "out_back")
    pile_a, pile_b = pile(a1, a2), pile(b1, b2)
    a3, b3 = over_batch(pile_a, 2, "in_near2"), over_batch(pile_b, 1, "out_near2")
    (c1, d1) = after((c1, d1), (pile_a, pile_b))
    c2, d2 = over_batch(c1, 2, "in_far"), over_batch(d1, 1, "out_far")
    height = quarter + quarter // 4 + quarter // 12 + LINE
    piece = pl.pallas_call(
        heads_piece_kernel,
        out_shape=shape((2 * height - quarter - LINE, wide), BF),
        in_specs=vmem(6),
        out_specs=vmem(1)[0],
        compiler_params=params(32),
        name="heads_piece",
    )(qkv, qkv_got, wo_sum, wo_sent, wrow, sum_in)

    (piece,) = after((piece,), (c1, d1))
    heads_far = over_ctx(piece, 2, "heads_back")
    pile_c, pile_d = pile(c1, c2), pile(d1, d2)
    c3, d3 = over_batch(pile_c, 1, "in_far2"), over_batch(pile_d, 2, "out_far2")
    (heads_far,) = after((heads_far,), (a3, b3))
    (near_blocks,) = after((near_blocks,), (heads_far,))
    near_got = over_ctx(near_blocks, 2, "sends")
    far_pile = pile(far_block, near_got[high:])
    far_got = over_ctx(far_pile, 1, "sends")
    e1 = pl.pallas_call(
        functools.partial(heads_pair_kernel, quarter, height),
        out_shape=shape((2 * height, wide), BF),
        in_specs=vmem(2),
        out_specs=vmem(1)[0],
        compiler_params=params(16),
        name="heads_pair",
    )(piece, heads_far)
    f1 = over_ctx(e1, 1, "heads_back")
    (e1, f1) = after((e1, f1), (pile_c, pile_d))
    e2, f2 = over_batch(e1, 1, "heads_near"), over_batch(f1, 2, "heads_far")
    (e1, e2, f1, f2) = after((e1, e2, f1, f2), (c3, d3, far_pile))
    e3 = over_batch(pile(e1, e2), 2, "heads_near2")
    f3 = over_batch(pile(f1, f2), 1, "heads_far2")
    out_second = pieces_out(
        rows_out_kernel, "rows_out", index, (b1, b2, b3, d1, d2, d3), (ff_own, width), 16
    )
    out_first = pieces_out(
        cols_out_kernel, "cols_out", index, (a1, a2, a3, c1, c2, c3), (part, 2 * ff_own), 32
    )
    out_q, out_k, out_v, out_wo, gain_one, gain_two, out_table = heads_out(
        index, (e1, e2, e3, f1, f2, f3), small, width, heads, nbuck
    )
    grad_x, grad_memk, grad_memv = call(
        input_end_kernel,
        "input_back",
        index,
        [own_block, near_got, far_got, x, small, small2, grad_hidden],
        [shape((rows, width), BF), shape((mem, width), F32), shape((mem, width), F32)],
        [pltpu.VMEM((4,) + own_block.shape, BF), pltpu.SemaphoreType.DMA((6,))]
        + [pltpu.VMEM((width, width), BF)] * 3,
        far=(w_query, w_key, w_value, w_query2, w_key2, w_value2),
    )
    return (
        result[None],
        grad_x[None],
        grad_memk[None],
        grad_memv[None],
        gain_one,
        gain_two,
        out_table,
        out_q,
        out_k,
        out_v,
        out_wo.reshape(part, width),
        out_first,
        out_second,
    )


def input_end_kernel(idx, *refs):
    wq, wk, wv, wq2, wk2, wv2 = refs[:6]
    own, near, far, x, small, small2, grad_hidden = refs[6:13]
    out_ref, memk_ref, memv_ref, scr, sems, *w_scr = refs[13:]
    high = own.shape[0]
    parts = (own, far.at[:high], near.at[:high], far.at[high:])
    here, wt = idx[1], idx[2]
    rows = x.shape[0]
    mem = memk_ref.shape[0]
    copies = fetch_rows(sems, wt, list(zip(w_scr, (wq, wk, wv), (wq2, wk2, wv2))))
    for step in range(4):
        scr[here ^ step] = parts[step][...]
    for copy in copies:
        copy.wait()

    def wide(at, count):
        return jnp.concatenate([scr[c, at : at + count, :] for c in range(4)], axis=1)

    grad_norm = sum(nt(wide(p * rows, rows), whole[...]) for p, whole in enumerate(w_scr))
    scaled, inverse = norm(x[...].astype(F32))
    e = grad_norm * both_gains(wt, small, small2, 0)
    grad = grad_hidden[...] + inverse * (
        e - scaled * jnp.mean(e * scaled, axis=-1, keepdims=True)
    )
    out_ref[...] = grad.astype(BF)
    memk_ref[...] = wide(3 * rows + MEM_K, mem).astype(F32)
    memv_ref[...] = wide(3 * rows + MEM_V, mem).astype(F32)


def solution(mesh):
    tokens = P(("batch", "wt"), "ctx", None)
    memory = P(("batch", "wt"), None, None)
    matrix = P("wt", None)
    vector = P("wt")
    sizes = (mesh.shape["batch"], mesh.shape["ctx"], mesh.shape["wt"])
    body = paired if sizes == (4, 4, 2) else functools.partial(general, sizes)
    return jax.shard_map(
        body,
        mesh=mesh,
        in_specs=(
            tokens, memory, memory, vector, matrix, matrix, matrix, matrix, matrix, vector,
            matrix, matrix, P(), tokens,
        ),
        out_specs=(
            tokens, tokens, memory, memory, vector, vector, matrix, matrix, matrix, matrix,
            matrix, matrix, matrix,
        ),
        check_vma=False,
    )
```

```python
import functools

import jax
import jax.numpy as jnp
from jax import lax
from jax.experimental import pallas as pl
from jax.experimental.pallas import tpu as pltpu
from jax.sharding import PartitionSpec as P

EPS = 1e-06
F32 = jnp.float32
BF = jnp.bfloat16
LANES = 128


def nn(left, right):
    return lax.dot_general(left, right, (((1,), (0,)), ((), ())), preferred_element_type=F32)


def nt(left, right):
    return lax.dot_general(left, right, (((1,), (1,)), ((), ())), preferred_element_type=F32)


def tn(left, right):
    return lax.dot_general(left, right, (((0,), (0,)), ((), ())), preferred_element_type=F32)


def vmem(count):
    return [pl.BlockSpec(memory_space=pltpu.VMEM)] * count


def smem():
    return pl.BlockSpec(memory_space=pltpu.SMEM)


def shape(dims, kind):
    return jax.ShapeDtypeStruct(dims, kind)


def params(mib):
    return pltpu.CompilerParams(vmem_limit_bytes=mib << 20)


def flip(value, axis, size, step):
    return lax.ppermute(value, axis, [(i, i ^ step) for i in range(size)])


def gather_flip(value, axis, size):
    return [value] + [flip(value, axis, size, step) for step in range(1, size)]


def canonical(parts, index):
    whole = jnp.zeros((len(parts),) + parts[0].shape, parts[0].dtype)
    for step, part in enumerate(parts):
        whole = lax.dynamic_update_index_in_dim(whole, part, index ^ step, 0)
    return whole


def gather_wt(value, size):
    if size == 2:
        own = lax.axis_index("wt") == 0
        other = flip(value, "wt", 2, 1)
        return jnp.stack([jnp.where(own, value, other), jnp.where(own, other, value)])
    return lax.all_gather(value, "wt", axis=0)


def sum_wt(value, size):
    rows = value.shape[0] // size
    if size == 2:
        index = lax.axis_index("wt")
        mine = lax.dynamic_slice_in_dim(value, index * rows, rows, 0)
        theirs = lax.dynamic_slice_in_dim(value, (1 - index) * rows, rows, 0)
        return mine.astype(F32) + flip(theirs, "wt", 2, 1).astype(F32)
    return lax.psum_scatter(value, "wt", scatter_dimension=0, tiled=True).astype(F32)


def sum_flip(blocks, index, axis, size):
    total = lax.dynamic_index_in_dim(blocks, index, 0, keepdims=False).astype(F32)
    for step in range(1, size):
        block = lax.dynamic_index_in_dim(blocks, index ^ step, 0, keepdims=False)
        total = total + flip(block, axis, size, step).astype(F32)
    return total


def norm(values):
    inverse = lax.rsqrt(jnp.mean(values * values, axis=-1, keepdims=True) + EPS)
    return values * inverse, inverse


def one_hot_rows(bucket_row, buckets):
    ids = lax.broadcasted_iota(jnp.int32, (buckets, bucket_row.shape[1]), 0)
    return (ids == bucket_row).astype(F32)


def attend_kernel(nc, heads, hsize, mem, idx, *refs):
    xs = refs[:nc]
    wq, wk, wv, gain, pk, pv, tab, bucket_row = refs[nc : nc + 8]
    n1_ref, q_ref, k_ref, v_ref, pt_ref, pm_ref, mix_ref = refs[nc + 8 : nc + 15]
    outs = refs[nc + 15 : nc + 15 + nc]
    att_scr = refs[nc + 15 + nc]
    here = idx[0]
    rows = xs[0].shape[0]
    length = nc * rows
    for step in range(nc):
        scaled, _ = norm(xs[step][...].astype(F32))
        at = pl.multiple_of((here ^ step) * rows, rows)
        n1_ref[pl.ds(at, rows), :] = (scaled * gain[...]).astype(BF)
    normed = n1_ref[...]
    q_ref[...] = nn(normed, wq[...]).astype(BF)
    k_ref[...] = nn(normed, wk[...]).astype(BF)
    v_ref[...] = nn(normed, wv[...]).astype(BF)
    vals_t = v_ref[...].T
    pv_t = pv[...].astype(F32).T.astype(BF)
    hot = one_hot_rows(bucket_row[...], tab.shape[1])
    lines = nn(tab[...], hot)
    for h in range(heads):
        part = slice(h * hsize, (h + 1) * hsize)
        query = q_ref[:, part]
        line = jnp.broadcast_to(lines[h : h + 1, :], (LANES, 2 * length))
        spread = pltpu.roll(line, 0, 1, stride=1, stride_axis=0)
        bias = jnp.concatenate(
            [spread[:, length - at : 2 * length - at] for at in range(0, length, LANES)], axis=0
        )
        score = nt(k_ref[:, part], query) + bias
        front = nt(pk[:, part], query)
        top = jnp.maximum(
            jnp.max(score, axis=0, keepdims=True), jnp.max(front, axis=0, keepdims=True)
        )
        score = jnp.exp(score - top)
        front = jnp.exp(front - top)
        total = jnp.sum(score, axis=0, keepdims=True) + jnp.sum(front, axis=0, keepdims=True)
        scale = 1.0 / total
        prob = (score * scale).astype(BF)
        prob_mem = (front * scale).astype(BF)
        pt_ref[h] = prob
        pm_ref[h] = prob_mem
        mix_ref[part, :] = nn(vals_t[part, :], prob) + nn(pv_t[part, :], prob_mem)
    att_scr[...] = mix_ref[...].T.astype(BF)
    for step in range(nc):
        at = pl.multiple_of((here ^ step) * rows, rows)
        outs[step][...] = att_scr[pl.ds(at, rows), :]


def attend(nc, heads, hsize, index, xs, wq, wk, wv, gain, pk, pv, tab, bucket_row):
    rows, width = xs[0].shape
    length = rows * nc
    cols = heads * hsize
    mem = pk.shape[0]
    out = [
        shape((length, width), BF),
        shape((length, cols), BF),
        shape((length, cols), BF),
        shape((length, cols), BF),
        shape((heads, length, length), BF),
        shape((heads, mem, length), BF),
        shape((cols, length), F32),
    ] + [shape((rows, cols), BF)] * nc
    return pl.pallas_call(
        functools.partial(attend_kernel, nc, heads, hsize, mem),
        out_shape=out,
        in_specs=[smem()] + vmem(nc + 8),
        out_specs=vmem(len(out)),
        scratch_shapes=[pltpu.VMEM((length, cols), BF)],
        compiler_params=params(24),
        name="attend",
    )(index, *xs, wq, wk, wv, gain, pk, pv, tab, bucket_row)


def branch_kernel(nc, idx, *refs):
    parts = refs[:nc]
    x, wo, gain = refs[nc : nc + 3]
    hidden_ref, n2_ref, att_ref = refs[nc + 3 : nc + 6]
    here = idx[0]
    cols = parts[0].shape[1]
    for step in range(nc):
        att_ref[here ^ step] = parts[step][...]
    hidden = x[...].astype(F32)
    for c in range(nc):
        hidden = hidden + nn(att_ref[c], wo[c * cols : (c + 1) * cols, :])
    hidden_ref[...] = hidden
    scaled, _ = norm(hidden)
    n2_ref[...] = (scaled * gain[...]).astype(BF)


def branch(nc, index, parts, x, wo, gain):
    rows, cols = parts[0].shape
    out = [shape(x.shape, F32), shape(x.shape, BF), shape((nc, rows, cols), BF)]
    return pl.pallas_call(
        functools.partial(branch_kernel, nc),
        out_shape=out,
        in_specs=[smem()] + vmem(nc + 3),
        out_specs=vmem(3),
        compiler_params=params(32),
        name="branch",
    )(index, *parts, x, wo, gain)


def branch_back_kernel(nb, nc, idx, *refs):
    parts = refs[:nb]
    hidden_ref, gain, g, wo = refs[nb : nb + 4]
    grad_ref, low_ref = refs[nb + 4 : nb + 6]
    outs = refs[nb + 6 : nb + 6 + nc]
    here = idx[0]
    cols = outs[0].shape[1]
    grad_norm = parts[0][...].astype(F32)
    for part in parts[1:]:
        grad_norm = grad_norm + part[...].astype(F32)
    scaled, inverse = norm(hidden_ref[...])
    e = grad_norm * gain[...]
    grad = g[...].astype(F32) + inverse * (
        e - scaled * jnp.mean(e * scaled, axis=-1, keepdims=True)
    )
    grad_ref[...] = grad
    low = grad.astype(BF)
    low_ref[...] = low
    for step in range(nc):
        at = pl.multiple_of((here ^ step) * cols, 8)
        outs[step][...] = nt(low, wo[pl.ds(at, cols), :]).astype(BF)


def branch_back(nb, nc, index, parts, hidden, gain, g, wo):
    rows, width = hidden.shape
    cols = width // nc
    out = [shape((rows, width), F32), shape((rows, width), BF)] + [shape((rows, cols), BF)] * nc
    return pl.pallas_call(
        functools.partial(branch_back_kernel, nb, nc),
        out_shape=out,
        in_specs=[smem()] + vmem(nb + 4),
        out_specs=vmem(len(out)),
        compiler_params=params(32),
        name="branch_back",
    )(index, *parts, hidden, gain, g, wo)


MEM_K, MEM_V, MEM_END = 0, 32, 64


def attend_back_kernel(nc, heads, hsize, idx, *refs):
    gms = refs[:nc]
    pt, pm, q, k, v, mix, pk, pv, bucket_row = refs[nc : nc + 9]
    grad_ref, table_ref = refs[nc + 9 : nc + 11]
    outs = refs[nc + 11 : nc + 11 + nc]
    gm_scr, gqt_scr, acc = refs[nc + 11 + nc :]
    here = idx[0]
    rows, cols = gms[0].shape
    length = rows * nc
    mem = pk.shape[0]
    for step in range(nc):
        at = pl.multiple_of((here ^ step) * rows, rows)
        gm_scr[pl.ds(at, rows), :] = gms[step][...]
    gm_t = gm_scr[...].T
    keys_t = k[...].T
    pk_t = pk[...].astype(F32).T.astype(BF)
    lines = []
    for h in range(heads):
        part = slice(h * hsize, (h + 1) * hsize)
        gm = gm_scr[:, part]
        query = q[:, part]
        spread = jnp.sum(gm_t[part, :].astype(F32) * mix[part, :], axis=0, keepdims=True)
        prob = pt[h]
        prob_mem = pm[h]
        score = prob.astype(F32) * (nt(v[:, part], gm) - spread)
        front = (prob_mem.astype(F32) * (nt(pv[:, part], gm) - spread)).astype(BF)
        low = score.astype(BF)
        gqt_scr[part, :] = nn(keys_t[part, :], low) + nn(pk_t[part, :], front)
        grad_ref[:, cols + h * hsize : cols + (h + 1) * hsize] = nn(low, query).astype(BF)
        grad_ref[:, 2 * cols + h * hsize : 2 * cols + (h + 1) * hsize] = nn(prob, gm).astype(BF)
        mem_k = nn(front, query).astype(BF)
        mem_v = nn(prob_mem, gm).astype(BF)
        for step in range(nc):
            outs[step][3 * rows + MEM_K : 3 * rows + MEM_K + mem, part] = mem_k
            outs[step][3 * rows + MEM_V : 3 * rows + MEM_V + mem, part] = mem_v
        acc[...] = jnp.zeros_like(acc)
        for at in range(0, length, LANES):
            acc[:, length - at : 2 * length - at] += score[at : at + LANES, :]
        fold = acc[...]
        half = LANES // 2
        while half >= 8:
            fold = fold[:half] + pltpu.roll(fold[half:], 2 * length - half, 1)
            half //= 2
        line = fold[0:1]
        for i in range(1, 8):
            line = line + pltpu.roll(fold[i : i + 1], 2 * length - i, 1)
        lines.append(line)
    lines.append(jnp.zeros((8 - heads, 2 * length), F32))
    hot = one_hot_rows(bucket_row[...], table_ref.shape[0])
    table_ref[...] = lax.dot_general(
        hot,
        jnp.concatenate(lines, axis=0),
        (((1,), (1,)), ((), ())),
        precision=lax.Precision.HIGHEST,
        preferred_element_type=F32,
    )
    grad_ref[:, :cols] = gqt_scr[...].T.astype(BF)
    for step in range(nc):
        at = pl.multiple_of((here ^ step) * rows, rows)
        for p in range(3):
            outs[step][p * rows : (p + 1) * rows, :] = grad_ref[
                pl.ds(at, rows), p * cols : (p + 1) * cols
            ]


def attend_back(nc, heads, hsize, index, gms, pt, pm, q, k, v, mix, pk, pv, bucket_row, nbuck):
    rows, cols = gms[0].shape
    length = rows * nc
    out = [shape((length, 3 * cols), BF), shape((nbuck, 8), F32)] + [
        shape((3 * rows + MEM_END, cols), BF)
    ] * nc
    return pl.pallas_call(
        functools.partial(attend_back_kernel, nc, heads, hsize),
        out_shape=out,
        in_specs=[smem()] + vmem(nc + 9),
        out_specs=vmem(len(out)),
        scratch_shapes=[
            pltpu.VMEM((length, cols), BF),
            pltpu.VMEM((cols, length), F32),
            pltpu.VMEM((LANES, 2 * length), F32),
        ],
        compiler_params=params(24),
        name="attend_back",
    )(index, *gms, pt, pm, q, k, v, mix, pk, pv, bucket_row)


def input_back_kernel(nc, mem, idx, *refs):
    parts = refs[:nc]
    x, wq, wk, wv, gain, grad_hidden = refs[nc : nc + 6]
    out_ref, memk_ref, memv_ref = refs[nc + 6 : nc + 9]
    scr = refs[nc + 9]
    here = idx[0]
    rows = x.shape[0]
    for step in range(nc):
        scr[here ^ step] = parts[step][...]

    def wide(at, count):
        return jnp.concatenate([scr[c, at : at + count, :] for c in range(nc)], axis=1)

    grad_norm = (
        nt(wide(0, rows), wq[...])
        + nt(wide(rows, rows), wk[...])
        + nt(wide(2 * rows, rows), wv[...])
    )
    scaled, inverse = norm(x[...].astype(F32))
    e = grad_norm * gain[...]
    grad = grad_hidden[...] + inverse * (
        e - scaled * jnp.mean(e * scaled, axis=-1, keepdims=True)
    )
    out_ref[...] = grad.astype(BF)
    memk_ref[...] = wide(3 * rows + MEM_K, mem).astype(F32)
    memv_ref[...] = wide(3 * rows + MEM_V, mem).astype(F32)


def input_back(nc, mem, index, parts, x, wq, wk, wv, gain, grad_hidden):
    rows, width = x.shape
    out = [shape((rows, width), BF), shape((mem, width), F32), shape((mem, width), F32)]
    return pl.pallas_call(
        functools.partial(input_back_kernel, nc, mem),
        out_shape=out,
        in_specs=[smem()] + vmem(nc + 6),
        out_specs=vmem(3),
        scratch_shapes=[pltpu.VMEM((nc,) + parts[0].shape, BF)],
        compiler_params=params(32),
        name="input_back",
    )(index, *parts, x, wq, wk, wv, gain, grad_hidden)


def general(
    sizes,
    inputs,
    prefix_keys,
    prefix_values,
    gain_attn,
    w_query,
    w_key,
    w_value,
    w_out,
    bias_table,
    gain_ffn,
    w_in,
    w_back,
    buckets,
    out_grad,
):
    nb, nc, nw = sizes
    b, c, w = lax.axis_index("batch"), lax.axis_index("ctx"), lax.axis_index("wt")
    x, g = inputs[0], out_grad[0]
    rows, width = x.shape
    all_heads = bias_table.shape[1]
    heads = all_heads // nc
    hsize = width // all_heads
    cols = heads * hsize
    mem = prefix_keys.shape[1]
    length = rows * nc
    part = width // nw
    ff_own = w_back.shape[0]
    ff_part = ff_own // nb
    nbuck = bias_table.shape[0] * nw
    index_c = jnp.reshape(c, (1,))

    xs = gather_flip(x, "ctx", nc)
    wq = gather_wt(w_query, nw).reshape(width, width)
    wk = gather_wt(w_key, nw).reshape(width, width)
    wv = gather_wt(w_value, nw).reshape(width, width)
    small = gather_wt(
        jnp.concatenate([gain_attn, gain_ffn, bias_table.reshape(-1)]).reshape(1, -1), nw
    ).reshape(nw, -1)
    gain_one = small[:, :part].reshape(1, width).astype(F32)
    gain_two = small[:, part : 2 * part].reshape(1, width).astype(F32)
    table = small[:, 2 * part :].reshape(nbuck, all_heads)
    wo = gather_wt(w_out, nw).reshape(width, width)
    in_cut = jnp.concatenate(
        [
            lax.dynamic_slice_in_dim(w_in, o * ff_own + b * ff_part, ff_part, 1)
            for o in range(nw)
        ],
        axis=1,
    )
    w_first = gather_wt(in_cut, nw).reshape(width, nw * ff_part)
    back_cut = lax.dynamic_slice_in_dim(w_back, b * ff_part, ff_part, 0)
    w_second = gather_wt(back_cut, nw).reshape(nw * ff_part, width)
    gs = gather_flip(g, "batch", nb)

    def head_cols(value):
        return lax.dynamic_slice_in_dim(value, c * cols, cols, 1)

    pk, pv = head_cols(prefix_keys[0]), head_cols(prefix_values[0])
    tab = jnp.pad(
        lax.dynamic_slice_in_dim(table, c * heads, heads, 1).T.astype(F32), ((0, 8 - heads), (0, 0))
    )
    bucket_row = jnp.pad(buckets[::-1].reshape(1, -1), ((0, 0), (1, 0)), constant_values=-1)

    (normed1, q, k, v, pt, pm, mix, *mixed) = attend(
        nc, heads, hsize, index_c, xs, head_cols(wq), head_cols(wk), head_cols(wv),
        gain_one, pk, pv, tab, bucket_row,
    )
    mixed = mixed[:1] + [flip(mixed[s], "ctx", nc, s) for s in range(1, nc)]
    hidden, normed2, attended = branch(nc, index_c, mixed, x, wo, gain_two)

    n2 = jnp.concatenate(gather_flip(normed2, "batch", nb), axis=0)
    g_all = jnp.concatenate(gs, axis=0)
    inner = nn(n2, w_first)
    act_value, act_pull = jax.vjp(functools.partial(jax.nn.gelu, approximate=True), inner)
    act = act_value.astype(BF)
    grad_act = nt(g_all, w_second)
    grad_inner = act_pull(grad_act)[0].astype(BF)
    part_norm = nt(grad_inner, w_first).astype(BF)
    part_out = nn(act, w_second).astype(BF)
    grad_second = tn(act, g_all).astype(BF)
    grad_first = tn(n2, grad_inner).astype(BF)

    def cut(value, s):
        return value[s * rows : (s + 1) * rows]

    norm_parts = [cut(part_norm, 0)] + [
        flip(cut(part_norm, s), "batch", nb, s) for s in range(1, nb)
    ]
    (grad_hidden, grad_low, *gms) = branch_back(
        nb, nc, index_c, norm_parts, hidden, gain_two, g, wo
    )
    gms = gms[:1] + [flip(gms[s], "ctx", nc, s) for s in range(1, nc)]
    (grad_heads, grad_table, *sends) = attend_back(
        nc, heads, hsize, index_c, gms, pt, pm, q, k, v, mix, pk, pv, bucket_row, nbuck
    )
    sends = sends[:1] + [flip(sends[s], "ctx", nc, s) for s in range(1, nc)]
    grad_x, grad_memk, grad_memv = input_back(
        nc, mem, index_c, sends, x, wq, wk, wv, gain_one, grad_hidden
    )

    result = hidden + cut(part_out, 0).astype(F32)
    for s in range(1, nb):
        result = result + flip(cut(part_out, s), "batch", nb, s).astype(F32)

    def ctx_total(value):
        own = sum_wt(value, nw)
        size = own.shape[0] // nc
        own = sum_flip(own.astype(BF).reshape(nc, size, own.shape[1]), c, "ctx", nc)
        whole = canonical(gather_flip(own.astype(BF), "ctx", nc), c)
        return whole.reshape(nc * size, -1)

    second = gather_flip(ctx_total(grad_second), "batch", nb)
    out_second = canonical([p.astype(F32) for p in second], b).reshape(ff_own, width)
    first = gather_flip(ctx_total(grad_first), "batch", nb)
    out_first = jnp.zeros((part, nw * ff_own), F32)
    for s, piece in enumerate(first):
        for o in range(nw):
            out_first = lax.dynamic_update_slice(
                out_first,
                piece[:, o * ff_part : (o + 1) * ff_part].astype(F32),
                (0, o * ff_own + (b ^ s) * ff_part),
            )

    grad_wo = jnp.einsum("cqd,qe->cde", attended, grad_low, preferred_element_type=F32)
    own_wo = sum_wt(grad_wo.astype(BF).reshape(width, width), nw).astype(BF)
    own_wo = sum_flip(own_wo.reshape(nc, part // nc, width), c, "ctx", nc).astype(BF)
    own_wo = sum_flip(own_wo.reshape(nb, part // nc // nb, width), b, "batch", nb).astype(BF)
    own_wo = canonical(gather_flip(own_wo, "batch", nb), b).reshape(part // nc, width)
    out_wo = canonical(gather_flip(own_wo, "ctx", nc), c).reshape(part, width).astype(F32)

    grad_qkv = sum_wt(tn(normed1, grad_heads).astype(BF), nw).astype(BF)
    line = jnp.pad(grad_table[:, :heads].reshape(1, -1), ((0, 15), (0, 3 * cols - heads * nbuck)))
    if nw == 2:
        line = line.astype(BF)
        line = line.astype(F32) + flip(line, "wt", 2, 1).astype(F32)
    else:
        line = lax.psum(line, "wt")
    size = part // nb
    blocks = jnp.concatenate(
        [
            grad_qkv.reshape(nb, size, 3 * cols),
            jnp.broadcast_to(line.astype(BF)[None], (nb, 16, 3 * cols)),
        ],
        axis=1,
    )
    block = sum_flip(blocks, b, "batch", nb).astype(BF)
    pieces = canonical(gather_flip(block, "ctx", nc), c)
    table_sum = pieces[:, size, : heads * nbuck].astype(F32).reshape(nc, nbuck, heads)
    table_sum = jnp.transpose(table_sum, (1, 0, 2)).reshape(nbuck, all_heads)
    own_buckets = nbuck // nw
    out_table = lax.dynamic_slice_in_dim(table_sum, w * own_buckets, own_buckets, 0)
    wide = canonical(gather_flip(pieces[:, :size], "batch", nb), b)
    wide = wide.reshape(nb, nc, size, 3, cols)
    wide = jnp.transpose(wide, (3, 0, 2, 1, 4)).reshape(3, part, width).astype(F32)
    out_q, out_k, out_v = wide[0], wide[1], wide[2]

    def gain_sum(pairs, gain):
        total = sum(jnp.sum(left * right.astype(F32), axis=1) for left, right in pairs)
        return total / gain.astype(F32)

    gain_two_grad = gain_sum([(out_first, w_in)], gain_ffn)
    gain_one_grad = gain_sum([(out_q, w_query), (out_k, w_key), (out_v, w_value)], gain_attn)
    return (
        result.astype(BF)[None],
        grad_x[None],
        grad_memk[None],
        grad_memv[None],
        gain_one_grad,
        gain_two_grad,
        out_table,
        out_q,
        out_k,
        out_v,
        out_wo,
        out_first,
        out_second,
    )


NEAR_LAST = (0, 2, 1, 3)
LINE = 8


def call(kernel, name, index, args, out, scratch=(), mib=24, far=()):
    stay = [pl.BlockSpec(memory_space=pltpu.HBM)] * len(far)
    return pl.pallas_call(
        kernel,
        out_shape=out,
        in_specs=[smem()] + stay + vmem(len(args)),
        out_specs=vmem(len(out)),
        scratch_shapes=list(scratch),
        compiler_params=params(mib),
        name=name,
    )(index, *far, *args)


def after(values, earlier):
    return lax.optimization_barrier((tuple(values), tuple(earlier)))[0]


def both_gains(wt, own, other, row):
    mine, theirs = own[row : row + 1, :].astype(F32), other[row : row + 1, :].astype(F32)
    first = jnp.where(wt == 0, mine, theirs)
    second = jnp.where(wt == 0, theirs, mine)
    return jnp.concatenate([first, second], axis=1)


def fetch_rows(sems, wt, pairs):
    copies = []
    for i, (scr, own, other) in enumerate(pairs):
        rows = own.shape[0]
        for j, (source, place) in enumerate(((own, wt), (other, 1 - wt))):
            to = scr.at[pl.ds(pl.multiple_of(place * rows, rows), rows), :]
            copies.append(pltpu.make_async_copy(source, to, sems.at[2 * i + j]))
            copies[-1].start()
    return copies


TABLE_ROW = 8


def heads_kernel(heads, hsize, own_buckets, idx, *refs):
    wq, wk, wv, wq2, wk2, wv2 = refs[:6]
    fars = refs[6:11]
    x = refs[11]
    n1_ref, q_ref, k_ref, v_ref, pt_ref, pm_ref, mix_ref, wrow_ref, pk_ref, pv_ref = refs[12:22]
    outs = refs[22:26]
    att_scr, line_scr, sems, more_sems, *scrs = refs[26:]
    w_scr, nears = scrs[:3], scrs[3:]
    small, small2, pk_all, pv_all, bucket_row = nears
    more = [
        pltpu.make_async_copy(source, to, more_sems.at[i])
        for i, (source, to) in enumerate(zip(fars, nears))
    ]
    for copy in more:
        copy.start()
    batch, here, wt = idx[0], idx[1], idx[2]
    length, width = x.shape
    rows = length // 4
    half = wq.shape[0]
    cols = heads * hsize
    window = w_scr[0].shape[1]
    shift = window - cols
    odd = here % 2
    lanes = pl.ds(pl.multiple_of((here * cols - odd * shift), LANES), window)
    copies = fetch_rows(
        sems,
        wt,
        [
            (scr, own.at[:, lanes], other.at[:, lanes])
            for scr, own, other in zip(w_scr, (wq, wk, wv), (wq2, wk2, wv2))
        ],
    )
    for copy in more:
        copy.wait()
    for j in range(4):

        @pl.when(here == j)
        def _():
            take = slice(j * cols, (j + 1) * cols)
            pk_ref[...] = pk_all[:, take]
            pv_ref[...] = pv_all[:, take]

    def own_cols(value):
        return jnp.where(odd == 0, value[:, :cols], value[:, shift:])

    gain = both_gains(wt, small, small2, 0)
    scaled, _ = norm(x[...].astype(F32))
    n1_ref[...] = (scaled * gain).astype(BF)
    normed = n1_ref[...]
    for copy in copies:
        copy.wait()
    quarter = half // 4
    at = pl.multiple_of(wt * half + batch * quarter, quarter)
    for p, (scr, out) in enumerate(zip(w_scr, (q_ref, k_ref, v_ref))):
        out[...] = own_cols(nn(normed, scr[...])).astype(BF)
        wrow_ref[:, p * cols : (p + 1) * cols] = own_cols(
            scr[pl.ds(at, quarter), :].astype(F32)
        ).astype(BF)
    vals_t = v_ref[...].T
    pv_t = pv_ref[...].astype(F32).T.astype(BF)
    tab, tab2 = (
        ref[TABLE_ROW : TABLE_ROW + own_buckets, :LANES].astype(F32) for ref in (small, small2)
    )
    ids = lax.broadcasted_iota(jnp.int32, (own_buckets, 2 * length), 0)
    lines = tn(tab, (ids + wt * own_buckets == bucket_row[...]).astype(F32))
    lines = lines + tn(
        tab2, (ids + (1 - wt) * own_buckets == bucket_row[...]).astype(F32)
    )
    line_scr[...] = lines[: line_scr.shape[0]]
    for h in range(heads):
        part = slice(h * hsize, (h + 1) * hsize)
        query = q_ref[:, part]
        line = jnp.broadcast_to(line_scr[pl.ds(here * heads + h, 1), :], (LANES, 2 * length))
        spread = pltpu.roll(line, 0, 1, stride=1, stride_axis=0)
        bias = jnp.concatenate(
            [spread[:, length - at : 2 * length - at] for at in range(0, length, LANES)], axis=0
        )
        score = nt(k_ref[:, part], query) + bias
        front = nt(pk_ref[:, part], query)
        top = jnp.maximum(
            jnp.max(score, axis=0, keepdims=True), jnp.max(front, axis=0, keepdims=True)
        )
        score = jnp.exp(score - top)
        front = jnp.exp(front - top)
        total = jnp.sum(score, axis=0, keepdims=True) + jnp.sum(front, axis=0, keepdims=True)
        scale = 1.0 / total
        prob = (score * scale).astype(BF)
        prob_mem = (front * scale).astype(BF)
        pt_ref[h] = prob
        pm_ref[h] = prob_mem
        mix_ref[part, :] = nn(vals_t[part, :], prob) + nn(pv_t[part, :], prob_mem)
    att_scr[...] = mix_ref[...].T.astype(BF)
    for step in range(4):
        at = pl.multiple_of((here ^ step) * rows, rows)
        outs[step][...] = att_scr[pl.ds(at, rows), :]


def hidden_kernel(idx, *refs):
    wo, wo2 = refs[:2]
    parts = refs[2:6]
    x, small, small2 = refs[6:9]
    hidden_ref, n2_ref, att_ref, wo_ref, sems = refs[9:]
    here, wt = idx[1], idx[2]
    cols = parts[0].shape[1]
    half = wo.shape[0]
    copies = fetch_rows(sems, wt, [(wo_ref, wo, wo2)])
    for step in range(4):
        att_ref[here ^ step] = parts[step][...]
    for copy in copies:
        copy.wait()
    hidden = x[...].astype(F32)
    for c in range(4):
        hidden = hidden + nn(att_ref[c], wo_ref[c * cols : (c + 1) * cols, :])
    hidden_ref[...] = hidden
    scaled, _ = norm(hidden)
    n2_ref[...] = (scaled * both_gains(wt, small, small2, 1)).astype(BF)


def gelu_parts(v):
    scale = 0.7978845608028654
    square = v * v
    t = jnp.tanh(scale * v * (1.0 + 0.044715 * square))
    grad = 0.5 * (1.0 + t) + 0.5 * v * (1.0 - t * t) * scale * (1.0 + 0.134145 * square)
    return 0.5 * v * (1.0 + t), grad


def own_columns(batch, ff_own, block):
    return [pl.ds(pl.multiple_of(o * ff_own + batch * block, block), block) for o in range(2)]


def ffn_kernel(idx, *refs):
    w1, w1b, w2, w2b = refs[:4]
    n2s, gs = refs[4:8], refs[8:12]
    norms = refs[12:16]
    act_ref, gi_ref, w2_ref, w1_scr, sems = refs[16:]
    batch, wt = idx[0], idx[2]
    half = w1.shape[0]
    block = w1_scr.shape[1] // 2
    ff_own = w2.shape[0]
    copies = []
    for j, (source, place) in enumerate(((w1, wt), (w1b, 1 - wt))):
        to = pl.ds(pl.multiple_of(place * half, half), half)
        for o, cut in enumerate(own_columns(batch, ff_own, block)):
            copies.append(
                pltpu.make_async_copy(
                    source.at[:, cut],
                    w1_scr.at[to, o * block : (o + 1) * block],
                    sems.at[2 * j + o],
                )
            )
    cut = pl.ds(pl.multiple_of(batch * block, block), block)
    for j, (source, place) in enumerate(((w2, wt), (w2b, 1 - wt))):
        to = pl.ds(pl.multiple_of(place * block, block), block)
        copies.append(pltpu.make_async_copy(source.at[cut, :], w2_ref.at[to, :], sems.at[4 + j]))
    for copy in copies:
        copy.start()
    for copy in copies[:4]:
        copy.wait()
    rows = n2s[0].shape[0]
    for s in range(4):
        at = slice(s * rows, (s + 1) * rows)
        act, slope = gelu_parts(nn(n2s[s][...], w1_scr[...]))
        if s == 0:
            for copy in copies[4:]:
                copy.wait()
        act_ref[at, :] = act.astype(BF)
        grad = (nt(gs[s][...], w2_ref[...]).astype(BF).astype(F32) * slope).astype(BF)
        gi_ref[at, :] = grad
        norms[s][...] = nt(grad, w1_scr[...]).astype(BF)


def ffn_back_kernel(idx, *refs):
    n2s, gs = refs[:4], refs[4:8]
    act, gi = refs[8:10]
    mine, theirs, all_scr, scr = refs[10:]
    here, wt = idx[1], idx[2]
    rows = n2s[0].shape[0]
    size = scr.shape[0] // 8

    def spread(p):
        for i, out in enumerate((mine, theirs)):
            for j, place in enumerate(NEAR_LAST):
                at = pl.multiple_of(((wt ^ i) * 4 + (here ^ place)) * size, size)
                to = (4 * (j // 2) + 2 * p + j % 2) * size
                out[to : to + size, :] = scr[pl.ds(at, size), :]

    for s in range(4):
        all_scr[s * rows : (s + 1) * rows, :] = n2s[s][...]
    scr[...] = tn(all_scr[...], gi[...]).astype(BF)
    spread(0)
    for s in range(4):
        all_scr[s * rows : (s + 1) * rows, :] = gs[s][...]
    scr[...] = tn(act[...], all_scr[...]).astype(BF)
    spread(1)


def hidden_back_kernel(idx, *refs):
    parts = refs[:4]
    hidden_ref, small, small2, g, wo = refs[4:9]
    grad_ref, low_ref = refs[9:11]
    outs = refs[11:]
    here, wt = idx[1], idx[2]
    cols = outs[0].shape[1]
    half = wo.shape[0] // 2
    grad_norm = parts[0][...].astype(F32)
    for part in parts[1:]:
        grad_norm = grad_norm + part[...].astype(F32)
    scaled, inverse = norm(hidden_ref[...])
    e = grad_norm * both_gains(wt, small, small2, 1)
    grad = g[...].astype(F32) + inverse * (
        e - scaled * jnp.mean(e * scaled, axis=-1, keepdims=True)
    )
    grad_ref[...] = grad
    low = grad.astype(BF)
    low_ref[...] = low
    for step in range(4):
        at = pl.multiple_of((here ^ step) * cols, cols)
        outs[step][...] = nt(low, wo[pl.ds(at, cols), :]).astype(BF)


def wo_back_kernel(idx, att, low, act, w2, mine, theirs, keep, send, scr):
    rows = low.shape[0]
    batch, here, wt = idx[0], idx[1], idx[2]
    size = att.shape[2]
    for c in range(4):
        scr[c * size : (c + 1) * size, :] = tn(att[c], low[...])
    size = scr.shape[0] // 32
    for i, out in enumerate((mine, theirs)):
        for q, far in enumerate(NEAR_LAST):
            for p, place in enumerate(NEAR_LAST):
                at = (((wt ^ i) * 4 + (here ^ place)) * 4 + (batch ^ far)) * size
                to = (4 * q + p) * size
                out[to : to + size, :] = scr[pl.ds(pl.multiple_of(at, 8), size), :].astype(BF)
    for s, (out, to) in enumerate(((keep, 0), (keep, rows), (send, 0), (send, rows))):
        out[to : to + rows, :] = nn(act[s * rows : (s + 1) * rows, :], w2[...]).astype(BF)


def heads_back_kernel(heads, hsize, idx, *refs):
    gms = refs[:4]
    pt, pm, q, k, v, mix, pk, pv, bucket_row, n1 = refs[4:14]
    mine, theirs = refs[14:16]
    own_out, near_out, far_out = refs[16:19]
    gm_scr, gqt_scr, acc, grad_scr, w_scr = refs[19:]
    batch, here, wt = idx[0], idx[1], idx[2]
    rows, cols = gms[0].shape
    length = 4 * rows
    mem = pk.shape[0]
    high = own_out.shape[0]
    outs = (own_out, far_out, near_out.at[:high], near_out.at[high:])
    for step in range(4):
        at = pl.multiple_of((here ^ step) * rows, rows)
        gm_scr[pl.ds(at, rows), :] = gms[step][...]
    gm_t = gm_scr[...].T
    keys_t = k[...].T
    pk_t = pk[...].astype(F32).T.astype(BF)
    lines = []
    for h in range(heads):
        part = slice(h * hsize, (h + 1) * hsize)
        gm = gm_scr[:, part]
        query = q[:, part]
        spread = jnp.sum(gm_t[part, :].astype(F32) * mix[part, :], axis=0, keepdims=True)
        prob = pt[h]
        prob_mem = pm[h]
        score = prob.astype(F32) * (nt(v[:, part], gm) - spread)
        front = (prob_mem.astype(F32) * (nt(pv[:, part], gm) - spread)).astype(BF)
        low = score.astype(BF)
        gqt_scr[part, :] = nn(keys_t[part, :], low) + nn(pk_t[part, :], front)
        grad_scr[1, :, part] = nn(low, query).astype(BF)
        grad_scr[2, :, part] = nn(prob, gm).astype(BF)
        mem_k = nn(front, query).astype(BF)
        mem_v = nn(prob_mem, gm).astype(BF)
        for step in range(4):
            outs[step][3 * rows + MEM_K : 3 * rows + MEM_K + mem, part] = mem_k
            outs[step][3 * rows + MEM_V : 3 * rows + MEM_V + mem, part] = mem_v
        acc[...] = jnp.zeros_like(acc)
        for at in range(0, length, LANES):
            acc[:, length - at : 2 * length - at] += score[at : at + LANES, :]
        fold = acc[...]
        size = LANES // 2
        while size >= 8:
            fold = fold[:size] + pltpu.roll(fold[size:], 2 * length - size, 1)
            size //= 2
        line = fold[0:1]
        for i in range(1, 8):
            line = line + pltpu.roll(fold[i : i + 1], 2 * length - i, 1)
        lines.append(line)
    grad_scr[0] = gqt_scr[...].T.astype(BF)
    normed = n1[...]
    for p in range(3):
        w_scr[:, p * cols : (p + 1) * cols] = tn(normed, grad_scr[p]).astype(BF)
    size = w_scr.shape[0] // 8
    for i, out in enumerate((mine, theirs)):
        for j, far in enumerate(NEAR_LAST):
            at = pl.multiple_of(((wt ^ i) * 4 + (batch ^ far)) * size, size)
            out[j * size : (j + 1) * size, :] = w_scr[pl.ds(at, size), :]
    lines.append(jnp.zeros((LINE - heads, 2 * length), F32))
    table = lax.dot_general(
        jnp.concatenate(lines, axis=0),
        one_hot_rows(bucket_row[...], LANES),
        (((1,), (1,)), ((), ())),
        precision=lax.Precision.HIGHEST,
        preferred_element_type=F32,
    )
    wide = w_scr.shape[1]
    table = jnp.concatenate([table, jnp.zeros((LINE, wide - LANES), F32)], axis=1)
    for out in (mine, theirs):
        out[4 * size :, :] = table.astype(BF)
    for step in range(4):
        at = pl.multiple_of((here ^ step) * rows, rows)
        for p in range(3):
            outs[step][p * rows : (p + 1) * rows, :] = grad_scr[p, pl.ds(at, rows), :]


def halving_kernel(lines, *refs):
    count = len(lines)
    for i, line in enumerate(lines):
        own, got = refs[2 * i], refs[2 * i + 1]
        keep, send = refs[2 * count + 2 * i], refs[2 * count + 2 * i + 1]
        total = (own[...].astype(F32) + got[...].astype(F32)).astype(BF)
        half = (total.shape[0] - line) // 2
        keep[:half, :] = total[:half]
        send[:half, :] = total[half : 2 * half]
        if line:
            keep[half:, :] = total[2 * half :]
            send[half:, :] = total[2 * half :]


def halving(name, items):
    args, out = [], []
    for own, got, line in items:
        args += [own, got]
        out += [shape(((own.shape[0] - line) // 2 + line, own.shape[1]), BF)] * 2
    return pl.pallas_call(
        functools.partial(halving_kernel, [line for _, _, line in items]),
        out_shape=out,
        in_specs=vmem(len(args)),
        out_specs=vmem(len(out)),
        compiler_params=params(32),
        name=name,
    )(*args)


def add_kernel(left, right, out):
    out[...] = (left[...].astype(F32) + right[...].astype(F32)).astype(BF)


def row_sums(values):
    return lax.dot_general(
        jnp.ones((8, values.shape[1]), F32),
        values,
        (((1,), (1,)), ((), ())),
        precision=lax.Precision.HIGHEST,
        preferred_element_type=F32,
    )


def add_swapped(out, own, got, half):
    for i in range(2):
        left = own[i * half : (i + 1) * half, :].astype(F32)
        right = got[(1 - i) * half : (2 - i) * half, :].astype(F32)
        out[i * half : (i + 1) * half, :] = (left + right).astype(BF)


def ffn_piece_kernel(idx, w_in, own, got, a_ref, b_ref, sum_ref, w_scr, sems):
    batch, here = idx[0], idx[1]
    quarter, width = w_scr.shape
    block = width // 2
    rows = pl.ds(pl.multiple_of(here * quarter, quarter), quarter)
    copies = [
        pltpu.make_async_copy(
            w_in.at[rows, cut], w_scr.at[:, o * block : (o + 1) * block], sems.at[o]
        )
        for o, cut in enumerate(own_columns(batch, w_in.shape[1] // 2, block))
    ]
    for copy in copies:
        copy.start()
    add_swapped(a_ref, own.at[: 2 * quarter], got.at[: 2 * quarter], quarter)
    add_swapped(b_ref, own.at[2 * quarter :], got.at[2 * quarter :], quarter)
    for copy in copies:
        copy.wait()
    sum_ref[...] = row_sums(a_ref[:quarter, :].astype(F32) * w_scr[...].astype(F32))


def heads_pair_kernel(size, height, own, got, out):
    rest = own.shape[0] - height
    out[:height, :] = own[:height, :]
    out[height:, :] = got[:height, :]
    for at, left, right in ((size, size, height), (height + size, height, size)):
        out[at : at + rest, :] = (
            own[left : left + rest, :].astype(F32) + got[right : right + rest, :].astype(F32)
        ).astype(BF)


def heads_piece_kernel(qkv, qkv2, wo, wo2, wrow, sum_in, piece_ref):
    size, width = wo.shape
    quarter = wrow.shape[0]
    wide = wrow.shape[1]
    heads = qkv[...].astype(F32) + qkv2[...].astype(F32)
    piece_ref[:quarter, :] = heads[:quarter].astype(BF)
    sum_heads = row_sums(heads[:quarter] * wrow[...].astype(F32))
    third = size // 3
    cols = width - wide
    for part, at in ((wo, quarter), (wo2, quarter + size + third + LINE)):
        piece_ref[at : at + size, :] = part[:, :wide]
        for o in range(3):
            piece_ref[at + size : at + size + third, o * cols : (o + 1) * cols] = part[
                o * third : (o + 1) * third, wide:
            ]
    row = lax.broadcasted_iota(jnp.int32, (LINE, quarter), 0)
    sums = jnp.where(row == LINE - 2, sum_heads, jnp.where(row == LINE - 1, sum_in[...], 0.0))
    at = quarter + size + third
    line = heads[quarter:]
    pad = jnp.zeros((LINE, LANES), F32)
    sums = jnp.concatenate([sums, jnp.zeros((LINE, LANES - quarter), F32)], axis=1)
    line = line + jnp.concatenate([pad, sums, jnp.zeros((LINE, wide - 2 * LANES), F32)], axis=1)
    piece_ref[at : at + LINE, :] = line.astype(BF)


def ctx_pieces(refs, at, order):
    one, two, four, one2, two2, four2 = refs
    rows = one.shape[0]
    size = rows // 2
    first = ((one, 0), (two, 0), (four, 0), (four, rows))
    last = ((one2, 0), (four2, 0), (two2, 0), (four2, rows))
    if order == 2:
        first = ((one, 0), (four, 0), (two, 0), (four, rows))
        last = ((one2, 0), (two2, 0), (four2, 0), (four2, rows))
    near, far = first[at], last[at]
    found = []
    for (ref, start), places in ((near, (0, 2)), (far, (1, 3))):
        for i, place in enumerate(places):
            found.append((place, ref, start + i * size, size))
    return found


def rows_out_kernel(idx, *refs):
    out, scr, sems = refs[6:]
    copies = []
    for at in range(4):
        for place, ref, start, size in ctx_pieces(refs[:6], at, 2):
            row = len(copies) * size
            scr[row : row + size, :] = ref[start : start + size, :].astype(F32)
            to = pl.multiple_of(((idx[0] ^ at) * 4 + (idx[1] ^ place)) * size, size)
            copies.append(
                pltpu.make_async_copy(
                    scr.at[row : row + size, :], out.at[pl.ds(to, size), :], sems.at[len(copies)]
                )
            )
            copies[-1].start()
    for copy in copies:
        copy.wait()


def cols_out_kernel(idx, *refs):
    out, scr, sems = refs[6:]
    copies = []
    block = scr.shape[1] // 2
    for at in range(4):
        for place, ref, start, size in ctx_pieces(refs[:6], at, 1):
            row = (len(copies) // 2) * size
            scr[row : row + size, :] = ref[start : start + size, :].astype(F32)
            to = pl.multiple_of((idx[1] ^ place) * size, size)
            for o in range(2):
                col = pl.multiple_of((4 * o + (idx[0] ^ at)) * block, block)
                copies.append(
                    pltpu.make_async_copy(
                        scr.at[row : row + size, o * block : (o + 1) * block],
                        out.at[pl.ds(to, size), pl.ds(col, block)],
                        sems.at[len(copies)],
                    )
                )
                copies[-1].start()
    for copy in copies:
        copy.wait()


def pieces_out(kernel, name, index, pieces, dims, copies):
    rows, width = pieces[0].shape
    return pl.pallas_call(
        kernel,
        out_shape=shape(dims, F32),
        in_specs=[smem()] + vmem(6),
        out_specs=pl.BlockSpec(memory_space=pltpu.HBM),
        scratch_shapes=[
            pltpu.VMEM((8 * rows, width), F32),
            pltpu.SemaphoreType.DMA((copies,)),
        ],
        compiler_params=params(16),
        name=name,
    )(index, *pieces)


def heads_out_kernel(heads, buckets, idx, *refs):
    small = refs[6]
    oq, ok, ov, oo, gain_one, gain_two, table, scr, lines, tab_scr = refs[7:]
    step = pl.program_id(0)
    quarter, width = oq.shape
    cols = width // 4
    wide = 3 * cols
    size = quarter // 4
    third = size // 3
    for at in range(4):

        @pl.when(step == at)
        def _():
            for place, ref, start, height in ctx_pieces(refs[:6], at, 1):
                scr[idx[1] ^ place] = ref[start : start + height, :]

    for c in range(4):
        part = scr[c].astype(F32)
        for o, out in enumerate((oq, ok, ov)):
            out[:, c * cols : (c + 1) * cols] = part[:quarter, o * cols : (o + 1) * cols]
        oo[c, 0, :, :wide] = part[quarter : quarter + size]
        for o in range(3):
            oo[c, 0, o * third : (o + 1) * third, wide:] = part[
                quarter + size : quarter + size + third, o * cols : (o + 1) * cols
            ]
        lines[idx[0] ^ step, c] = part[quarter + size + third :]

    @pl.when(step == 3)
    def _():
        seen = [[lines[b, c] for c in range(4)] for b in range(4)]
        take = slice(LANES, LANES + quarter)
        one = jnp.concatenate(
            [sum(seen[b][c][LINE - 2 : LINE - 1, take] for c in range(4)) for b in range(4)], axis=1
        )
        two = jnp.concatenate(
            [sum(seen[b][c][LINE - 1 : LINE, take] for b in range(4)) for c in range(4)], axis=1
        )
        gain_one[...] = (one / small[0:1, :].astype(F32))[0]
        gain_two[...] = (two / small[1:2, :].astype(F32))[0]
        rest = [seen[0][c][:heads, :LANES] for c in range(4)]
        rest.append(jnp.zeros((LANES - 4 * heads, LANES), F32))
        tab_scr[...] = jnp.concatenate(rest, axis=0).T
        own_buckets = buckets // 2
        at = pl.multiple_of(idx[2] * own_buckets, 8)
        table[...] = tab_scr[pl.ds(at, own_buckets), : 4 * heads]


def heads_out(index, pieces, small, width, heads, buckets):
    height, wide = pieces[0].shape[0] // 2, pieces[0].shape[1]
    part = width // 2
    quarter = part // 4
    size = quarter // 4
    block = pl.BlockSpec((quarter, width), lambda step, idx: (idx[0] ^ step, 0))
    whole = [pl.BlockSpec(p.shape, lambda step, idx: (0, 0)) for p in (*pieces, small)]
    return pl.pallas_call(
        functools.partial(heads_out_kernel, heads, buckets),
        out_shape=[shape((part, width), F32)] * 3
        + [
            shape((4, 4, size, width), F32),
            shape((part,), F32),
            shape((part,), F32),
            shape((buckets // 2, 4 * heads), F32),
        ],
        grid_spec=pltpu.PrefetchScalarGridSpec(
            num_scalar_prefetch=1,
            grid=(4,),
            in_specs=whole,
            out_specs=[block] * 3
            + [
                pl.BlockSpec((4, 1, size, width), lambda step, idx: (0, idx[0] ^ step, 0, 0)),
                pl.BlockSpec((part,), lambda step, idx: (0,)),
                pl.BlockSpec((part,), lambda step, idx: (0,)),
                pl.BlockSpec((buckets // 2, 4 * heads), lambda step, idx: (0, 0)),
            ],
            scratch_shapes=[
                pltpu.VMEM((4, height, wide), BF),
                pltpu.VMEM((4, 4, LINE, wide), F32),
                pltpu.VMEM((LANES, LANES), F32),
            ],
        ),
        compiler_params=params(32),
        name="heads_out",
    )(index, *pieces, small)


def paired(
    inputs,
    prefix_keys,
    prefix_values,
    gain_attn,
    w_query,
    w_key,
    w_value,
    w_out,
    bias_table,
    gain_ffn,
    w_in,
    w_back,
    buckets,
    out_grad,
):
    b, c, w = lax.axis_index("batch"), lax.axis_index("ctx"), lax.axis_index("wt")
    index = jnp.stack([b, c, w])
    x, g = inputs[0], out_grad[0]
    rows, width = x.shape
    all_heads = bias_table.shape[1]
    heads = all_heads // 4
    hsize = width // all_heads
    cols = heads * hsize
    wide = 3 * cols
    mem = prefix_keys.shape[1]
    length = 4 * rows
    part = width // 2
    quarter = part // 4
    ff_own = w_back.shape[0]
    ff_part = ff_own // 4
    nbuck = 2 * bias_table.shape[0]

    def over_wt(value, name):
        with jax.named_scope(name + "_w"):
            return flip(value, "wt", 2, 1)

    def over_ctx(value, step, name):
        with jax.named_scope(name + "_z" + str(step)):
            return flip(value, "ctx", 4, step)

    def over_batch(value, step, name):
        with jax.named_scope(name + "_b" + str(step)):
            return flip(value, "batch", 4, step)

    own_buckets = nbuck // 2
    small = jnp.concatenate(
        [
            jnp.pad(jnp.stack([gain_attn, gain_ffn]), ((0, TABLE_ROW - 2), (0, 0))),
            jnp.pad(bias_table, ((0, 0), (0, part - all_heads))),
        ]
    )
    w_query2, w_key2, w_value2 = [over_wt(v, "weight") for v in (w_query, w_key, w_value)]
    small2 = over_wt(small, "small")
    g_near = over_batch(g, 1, "g")
    x_all = lax.all_gather(x, "ctx", axis=0, tiled=True)
    bucket_row = jnp.pad(buckets[::-1].reshape(1, -1), ((0, 0), (1, 0)), constant_values=-1)

    tokens = shape((length, cols), BF)
    few = (small, small2, prefix_keys[0], prefix_values[0], bucket_row)
    (n1, q, k, v, pt, pm, mix, wrow, pk, pv, *mixed) = call(
        functools.partial(heads_kernel, heads, hsize, own_buckets),
        "attend",
        index,
        [x_all],
        [shape((length, width), BF)]
        + [tokens] * 3
        + [
            shape((heads, length, length), BF),
            shape((heads, mem, length), BF),
            shape((cols, length), F32),
            shape((quarter, wide), BF),
            shape((mem, cols), BF),
            shape((mem, cols), BF),
        ]
        + [shape((rows, cols), BF)] * 4,
        [
            pltpu.VMEM((length, cols), BF),
            pltpu.VMEM((16, 2 * length), F32),
            pltpu.SemaphoreType.DMA((6,)),
            pltpu.SemaphoreType.DMA((len(few),)),
        ]
        + [pltpu.VMEM((width, -(-cols // LANES) * LANES), BF)] * 3
        + [pltpu.VMEM(v.shape, v.dtype) for v in few],
        far=(w_query, w_key, w_value, w_query2, w_key2, w_value2, *few),
    )
    (g_pair, w_out_sent) = after((jnp.concatenate([g, g_near]), w_out), mixed[:1])
    w_out2 = over_wt(w_out_sent, "weight")
    g_far = over_batch(g_pair, 2, "g")
    mixed = mixed[:1] + [over_ctx(mixed[s], s, "mixed") for s in range(1, 4)]
    (*mixed, w_out2, g_far) = after((*mixed, w_out2, g_far), ())
    square = shape((width, width), BF)
    hidden, n2, attended, wo = call(
        hidden_kernel,
        "hidden",
        index,
        [*mixed, x, small, small2],
        [shape((rows, width), F32), shape((rows, width), BF), shape((4, rows, cols), BF), square],
        [pltpu.SemaphoreType.DMA((2,))],
        far=(w_out, w_out2),
    )

    n2s = [n2] + [over_batch(n2, s, "n2") for s in range(1, 4)]
    (w_in_sent, w_back_sent) = after((w_in, w_back), (n2,))
    w_in2, w_back2 = over_wt(w_in_sent, "in"), over_wt(w_back_sent, "back")
    gs = (g, g_near, g_far[:rows], g_far[rows:])
    hid = shape((length, 2 * ff_part), BF)
    *norms, act, gi, w_second = call(
        ffn_kernel,
        "ffn",
        index,
        [*n2s, *gs],
        [shape((rows, width), BF)] * 4 + [hid, hid, shape((2 * ff_part, width), BF)],
        [pltpu.VMEM((width, 2 * ff_part), BF), pltpu.SemaphoreType.DMA((6,))],
        far=(w_in, w_in2, w_back, w_back2),
    )
    norms = norms[:1] + [over_batch(norms[s], s, "norm") for s in range(1, 4)]
    ffn, ffn_sent = call(
        ffn_back_kernel,
        "ffn_back",
        index,
        [*n2s, *gs, act, gi],
        [square, square],
        [pltpu.VMEM((length, width), BF), pltpu.VMEM((width, width), BF)],
    )
    ffn, ffn_sent = halving("ffn_wt", [(ffn, over_wt(ffn_sent, "ffn"), 0)])
    ffn_got = over_ctx(ffn_sent, 1, "ffn")
    norms = after(norms, (ffn, ffn_sent))
    grad_hidden, low, *gms = call(
        hidden_back_kernel,
        "hidden_back",
        index,
        [*norms, hidden, small, small2, g, wo],
        [shape((rows, width), F32), shape((rows, width), BF)] + [shape((rows, cols), BF)] * 4,
    )
    ffn = pl.pallas_call(
        add_kernel,
        out_shape=shape((part, width), BF),
        in_specs=vmem(2),
        out_specs=vmem(1)[0],
        compiler_params=params(16),
        name="ffn_near",
    )(ffn, ffn_got)
    gms = list(gms[:1]) + [over_ctx(gms[s], s, "gm") for s in range(1, 4)]
    (ffn_sent,) = after((ffn,), gms[1:])
    ffn_got = over_ctx(ffn_sent, 2, "ffn")
    high = 3 * rows + MEM_END
    (qkv, qkv_sent, own_block, near_blocks, far_block) = call(
        functools.partial(heads_back_kernel, heads, hsize),
        "attend_back",
        index,
        [*gms, pt, pm, q, k, v, mix, pk, pv, bucket_row, n1],
        [shape((part + LINE, wide), BF)] * 2
        + [shape((n * high, cols), BF) for n in (1, 2, 1)],
        [
            pltpu.VMEM((length, cols), BF),
            pltpu.VMEM((cols, length), F32),
            pltpu.VMEM((LANES, 2 * length), F32),
            pltpu.VMEM((3, length, cols), BF),
            pltpu.VMEM((width, wide), BF),
        ],
    )
    (low,) = after((low,), (qkv,))
    wo_sum, wo_sent, outs, outs_sent = call(
        wo_back_kernel,
        "wo_back",
        index,
        [attended, low, act, w_second],
        [shape((part, width), BF)] * 2 + [shape((2 * rows, width), BF)] * 2,
        [pltpu.VMEM((width, width), F32)],
    )
    outs_got = over_batch(outs_sent, 2, "outs")
    wo_sum, wo_sent = halving("wo_wt", [(wo_sum, over_wt(wo_sent, "wo"), 0)])
    wo_sum, wo_sent = halving("wo_near", [(wo_sum, over_batch(wo_sent, 1, "wo"), 0)])

    outs, outs_sent = halving("outs_far", [(outs, outs_got, 0)])
    (outs_sent, wo_sent) = after((outs_sent, wo_sent), (outs, wo_sum))
    wo_sum, wo_sent = halving("wo_far", [(wo_sum, over_batch(wo_sent, 2, "wo"), 0)])
    outs_got = over_batch(outs_sent, 1, "outs")
    qkv, qkv_sent = halving("qkv_wt", [(qkv, over_wt(qkv_sent, "qkv"), LINE)])
    qkv, qkv_sent = halving("qkv_near", [(qkv, over_batch(qkv_sent, 1, "qkv"), LINE)])
    qkv_got = over_batch(qkv_sent, 2, "qkv")
    (ffn_got,) = after((ffn_got,), (qkv_got, outs_got, wo_sum, wo_sent))
    a1, b1, sum_in = call(
        ffn_piece_kernel,
        "ffn_piece",
        index,
        [ffn, ffn_got],
        [shape((2 * quarter, width), BF)] * 2 + [shape((8, quarter), F32)],
        [pltpu.VMEM((quarter, width), BF), pltpu.SemaphoreType.DMA((2,))],
        far=(w_in,),
    )

    (wo_sent,) = after((wo_sent,), (a1,))
    wo_sum, wo_sent = halving("wo_last", [(wo_sum, over_ctx(wo_sent, 1, "wo"), 0)])
    def pile(one, two):
        return jnp.concatenate([one, two])

    result = (hidden + outs.astype(F32) + outs_got.astype(F32)).astype(BF)
    a2, b2 = over_batch(a1, 1, "in_near"), over_batch(b1, 2, "out_near")
    c1, d1 = over_ctx(a1, 1, "in_back"), over_ctx(b1, 1, "out_back")
    pile_a, pile_b = pile(a1, a2), pile(b1, b2)
    a3, b3 = over_batch(pile_a, 2, "in_near2"), over_batch(pile_b, 1, "out_near2")
    (c1, d1) = after((c1, d1), (pile_a, pile_b))
    c2, d2 = over_batch(c1, 2, "in_far"), over_batch(d1, 1, "out_far")
    height = quarter + quarter // 4 + quarter // 12 + LINE
    piece = pl.pallas_call(
        heads_piece_kernel,
        out_shape=shape((2 * height - quarter - LINE, wide), BF),
        in_specs=vmem(6),
        out_specs=vmem(1)[0],
        compiler_params=params(32),
        name="heads_piece",
    )(qkv, qkv_got, wo_sum, wo_sent, wrow, sum_in)

    (piece,) = after((piece,), (c1, d1))
    heads_far = over_ctx(piece, 2, "heads_back")
    pile_c, pile_d = pile(c1, c2), pile(d1, d2)
    c3, d3 = over_batch(pile_c, 1, "in_far2"), over_batch(pile_d, 2, "out_far2")
    (heads_far,) = after((heads_far,), (a3, b3))
    (near_blocks,) = after((near_blocks,), (heads_far,))
    near_got = over_ctx(near_blocks, 2, "sends")
    far_pile = pile(far_block, near_got[high:])
    far_got = over_ctx(far_pile, 1, "sends")
    e1 = pl.pallas_call(
        functools.partial(heads_pair_kernel, quarter, height),
        out_shape=shape((2 * height, wide), BF),
        in_specs=vmem(2),
        out_specs=vmem(1)[0],
        compiler_params=params(16),
        name="heads_pair",
    )(piece, heads_far)
    f1 = over_ctx(e1, 1, "heads_back")
    (e1, f1) = after((e1, f1), (pile_c, pile_d))
    e2, f2 = over_batch(e1, 1, "heads_near"), over_batch(f1, 2, "heads_far")
    (e1, e2, f1, f2) = after((e1, e2, f1, f2), (c3, d3, far_pile))
    e3 = over_batch(pile(e1, e2), 2, "heads_near2")
    f3 = over_batch(pile(f1, f2), 1, "heads_far2")
    out_second = pieces_out(
        rows_out_kernel, "rows_out", index, (b1, b2, b3, d1, d2, d3), (ff_own, width), 16
    )
    out_first = pieces_out(
        cols_out_kernel, "cols_out", index, (a1, a2, a3, c1, c2, c3), (part, 2 * ff_own), 32
    )
    out_q, out_k, out_v, out_wo, gain_one, gain_two, out_table = heads_out(
        index, (e1, e2, e3, f1, f2, f3), small, width, heads, nbuck
    )
    grad_x, grad_memk, grad_memv = call(
        input_end_kernel,
        "input_back",
        index,
        [own_block, near_got, far_got, x, small, small2, grad_hidden],
        [shape((rows, width), BF), shape((mem, width), F32), shape((mem, width), F32)],
        [pltpu.VMEM((4,) + own_block.shape, BF), pltpu.SemaphoreType.DMA((6,))]
        + [pltpu.VMEM((width, width), BF)] * 3,
        far=(w_query, w_key, w_value, w_query2, w_key2, w_value2),
    )
    return (
        result[None],
        grad_x[None],
        grad_memk[None],
        grad_memv[None],
        gain_one,
        gain_two,
        out_table,
        out_q,
        out_k,
        out_v,
        out_wo.reshape(part, width),
        out_first,
        out_second,
    )


def input_end_kernel(idx, *refs):
    wq, wk, wv, wq2, wk2, wv2 = refs[:6]
    own, near, far, x, small, small2, grad_hidden = refs[6:13]
    out_ref, memk_ref, memv_ref, scr, sems, *w_scr = refs[13:]
    high = own.shape[0]
    parts = (own, far.at[:high], near.at[:high], far.at[high:])
    here, wt = idx[1], idx[2]
    rows = x.shape[0]
    mem = memk_ref.shape[0]
    copies = fetch_rows(sems, wt, list(zip(w_scr, (wq, wk, wv), (wq2, wk2, wv2))))
    for step in range(4):
        scr[here ^ step] = parts[step][...]
    for copy in copies:
        copy.wait()

    def wide(at, count):
        return jnp.concatenate([scr[c, at : at + count, :] for c in range(4)], axis=1)

    grad_norm = sum(nt(wide(p * rows, rows), whole[...]) for p, whole in enumerate(w_scr))
    scaled, inverse = norm(x[...].astype(F32))
    e = grad_norm * both_gains(wt, small, small2, 0)
    grad = grad_hidden[...] + inverse * (
        e - scaled * jnp.mean(e * scaled, axis=-1, keepdims=True)
    )
    out_ref[...] = grad.astype(BF)
    memk_ref[...] = wide(3 * rows + MEM_K, mem).astype(F32)
    memv_ref[...] = wide(3 * rows + MEM_V, mem).astype(F32)


def solution(mesh):
    tokens = P(("batch", "wt"), "ctx", None)
    memory = P(("batch", "wt"), None, None)
    matrix = P("wt", None)
    vector = P("wt")
    sizes = (mesh.shape["batch"], mesh.shape["ctx"], mesh.shape["wt"])
    body = paired if sizes == (4, 4, 2) else functools.partial(general, sizes)
    return jax.shard_map(
        body,
        mesh=mesh,
        in_specs=(
            tokens, memory, memory, vector, matrix, matrix, matrix, matrix, matrix, vector,
            matrix, matrix, P(), tokens,
        ),
        out_specs=(
            tokens, tokens, memory, memory, vector, vector, matrix, matrix, matrix, matrix,
            matrix, matrix, matrix,
        ),
        check_vma=False,
    )
```

```python
import functools

import jax
import jax.numpy as jnp
from jax import lax
from jax.experimental import pallas as pl
from jax.experimental.pallas import tpu as pltpu
from jax.sharding import PartitionSpec as P

EPS = 1e-06
F32 = jnp.float32
BF = jnp.bfloat16
LANES = 128


def nn(left, right):
    return lax.dot_general(left, right, (((1,), (0,)), ((), ())), preferred_element_type=F32)


def nt(left, right):
    return lax.dot_general(left, right, (((1,), (1,)), ((), ())), preferred_element_type=F32)


def tn(left, right):
    return lax.dot_general(left, right, (((0,), (0,)), ((), ())), preferred_element_type=F32)


def vmem(count):
    return [pl.BlockSpec(memory_space=pltpu.VMEM)] * count


def smem():
    return pl.BlockSpec(memory_space=pltpu.SMEM)


def shape(dims, kind):
    return jax.ShapeDtypeStruct(dims, kind)


def params(mib):
    return pltpu.CompilerParams(vmem_limit_bytes=mib << 20)


def flip(value, axis, size, step):
    return lax.ppermute(value, axis, [(i, i ^ step) for i in range(size)])


def gather_flip(value, axis, size):
    return [value] + [flip(value, axis, size, step) for step in range(1, size)]


def canonical(parts, index):
    whole = jnp.zeros((len(parts),) + parts[0].shape, parts[0].dtype)
    for step, part in enumerate(parts):
        whole = lax.dynamic_update_index_in_dim(whole, part, index ^ step, 0)
    return whole


def gather_wt(value, size):
    if size == 2:
        own = lax.axis_index("wt") == 0
        other = flip(value, "wt", 2, 1)
        return jnp.stack([jnp.where(own, value, other), jnp.where(own, other, value)])
    return lax.all_gather(value, "wt", axis=0)


def sum_wt(value, size):
    rows = value.shape[0] // size
    if size == 2:
        index = lax.axis_index("wt")
        mine = lax.dynamic_slice_in_dim(value, index * rows, rows, 0)
        theirs = lax.dynamic_slice_in_dim(value, (1 - index) * rows, rows, 0)
        return mine.astype(F32) + flip(theirs, "wt", 2, 1).astype(F32)
    return lax.psum_scatter(value, "wt", scatter_dimension=0, tiled=True).astype(F32)


def sum_flip(blocks, index, axis, size):
    total = lax.dynamic_index_in_dim(blocks, index, 0, keepdims=False).astype(F32)
    for step in range(1, size):
        block = lax.dynamic_index_in_dim(blocks, index ^ step, 0, keepdims=False)
        total = total + flip(block, axis, size, step).astype(F32)
    return total


def norm(values):
    inverse = lax.rsqrt(jnp.mean(values * values, axis=-1, keepdims=True) + EPS)
    return values * inverse, inverse


def one_hot_rows(bucket_row, buckets):
    ids = lax.broadcasted_iota(jnp.int32, (buckets, bucket_row.shape[1]), 0)
    return (ids == bucket_row).astype(F32)


def attend_kernel(nc, heads, hsize, mem, idx, *refs):
    xs = refs[:nc]
    wq, wk, wv, gain, pk, pv, tab, bucket_row = refs[nc : nc + 8]
    n1_ref, q_ref, k_ref, v_ref, pt_ref, pm_ref, mix_ref = refs[nc + 8 : nc + 15]
    outs = refs[nc + 15 : nc + 15 + nc]
    att_scr = refs[nc + 15 + nc]
    here = idx[0]
    rows = xs[0].shape[0]
    length = nc * rows
    for step in range(nc):
        scaled, _ = norm(xs[step][...].astype(F32))
        at = pl.multiple_of((here ^ step) * rows, rows)
        n1_ref[pl.ds(at, rows), :] = (scaled * gain[...]).astype(BF)
    normed = n1_ref[...]
    q_ref[...] = nn(normed, wq[...]).astype(BF)
    k_ref[...] = nn(normed, wk[...]).astype(BF)
    v_ref[...] = nn(normed, wv[...]).astype(BF)
    vals_t = v_ref[...].T
    pv_t = pv[...].astype(F32).T.astype(BF)
    hot = one_hot_rows(bucket_row[...], tab.shape[1])
    lines = nn(tab[...], hot)
    for h in range(heads):
        part = slice(h * hsize, (h + 1) * hsize)
        query = q_ref[:, part]
        line = jnp.broadcast_to(lines[h : h + 1, :], (LANES, 2 * length))
        spread = pltpu.roll(line, 0, 1, stride=1, stride_axis=0)
        bias = jnp.concatenate(
            [spread[:, length - at : 2 * length - at] for at in range(0, length, LANES)], axis=0
        )
        score = nt(k_ref[:, part], query) + bias
        front = nt(pk[:, part], query)
        top = jnp.maximum(
            jnp.max(score, axis=0, keepdims=True), jnp.max(front, axis=0, keepdims=True)
        )
        score = jnp.exp(score - top)
        front = jnp.exp(front - top)
        total = jnp.sum(score, axis=0, keepdims=True) + jnp.sum(front, axis=0, keepdims=True)
        scale = 1.0 / total
        prob = (score * scale).astype(BF)
        prob_mem = (front * scale).astype(BF)
        pt_ref[h] = prob
        pm_ref[h] = prob_mem
        mix_ref[part, :] = nn(vals_t[part, :], prob) + nn(pv_t[part, :], prob_mem)
    att_scr[...] = mix_ref[...].T.astype(BF)
    for step in range(nc):
        at = pl.multiple_of((here ^ step) * rows, rows)
        outs[step][...] = att_scr[pl.ds(at, rows), :]


def attend(nc, heads, hsize, index, xs, wq, wk, wv, gain, pk, pv, tab, bucket_row):
    rows, width = xs[0].shape
    length = rows * nc
    cols = heads * hsize
    mem = pk.shape[0]
    out = [
        shape((length, width), BF),
        shape((length, cols), BF),
        shape((length, cols), BF),
        shape((length, cols), BF),
        shape((heads, length, length), BF),
        shape((heads, mem, length), BF),
        shape((cols, length), F32),
    ] + [shape((rows, cols), BF)] * nc
    return pl.pallas_call(
        functools.partial(attend_kernel, nc, heads, hsize, mem),
        out_shape=out,
        in_specs=[smem()] + vmem(nc + 8),
        out_specs=vmem(len(out)),
        scratch_shapes=[pltpu.VMEM((length, cols), BF)],
        compiler_params=params(24),
        name="attend",
    )(index, *xs, wq, wk, wv, gain, pk, pv, tab, bucket_row)


def branch_kernel(nc, idx, *refs):
    parts = refs[:nc]
    x, wo, gain = refs[nc : nc + 3]
    hidden_ref, n2_ref, att_ref = refs[nc + 3 : nc + 6]
    here = idx[0]
    cols = parts[0].shape[1]
    for step in range(nc):
        att_ref[here ^ step] = parts[step][...]
    hidden = x[...].astype(F32)
    for c in range(nc):
        hidden = hidden + nn(att_ref[c], wo[c * cols : (c + 1) * cols, :])
    hidden_ref[...] = hidden
    scaled, _ = norm(hidden)
    n2_ref[...] = (scaled * gain[...]).astype(BF)


def branch(nc, index, parts, x, wo, gain):
    rows, cols = parts[0].shape
    out = [shape(x.shape, F32), shape(x.shape, BF), shape((nc, rows, cols), BF)]
    return pl.pallas_call(
        functools.partial(branch_kernel, nc),
        out_shape=out,
        in_specs=[smem()] + vmem(nc + 3),
        out_specs=vmem(3),
        compiler_params=params(32),
        name="branch",
    )(index, *parts, x, wo, gain)


def branch_back_kernel(nb, nc, idx, *refs):
    parts = refs[:nb]
    hidden_ref, gain, g, wo = refs[nb : nb + 4]
    grad_ref, low_ref = refs[nb + 4 : nb + 6]
    outs = refs[nb + 6 : nb + 6 + nc]
    here = idx[0]
    cols = outs[0].shape[1]
    grad_norm = parts[0][...].astype(F32)
    for part in parts[1:]:
        grad_norm = grad_norm + part[...].astype(F32)
    scaled, inverse = norm(hidden_ref[...])
    e = grad_norm * gain[...]
    grad = g[...].astype(F32) + inverse * (
        e - scaled * jnp.mean(e * scaled, axis=-1, keepdims=True)
    )
    grad_ref[...] = grad
    low = grad.astype(BF)
    low_ref[...] = low
    for step in range(nc):
        at = pl.multiple_of((here ^ step) * cols, 8)
        outs[step][...] = nt(low, wo[pl.ds(at, cols), :]).astype(BF)


def branch_back(nb, nc, index, parts, hidden, gain, g, wo):
    rows, width = hidden.shape
    cols = width // nc
    out = [shape((rows, width), F32), shape((rows, width), BF)] + [shape((rows, cols), BF)] * nc
    return pl.pallas_call(
        functools.partial(branch_back_kernel, nb, nc),
        out_shape=out,
        in_specs=[smem()] + vmem(nb + 4),
        out_specs=vmem(len(out)),
        compiler_params=params(32),
        name="branch_back",
    )(index, *parts, hidden, gain, g, wo)


MEM_K, MEM_V, MEM_END = 0, 32, 64


def attend_back_kernel(nc, heads, hsize, idx, *refs):
    gms = refs[:nc]
    pt, pm, q, k, v, mix, pk, pv, bucket_row = refs[nc : nc + 9]
    grad_ref, table_ref = refs[nc + 9 : nc + 11]
    outs = refs[nc + 11 : nc + 11 + nc]
    gm_scr, gqt_scr, acc = refs[nc + 11 + nc :]
    here = idx[0]
    rows, cols = gms[0].shape
    length = rows * nc
    mem = pk.shape[0]
    for step in range(nc):
        at = pl.multiple_of((here ^ step) * rows, rows)
        gm_scr[pl.ds(at, rows), :] = gms[step][...]
    gm_t = gm_scr[...].T
    keys_t = k[...].T
    pk_t = pk[...].astype(F32).T.astype(BF)
    lines = []
    for h in range(heads):
        part = slice(h * hsize, (h + 1) * hsize)
        gm = gm_scr[:, part]
        query = q[:, part]
        spread = jnp.sum(gm_t[part, :].astype(F32) * mix[part, :], axis=0, keepdims=True)
        prob = pt[h]
        prob_mem = pm[h]
        score = prob.astype(F32) * (nt(v[:, part], gm) - spread)
        front = (prob_mem.astype(F32) * (nt(pv[:, part], gm) - spread)).astype(BF)
        low = score.astype(BF)
        gqt_scr[part, :] = nn(keys_t[part, :], low) + nn(pk_t[part, :], front)
        grad_ref[:, cols + h * hsize : cols + (h + 1) * hsize] = nn(low, query).astype(BF)
        grad_ref[:, 2 * cols + h * hsize : 2 * cols + (h + 1) * hsize] = nn(prob, gm).astype(BF)
        mem_k = nn(front, query).astype(BF)
        mem_v = nn(prob_mem, gm).astype(BF)
        for step in range(nc):
            outs[step][3 * rows + MEM_K : 3 * rows + MEM_K + mem, part] = mem_k
            outs[step][3 * rows + MEM_V : 3 * rows + MEM_V + mem, part] = mem_v
        acc[...] = jnp.zeros_like(acc)
        for at in range(0, length, LANES):
            acc[:, length - at : 2 * length - at] += score[at : at + LANES, :]
        fold = acc[...]
        half = LANES // 2
        while half >= 8:
            fold = fold[:half] + pltpu.roll(fold[half:], 2 * length - half, 1)
            half //= 2
        line = fold[0:1]
        for i in range(1, 8):
            line = line + pltpu.roll(fold[i : i + 1], 2 * length - i, 1)
        lines.append(line)
    lines.append(jnp.zeros((8 - heads, 2 * length), F32))
    hot = one_hot_rows(bucket_row[...], table_ref.shape[0])
    table_ref[...] = lax.dot_general(
        hot,
        jnp.concatenate(lines, axis=0),
        (((1,), (1,)), ((), ())),
        precision=lax.Precision.HIGHEST,
        preferred_element_type=F32,
    )
    grad_ref[:, :cols] = gqt_scr[...].T.astype(BF)
    for step in range(nc):
        at = pl.multiple_of((here ^ step) * rows, rows)
        for p in range(3):
            outs[step][p * rows : (p + 1) * rows, :] = grad_ref[
                pl.ds(at, rows), p * cols : (p + 1) * cols
            ]


def attend_back(nc, heads, hsize, index, gms, pt, pm, q, k, v, mix, pk, pv, bucket_row, nbuck):
    rows, cols = gms[0].shape
    length = rows * nc
    out = [shape((length, 3 * cols), BF), shape((nbuck, 8), F32)] + [
        shape((3 * rows + MEM_END, cols), BF)
    ] * nc
    return pl.pallas_call(
        functools.partial(attend_back_kernel, nc, heads, hsize),
        out_shape=out,
        in_specs=[smem()] + vmem(nc + 9),
        out_specs=vmem(len(out)),
        scratch_shapes=[
            pltpu.VMEM((length, cols), BF),
            pltpu.VMEM((cols, length), F32),
            pltpu.VMEM((LANES, 2 * length), F32),
        ],
        compiler_params=params(24),
        name="attend_back",
    )(index, *gms, pt, pm, q, k, v, mix, pk, pv, bucket_row)


def input_back_kernel(nc, mem, idx, *refs):
    parts = refs[:nc]
    x, wq, wk, wv, gain, grad_hidden = refs[nc : nc + 6]
    out_ref, memk_ref, memv_ref = refs[nc + 6 : nc + 9]
    scr = refs[nc + 9]
    here = idx[0]
    rows = x.shape[0]
    for step in range(nc):
        scr[here ^ step] = parts[step][...]

    def wide(at, count):
        return jnp.concatenate([scr[c, at : at + count, :] for c in range(nc)], axis=1)

    grad_norm = (
        nt(wide(0, rows), wq[...])
        + nt(wide(rows, rows), wk[...])
        + nt(wide(2 * rows, rows), wv[...])
    )
    scaled, inverse = norm(x[...].astype(F32))
    e = grad_norm * gain[...]
    grad = grad_hidden[...] + inverse * (
        e - scaled * jnp.mean(e * scaled, axis=-1, keepdims=True)
    )
    out_ref[...] = grad.astype(BF)
    memk_ref[...] = wide(3 * rows + MEM_K, mem).astype(F32)
    memv_ref[...] = wide(3 * rows + MEM_V, mem).astype(F32)


def input_back(nc, mem, index, parts, x, wq, wk, wv, gain, grad_hidden):
    rows, width = x.shape
    out = [shape((rows, width), BF), shape((mem, width), F32), shape((mem, width), F32)]
    return pl.pallas_call(
        functools.partial(input_back_kernel, nc, mem),
        out_shape=out,
        in_specs=[smem()] + vmem(nc + 6),
        out_specs=vmem(3),
        scratch_shapes=[pltpu.VMEM((nc,) + parts[0].shape, BF)],
        compiler_params=params(32),
        name="input_back",
    )(index, *parts, x, wq, wk, wv, gain, grad_hidden)


def general(
    sizes,
    inputs,
    prefix_keys,
    prefix_values,
    gain_attn,
    w_query,
    w_key,
    w_value,
    w_out,
    bias_table,
    gain_ffn,
    w_in,
    w_back,
    buckets,
    out_grad,
):
    nb, nc, nw = sizes
    b, c, w = lax.axis_index("batch"), lax.axis_index("ctx"), lax.axis_index("wt")
    x, g = inputs[0], out_grad[0]
    rows, width = x.shape
    all_heads = bias_table.shape[1]
    heads = all_heads // nc
    hsize = width // all_heads
    cols = heads * hsize
    mem = prefix_keys.shape[1]
    length = rows * nc
    part = width // nw
    ff_own = w_back.shape[0]
    ff_part = ff_own // nb
    nbuck = bias_table.shape[0] * nw
    index_c = jnp.reshape(c, (1,))

    xs = gather_flip(x, "ctx", nc)
    wq = gather_wt(w_query, nw).reshape(width, width)
    wk = gather_wt(w_key, nw).reshape(width, width)
    wv = gather_wt(w_value, nw).reshape(width, width)
    small = gather_wt(
        jnp.concatenate([gain_attn, gain_ffn, bias_table.reshape(-1)]).reshape(1, -1), nw
    ).reshape(nw, -1)
    gain_one = small[:, :part].reshape(1, width).astype(F32)
    gain_two = small[:, part : 2 * part].reshape(1, width).astype(F32)
    table = small[:, 2 * part :].reshape(nbuck, all_heads)
    wo = gather_wt(w_out, nw).reshape(width, width)
    in_cut = jnp.concatenate(
        [
            lax.dynamic_slice_in_dim(w_in, o * ff_own + b * ff_part, ff_part, 1)
            for o in range(nw)
        ],
        axis=1,
    )
    w_first = gather_wt(in_cut, nw).reshape(width, nw * ff_part)
    back_cut = lax.dynamic_slice_in_dim(w_back, b * ff_part, ff_part, 0)
    w_second = gather_wt(back_cut, nw).reshape(nw * ff_part, width)
    gs = gather_flip(g, "batch", nb)

    def head_cols(value):
        return lax.dynamic_slice_in_dim(value, c * cols, cols, 1)

    pk, pv = head_cols(prefix_keys[0]), head_cols(prefix_values[0])
    tab = jnp.pad(
        lax.dynamic_slice_in_dim(table, c * heads, heads, 1).T.astype(F32), ((0, 8 - heads), (0, 0))
    )
    bucket_row = jnp.pad(buckets[::-1].reshape(1, -1), ((0, 0), (1, 0)), constant_values=-1)

    (normed1, q, k, v, pt, pm, mix, *mixed) = attend(
        nc, heads, hsize, index_c, xs, head_cols(wq), head_cols(wk), head_cols(wv),
        gain_one, pk, pv, tab, bucket_row,
    )
    mixed = mixed[:1] + [flip(mixed[s], "ctx", nc, s) for s in range(1, nc)]
    hidden, normed2, attended = branch(nc, index_c, mixed, x, wo, gain_two)

    n2 = jnp.concatenate(gather_flip(normed2, "batch", nb), axis=0)
    g_all = jnp.concatenate(gs, axis=0)
    inner = nn(n2, w_first)
    act_value, act_pull = jax.vjp(functools.partial(jax.nn.gelu, approximate=True), inner)
    act = act_value.astype(BF)
    grad_act = nt(g_all, w_second)
    grad_inner = act_pull(grad_act)[0].astype(BF)
    part_norm = nt(grad_inner, w_first).astype(BF)
    part_out = nn(act, w_second).astype(BF)
    grad_second = tn(act, g_all).astype(BF)
    grad_first = tn(n2, grad_inner).astype(BF)

    def cut(value, s):
        return value[s * rows : (s + 1) * rows]

    norm_parts = [cut(part_norm, 0)] + [
        flip(cut(part_norm, s), "batch", nb, s) for s in range(1, nb)
    ]
    (grad_hidden, grad_low, *gms) = branch_back(
        nb, nc, index_c, norm_parts, hidden, gain_two, g, wo
    )
    gms = gms[:1] + [flip(gms[s], "ctx", nc, s) for s in range(1, nc)]
    (grad_heads, grad_table, *sends) = attend_back(
        nc, heads, hsize, index_c, gms, pt, pm, q, k, v, mix, pk, pv, bucket_row, nbuck
    )
    sends = sends[:1] + [flip(sends[s], "ctx", nc, s) for s in range(1, nc)]
    grad_x, grad_memk, grad_memv = input_back(
        nc, mem, index_c, sends, x, wq, wk, wv, gain_one, grad_hidden
    )

    result = hidden + cut(part_out, 0).astype(F32)
    for s in range(1, nb):
        result = result + flip(cut(part_out, s), "batch", nb, s).astype(F32)

    def ctx_total(value):
        own = sum_wt(value, nw)
        size = own.shape[0] // nc
        own = sum_flip(own.astype(BF).reshape(nc, size, own.shape[1]), c, "ctx", nc)
        whole = canonical(gather_flip(own.astype(BF), "ctx", nc), c)
        return whole.reshape(nc * size, -1)

    second = gather_flip(ctx_total(grad_second), "batch", nb)
    out_second = canonical([p.astype(F32) for p in second], b).reshape(ff_own, width)
    first = gather_flip(ctx_total(grad_first), "batch", nb)
    out_first = jnp.zeros((part, nw * ff_own), F32)
    for s, piece in enumerate(first):
        for o in range(nw):
            out_first = lax.dynamic_update_slice(
                out_first,
                piece[:, o * ff_part : (o + 1) * ff_part].astype(F32),
                (0, o * ff_own + (b ^ s) * ff_part),
            )

    grad_wo = jnp.einsum("cqd,qe->cde", attended, grad_low, preferred_element_type=F32)
    own_wo = sum_wt(grad_wo.astype(BF).reshape(width, width), nw).astype(BF)
    own_wo = sum_flip(own_wo.reshape(nc, part // nc, width), c, "ctx", nc).astype(BF)
    own_wo = sum_flip(own_wo.reshape(nb, part // nc // nb, width), b, "batch", nb).astype(BF)
    own_wo = canonical(gather_flip(own_wo, "batch", nb), b).reshape(part // nc, width)
    out_wo = canonical(gather_flip(own_wo, "ctx", nc), c).reshape(part, width).astype(F32)

    grad_qkv = sum_wt(tn(normed1, grad_heads).astype(BF), nw).astype(BF)
    line = jnp.pad(grad_table[:, :heads].reshape(1, -1), ((0, 15), (0, 3 * cols - heads * nbuck)))
    if nw == 2:
        line = line.astype(BF)
        line = line.astype(F32) + flip(line, "wt", 2, 1).astype(F32)
    else:
        line = lax.psum(line, "wt")
    size = part // nb
    blocks = jnp.concatenate(
        [
            grad_qkv.reshape(nb, size, 3 * cols),
            jnp.broadcast_to(line.astype(BF)[None], (nb, 16, 3 * cols)),
        ],
        axis=1,
    )
    block = sum_flip(blocks, b, "batch", nb).astype(BF)
    pieces = canonical(gather_flip(block, "ctx", nc), c)
    table_sum = pieces[:, size, : heads * nbuck].astype(F32).reshape(nc, nbuck, heads)
    table_sum = jnp.transpose(table_sum, (1, 0, 2)).reshape(nbuck, all_heads)
    own_buckets = nbuck // nw
    out_table = lax.dynamic_slice_in_dim(table_sum, w * own_buckets, own_buckets, 0)
    wide = canonical(gather_flip(pieces[:, :size], "batch", nb), b)
    wide = wide.reshape(nb, nc, size, 3, cols)
    wide = jnp.transpose(wide, (3, 0, 2, 1, 4)).reshape(3, part, width).astype(F32)
    out_q, out_k, out_v = wide[0], wide[1], wide[2]

    def gain_sum(pairs, gain):
        total = sum(jnp.sum(left * right.astype(F32), axis=1) for left, right in pairs)
        return total / gain.astype(F32)

    gain_two_grad = gain_sum([(out_first, w_in)], gain_ffn)
    gain_one_grad = gain_sum([(out_q, w_query), (out_k, w_key), (out_v, w_value)], gain_attn)
    return (
        result.astype(BF)[None],
        grad_x[None],
        grad_memk[None],
        grad_memv[None],
        gain_one_grad,
        gain_two_grad,
        out_table,
        out_q,
        out_k,
        out_v,
        out_wo,
        out_first,
        out_second,
    )


NEAR_LAST = (0, 2, 1, 3)
LINE = 8


def call(kernel, name, index, args, out, scratch=(), mib=24, far=()):
    stay = [pl.BlockSpec(memory_space=pltpu.HBM)] * len(far)
    return pl.pallas_call(
        kernel,
        out_shape=out,
        in_specs=[smem()] + stay + vmem(len(args)),
        out_specs=vmem(len(out)),
        scratch_shapes=list(scratch),
        compiler_params=params(mib),
        name=name,
    )(index, *far, *args)


def after(values, earlier):
    return lax.optimization_barrier((tuple(values), tuple(earlier)))[0]


def both_gains(wt, own, other, row):
    mine, theirs = own[row : row + 1, :].astype(F32), other[row : row + 1, :].astype(F32)
    first = jnp.where(wt == 0, mine, theirs)
    second = jnp.where(wt == 0, theirs, mine)
    return jnp.concatenate([first, second], axis=1)


def fetch_rows(sems, wt, pairs):
    copies = []
    for i, (scr, own, other) in enumerate(pairs):
        rows = own.shape[0]
        for j, (source, place) in enumerate(((own, wt), (other, 1 - wt))):
            to = scr.at[pl.ds(pl.multiple_of(place * rows, rows), rows), :]
            copies.append(pltpu.make_async_copy(source, to, sems.at[2 * i + j]))
            copies[-1].start()
    return copies


TABLE_ROW = 8


def heads_kernel(heads, hsize, own_buckets, idx, *refs):
    wq, wk, wv, wq2, wk2, wv2 = refs[:6]
    fars = refs[6:11]
    x = refs[11]
    n1_ref, q_ref, k_ref, v_ref, pt_ref, pm_ref, mix_ref, wrow_ref, pk_ref, pv_ref = refs[12:22]
    outs = refs[22:26]
    att_scr, line_scr, sems, more_sems, *scrs = refs[26:]
    w_scr, nears = scrs[:3], scrs[3:]
    small, small2, pk_all, pv_all, bucket_row = nears
    more = [
        pltpu.make_async_copy(source, to, more_sems.at[i])
        for i, (source, to) in enumerate(zip(fars, nears))
    ]
    for copy in more:
        copy.start()
    batch, here, wt = idx[0], idx[1], idx[2]
    length, width = x.shape
    rows = length // 4
    half = wq.shape[0]
    cols = heads * hsize
    window = w_scr[0].shape[1]
    shift = window - cols
    odd = here % 2
    lanes = pl.ds(pl.multiple_of((here * cols - odd * shift), LANES), window)
    copies = fetch_rows(
        sems,
        wt,
        [
            (scr, own.at[:, lanes], other.at[:, lanes])
            for scr, own, other in zip(w_scr, (wq, wk, wv), (wq2, wk2, wv2))
        ],
    )
    for copy in more:
        copy.wait()
    for j in range(4):

        @pl.when(here == j)
        def _():
            take = slice(j * cols, (j + 1) * cols)
            pk_ref[...] = pk_all[:, take]
            pv_ref[...] = pv_all[:, take]

    def own_cols(value):
        return jnp.where(odd == 0, value[:, :cols], value[:, shift:])

    gain = both_gains(wt, small, small2, 0)
    scaled, _ = norm(x[...].astype(F32))
    n1_ref[...] = (scaled * gain).astype(BF)
    normed = n1_ref[...]
    for copy in copies:
        copy.wait()
    quarter = half // 4
    at = pl.multiple_of(wt * half + batch * quarter, quarter)
    for p, (scr, out) in enumerate(zip(w_scr, (q_ref, k_ref, v_ref))):
        out[...] = own_cols(nn(normed, scr[...])).astype(BF)
        wrow_ref[:, p * cols : (p + 1) * cols] = own_cols(
            scr[pl.ds(at, quarter), :].astype(F32)
        ).astype(BF)
    vals_t = v_ref[...].T
    pv_t = pv_ref[...].astype(F32).T.astype(BF)
    tab, tab2 = (
        ref[TABLE_ROW : TABLE_ROW + own_buckets, :LANES].astype(F32) for ref in (small, small2)
    )
    ids = lax.broadcasted_iota(jnp.int32, (own_buckets, 2 * length), 0)
    lines = tn(tab, (ids + wt * own_buckets == bucket_row[...]).astype(F32))
    lines = lines + tn(
        tab2, (ids + (1 - wt) * own_buckets == bucket_row[...]).astype(F32)
    )
    line_scr[...] = lines[: line_scr.shape[0]]
    for h in range(heads):
        part = slice(h * hsize, (h + 1) * hsize)
        query = q_ref[:, part]
        line = jnp.broadcast_to(line_scr[pl.ds(here * heads + h, 1), :], (LANES, 2 * length))
        spread = pltpu.roll(line, 0, 1, stride=1, stride_axis=0)
        bias = jnp.concatenate(
            [spread[:, length - at : 2 * length - at] for at in range(0, length, LANES)], axis=0
        )
        score = nt(k_ref[:, part], query) + bias
        front = nt(pk_ref[:, part], query)
        top = jnp.maximum(
            jnp.max(score, axis=0, keepdims=True), jnp.max(front, axis=0, keepdims=True)
        )
        score = jnp.exp(score - top)
        front = jnp.exp(front - top)
        total = jnp.sum(score, axis=0, keepdims=True) + jnp.sum(front, axis=0, keepdims=True)
        scale = 1.0 / total
        prob = (score * scale).astype(BF)
        prob_mem = (front * scale).astype(BF)
        pt_ref[h] = prob
        pm_ref[h] = prob_mem
        mix_ref[part, :] = nn(vals_t[part, :], prob) + nn(pv_t[part, :], prob_mem)
    att_scr[...] = mix_ref[...].T.astype(BF)
    for step in range(4):
        at = pl.multiple_of((here ^ step) * rows, rows)
        outs[step][...] = att_scr[pl.ds(at, rows), :]


def hidden_kernel(idx, *refs):
    wo, wo2 = refs[:2]
    parts = refs[2:6]
    x, small, small2 = refs[6:9]
    hidden_ref, n2_ref, att_ref, wo_ref, sems = refs[9:]
    here, wt = idx[1], idx[2]
    cols = parts[0].shape[1]
    half = wo.shape[0]
    copies = fetch_rows(sems, wt, [(wo_ref, wo, wo2)])
    for step in range(4):
        att_ref[here ^ step] = parts[step][...]
    for copy in copies:
        copy.wait()
    hidden = x[...].astype(F32)
    for c in range(4):
        hidden = hidden + nn(att_ref[c], wo_ref[c * cols : (c + 1) * cols, :])
    hidden_ref[...] = hidden
    scaled, _ = norm(hidden)
    n2_ref[...] = (scaled * both_gains(wt, small, small2, 1)).astype(BF)


def gelu_parts(v):
    scale = 0.7978845608028654
    square = v * v
    t = jnp.tanh(scale * v * (1.0 + 0.044715 * square))
    grad = 0.5 * (1.0 + t) + 0.5 * v * (1.0 - t * t) * scale * (1.0 + 0.134145 * square)
    return 0.5 * v * (1.0 + t), grad


def own_columns(batch, ff_own, block):
    return [pl.ds(pl.multiple_of(o * ff_own + batch * block, block), block) for o in range(2)]


def ffn_kernel(idx, *refs):
    w1, w1b, w2, w2b = refs[:4]
    n2s, gs = refs[4:8], refs[8:12]
    norms = refs[12:16]
    act_ref, gi_ref, w2_ref, w1_scr, sems = refs[16:]
    batch, wt = idx[0], idx[2]
    half = w1.shape[0]
    block = w1_scr.shape[1] // 2
    ff_own = w2.shape[0]
    copies = []
    for j, (source, place) in enumerate(((w1, wt), (w1b, 1 - wt))):
        to = pl.ds(pl.multiple_of(place * half, half), half)
        for o, cut in enumerate(own_columns(batch, ff_own, block)):
            copies.append(
                pltpu.make_async_copy(
                    source.at[:, cut],
                    w1_scr.at[to, o * block : (o + 1) * block],
                    sems.at[2 * j + o],
                )
            )
    cut = pl.ds(pl.multiple_of(batch * block, block), block)
    for j, (source, place) in enumerate(((w2, wt), (w2b, 1 - wt))):
        to = pl.ds(pl.multiple_of(place * block, block), block)
        copies.append(pltpu.make_async_copy(source.at[cut, :], w2_ref.at[to, :], sems.at[4 + j]))
    for copy in copies:
        copy.start()
    for copy in copies[:4]:
        copy.wait()
    rows = n2s[0].shape[0]
    for s in range(4):
        at = slice(s * rows, (s + 1) * rows)
        act, slope = gelu_parts(nn(n2s[s][...], w1_scr[...]))
        if s == 0:
            for copy in copies[4:]:
                copy.wait()
        act_ref[at, :] = act.astype(BF)
        grad = (nt(gs[s][...], w2_ref[...]).astype(BF).astype(F32) * slope).astype(BF)
        gi_ref[at, :] = grad
        norms[s][...] = nt(grad, w1_scr[...]).astype(BF)


def ffn_back_kernel(idx, *refs):
    n2s, gs = refs[:4], refs[4:8]
    act, gi = refs[8:10]
    mine, theirs, all_scr, scr = refs[10:]
    here, wt = idx[1], idx[2]
    rows = n2s[0].shape[0]
    size = scr.shape[0] // 8

    def spread(p):
        for i, out in enumerate((mine, theirs)):
            for j, place in enumerate(NEAR_LAST):
                at = pl.multiple_of(((wt ^ i) * 4 + (here ^ place)) * size, size)
                to = (4 * (j // 2) + 2 * p + j % 2) * size
                out[to : to + size, :] = scr[pl.ds(at, size), :]

    for s in range(4):
        all_scr[s * rows : (s + 1) * rows, :] = n2s[s][...]
    scr[...] = tn(all_scr[...], gi[...]).astype(BF)
    spread(0)
    for s in range(4):
        all_scr[s * rows : (s + 1) * rows, :] = gs[s][...]
    scr[...] = tn(act[...], all_scr[...]).astype(BF)
    spread(1)


def hidden_back_kernel(idx, *refs):
    parts = refs[:4]
    hidden_ref, small, small2, g, wo = refs[4:9]
    grad_ref, low_ref = refs[9:11]
    outs = refs[11:]
    here, wt = idx[1], idx[2]
    cols = outs[0].shape[1]
    half = wo.shape[0] // 2
    grad_norm = parts[0][...].astype(F32)
    for part in parts[1:]:
        grad_norm = grad_norm + part[...].astype(F32)
    scaled, inverse = norm(hidden_ref[...])
    e = grad_norm * both_gains(wt, small, small2, 1)
    grad = g[...].astype(F32) + inverse * (
        e - scaled * jnp.mean(e * scaled, axis=-1, keepdims=True)
    )
    grad_ref[...] = grad
    low = grad.astype(BF)
    low_ref[...] = low
    for step in range(4):
        at = pl.multiple_of((here ^ step) * cols, cols)
        outs[step][...] = nt(low, wo[pl.ds(at, cols), :]).astype(BF)


def wo_back_kernel(idx, att, low, act, w2, mine, theirs, keep, send, scr):
    rows = low.shape[0]
    batch, here, wt = idx[0], idx[1], idx[2]
    size = att.shape[2]
    for c in range(4):
        scr[c * size : (c + 1) * size, :] = tn(att[c], low[...])
    size = scr.shape[0] // 32
    for i, out in enumerate((mine, theirs)):
        for q, far in enumerate(NEAR_LAST):
            for p, place in enumerate(NEAR_LAST):
                at = (((wt ^ i) * 4 + (here ^ place)) * 4 + (batch ^ far)) * size
                to = (4 * q + p) * size
                out[to : to + size, :] = scr[pl.ds(pl.multiple_of(at, 8), size), :].astype(BF)
    for s, (out, to) in enumerate(((keep, 0), (keep, rows), (send, 0), (send, rows))):
        out[to : to + rows, :] = nn(act[s * rows : (s + 1) * rows, :], w2[...]).astype(BF)


def heads_back_kernel(heads, hsize, idx, *refs):
    gms = refs[:4]
    pt, pm, q, k, v, mix, pk, pv, bucket_row, n1 = refs[4:14]
    mine, theirs = refs[14:16]
    own_out, near_out, far_out = refs[16:19]
    gm_scr, gqt_scr, acc, grad_scr, w_scr = refs[19:]
    batch, here, wt = idx[0], idx[1], idx[2]
    rows, cols = gms[0].shape
    length = 4 * rows
    mem = pk.shape[0]
    high = own_out.shape[0]
    outs = (own_out, far_out, near_out.at[:high], near_out.at[high:])
    for step in range(4):
        at = pl.multiple_of((here ^ step) * rows, rows)
        gm_scr[pl.ds(at, rows), :] = gms[step][...]
    gm_t = gm_scr[...].T
    keys_t = k[...].T
    pk_t = pk[...].astype(F32).T.astype(BF)
    lines = []
    for h in range(heads):
        part = slice(h * hsize, (h + 1) * hsize)
        gm = gm_scr[:, part]
        query = q[:, part]
        spread = jnp.sum(gm_t[part, :].astype(F32) * mix[part, :], axis=0, keepdims=True)
        prob = pt[h]
        prob_mem = pm[h]
        score = prob.astype(F32) * (nt(v[:, part], gm) - spread)
        front = (prob_mem.astype(F32) * (nt(pv[:, part], gm) - spread)).astype(BF)
        low = score.astype(BF)
        gqt_scr[part, :] = nn(keys_t[part, :], low) + nn(pk_t[part, :], front)
        grad_scr[1, :, part] = nn(low, query).astype(BF)
        grad_scr[2, :, part] = nn(prob, gm).astype(BF)
        mem_k = nn(front, query).astype(BF)
        mem_v = nn(prob_mem, gm).astype(BF)
        for step in range(4):
            outs[step][3 * rows + MEM_K : 3 * rows + MEM_K + mem, part] = mem_k
            outs[step][3 * rows + MEM_V : 3 * rows + MEM_V + mem, part] = mem_v
        acc[...] = jnp.zeros_like(acc)
        for at in range(0, length, LANES):
            acc[:, length - at : 2 * length - at] += score[at : at + LANES, :]
        fold = acc[...]
        size = LANES // 2
        while size >= 8:
            fold = fold[:size] + pltpu.roll(fold[size:], 2 * length - size, 1)
            size //= 2
        line = fold[0:1]
        for i in range(1, 8):
            line = line + pltpu.roll(fold[i : i + 1], 2 * length - i, 1)
        lines.append(line)
    grad_scr[0] = gqt_scr[...].T.astype(BF)
    normed = n1[...]
    for p in range(3):
        w_scr[:, p * cols : (p + 1) * cols] = tn(normed, grad_scr[p]).astype(BF)
    size = w_scr.shape[0] // 8
    for i, out in enumerate((mine, theirs)):
        for j, far in enumerate(NEAR_LAST):
            at = pl.multiple_of(((wt ^ i) * 4 + (batch ^ far)) * size, size)
            out[j * size : (j + 1) * size, :] = w_scr[pl.ds(at, size), :]
    lines.append(jnp.zeros((LINE - heads, 2 * length), F32))
    table = lax.dot_general(
        jnp.concatenate(lines, axis=0),
        one_hot_rows(bucket_row[...], LANES),
        (((1,), (1,)), ((), ())),
        precision=lax.Precision.HIGHEST,
        preferred_element_type=F32,
    )
    wide = w_scr.shape[1]
    table = jnp.concatenate([table, jnp.zeros((LINE, wide - LANES), F32)], axis=1)
    for out in (mine, theirs):
        out[4 * size :, :] = table.astype(BF)
    for step in range(4):
        at = pl.multiple_of((here ^ step) * rows, rows)
        for p in range(3):
            outs[step][p * rows : (p + 1) * rows, :] = grad_scr[p, pl.ds(at, rows), :]


def halving_kernel(lines, *refs):
    count = len(lines)
    for i, line in enumerate(lines):
        own, got = refs[2 * i], refs[2 * i + 1]
        keep, send = refs[2 * count + 2 * i], refs[2 * count + 2 * i + 1]
        total = (own[...].astype(F32) + got[...].astype(F32)).astype(BF)
        half = (total.shape[0] - line) // 2
        keep[:half, :] = total[:half]
        send[:half, :] = total[half : 2 * half]
        if line:
            keep[half:, :] = total[2 * half :]
            send[half:, :] = total[2 * half :]


def halving(name, items):
    args, out = [], []
    for own, got, line in items:
        args += [own, got]
        out += [shape(((own.shape[0] - line) // 2 + line, own.shape[1]), BF)] * 2
    return pl.pallas_call(
        functools.partial(halving_kernel, [line for _, _, line in items]),
        out_shape=out,
        in_specs=vmem(len(args)),
        out_specs=vmem(len(out)),
        compiler_params=params(32),
        name=name,
    )(*args)


def add_kernel(left, right, out):
    out[...] = (left[...].astype(F32) + right[...].astype(F32)).astype(BF)


def row_sums(values):
    return lax.dot_general(
        jnp.ones((8, values.shape[1]), F32),
        values,
        (((1,), (1,)), ((), ())),
        precision=lax.Precision.HIGHEST,
        preferred_element_type=F32,
    )


def add_swapped(out, own, got, half):
    for i in range(2):
        left = own[i * half : (i + 1) * half, :].astype(F32)
        right = got[(1 - i) * half : (2 - i) * half, :].astype(F32)
        out[i * half : (i + 1) * half, :] = (left + right).astype(BF)


def ffn_piece_kernel(idx, w_in, own, got, a_ref, b_ref, sum_ref, w_scr, sems):
    batch, here = idx[0], idx[1]
    quarter, width = w_scr.shape
    block = width // 2
    rows = pl.ds(pl.multiple_of(here * quarter, quarter), quarter)
    copies = [
        pltpu.make_async_copy(
            w_in.at[rows, cut], w_scr.at[:, o * block : (o + 1) * block], sems.at[o]
        )
        for o, cut in enumerate(own_columns(batch, w_in.shape[1] // 2, block))
    ]
    for copy in copies:
        copy.start()
    add_swapped(a_ref, own.at[: 2 * quarter], got.at[: 2 * quarter], quarter)
    add_swapped(b_ref, own.at[2 * quarter :], got.at[2 * quarter :], quarter)
    for copy in copies:
        copy.wait()
    sum_ref[...] = row_sums(a_ref[:quarter, :].astype(F32) * w_scr[...].astype(F32))


def heads_pair_kernel(size, height, own, got, out):
    rest = own.shape[0] - height
    out[:height, :] = own[:height, :]
    out[height:, :] = got[:height, :]
    for at, left, right in ((size, size, height), (height + size, height, size)):
        out[at : at + rest, :] = (
            own[left : left + rest, :].astype(F32) + got[right : right + rest, :].astype(F32)
        ).astype(BF)


def heads_piece_kernel(qkv, qkv2, wo, wo2, wrow, sum_in, piece_ref):
    size, width = wo.shape
    quarter = wrow.shape[0]
    wide = wrow.shape[1]
    heads = qkv[...].astype(F32) + qkv2[...].astype(F32)
    piece_ref[:quarter, :] = heads[:quarter].astype(BF)
    sum_heads = row_sums(heads[:quarter] * wrow[...].astype(F32))
    third = size // 3
    cols = width - wide
    for part, at in ((wo, quarter), (wo2, quarter + size + third + LINE)):
        piece_ref[at : at + size, :] = part[:, :wide]
        for o in range(3):
            piece_ref[at + size : at + size + third, o * cols : (o + 1) * cols] = part[
                o * third : (o + 1) * third, wide:
            ]
    row = lax.broadcasted_iota(jnp.int32, (LINE, quarter), 0)
    sums = jnp.where(row == LINE - 2, sum_heads, jnp.where(row == LINE - 1, sum_in[...], 0.0))
    at = quarter + size + third
    line = heads[quarter:]
    pad = jnp.zeros((LINE, LANES), F32)
    sums = jnp.concatenate([sums, jnp.zeros((LINE, LANES - quarter), F32)], axis=1)
    line = line + jnp.concatenate([pad, sums, jnp.zeros((LINE, wide - 2 * LANES), F32)], axis=1)
    piece_ref[at : at + LINE, :] = line.astype(BF)


def ctx_pieces(refs, at, order):
    one, two, four, one2, two2, four2 = refs
    rows = one.shape[0]
    size = rows // 2
    first = ((one, 0), (two, 0), (four, 0), (four, rows))
    last = ((one2, 0), (four2, 0), (two2, 0), (four2, rows))
    if order == 2:
        first = ((one, 0), (four, 0), (two, 0), (four, rows))
        last = ((one2, 0), (two2, 0), (four2, 0), (four2, rows))
    near, far = first[at], last[at]
    found = []
    for (ref, start), places in ((near, (0, 2)), (far, (1, 3))):
        for i, place in enumerate(places):
            found.append((place, ref, start + i * size, size))
    return found


def rows_out_kernel(idx, *refs):
    out, scr, sems = refs[6:]
    copies = []
    for at in range(4):
        for place, ref, start, size in ctx_pieces(refs[:6], at, 2):
            row = len(copies) * size
            scr[row : row + size, :] = ref[start : start + size, :].astype(F32)
            to = pl.multiple_of(((idx[0] ^ at) * 4 + (idx[1] ^ place)) * size, size)
            copies.append(
                pltpu.make_async_copy(
                    scr.at[row : row + size, :], out.at[pl.ds(to, size), :], sems.at[len(copies)]
                )
            )
            copies[-1].start()
    for copy in copies:
        copy.wait()


def cols_out_kernel(idx, *refs):
    out, scr, sems = refs[6:]
    copies = []
    block = scr.shape[1] // 2
    for at in range(4):
        for place, ref, start, size in ctx_pieces(refs[:6], at, 1):
            row = (len(copies) // 2) * size
            scr[row : row + size, :] = ref[start : start + size, :].astype(F32)
            to = pl.multiple_of((idx[1] ^ place) * size, size)
            for o in range(2):
                col = pl.multiple_of((4 * o + (idx[0] ^ at)) * block, block)
                copies.append(
                    pltpu.make_async_copy(
                        scr.at[row : row + size, o * block : (o + 1) * block],
                        out.at[pl.ds(to, size), pl.ds(col, block)],
                        sems.at[len(copies)],
                    )
                )
                copies[-1].start()
    for copy in copies:
        copy.wait()


def pieces_out(kernel, name, index, pieces, dims, copies):
    rows, width = pieces[0].shape
    return pl.pallas_call(
        kernel,
        out_shape=shape(dims, F32),
        in_specs=[smem()] + vmem(6),
        out_specs=pl.BlockSpec(memory_space=pltpu.HBM),
        scratch_shapes=[
            pltpu.VMEM((8 * rows, width), F32),
            pltpu.SemaphoreType.DMA((copies,)),
        ],
        compiler_params=params(16),
        name=name,
    )(index, *pieces)


def heads_out_kernel(heads, buckets, idx, *refs):
    small = refs[6]
    oq, ok, ov, oo, gain_one, gain_two, table, scr, lines, tab_scr = refs[7:]
    step = pl.program_id(0)
    quarter, width = oq.shape
    cols = width // 4
    wide = 3 * cols
    size = quarter // 4
    third = size // 3
    for at in range(4):

        @pl.when(step == at)
        def _():
            for place, ref, start, height in ctx_pieces(refs[:6], at, 1):
                scr[idx[1] ^ place] = ref[start : start + height, :]

    for c in range(4):
        part = scr[c].astype(F32)
        for o, out in enumerate((oq, ok, ov)):
            out[:, c * cols : (c + 1) * cols] = part[:quarter, o * cols : (o + 1) * cols]
        oo[c, 0, :, :wide] = part[quarter : quarter + size]
        for o in range(3):
            oo[c, 0, o * third : (o + 1) * third, wide:] = part[
                quarter + size : quarter + size + third, o * cols : (o + 1) * cols
            ]
        lines[idx[0] ^ step, c] = part[quarter + size + third :]

    @pl.when(step == 3)
    def _():
        seen = [[lines[b, c] for c in range(4)] for b in range(4)]
        take = slice(LANES, LANES + quarter)
        one = jnp.concatenate(
            [sum(seen[b][c][LINE - 2 : LINE - 1, take] for c in range(4)) for b in range(4)], axis=1
        )
        two = jnp.concatenate(
            [sum(seen[b][c][LINE - 1 : LINE, take] for b in range(4)) for c in range(4)], axis=1
        )
        gain_one[...] = (one / small[0:1, :].astype(F32))[0]
        gain_two[...] = (two / small[1:2, :].astype(F32))[0]
        rest = [seen[0][c][:heads, :LANES] for c in range(4)]
        rest.append(jnp.zeros((LANES - 4 * heads, LANES), F32))
        tab_scr[...] = jnp.concatenate(rest, axis=0).T
        own_buckets = buckets // 2
        at = pl.multiple_of(idx[2] * own_buckets, 8)
        table[...] = tab_scr[pl.ds(at, own_buckets), : 4 * heads]


def heads_out(index, pieces, small, width, heads, buckets):
    height, wide = pieces[0].shape[0] // 2, pieces[0].shape[1]
    part = width // 2
    quarter = part // 4
    size = quarter // 4
    block = pl.BlockSpec((quarter, width), lambda step, idx: (idx[0] ^ step, 0))
    whole = [pl.BlockSpec(p.shape, lambda step, idx: (0, 0)) for p in (*pieces, small)]
    return pl.pallas_call(
        functools.partial(heads_out_kernel, heads, buckets),
        out_shape=[shape((part, width), F32)] * 3
        + [
            shape((4, 4, size, width), F32),
            shape((part,), F32),
            shape((part,), F32),
            shape((buckets // 2, 4 * heads), F32),
        ],
        grid_spec=pltpu.PrefetchScalarGridSpec(
            num_scalar_prefetch=1,
            grid=(4,),
            in_specs=whole,
            out_specs=[block] * 3
            + [
                pl.BlockSpec((4, 1, size, width), lambda step, idx: (0, idx[0] ^ step, 0, 0)),
                pl.BlockSpec((part,), lambda step, idx: (0,)),
                pl.BlockSpec((part,), lambda step, idx: (0,)),
                pl.BlockSpec((buckets // 2, 4 * heads), lambda step, idx: (0, 0)),
            ],
            scratch_shapes=[
                pltpu.VMEM((4, height, wide), BF),
                pltpu.VMEM((4, 4, LINE, wide), F32),
                pltpu.VMEM((LANES, LANES), F32),
            ],
        ),
        compiler_params=params(32),
        name="heads_out",
    )(index, *pieces, small)


def paired(
    inputs,
    prefix_keys,
    prefix_values,
    gain_attn,
    w_query,
    w_key,
    w_value,
    w_out,
    bias_table,
    gain_ffn,
    w_in,
    w_back,
    buckets,
    out_grad,
):
    b, c, w = lax.axis_index("batch"), lax.axis_index("ctx"), lax.axis_index("wt")
    index = jnp.stack([b, c, w])
    x, g = inputs[0], out_grad[0]
    rows, width = x.shape
    all_heads = bias_table.shape[1]
    heads = all_heads // 4
    hsize = width // all_heads
    cols = heads * hsize
    wide = 3 * cols
    mem = prefix_keys.shape[1]
    length = 4 * rows
    part = width // 2
    quarter = part // 4
    ff_own = w_back.shape[0]
    ff_part = ff_own // 4
    nbuck = 2 * bias_table.shape[0]

    def over_wt(value, name):
        with jax.named_scope(name + "_w"):
            return flip(value, "wt", 2, 1)

    def over_ctx(value, step, name):
        with jax.named_scope(name + "_z" + str(step)):
            return flip(value, "ctx", 4, step)

    def over_batch(value, step, name):
        with jax.named_scope(name + "_b" + str(step)):
            return flip(value, "batch", 4, step)

    own_buckets = nbuck // 2
    small = jnp.concatenate(
        [
            jnp.pad(jnp.stack([gain_attn, gain_ffn]), ((0, TABLE_ROW - 2), (0, 0))),
            jnp.pad(bias_table, ((0, 0), (0, part - all_heads))),
        ]
    )
    w_query2, w_key2, w_value2 = [over_wt(v, "weight") for v in (w_query, w_key, w_value)]
    small2 = over_wt(small, "small")
    g_near = over_batch(g, 1, "g")
    x_all = lax.all_gather(x, "ctx", axis=0, tiled=True)
    bucket_row = jnp.pad(buckets[::-1].reshape(1, -1), ((0, 0), (1, 0)), constant_values=-1)

    tokens = shape((length, cols), BF)
    few = (small, small2, prefix_keys[0], prefix_values[0], bucket_row)
    (n1, q, k, v, pt, pm, mix, wrow, pk, pv, *mixed) = call(
        functools.partial(heads_kernel, heads, hsize, own_buckets),
        "attend",
        index,
        [x_all],
        [shape((length, width), BF)]
        + [tokens] * 3
        + [
            shape((heads, length, length), BF),
            shape((heads, mem, length), BF),
            shape((cols, length), F32),
            shape((quarter, wide), BF),
            shape((mem, cols), BF),
            shape((mem, cols), BF),
        ]
        + [shape((rows, cols), BF)] * 4,
        [
            pltpu.VMEM((length, cols), BF),
            pltpu.VMEM((16, 2 * length), F32),
            pltpu.SemaphoreType.DMA((6,)),
            pltpu.SemaphoreType.DMA((len(few),)),
        ]
        + [pltpu.VMEM((width, -(-cols // LANES) * LANES), BF)] * 3
        + [pltpu.VMEM(v.shape, v.dtype) for v in few],
        far=(w_query, w_key, w_value, w_query2, w_key2, w_value2, *few),
    )
    (g_pair, w_out_sent) = after((jnp.concatenate([g, g_near]), w_out), mixed[:1])
    w_out2 = over_wt(w_out_sent, "weight")
    g_far = over_batch(g_pair, 2, "g")
    mixed = mixed[:1] + [over_ctx(mixed[s], s, "mixed") for s in range(1, 4)]
    (*mixed, w_out2, g_far) = after((*mixed, w_out2, g_far), ())
    square = shape((width, width), BF)
    hidden, n2, attended, wo = call(
        hidden_kernel,
        "hidden",
        index,
        [*mixed, x, small, small2],
        [shape((rows, width), F32), shape((rows, width), BF), shape((4, rows, cols), BF), square],
        [pltpu.SemaphoreType.DMA((2,))],
        far=(w_out, w_out2),
    )

    n2s = [n2] + [over_batch(n2, s, "n2") for s in range(1, 4)]
    (w_in_sent, w_back_sent) = after((w_in, w_back), (n2,))
    w_in2, w_back2 = over_wt(w_in_sent, "in"), over_wt(w_back_sent, "back")
    gs = (g, g_near, g_far[:rows], g_far[rows:])
    hid = shape((length, 2 * ff_part), BF)
    *norms, act, gi, w_second = call(
        ffn_kernel,
        "ffn",
        index,
        [*n2s, *gs],
        [shape((rows, width), BF)] * 4 + [hid, hid, shape((2 * ff_part, width), BF)],
        [pltpu.VMEM((width, 2 * ff_part), BF), pltpu.SemaphoreType.DMA((6,))],
        far=(w_in, w_in2, w_back, w_back2),
    )
    norms = norms[:1] + [over_batch(norms[s], s, "norm") for s in range(1, 4)]
    ffn, ffn_sent = call(
        ffn_back_kernel,
        "ffn_back",
        index,
        [*n2s, *gs, act, gi],
        [square, square],
        [pltpu.VMEM((length, width), BF), pltpu.VMEM((width, width), BF)],
    )
    ffn, ffn_sent = halving("ffn_wt", [(ffn, over_wt(ffn_sent, "ffn"), 0)])
    ffn_got = over_ctx(ffn_sent, 1, "ffn")
    norms = after(norms, (ffn, ffn_sent))
    grad_hidden, low, *gms = call(
        hidden_back_kernel,
        "hidden_back",
        index,
        [*norms, hidden, small, small2, g, wo],
        [shape((rows, width), F32), shape((rows, width), BF)] + [shape((rows, cols), BF)] * 4,
    )
    ffn = pl.pallas_call(
        add_kernel,
        out_shape=shape((part, width), BF),
        in_specs=vmem(2),
        out_specs=vmem(1)[0],
        compiler_params=params(16),
        name="ffn_near",
    )(ffn, ffn_got)
    gms = list(gms[:1]) + [over_ctx(gms[s], s, "gm") for s in range(1, 4)]
    (ffn_sent,) = after((ffn,), gms[1:])
    ffn_got = over_ctx(ffn_sent, 2, "ffn")
    high = 3 * rows + MEM_END
    (qkv, qkv_sent, own_block, near_blocks, far_block) = call(
        functools.partial(heads_back_kernel, heads, hsize),
        "attend_back",
        index,
        [*gms, pt, pm, q, k, v, mix, pk, pv, bucket_row, n1],
        [shape((part + LINE, wide), BF)] * 2
        + [shape((n * high, cols), BF) for n in (1, 2, 1)],
        [
            pltpu.VMEM((length, cols), BF),
            pltpu.VMEM((cols, length), F32),
            pltpu.VMEM((LANES, 2 * length), F32),
            pltpu.VMEM((3, length, cols), BF),
            pltpu.VMEM((width, wide), BF),
        ],
    )
    (low,) = after((low,), (qkv,))
    wo_sum, wo_sent, outs, outs_sent = call(
        wo_back_kernel,
        "wo_back",
        index,
        [attended, low, act, w_second],
        [shape((part, width), BF)] * 2 + [shape((2 * rows, width), BF)] * 2,
        [pltpu.VMEM((width, width), F32)],
    )
    outs_got = over_batch(outs_sent, 2, "outs")
    wo_sum, wo_sent = halving("wo_wt", [(wo_sum, over_wt(wo_sent, "wo"), 0)])
    wo_sum, wo_sent = halving("wo_near", [(wo_sum, over_batch(wo_sent, 1, "wo"), 0)])

    outs, outs_sent = halving("outs_far", [(outs, outs_got, 0)])
    (outs_sent, wo_sent) = after((outs_sent, wo_sent), (outs, wo_sum))
    wo_sum, wo_sent = halving("wo_far", [(wo_sum, over_batch(wo_sent, 2, "wo"), 0)])
    outs_got = over_batch(outs_sent, 1, "outs")
    qkv, qkv_sent = halving("qkv_wt", [(qkv, over_wt(qkv_sent, "qkv"), LINE)])
    qkv, qkv_sent = halving("qkv_near", [(qkv, over_batch(qkv_sent, 1, "qkv"), LINE)])
    qkv_got = over_batch(qkv_sent, 2, "qkv")
    (ffn_got,) = after((ffn_got,), (qkv_got, outs_got, wo_sum, wo_sent))
    a1, b1, sum_in = call(
        ffn_piece_kernel,
        "ffn_piece",
        index,
        [ffn, ffn_got],
        [shape((2 * quarter, width), BF)] * 2 + [shape((8, quarter), F32)],
        [pltpu.VMEM((quarter, width), BF), pltpu.SemaphoreType.DMA((2,))],
        far=(w_in,),
    )

    (wo_sent,) = after((wo_sent,), (a1,))
    wo_sum, wo_sent = halving("wo_last", [(wo_sum, over_ctx(wo_sent, 1, "wo"), 0)])
    def pile(one, two):
        return jnp.concatenate([one, two])

    result = (hidden + outs.astype(F32) + outs_got.astype(F32)).astype(BF)
    a2, b2 = over_batch(a1, 1, "in_near"), over_batch(b1, 2, "out_near")
    c1, d1 = over_ctx(a1, 1, "in_back"), over_ctx(b1, 1, "out_back")
    pile_a, pile_b = pile(a1, a2), pile(b1, b2)
    a3, b3 = over_batch(pile_a, 2, "in_near2"), over_batch(pile_b, 1, "out_near2")
    (c1, d1) = after((c1, d1), (pile_a, pile_b))
    c2, d2 = over_batch(c1, 2, "in_far"), over_batch(d1, 1, "out_far")
    height = quarter + quarter // 4 + quarter // 12 + LINE
    piece = pl.pallas_call(
        heads_piece_kernel,
        out_shape=shape((2 * height - quarter - LINE, wide), BF),
        in_specs=vmem(6),
        out_specs=vmem(1)[0],
        compiler_params=params(32),
        name="heads_piece",
    )(qkv, qkv_got, wo_sum, wo_sent, wrow, sum_in)

    (piece,) = after((piece,), (c1, d1))
    heads_far = over_ctx(piece, 2, "heads_back")
    pile_c, pile_d = pile(c1, c2), pile(d1, d2)
    c3, d3 = over_batch(pile_c, 1, "in_far2"), over_batch(pile_d, 2, "out_far2")
    (heads_far,) = after((heads_far,), (a3, b3))
    (near_blocks,) = after((near_blocks,), (heads_far,))
    near_got = over_ctx(near_blocks, 2, "sends")
    far_pile = pile(far_block, near_got[high:])
    far_got = over_ctx(far_pile, 1, "sends")
    e1 = pl.pallas_call(
        functools.partial(heads_pair_kernel, quarter, height),
        out_shape=shape((2 * height, wide), BF),
        in_specs=vmem(2),
        out_specs=vmem(1)[0],
        compiler_params=params(16),
        name="heads_pair",
    )(piece, heads_far)
    f1 = over_ctx(e1, 1, "heads_back")
    (e1, f1) = after((e1, f1), (pile_c, pile_d))
    e2, f2 = over_batch(e1, 1, "heads_near"), over_batch(f1, 2, "heads_far")
    (e1, e2, f1, f2) = after((e1, e2, f1, f2), (c3, d3, far_pile, result))
    e3 = over_batch(pile(e1, e2), 2, "heads_near2")
    f3 = over_batch(pile(f1, f2), 1, "heads_far2")
    out_second = pieces_out(
        rows_out_kernel, "rows_out", index, (b1, b2, b3, d1, d2, d3), (ff_own, width), 16
    )
    out_first = pieces_out(
        cols_out_kernel, "cols_out", index, (a1, a2, a3, c1, c2, c3), (part, 2 * ff_own), 32
    )
    out_q, out_k, out_v, out_wo, gain_one, gain_two, out_table = heads_out(
        index, (e1, e2, e3, f1, f2, f3), small, width, heads, nbuck
    )
    grad_x, grad_memk, grad_memv = call(
        input_end_kernel,
        "input_back",
        index,
        [own_block, near_got, far_got, x, small, small2, grad_hidden],
        [shape((rows, width), BF), shape((mem, width), F32), shape((mem, width), F32)],
        [pltpu.VMEM((4,) + own_block.shape, BF), pltpu.SemaphoreType.DMA((6,))]
        + [pltpu.VMEM((width, width), BF)] * 3,
        far=(w_query, w_key, w_value, w_query2, w_key2, w_value2),
    )
    return (
        result[None],
        grad_x[None],
        grad_memk[None],
        grad_memv[None],
        gain_one,
        gain_two,
        out_table,
        out_q,
        out_k,
        out_v,
        out_wo.reshape(part, width),
        out_first,
        out_second,
    )


def input_end_kernel(idx, *refs):
    wq, wk, wv, wq2, wk2, wv2 = refs[:6]
    own, near, far, x, small, small2, grad_hidden = refs[6:13]
    out_ref, memk_ref, memv_ref, scr, sems, *w_scr = refs[13:]
    high = own.shape[0]
    parts = (own, far.at[:high], near.at[:high], far.at[high:])
    here, wt = idx[1], idx[2]
    rows = x.shape[0]
    mem = memk_ref.shape[0]
    copies = fetch_rows(sems, wt, list(zip(w_scr, (wq, wk, wv), (wq2, wk2, wv2))))
    for step in range(4):
        scr[here ^ step] = parts[step][...]
    for copy in copies:
        copy.wait()

    def wide(at, count):
        return jnp.concatenate([scr[c, at : at + count, :] for c in range(4)], axis=1)

    grad_norm = sum(nt(wide(p * rows, rows), whole[...]) for p, whole in enumerate(w_scr))
    scaled, inverse = norm(x[...].astype(F32))
    e = grad_norm * both_gains(wt, small, small2, 0)
    grad = grad_hidden[...] + inverse * (
        e - scaled * jnp.mean(e * scaled, axis=-1, keepdims=True)
    )
    out_ref[...] = grad.astype(BF)
    memk_ref[...] = wide(3 * rows + MEM_K, mem).astype(F32)
    memv_ref[...] = wide(3 * rows + MEM_V, mem).astype(F32)


def solution(mesh):
    tokens = P(("batch", "wt"), "ctx", None)
    memory = P(("batch", "wt"), None, None)
    matrix = P("wt", None)
    vector = P("wt")
    sizes = (mesh.shape["batch"], mesh.shape["ctx"], mesh.shape["wt"])
    body = paired if sizes == (4, 4, 2) else functools.partial(general, sizes)
    return jax.shard_map(
        body,
        mesh=mesh,
        in_specs=(
            tokens, memory, memory, vector, matrix, matrix, matrix, matrix, matrix, vector,
            matrix, matrix, P(), tokens,
        ),
        out_specs=(
            tokens, tokens, memory, memory, vector, vector, matrix, matrix, matrix, matrix,
            matrix, matrix, matrix,
        ),
        check_vma=False,
    )
```
